32 devices in a mesh: dp: 8 (over z, x), tensor: 4 (over y, core).
Axes of the slice: x: 2, y: 2, z: 4, core: 2. Of those that a mesh axis runs over, the one named last changes fastest.
Arguments:
- inputs: bfloat16 [16, 1024, 768], P('dp'), may hold values from -6 to 6
- cotangent: bfloat16 [16, 1024, 768], P('dp', 'tensor'), may hold values from -6 to 6
- lengths: int32 [16], P('dp'), may hold values from 512 to 1024, as said below
- qkv_weight: bfloat16 [768, 3, 768], P(None, None, 'tensor'), may hold values from -0.21875 to 0.21875
- qkv_bias: bfloat16 [2, 768], P(None, 'tensor'), may hold values from -0.29882812 to 0.29882812
- out_weight: bfloat16 [768, 768], P('tensor'), may hold values from -4 to 4
- out_bias: bfloat16 [768], replicated, may hold values from -0.59765625 to 0.59765625
- first_gain: bfloat16 [768], replicated, may hold values from 0.5 to 1.5
- first_shift: bfloat16 [768], replicated, may hold values from -0.59765625 to 0.59765625
- up_weight: bfloat16 [768, 3072], P(None, 'tensor'), may hold values from -0.21875 to 0.21875
- up_bias: bfloat16 [3072], P('tensor'), may hold values from -0.59765625 to 0.59765625
- down_weight: bfloat16 [3072, 768], P('tensor'), may hold values from -0.109375 to 0.109375
- down_bias: bfloat16 [768], replicated, may hold values from -0.59765625 to 0.59765625
- second_gain: bfloat16 [768], replicated, may hold values from 0.5 to 1.5
- second_shift: bfloat16 [768], replicated, may hold values from -0.59765625 to 0.59765625
Outputs:
- outputs: bfloat16 [16, 1024, 768], P('dp', 'tensor')
- input_grad: bfloat16 [16, 1024, 768], P('dp', 'tensor')
- qkv_weight_grad: float32 [768, 3, 768], P('dp', None, 'tensor')
- qkv_bias_grad: float32 [2, 768], P(None, 'tensor')
- out_weight_grad: float32 [768, 768], P(('tensor', 'dp'))
- out_bias_grad: float32 [768], replicated
- first_gain_grad: float32 [768], replicated
- first_shift_grad: float32 [768], replicated
- up_weight_grad: float32 [768, 3072], P('dp', 'tensor')
- up_bias_grad: float32 [3072], P('tensor')
- down_weight_grad: float32 [3072, 768], P(('tensor', 'dp'))
- down_bias_grad: float32 [768], replicated
- second_gain_grad: float32 [768], replicated
- second_shift_grad: float32 [768], replicated
The draws below stay inside these ranges and needn't reach their ends.
Inputs may be any that keep to these rules, and one draw needn't show every extreme that they name: `lengths`: each sequence has at least half of 1024 valid slots; in every draw some sequence has all 1024 slots valid and some has exactly half of 1024.
All inputs are finite; a program needn't handle non-finite values.
Results may differ from the reference program's by a relative error of at most 0.018.
Values may be sent and summed in bfloat16 or wider, within the bound.
No kernel may reach another device: no remote copies, remote signals or barrier semaphores. Data moves between devices by JAX's collectives and lax.ppermute only.
A program may use at most 192 MiB of HBM per device.

```python
import jax
import jax.numpy as jnp
from jax import lax

D = 768
HEADS = 12
HEAD = 64
FF = 3072
SEQ = 1024
NSEQ = 16


def draw_lengths(key, part):
    first_key, second_key, third_key = jax.random.split(jax.random.fold_in(key, 11), 3)
    values = jax.random.randint(first_key, (NSEQ,), SEQ // 2, SEQ + 1)
    full_at = jax.random.randint(second_key, (), 0, NSEQ)
    half_at = (full_at + 1 + jax.random.randint(third_key, (), 0, NSEQ - 1)) % NSEQ
    positions = jnp.arange(NSEQ)
    values = jnp.where(positions == full_at, SEQ, values)
    values = jnp.where(positions == half_at, SEQ // 2, values)
    return values.astype(jnp.int32)


def shard_levels(own_key, dims, cuts, smallest, largest):
    def one(axis_at, parts):
        steps = jax.random.uniform(jax.random.fold_in(jax.random.fold_in(own_key, 6), axis_at), (parts,), jnp.float32, smallest / len(cuts), largest / len(cuts))
        return jnp.repeat(jnp.exp(steps), dims[axis_at] // parts).reshape((-1,) + (1,) * (len(dims) - axis_at - 1))

    loudness = one(*cuts[0])
    for cut in cuts[1:]:
        loudness = loudness * one(*cut)
    return loudness


def centred(stream_key, dims, width, limit, cuts=(), held_as=jnp.bfloat16):
    values = width * jax.random.normal(stream_key, dims, jnp.float32)
    if cuts:
        values = values * shard_levels(stream_key, dims, cuts, -0.22, 0.18)
    return jnp.clip(values, -limit, limit).astype(held_as)


def setup_inputs(seed: int = 0) -> dict:
    streams_of = jax.random.split(jax.random.key(seed), 16)
    return {
        "inputs": centred(streams_of[0], (NSEQ, SEQ, D), 1.0, 6.0, ((0, 8),)),
        "cotangent": centred(streams_of[1], (NSEQ, SEQ, D), 1.0, 6.0, ((0, 8), (1, 4))),
        "lengths": draw_lengths(jax.random.fold_in(streams_of[15], 71), 0),
        "qkv_weight": centred(streams_of[3], (D, 3, D), D ** -0.5, 0.21875, ((2, 4),)),
        "qkv_bias": centred(streams_of[4], (2, D), 0.05, 0.29882812, ((1, 4),)),
        "out_weight": centred(streams_of[5], (D, D), (max(1, D * 3 // SEQ)) ** -0.5, 4.0, ((0, 4),)),
        "out_bias": centred(streams_of[6], (D,), 0.1, 0.59765625),
        "first_gain": jnp.clip(1.0 + 0.1 * jax.random.normal(streams_of[7], (D,), jnp.float32), 0.5, 1.5).astype(jnp.bfloat16),
        "first_shift": centred(streams_of[8], (D,), 0.1, 0.59765625),
        "up_weight": centred(streams_of[9], (D, FF), D ** -0.5, 0.21875, ((1, 4),)),
        "up_bias": centred(streams_of[10], (FF,), 0.1, 0.59765625, ((0, 4),)),
        "down_weight": centred(streams_of[11], (FF, D), FF ** -0.5, 0.109375, ((0, 4),)),
        "down_bias": centred(streams_of[12], (D,), 0.1, 0.59765625),
        "second_gain": jnp.clip(1.0 + 0.1 * jax.random.normal(streams_of[13], (D,), jnp.float32), 0.5, 1.5).astype(jnp.bfloat16),
        "second_shift": centred(streams_of[14], (D,), 0.1, 0.59765625),
    }


@jax.custom_vjp
def low(v):
    return lax.optimization_barrier(v.astype(jnp.bfloat16)).astype(jnp.float32)

@jax.custom_vjp
def low_back(v):
    return v

def low_keep(v):
    return (low(v), None)

def low_pass(kept, grad):
    return (grad,)

def back_keep(v):
    return (v, None)

def back_low(kept, grad):
    return (low(grad),)
low.defvjp(low_keep, low_pass)
low_back.defvjp(back_keep, back_low)

def matmul(left, right):
    return jnp.dot(left, right, precision=lax.Precision.HIGHEST)

def norm_rows(values, gain_row, shift_row):
    center = values - lax.optimization_barrier(jnp.mean(values, axis=-1, keepdims=True))
    spread = lax.optimization_barrier(jnp.mean(center * center, axis=-1, keepdims=True))
    return center * lax.rsqrt(spread + 1e-12) * gain_row + shift_row

def attend(query_part, key_rows, value_rows, alive_cols):
    scores = jnp.einsum('bhd,shd->hbs', query_part, key_rows, precision=lax.Precision.HIGHEST) * (1.0 / 8.0 * 8.0 / jnp.sqrt(jnp.float32(HEAD)))
    scores = low_back(scores)
    scores = jnp.where(alive_cols[None, None, :], scores, -1e+30)
    row_max = lax.optimization_barrier(jnp.max(scores, axis=-1, keepdims=True))
    exp_scores = jnp.exp(scores - row_max)
    soft_probs = low(exp_scores / lax.optimization_barrier(jnp.sum(exp_scores, axis=-1, keepdims=True)))
    return jnp.einsum('hbs,shd->bhd', soft_probs, value_rows, precision=lax.Precision.HIGHEST)

def forward(tokens, alive_cols, qkv_weight, qkv_bias, out_weight, out_bias, first_gain, first_shift, up_weight, up_bias, down_weight, down_bias, second_gain, second_shift):
    projected = jnp.einsum('sd,dkc->skc', tokens, qkv_weight, precision=lax.Precision.HIGHEST)
    query_rows = low_back(low(projected[:, 0] + qkv_bias[0]))
    key_rows = low_back(low(projected[:, 1]))
    value_rows = low_back(low(projected[:, 2] + qkv_bias[1]))
    block_rows = min(512, SEQ)
    query_blocks = query_rows.reshape(SEQ // block_rows, block_rows, HEADS, HEAD)
    key_rows = key_rows.reshape(SEQ, HEADS, HEAD)
    value_rows = value_rows.reshape(SEQ, HEADS, HEAD)

    def one_block(query_part):
        return attend(query_part, key_rows, value_rows, alive_cols)
    context = lax.map(jax.checkpoint(one_block), query_blocks)
    context = low_back(low(context.reshape(SEQ, D)))
    attention = low_back(matmul(context, out_weight))
    first_norm = norm_rows(attention + out_bias + tokens, first_gain, first_shift)
    hidden = low_back(matmul(low(first_norm), up_weight) + up_bias)
    active = low(jax.nn.gelu(hidden, approximate=False))
    second_in = low_back(matmul(active, down_weight)) + down_bias + first_norm
    return norm_rows(second_in, second_gain, second_shift)

def reference(inputs, cotangent, lengths, qkv_weight, qkv_bias, out_weight, out_bias, first_gain, first_shift, up_weight, up_bias, down_weight, down_bias, second_gain, second_shift):
    weight_args = tuple((weight_arg.astype(jnp.float32) for weight_arg in (qkv_weight, qkv_bias, out_weight, out_bias, first_gain, first_shift, up_weight, up_bias, down_weight, down_bias, second_gain, second_shift)))
    positions = jnp.arange(SEQ).astype(jnp.int32)

    def one_sequence(totals, sequence):
        tokens, upstream, length = sequence
        alive_cols = positions < length.astype(jnp.int32)

        def inner_forward(token_values, *weight_values):
            return forward(token_values, alive_cols, *weight_values)
        result, pull_back = jax.vjp(inner_forward, tokens.astype(jnp.float32), *weight_args)
        seed_grad = jnp.where(alive_cols[:, None], upstream.astype(jnp.float32), 0.0)
        grads = pull_back(seed_grad)
        totals = tuple((total_sum + grad_part for total_sum, grad_part in zip(totals, grads[1:])))
        return (totals, (result.astype(jnp.bfloat16), grads[0].astype(jnp.bfloat16)))
    zero_sums = tuple((jnp.zeros_like(weight_arg) for weight_arg in weight_args))
    totals, (results, input_grads) = lax.scan(one_sequence, zero_sums, (inputs, cotangent, lengths))
    return (results, input_grads, totals[0], totals[1], totals[2], totals[3], totals[4], totals[5], totals[6], totals[7], totals[8], totals[9], totals[10], totals[11])
```

```python
import functools

import jax
import jax.numpy as jnp
from jax import lax
from jax.experimental import pallas as pl
from jax.experimental.pallas import tpu as pltpu
from jax.sharding import PartitionSpec as P

HEAD = 64
NT = (((1,), (1,)), ((), ()))
NN = (((1,), (0,)), ((), ()))
TN = (((0,), (0,)), ((), ()))
bf16 = jnp.bfloat16
f32 = jnp.float32
VM = pl.BlockSpec(memory_space=pltpu.VMEM)
SM = pl.BlockSpec(memory_space=pltpu.SMEM)
HB = pl.BlockSpec(memory_space=pl.ANY)


def mm(a, b, dims=NN):
    return lax.dot_general(a, b, dims, preferred_element_type=f32)


def head_cols(a,h):
    lane=lax.broadcasted_iota(jnp.int32,a.shape,1)
    return jnp.where((lane>=HEAD*h)&(lane<HEAD*(h+1)),a,jnp.zeros_like(a))

def fwd_kernel(info, x_ref, w_ref, b_ref, q_ref, k_ref, v_ref, lse_ref, c0, c1, c2, c3, vT_ref, *, which, peers, heads, block):
    length = info[which]
    me = info[2]
    x=x_ref[...]
    q=mm(x,w_ref[0],NT)+b_ref[0:1,:].astype(f32)
    q_ref[...]=q.astype(bf16)*jnp.asarray(0.125,bf16)
    k_ref[...]=mm(x,w_ref[1],NT).astype(bf16)
    v=(mm(x,w_ref[2],NT)+b_ref[1:2,:].astype(f32)).astype(bf16)
    v_ref[...]=v
    vT_ref[...]=v.T
    seq=x.shape[0]
    outs=(c0,c1,c2,c3)
    for s in range(peers):
        at=(me^s)*block
        at=pl.multiple_of(at,block)
        qb=q_ref[pl.ds(at,block),:]
        parts=[]
        for h in range(heads):
            sT=mm(k_ref[...],head_cols(qb,h),NT)
            row=lax.broadcasted_iota(jnp.int32,sT.shape,0)
            sT=jnp.where(row<length,sT,-1e30)
            m=jnp.max(sT,axis=0,keepdims=True)
            p=jnp.exp(sT-m)
            l=jnp.sum(p,axis=0,keepdims=True)
            c=mm(vT_ref[HEAD*h:HEAD*(h+1),:],p.astype(bf16))
            parts.append(c*(1.0/l))
            lse_ref[s,h:h+1,:]=m+jnp.log(l)
        ctxT=jnp.concatenate(parts,axis=0)
        outs[s][...]=ctxT.T.astype(bf16)

def attend_fwd(which,info,x,wT,bias,peers=4):
    seq,D=x.shape; width=wT.shape[1]; heads=width//HEAD; block=seq//peers
    outs=[jax.ShapeDtypeStruct((seq,width),bf16)]*3+[jax.ShapeDtypeStruct((peers,8,block),f32)]+[jax.ShapeDtypeStruct((block,width),bf16)]*peers
    return pl.pallas_call(functools.partial(fwd_kernel,which=which,peers=peers,heads=heads,block=block),
        out_shape=outs,
        in_specs=[SM,VM,VM,VM],
        out_specs=[VM]*len(outs),
        scratch_shapes=[pltpu.VMEM((width,seq),bf16)],
        compiler_params=pltpu.CompilerParams(vmem_limit_bytes=48<<20),
        cost_estimate=pl.CostEstimate(flops=2*seq*D*3*width+4*seq*seq*width*4,bytes_accessed=seq*D*2+8*seq*width*2,transcendentals=heads*seq*seq),
        name="attend_fwd")(info,x,wT,bias)

def bwd_kernel(info, x_ref, w_ref, q_ref, k_ref, v_ref, lse_ref, *rest, which, peers, heads, block, first):
    cs=rest[:peers]; gs=rest[peers:2*peers]; rest=rest[2*peers:]
    if not first:
        pw_ref,pb_ref=rest[:2]; rest=rest[2:]
    p_refs=rest[:peers]; dw_ref,db_ref,dqT,dk,dv,kT,low=rest[peers:]
    length = info[which]
    me = info[2]
    kT[...]=k_ref[...].T
    dk[...]=jnp.zeros_like(dk); dv[...]=jnp.zeros_like(dv)
    for s in range(peers):
        at=pl.multiple_of((me^s)*block,block)
        live=at<length
        @pl.when(jnp.logical_not(live))
        def _():
            dqT[:,pl.ds(at,block)]=jnp.zeros((dqT.shape[0],block),f32)
        @pl.when(live)
        def _():
            qb=q_ref[pl.ds(at,block),:]
            g=gs[s][...]
            prodT=(g.astype(f32)*cs[s][...].astype(f32)).T
            for h in range(heads):
                rows=slice(HEAD*h,HEAD*(h+1))
                qh=head_cols(qb,h); gh=head_cols(g,h)
                sT=mm(k_ref[...],qh,NT)
                row=lax.broadcasted_iota(jnp.int32,sT.shape,0)
                pT=jnp.where(row<length,jnp.exp(sT-lse_ref[s,h:h+1,:]),0.0)
                dpT=mm(v_ref[...],gh,NT)
                inner=jnp.sum(prodT[rows],axis=0,keepdims=True)
                dsT=(pT*(dpT-inner)).astype(bf16)
                dv[...]+=mm(pT.astype(bf16),gh)
                dk[...]+=mm(dsT,qh)
                dqT[rows,pl.ds(at,block)]=mm(kT[rows,:],dsT)*0.125
    low[0]=dqT[...].T.astype(bf16)
    low[1]=dk[...].astype(bf16); low[2]=dv[...].astype(bf16)
    xT=x_ref[...].T
    for i in range(3):
        w=mm(xT,low[i])
        dw_ref[i]=w if first else w+pw_ref[i]
    db=jnp.concatenate([jnp.sum(low[i].astype(f32),axis=0,keepdims=True) for i in (0,2)],axis=0)
    db_ref[...]=db if first else db+pb_ref[...]
    for s in range(peers):
        at=pl.multiple_of((me^s)*block,block)
        tot=sum(mm(low[i,pl.ds(at,block),:],w_ref[i]) for i in range(3))
        p_refs[s][...]=tot.astype(bf16)

def attend_bwd(which,info,x,wT,q,k,v,lse,cs,gs,prev=None):
    peers=len(cs)
    seq,D=x.shape; width=wT.shape[1]; heads=width//HEAD; block=seq//peers
    outs=[jax.ShapeDtypeStruct((block,D),bf16)]*peers+[jax.ShapeDtypeStruct((3,D,width),f32),jax.ShapeDtypeStruct((2,width),f32)]
    args=[x,wT,q,k,v,lse,*cs,*gs]+([] if prev is None else list(prev))
    return pl.pallas_call(functools.partial(bwd_kernel,which=which,peers=peers,heads=heads,block=block,first=prev is None),
        out_shape=outs,
        in_specs=[SM]+[VM]*len(args),
        out_specs=[VM]*len(outs),
        scratch_shapes=[pltpu.VMEM((width,seq),f32),pltpu.VMEM((seq,width),f32),pltpu.VMEM((seq,width),f32),pltpu.VMEM((width,seq),bf16),pltpu.VMEM((3,seq,width),bf16)],
        compiler_params=pltpu.CompilerParams(vmem_limit_bytes=52<<20),
        cost_estimate=pl.CostEstimate(flops=4*seq*D*3*width+10*seq*seq*width*4,bytes_accessed=seq*D*4+12*seq*width*2,transcendentals=heads*seq*seq),
        name="attend_bwd")(info,*args)


def gelu_parts(h):
    z = jnp.abs(h) * 0.7071067811865476
    t = 1.0 / (1.0 + 0.3275911 * z)
    poly = t * (0.254829592 + t * (-0.284496736 + t * (1.421413741 + t * (-1.453152027 + t * 1.061405429))))
    bell = jnp.exp(-0.5 * h * h)
    tail = 0.5 * poly * bell
    phi_cum = jnp.where(h < 0, tail, 1.0 - tail)
    return h * phi_cum, phi_cum + h * (bell * 0.3989422804014327)


def mlp_first_kernel(xs, par, *rest, peers, batch, width):
    cs = rest[: batch * peers]
    packs = rest[batch * peers : batch * peers + peers]
    up0, up1, dn0, dn1 = rest[batch * peers + peers : batch * peers + peers + 4]
    nv1, r1, low, act, slope, acc = rest[batch * peers + peers + 4 :]
    rows = xs.shape[1]
    for s in range(batch):
        here = slice(s * rows, (s + 1) * rows)
        total = par[0:1, :] + xs[s].astype(f32)
        for k in range(peers):
            total = total + mm(cs[s * peers + k][...], packs[k][0:width, :])
        center = total - jnp.mean(total, axis=1, keepdims=True)
        r = lax.rsqrt(jnp.mean(center * center, axis=1, keepdims=True) + 1e-12)
        nv = center * r
        nv1[here] = nv
        r1[here] = r
        low[here] = (nv * par[1:2, :] + par[2:3, :]).astype(bf16)
    for k, (up, dn) in enumerate(((up0, dn0), (up1, dn1))):
        mlp_up(k, low, up, packs[k], width, act.at[k], slope.at[k])
        part = mm(act[k], dn[...])
        acc[...] = part if k == 0 else acc[...] + part


def mlp_up(k, low, up, pack, width, act, slope):
    units = up.shape[1]
    step = 256
    for n in range(0, units, step):
        cols = slice(n, n + step)
        hidden = mm(low[...], up[:, cols]) + pack[width : width + 1, cols].astype(f32)
        a, g = gelu_parts(hidden)
        act[:, cols] = a.astype(bf16)
        slope[:, cols] = g.astype(bf16)


def mlp_first(xs, par, cs, packs, ups, dns):
    batch, rows, d = xs.shape
    peers = len(packs)
    width = cs[0].shape[1]
    n = batch * rows
    units = ups[0].shape[1]
    args = [xs, par, *cs, *packs, *ups, *dns]
    outs = [
        jax.ShapeDtypeStruct((n, d), f32),
        jax.ShapeDtypeStruct((n, 1), f32),
        jax.ShapeDtypeStruct((n, d), bf16),
        jax.ShapeDtypeStruct((2, n, units), bf16),
        jax.ShapeDtypeStruct((2, n, units), bf16),
        jax.ShapeDtypeStruct((n, d), f32),
    ]
    return pl.pallas_call(
        functools.partial(mlp_first_kernel, peers=peers, batch=batch, width=width),
        out_shape=outs,
        in_specs=[VM] * len(args),
        out_specs=[VM] * len(outs),
        compiler_params=pltpu.CompilerParams(vmem_limit_bytes=48 << 20),
        cost_estimate=pl.CostEstimate(
            flops=2 * n * d * (d + 4 * units), bytes_accessed=12 << 20, transcendentals=4 * n * units
        ),
        name="mlp_first",
    )(*args)


def mlp_second_kernel(info, cot, par, nv1, r1, low, act01, slope01, acc, *rest, batch, width):
    packs = rest[:4]
    up0, up1, dn0, dn1, u2a, u2b, d2a, d2b, u3a, u3b, d3a, d3b = rest[4:16]
    outs, act23, gh, gs_low, gfi, ga_low, g0, g1, g2, g3, small, ups, dns, slope23, gsec, sem = rest[16:]
    half = u2a.shape[0]
    first = pl.multiple_of(info[3] * half, half)
    second = pl.multiple_of((1 - info[3]) * half, half)
    copies = []

    def fetch(src, dst):
        c = pltpu.make_async_copy(src, dst, sem.at[len(copies)])
        c.start()
        copies.append(c)

    for k, (ua, ub, da, db) in ((2, (u2a, u2b, d2a, d2b)), (3, (u3a, u3b, d3a, d3b))):
        fetch(ua, ups.at[k, pl.ds(first, half)])
        fetch(ub, ups.at[k, pl.ds(second, half)])
        fetch(da, dns.at[k, pl.ds(first, half)])
        fetch(db, dns.at[k, pl.ds(second, half)])
    fetch(dn0, dns.at[0])
    fetch(dn1, dns.at[1])
    fetch(up0, ups.at[0])
    fetch(up1, ups.at[1])
    n, d = low.shape
    rows = n // batch
    units = ups.shape[2]
    for i, k in enumerate((2, 3)):
        copies[4 * i].wait()
        copies[4 * i + 1].wait()
        mlp_up(k, low, ups.at[k], packs[k], width, act23.at[i], slope23.at[i])
        copies[4 * i + 2].wait()
        copies[4 * i + 3].wait()
        acc2 = mm(act23[i], dns[k])
        gsec[...] = (acc[...] if i == 0 else gsec[...]) + acc2
    sums = [0.0] * 3
    for s in range(batch):
        here = slice(s * rows, (s + 1) * rows)
        total = gsec[here] + par[3:4, :] + (nv1[here] * par[1:2, :] + par[2:3, :])
        center = total - jnp.mean(total, axis=1, keepdims=True)
        r = lax.rsqrt(jnp.mean(center * center, axis=1, keepdims=True) + 1e-12)
        nv = center * r
        outs[s] = (nv * par[4:5, :] + par[5:6, :]).astype(bf16)
        at = info[2] * rows + lax.broadcasted_iota(jnp.int32, (rows, 1), 0)
        seed = jnp.where(at < info[s], cot[s].astype(f32), 0.0)
        sums[0] += jnp.sum(seed * nv, axis=0, keepdims=True)
        sums[1] += jnp.sum(seed, axis=0, keepdims=True)
        gu = seed * par[4:5, :]
        g = r * (gu - jnp.mean(gu, axis=1, keepdims=True) - nv * jnp.mean(gu * nv, axis=1, keepdims=True))
        sums[2] += jnp.sum(g, axis=0, keepdims=True)
        gsec[here] = g
        gs_low[here] = g.astype(bf16)
    small[...] = jnp.zeros_like(small)
    small[4:5, :] = sums[0]
    small[5:6, :] = sums[1]
    small[3:4, :] = sums[2]
    for c in copies[8:]:
        c.wait()
    step = 256
    for k in range(4):
        slope = slope01.at[k] if k < 2 else slope23.at[k - 2]
        for m in range(0, units, step):
            cols = slice(m, m + step)
            ga = mm(gs_low[...], dns[k, cols, :], NT)
            h = (ga * slope[:, cols].astype(f32)).astype(bf16)
            gh[k, :, cols] = h
            small[8 + k : 9 + k, cols] = jnp.sum(h.astype(f32), axis=0, keepdims=True)
        gsec[...] += mm(gh[k], ups[k], NT)
    sums = [0.0] * 3
    for s in range(batch):
        here = slice(s * rows, (s + 1) * rows)
        u = gsec[here]
        nv = nv1[here]
        sums[0] += jnp.sum(u * nv, axis=0, keepdims=True)
        sums[1] += jnp.sum(u, axis=0, keepdims=True)
        gu = u * par[1:2, :]
        g = r1[here] * (gu - jnp.mean(gu, axis=1, keepdims=True) - nv * jnp.mean(gu * nv, axis=1, keepdims=True))
        sums[2] += jnp.sum(g, axis=0, keepdims=True)
        gfi[here] = g
        low_g = g.astype(bf16)
        ga_low[here] = low_g
        for k, out in enumerate((g0, g1, g2, g3)):
            out[s] = mm(low_g, packs[k][0:width, :], NT).astype(bf16)
    small[1:2, :] = sums[0]
    small[2:3, :] = sums[1]
    small[0:1, :] = sums[2]


def mlp_second(info, cot, par, state, packs, weights):
    batch, rows, d = cot.shape
    n = batch * rows
    units = weights[0].shape[1]
    width = 192 if False else packs[0].shape[0] - 8
    args = [info, cot, par, *state, *packs, *weights]
    outs = [
        jax.ShapeDtypeStruct((batch, rows, d), bf16),
        jax.ShapeDtypeStruct((2, n, units), bf16),
        jax.ShapeDtypeStruct((4, n, units), bf16),
        jax.ShapeDtypeStruct((n, d), bf16),
        jax.ShapeDtypeStruct((n, d), f32),
        jax.ShapeDtypeStruct((n, d), bf16),
        *[jax.ShapeDtypeStruct((batch, rows, width), bf16)] * 4,
        jax.ShapeDtypeStruct((16, d), f32),
    ]
    return pl.pallas_call(
        functools.partial(mlp_second_kernel, batch=batch, width=width),
        out_shape=outs,
        in_specs=[SM] + [VM] * (2 + len(state) + len(packs)) + [HB] * len(weights),
        out_specs=[VM] * len(outs),
        scratch_shapes=[
            pltpu.VMEM((4, d, units), bf16),
            pltpu.VMEM((4, units, d), bf16),
            pltpu.VMEM((2, n, units), bf16),
            pltpu.VMEM((n, d), f32),
            pltpu.SemaphoreType.DMA((12,)),
        ],
        compiler_params=pltpu.CompilerParams(vmem_limit_bytes=56 << 20),
        cost_estimate=pl.CostEstimate(
            flops=2 * n * d * (d + 12 * units), bytes_accessed=24 << 20, transcendentals=4 * n * units
        ),
        name="mlp_second",
    )(*args)


def down_grads_kernel(act01, act23, gs_low, ga_low, *rest, batch, parts):
    cs = rest[:-3]
    keep, send, scr = rest[-3:]
    peers = len(cs) // batch
    units = act01.shape[2]
    width = cs[0].shape[1]
    rows = ga_low.shape[0] // batch
    ub, wb = units // parts, width // parts
    for k in (1, 3, 0, 2):
        act = act01.at[k] if k < 2 else act23.at[k - 2]
        out = (send if k % 2 else keep).at[k // 2]
        scr[0:units, :] = mm(act[...], gs_low[...], TN)
        scr[units : units + width, :] = sum(
            mm(cs[s * peers + k][...], ga_low[s * rows : (s + 1) * rows, :], TN) for s in range(batch)
        )
        for b in range(parts):
            out[b, 0:ub, :] = scr[b * ub : (b + 1) * ub, :].astype(bf16)
            out[b, ub : ub + wb, :] = scr[units + b * wb : units + (b + 1) * wb, :].astype(bf16)


def down_grads(act01, act23, gs_low, ga_low, cs, parts, batch):
    _, n, units = act01.shape
    d = gs_low.shape[1]
    width = cs[0].shape[1]
    args = [act01, act23, gs_low, ga_low, *cs]
    outs = [jax.ShapeDtypeStruct((2, parts, (units + width) // parts, d), bf16)] * 2
    return pl.pallas_call(
        functools.partial(down_grads_kernel, batch=batch, parts=parts),
        out_shape=outs,
        in_specs=[VM] * len(args),
        out_specs=[VM] * 2,
        scratch_shapes=[pltpu.VMEM((units + width, d), f32)],
        compiler_params=pltpu.CompilerParams(vmem_limit_bytes=40 << 20),
        cost_estimate=pl.CostEstimate(
            flops=8 * n * d * (units + width), bytes_accessed=10 << 20, transcendentals=0
        ),
        name="down_grads",
    )(*args)


def up_grads_kernel(low, gh, keep, send):
    d = low.shape[1]
    step = 256
    for k in (1, 3, 0, 2):
        out = (send if k % 2 else keep).at[k // 2]
        for m in range(0, d, step):
            out[m : m + step, :] = mm(low[:, m : m + step], gh[k], TN).astype(bf16)


def up_grads(low, gh):
    n, d = low.shape
    units = gh.shape[2]
    outs = [jax.ShapeDtypeStruct((2, d, units), bf16)] * 2
    return pl.pallas_call(
        up_grads_kernel,
        out_shape=outs,
        in_specs=[VM] * 2,
        out_specs=[VM] * 2,
        compiler_params=pltpu.CompilerParams(vmem_limit_bytes=40 << 20),
        cost_estimate=pl.CostEstimate(flops=8 * n * d * units, bytes_accessed=10 << 20, transcendentals=0),
        name="up_grads",
    )(low, gh)


def swap(x, axis, bit):
    size = lax.axis_size(axis)
    return lax.ppermute(x, axis, [(i, i ^ bit) for i in range(size)])


def summed(parts):
    return sum(p.astype(f32) for p in parts)


def spread(array, axis, parts):
    bits = parts.bit_length() - 1
    return array.reshape(*array.shape[:axis], *([2] * bits), *array.shape[axis + 1 :])


def halve(terms, axis, index, bit, mine):
    other = [lax.dynamic_index_in_dim(t, 1 - mine, axis, keepdims=False) for t in terms]
    kept = [lax.dynamic_index_in_dim(t, mine, axis, keepdims=False) for t in terms]
    return kept + [swap(summed(other).astype(bf16), "dp", bit)]


def body(
    inputs,
    cotangent,
    lengths,
    qkv_weight,
    qkv_bias,
    out_weight,
    out_bias,
    first_gain,
    first_shift,
    up_weight,
    up_bias,
    down_weight,
    down_bias,
    second_gain,
    second_shift,
):
    batch, seq, d = inputs.shape
    rows = cotangent.shape[1]
    width = out_weight.shape[0]
    parts = lax.axis_size("dp")
    bits = parts.bit_length() - 1
    t = lax.axis_index("tensor")
    dp = lax.axis_index("dp")
    bit_of = [(dp >> i) & 1 for i in range(bits)]
    info = jnp.stack([lengths[0], lengths[1], t, bit_of[0]]).astype(jnp.int32)
    par = jnp.stack([out_bias, first_gain, first_shift, down_bias, second_gain, second_shift, out_bias, out_bias])
    par = par.astype(f32)
    w_t = jnp.transpose(qkv_weight, (1, 2, 0))
    pack = jnp.concatenate([out_weight, up_bias[None], jnp.zeros((7, d), bf16)], axis=0)
    half = d // 2
    up_half = lax.dynamic_index_in_dim(up_weight.reshape(2, half, d), bit_of[0], 0, keepdims=False)
    dn_half = lax.dynamic_index_in_dim(down_weight.reshape(2, half, d), bit_of[0], 0, keepdims=False)
    pack2 = swap(pack, "tensor", 2)
    u2a = swap(up_half, "tensor", 2)
    d2a = swap(dn_half, "tensor", 2)
    pack1 = swap(pack, "tensor", 1)
    up1 = swap(up_weight, "tensor", 1)
    dn1 = swap(down_weight, "tensor", 1)
    u2b = swap(u2a, "dp", 1)
    d2b = swap(d2a, "dp", 1)
    pack3 = swap(pack2, "tensor", 1)
    u3a, u3b, d3a, d3b = [swap(x, "tensor", 1) for x in (u2a, u2b, d2a, d2b)]
    packs = [pack, pack1, pack2, pack3]
    shares = lax.dynamic_slice_in_dim(inputs, t * rows, rows, 1)
    saved = []
    ctx = []
    for s in range(batch):
        q, k, v, lse, *cs = attend_fwd(s, info, inputs[s], w_t, qkv_bias)
        got = [cs[0]] + [swap(cs[j], "tensor", j) for j in (1, 2, 3)]
        saved.append((q, k, v, lse, cs))
        ctx.extend(got)
    nv1, r1, low, act01, slope01, acc = mlp_first(
        shares, par, ctx, packs, [up_weight, up1], [down_weight, dn1]
    )
    outputs, act23, gh, gs_low, gfi, ga_low, g0, g1, g2, g3, small = mlp_second(
        info,
        cotangent,
        par,
        (nv1, r1, low, act01, slope01, acc),
        packs,
        [up_weight, up1, down_weight, dn1, u2a, u2b, d2a, d2b, u3a, u3b, d3a, d3b],
    )
    gctx = [[g0[s]] + [swap(g[s], "tensor", j) for j, g in ((1, g1), (2, g2), (3, g3))] for s in range(batch)]
    dkeep, dsend = down_grads(act01, act23, gs_low, ga_low, ctx, parts, batch)
    ukeep, usend = up_grads(low, gh)
    got = swap(dsend, "tensor", 1)
    terms = halve([spread(dkeep, 1, parts), spread(got, 1, parts)], bits, 0, 1, bit_of[0])
    far = swap(summed([x[1] for x in terms]).astype(bf16), "tensor", 2)
    terms = [x[0] for x in terms] + [far]
    for i in range(1, bits):
        terms = halve(terms, bits - 1 - i, i, 1 << i, bit_of[i])
    down_sum = summed(terms)
    got = swap(usend, "tensor", 1)
    far = swap(summed([ukeep[1], got[1]]).astype(bf16), "tensor", 2)
    terms = [spread(x.reshape(parts, d // parts, -1), 0, parts) for x in (ukeep[0], got[0], far)]
    for i in range(bits):
        terms = halve(terms, bits - 1 - i, i, 1 << i, bit_of[i])
    up_sum = summed(terms)
    got = swap(jnp.concatenate([small[0:6], small[9:10], small[11:12]]), "tensor", 1)
    mine = jnp.concatenate([small[0:6], small[8:9], small[10:11]]) + got
    got = swap(jnp.concatenate([mine[0:6], mine[7:8]]), "tensor", 2)
    mine = mine[0:7] + got
    for i in range(bits):
        mine = mine + swap(mine, "dp", 1 << i)
    prev = None
    input_list = []
    for s in range(batch):
        q, k, v, lse, cs = saved[s]
        *ps, dw, db = attend_bwd(s, info, inputs[s], w_t, q, k, v, lse, cs, gctx[s], prev)
        prev = (dw, db)
        r1_, r3_ = swap(ps[1], "tensor", 1), swap(ps[3], "tensor", 1)
        far = swap(summed([ps[2], r3_]).astype(bf16), "tensor", 2)
        input_list.append((summed([ps[0], r1_, far]) + gfi[s * rows : (s + 1) * rows]).astype(bf16))
    dw, db = prev
    terms = [spread(dw.reshape(3, parts, d // parts, width), 1, parts)]
    for i in range(bits):
        terms = halve(terms, 1 + bits - 1 - i, i, 1 << i, bit_of[i])
    qkv_sum = jnp.transpose(summed(terms), (1, 0, 2))
    for i in range(bits):
        db = db + swap(db, "dp", 1 << i)
    ub = d // parts
    return (
        outputs,
        jnp.stack(input_list, 0),
        qkv_sum,
        db,
        down_sum[ub:],
        mine[0],
        mine[1],
        mine[2],
        up_sum,
        mine[6],
        down_sum[:ub],
        mine[3],
        mine[4],
        mine[5],
    )


def solution(mesh):
    in_specs = (
        P("dp", None, None),
        P("dp", "tensor", None),
        P("dp"),
        P(None, None, "tensor"),
        P(None, "tensor"),
        P("tensor", None),
        P(),
        P(),
        P(),
        P(None, "tensor"),
        P("tensor"),
        P("tensor", None),
        P(),
        P(),
        P(),
    )
    out_specs = (
        P("dp", "tensor", None),
        P("dp", "tensor", None),
        P("dp", None, "tensor"),
        P(None, "tensor"),
        P(("tensor", "dp"), None),
        P(),
        P(),
        P(),
        P("dp", "tensor"),
        P("tensor"),
        P(("tensor", "dp"), None),
        P(),
        P(),
        P(),
    )
    return jax.shard_map(body, mesh=mesh, in_specs=in_specs, out_specs=out_specs, check_vma=False)
```

```python
import functools

import jax
import jax.numpy as jnp
from jax import lax
from jax.experimental import pallas as pl
from jax.experimental.pallas import tpu as pltpu
from jax.sharding import PartitionSpec as P

HEAD = 64
NT = (((1,), (1,)), ((), ()))
NN = (((1,), (0,)), ((), ()))
TN = (((0,), (0,)), ((), ()))
bf16 = jnp.bfloat16
f32 = jnp.float32
VM = pl.BlockSpec(memory_space=pltpu.VMEM)
SDS = jax.ShapeDtypeStruct
FWD_COST = (10**10, 1000)


def mm(a, b, dims=NN):
    return lax.dot_general(a, b, dims, preferred_element_type=f32)


class Fetch:
    def __init__(self, src, dst, sem):
        self.dst, self.copy = dst, pltpu.make_async_copy(src, dst, sem)
        self.copy.start()
        self.waiting = True

    def __call__(self):
        if self.waiting:
            self.copy.wait()
            self.waiting = False
        return self.dst


class Flush:
    def __init__(self, src, dst, sem):
        self.src, self.copy = src, pltpu.make_async_copy(src, dst, sem)
        self.started = False

    def start(self):
        if not self.started:
            self.copy.start()
        self.started = True


def call(name, body, info, ins, outs, scratch=(), vmem=40, cost=1000, **static):
    far_in = [i for i, a in enumerate(ins) if isinstance(a, tuple)]
    far_out = [i for i, o in enumerate(outs) if isinstance(o, list)]
    arrays = [a[0] if isinstance(a, tuple) else a for a in ins]
    shapes = [o[0] if isinstance(o, list) else o for o in outs]
    picked = [a[1] if isinstance(a, tuple) else None for a in ins]
    n_in, n_out = len(ins), len(outs)

    def kernel(info_ref, *refs):
        in_refs, refs = refs[:n_in], refs[n_in:]
        out_refs, refs = refs[:n_out], refs[n_out:]
        sem, refs = refs[-1], refs[:-1]
        buffers, rest = refs[: len(far_in) + len(far_out)], refs[len(far_in) + len(far_out) :]
        args = list(in_refs)
        for j, i in enumerate(far_in):
            view = picked[i][1]
            args[i] = Fetch(view(in_refs[i], info_ref), buffers[j], sem.at[j])
        results = list(out_refs)
        flushes = []
        for j, i in enumerate(far_out):
            at = len(far_in) + j
            results[i] = Flush(buffers[at], out_refs[i], sem.at[at])
            flushes.append(results[i])
        body(info_ref, *args, *results, *rest, **static)
        for i in far_in:
            args[i]()
        for f in flushes:
            f.start()
        for f in flushes:
            f.copy.wait()

    hbm = pl.BlockSpec(memory_space=pltpu.HBM)
    buffers = [pltpu.VMEM(picked[i][0], arrays[i].dtype) for i in far_in]
    buffers += [pltpu.VMEM(shapes[i].shape, shapes[i].dtype) for i in far_out]
    return pl.pallas_call(
        kernel,
        out_shape=shapes,
        grid_spec=pltpu.PrefetchScalarGridSpec(
            num_scalar_prefetch=1,
            grid=(1,),
            in_specs=[hbm if i in far_in else VM for i in range(n_in)],
            out_specs=[hbm if i in far_out else VM for i in range(n_out)],
            scratch_shapes=[*buffers, *scratch, pltpu.SemaphoreType.DMA((max(1, len(far_in) + len(far_out)),))],
        ),
        compiler_params=pltpu.CompilerParams(vmem_limit_bytes=vmem << 20),
        cost_estimate=pl.CostEstimate(flops=cost, bytes_accessed=1000, transcendentals=0),
        name=name,
    )(info, *arrays)


def whole(a):
    return (a, (a.shape, lambda ref, info: ref))


def prepare_kernel(info, out_w, bias, up, dn, pack, up_half, dn_half, scr, sem):
    half = up_half.shape[0]
    width = out_w.shape[0]
    rows = pl.ds(pl.multiple_of(info[3] * half, half), half)
    copies = [pltpu.make_async_copy(up.at[rows], up_half, sem.at[0])]
    copies.append(pltpu.make_async_copy(dn.at[rows], dn_half, sem.at[1]))
    copies.append(pltpu.make_async_copy(scr, pack, sem.at[2]))
    copies[0].start()
    copies[1].start()
    scr[0:width, :] = out_w[...]
    scr[width : width + 8, :] = jnp.broadcast_to(bias[...], (8, scr.shape[1]))
    copies[2].start()
    for c in copies:
        c.wait()


def prepare(info, out_w, bias, up, dn):
    width, d = out_w.shape
    hbm = pl.BlockSpec(memory_space=pltpu.HBM)
    half = SDS((up.shape[0] // 2, d), bf16)
    return pl.pallas_call(
        prepare_kernel,
        out_shape=[SDS((width + 8, d), bf16), half, half],
        grid_spec=pltpu.PrefetchScalarGridSpec(
            num_scalar_prefetch=1,
            grid=(1,),
            in_specs=[VM, VM, hbm, hbm],
            out_specs=[hbm] * 3,
            scratch_shapes=[pltpu.VMEM((width + 8, d), bf16), pltpu.SemaphoreType.DMA((3,))],
        ),
        cost_estimate=pl.CostEstimate(flops=1000, bytes_accessed=1000, transcendentals=0),
        name="prepare",
    )(info, out_w, bias, up, dn)


def head_cols(a, h):
    lane = lax.broadcasted_iota(jnp.int32, a.shape, 1)
    return jnp.where((lane >= HEAD * h) & (lane < HEAD * (h + 1)), a, jnp.zeros_like(a))


def attend_fwd_kernel(info, x_ref, w_ref, b_ref, q_out, k_out, v_out, lse_out, c_out, *rest, which):
    outs, v_t = rest[:-1], rest[-1]
    length = info[which]
    me = info[2]
    q_ref, k_ref, v_ref, lse_ref, c_ref = (o.src for o in (q_out, k_out, v_out, lse_out, c_out))
    peers, width, block = c_ref.shape
    heads = width // HEAD
    w = w_ref()
    x = x_ref()[...]
    q = mm(x, w[0], NT) + b_ref[0:1, :].astype(f32)
    q_ref[...] = q.astype(bf16) * jnp.asarray(0.125, bf16)
    k_ref[...] = mm(x, w[1], NT).astype(bf16)
    v = (mm(x, w[2], NT) + b_ref[1:2, :].astype(f32)).astype(bf16)
    v_ref[...] = v
    v_t[...] = v.T
    for o in (q_out, k_out, v_out):
        o.start()

    def one_block(s, carry):
        qb = q_ref[pl.ds(pl.multiple_of(s * block, block), block), :]
        for h in range(heads):
            scores = mm(k_ref[...], head_cols(qb, h), NT)
            row = lax.broadcasted_iota(jnp.int32, scores.shape, 0)
            scores = jnp.where(row < length, scores, -1e30)
            top = jnp.max(scores, axis=0, keepdims=True)
            p = jnp.exp(scores - top)
            total = jnp.sum(p, axis=0, keepdims=True)
            rows = slice(HEAD * h, HEAD * (h + 1))
            c_ref[s, rows, :] = (mm(v_t[rows, :], p.astype(bf16)) * (1.0 / total)).astype(bf16)
            lse_ref[s, h : h + 1, :] = top + jnp.log(total)
        return carry

    lax.fori_loop(0, peers, one_block, 0)
    for k, out in enumerate(outs):
        out.src[...] = c_ref[me ^ k]


def attend_fwd(which, info, inputs, w_t, bias, peers):
    _, seq, d = inputs.shape
    width = w_t.shape[1]
    block = seq // peers
    outs = [[SDS((seq, width), bf16)]] * 3
    outs += [[SDS((peers, 8, block), f32)], [SDS((peers, width, block), bf16)]]
    outs += [[SDS((width, block), bf16)]] * peers
    return call(
        "attend_fwd",
        attend_fwd_kernel,
        info,
        [(inputs, ((seq, d), lambda ref, info: ref.at[which])), whole(w_t), bias],
        outs,
        [pltpu.VMEM((width, seq), bf16)],
        cost=FWD_COST[which],
        which=which,
    )


def attend_bwd_kernel(info, x_ref, w_ref, q_in, k_in, v_in, lse_in, c_in, *rest, which, first, parts):
    peers = 4
    gs, rest = rest[:peers], rest[peers:]
    if not first:
        pw_in, pb_ref = rest[:2]
        rest = rest[2:]
    if first:
        keep, send, dw_out, db_ref, dq_t, dk, dv, k_t, low, g_ref = rest
    else:
        keep, send, w_keep, w_send, db_ref, dq_t, dk, dv, k_t, low, g_ref, dw_scr, pair = rest
    length = info[which]
    me = info[2]
    k_ref, q_ref, v_ref = k_in(), q_in(), v_in()
    lse_ref, c_ref = lse_in(), c_in()
    _, width, block = c_ref.shape
    heads = width // HEAD
    k_t[...] = k_ref[...].T
    dk[...] = jnp.zeros_like(dk)
    dv[...] = jnp.zeros_like(dv)
    for k in range(peers):
        g_ref[me ^ k] = gs[k]()[...]

    def one_block(s, carry):
        at = pl.multiple_of(s * block, block)

        @pl.when(at >= length)
        def _():
            dq_t[:, pl.ds(at, block)] = jnp.zeros((width, block), f32)

        @pl.when(at < length)
        def _():
            qb = q_ref[pl.ds(at, block), :]
            g_t = g_ref[s]
            g = g_t.T
            prod_t = g_t.astype(f32) * c_ref[s].astype(f32)
            for h in range(heads):
                rows = slice(HEAD * h, HEAD * (h + 1))
                qh = head_cols(qb, h)
                gh = head_cols(g, h)
                scores = mm(k_ref[...], qh, NT)
                row = lax.broadcasted_iota(jnp.int32, scores.shape, 0)
                p = jnp.where(row < length, jnp.exp(scores - lse_ref[s, h : h + 1, :]), 0.0)
                dp = mm(v_ref[...], gh, NT)
                inner = jnp.sum(prod_t[rows], axis=0, keepdims=True)
                ds = (p * (dp - inner)).astype(bf16)
                dv[...] += mm(p.astype(bf16), gh)
                dk[...] += mm(ds, qh)
                dq_t[rows, pl.ds(at, block)] = mm(k_t[rows, :], ds) * 0.125

        return carry

    lax.fori_loop(0, peers, one_block, 0)
    low[0] = dq_t[...].T.astype(bf16)
    low[1] = dk[...].astype(bf16)
    low[2] = dv[...].astype(bf16)
    w = w_ref()
    for s in range(peers):
        at = pl.multiple_of((me ^ s) * block, block)
        total = sum(mm(low[i, pl.ds(at, block), :], w[i]) for i in range(3))
        (send if s % 2 else keep).src[s // 2] = total.astype(bf16)
    send.start()
    keep.start()
    db = jnp.concatenate([rowsum(low[i].astype(f32)) for i in (0, 2)], axis=1)
    db = db if first else db + pb_ref[...]
    db_ref[...] = db
    x_t = x_ref()[...].T
    if first:
        for i in range(3):
            dw_out.src[i] = mm(x_t, low[i])
        return
    for i in range(3):
        dw_scr[i] = mm(x_t, low[i]) + pw_in()[i]
    d = dw_scr.shape[1]
    rows = d // parts
    half = 3 * rows // 2
    for b in range(parts):
        flat = dw_scr[:, b * rows : (b + 1) * rows, :].reshape(3 * rows, width)
        flat = jnp.concatenate([flat[0:half], flat[half : 2 * half]], axis=1)
        at = ((b >> 2) * 2 + (b & 1)) * half
        pair[((b >> 1) & 1) ^ info[4], at : at + half, :] = flat.astype(bf16)
    n = parts // 2 * half
    w_send.src[0:n, :] = pair[1]
    high = db.astype(bf16)
    w_send.src[n : n + 8, :] = jnp.concatenate(
        [high, (db - high.astype(f32)).astype(bf16), jnp.zeros((6, 2 * width), bf16)], axis=0
    )
    w_send.start()
    w_keep.src[...] = pair[0]


def attend_bwd(which, info, inputs, w_t, q, k, v, lse, c, gs, prev, parts):
    _, seq, d = inputs.shape
    peers, width, block = c.shape
    outs = [[SDS((2, block, d), bf16)]] * 2
    n = 3 * d // 4
    outs += [[SDS((n, 2 * width), bf16)], [SDS((n + 8, 2 * width), bf16)]] if prev else [[SDS((3, d, width), f32)]]
    outs += [SDS((1, 2 * width), f32)]
    scratch = [
        pltpu.VMEM((width, seq), f32),
        pltpu.VMEM((seq, width), f32),
        pltpu.VMEM((seq, width), f32),
        pltpu.VMEM((width, seq), bf16),
        pltpu.VMEM((3, seq, width), bf16),
        pltpu.VMEM((peers, width, block), bf16),
    ]
    if prev:
        scratch += [pltpu.VMEM((3, d, width), f32), pltpu.VMEM((2, n, 2 * width), bf16)]
    ins = [(inputs, ((seq, d), lambda ref, info: ref.at[which])), whole(w_t)]
    ins += [whole(a) for a in (q, k, v, lse, c)]
    ins += [(g, ((width, block), lambda ref, info: ref.at[which])) for g in gs]
    if prev:
        ins += [whole(prev[0]), prev[1]]
    return call(
        "attend_bwd", attend_bwd_kernel, info, ins, outs, scratch, which=which, first=not prev, parts=parts
    )


def gelu_parts(h):
    t = 1.0 / (1.0 + (0.3275911 * 0.7071067811865476) * jnp.abs(h))
    poly = t * (0.127414796 + t * (-0.142248368 + t * (0.7107068705 + t * (-0.7265760135 + t * 0.5307027145))))
    bell = jnp.exp2((-0.5 * 1.4426950408889634) * (h * h))
    tail = poly * bell
    cum = jnp.where(h < 0, tail, 1.0 - tail)
    return h * cum, cum + h * (bell * 0.3989422804014327)


def norm_parts(v):
    center = v - jnp.mean(v, axis=1, keepdims=True)
    r = lax.rsqrt(jnp.mean(center * center, axis=1, keepdims=True) + 1e-12)
    return center * r, r


def norm_back(u, gain, nv, r):
    gu = u * gain
    return r * (gu - jnp.mean(gu, axis=1, keepdims=True) - nv * jnp.mean(gu * nv, axis=1, keepdims=True))


def rowsum(v):
    return jnp.sum(v, axis=0, keepdims=True)


def first_norm_kernel(info, x_in, par, *rest):
    cs, packs = rest[:8], rest[8:12]
    nv_out, r_ref, low = rest[12:]
    nv_ref = nv_out.src
    x_ref = x_in()
    packs = [p() for p in packs]
    rows = x_ref.shape[1]
    width = cs[0].dst.shape[0]
    for s in range(2):
        here = slice(s * rows, (s + 1) * rows)
        total = par[0:1, :] + x_ref[s].astype(f32)
        for k in range(4):
            total = total + mm(cs[4 * s + k]()[...], packs[k][0:width, :], TN)
        nv, r = norm_parts(total)
        nv_ref[here] = nv
        r_ref[here] = r
        low[here] = (nv * par[1:2, :] + par[2:3, :]).astype(bf16)


def feed_kernel(info, low, low2, pack, *rest, width, far):
    if far:
        u_a, u_b, d_a, d_b, p_own, p_sib, act_out, slope_out, own, sib, up, dn = rest
        half = u_a.dst.shape[0]
        assemble(info, up, u_a(), u_b(), half)
    else:
        u_in, d_in, act_out, slope_out, own, sib = rest
        up = u_in()
    act, slope = act_out.src, slope_out.src
    units = up.shape[1]
    bias = pack()
    step = 256
    for j, rows in enumerate((low, low2)):

        def chunk(n, carry):
            cols = pl.ds(pl.multiple_of(n * step, step), step)
            hidden = mm(rows[...], up[:, cols]) + bias[width : width + 1, cols].astype(f32)
            a, g = gelu_parts(hidden)
            act[j, :, cols] = a.astype(bf16)
            slope[j, :, cols] = g.astype(bf16)
            return carry

        lax.fori_loop(0, units // step, chunk, 0)
    act_out.start()
    slope_out.start()
    if far:
        assemble(info, dn, d_a(), d_b(), half)
        sib[...] = (p_sib[...] + mm(act[1], dn[...])).astype(bf16)
        own[...] = p_own[...] + mm(act[0], dn[...])
    else:
        dn = d_in()
        own[...] = mm(act[0], dn[...])
        sib[...] = mm(act[1], dn[...])


def assemble(info, dst, a, b, half):
    dst[pl.ds(pl.multiple_of(info[3] * half, half), half)] = a[...]
    dst[pl.ds(pl.multiple_of((1 - info[3]) * half, half), half)] = b[...]


def second_norm_kernel(info, cot_in, par, nv_in, own, got, outs, gsec_out, gs_low, small):
    cot, nv_ref, gsec = cot_in(), nv_in(), gsec_out.src
    batch, rows, d = cot.shape
    sums = [0.0] * 3
    for s in range(batch):
        here = slice(s * rows, (s + 1) * rows)
        total = own[here] + got[here].astype(f32) + par[3:4, :] + (nv_ref[here] * par[1:2, :] + par[2:3, :])
        nv, r = norm_parts(total)
        outs.src[s] = (nv * par[4:5, :] + par[5:6, :]).astype(bf16)
        at = info[2] * rows + lax.broadcasted_iota(jnp.int32, (rows, 1), 0)
        seed = jnp.where(at < info[s], cot[s].astype(f32), 0.0)
        g = norm_back(seed, par[4:5, :], nv, r)
        sums = [a + rowsum(b) for a, b in zip(sums, (g, seed * nv, seed))]
        gsec[here] = g
        gs_low[here] = g.astype(bf16)
    small[...] = jnp.concatenate([*sums, jnp.zeros((5, d), f32)], axis=0)


def feed_back_kernel(info, gs, gs2, slope0, slope1, up0, dn0, u_a, u_b, d_a, d_b, gh_out, own, sib, ub, up2, dn2):
    gh = gh_out.src
    half = u_a.dst.shape[0]
    units = up0.dst.shape[1]
    ub[...] = jnp.zeros_like(ub)
    step = 256
    for k, slope in enumerate((slope0(), slope1())):
        if k:
            assemble(info, dn2, d_a(), d_b(), half)
            dn = dn2
        else:
            dn = dn0()
        for j, rows in enumerate((gs, gs2)):

            def chunk(n, carry):
                cols = pl.ds(pl.multiple_of(n * step, step), step)
                ga = mm(rows[...], dn[cols, :], NT)
                h = (ga * slope[j, :, cols].astype(f32)).astype(bf16)
                gh[k, j, :, cols] = h
                ub[k : k + 1, cols] += rowsum(h.astype(f32))
                return carry

            lax.fori_loop(0, units // step, chunk, 0)
    gh_out.start()
    assemble(info, up2, u_a(), u_b(), half)
    up = up0()
    sib[...] = (mm(gh[0, 1], up[...], NT) + mm(gh[1, 1], up2[...], NT)).astype(bf16)
    own[...] = mm(gh[0, 0], up[...], NT) + mm(gh[1, 0], up2[...], NT)


def first_back_kernel(info, par, nv_in, r_ref, own, got, gsec_in, small2, *rest):
    cs, packs = rest[:8], rest[8:12]
    gfi, g0, g1, g2, g3, okeep, osend, small, ga_low = rest[12:]
    nv_ref, gsec = nv_in(), gsec_in()
    packs = [p() for p in packs]
    n, d = own.shape
    rows = n // 2
    width = cs[0].dst.shape[0]
    sums = [0.0] * 3
    for s in range(2):
        here = slice(s * rows, (s + 1) * rows)
        u = own[here] + got[here].astype(f32) + gsec[here]
        nv = nv_ref[here]
        g = norm_back(u, par[1:2, :], nv, r_ref[here])
        sums = [a + rowsum(b) for a, b in zip(sums, (g, u * nv, u))]
        gfi.src[here] = g
        low = g.astype(bf16)
        ga_low[here] = low
        for k, out in enumerate((g0, g1, g2, g3)):
            out.src[s] = mm(packs[k][0:width, :], low, NT).astype(bf16)
    for out in (g3, g2, g1, g0, gfi):
        out.start()
    for k in range(4):
        total = mm(cs[k]()[...], ga_low[0:rows, :]) + mm(cs[4 + k]()[...], ga_low[rows:n, :])
        (osend if k % 2 else okeep).src[k // 2, 0:width, :] = total.astype(bf16)
    both = jnp.concatenate([*sums, small2[0:3, :], jnp.zeros((2, d), f32)], axis=0)
    small[...] = both
    high = both.astype(bf16)
    osend.src[0, width : width + 8, :] = high
    osend.src[1, width : width + 8, :] = (both - high.astype(f32)).astype(bf16)


def down_grads_kernel(info, act0, act1, gs, gs2, far_keep, far_send, keep, send, scr, *, parts):
    units = act0.dst.shape[2]
    block = units // parts
    step = 384
    for act, mine, theirs in ((act1(), far_keep, far_send), (act0(), keep, send)):
        for m in range(0, units, step):
            cols = slice(m, m + step)
            total = mm(act[0, :, cols], gs[...], TN) + mm(act[1, :, cols], gs2[...], TN)
            total = total.astype(bf16)
            for i in range(step // block):
                b = m // block + i
                scr[(b & 1) ^ info[3], b >> 1] = total[i * block : (i + 1) * block]
        theirs.src[...] = scr[1]
        theirs.start()
        mine.src[...] = scr[0]
        mine.start()


def up_grads_kernel(
    info, low, low2, gh_in, okeep, ogot, small, ub, far_keep, far_send, keep, send, sums, scr, *, parts, width
):
    gh = gh_in()
    units = low.shape[1]
    block = units // parts
    extra = width // parts
    joint = block + extra
    n = parts // 2 * joint
    step = 384
    got = ogot()
    both = small[...] + got[0, width : width + 8, :].astype(f32) + got[1, width : width + 8, :].astype(f32)
    both = jnp.concatenate([both[0:6], ub[0:2, :]], axis=0)
    sums[...] = both
    high = both.astype(bf16)
    far_send.src[n : n + 8, :] = high
    far_send.src[n + 8 : n + 16, :] = (both - high.astype(f32)).astype(bf16)
    for k, mine, theirs in ((1, far_keep, far_send), (0, keep, send)):
        for m in range(0, units, step):
            cols = slice(m, m + step)
            total = mm(low[:, cols], gh[k, 0], TN) + mm(low2[:, cols], gh[k, 1], TN)
            total = total.astype(bf16)
            for i in range(step // block):
                b = m // block + i
                scr[((b >> 1) & 1) ^ info[4], (b >> 2) * 2 + (b & 1), 0:block, :] = total[i * block : (i + 1) * block]
        o = (okeep()[k, 0:width, :].astype(f32) + got[k, 0:width, :].astype(f32)).astype(bf16)
        for b in range(parts):
            at = (b >> 2) * 2 + (b & 1)
            scr[((b >> 1) & 1) ^ info[4], at, block:joint, :] = o[b * extra : (b + 1) * extra]
        for b in range(parts // 2):
            theirs.src[b * joint : (b + 1) * joint, :] = scr[1, b]
            mine.src[b * joint : (b + 1) * joint, :] = scr[0, b]
        theirs.start()
        mine.start()


def swap(x, axis, bit):
    size = lax.axis_size(axis)
    return lax.ppermute(x, axis, [(i, i ^ bit) for i in range(size)])


def summed(parts):
    return sum(p.astype(f32) for p in parts)


def spread(array, axis, parts):
    bits = parts.bit_length() - 1
    return array.reshape(*array.shape[:axis], *([2] * bits), array.shape[axis] // parts, *array.shape[axis + 1 :])


def halve(terms, axis, bit, mine):
    other = [lax.dynamic_index_in_dim(t, 1 - mine, axis, keepdims=False) for t in terms]
    kept = [lax.dynamic_index_in_dim(t, mine, axis, keepdims=False) for t in terms]
    other = summed(other).astype(bf16)
    return kept + [swap(other, "dp", bit)], other


def body(
    inputs,
    cotangent,
    lengths,
    qkv_weight,
    qkv_bias,
    out_weight,
    out_bias,
    first_gain,
    first_shift,
    up_weight,
    up_bias,
    down_weight,
    down_bias,
    second_gain,
    second_shift,
):
    batch, seq, d = inputs.shape
    rows = cotangent.shape[1]
    n = batch * rows
    width = out_weight.shape[0]
    units = up_weight.shape[1]
    peers = lax.axis_size("tensor")
    parts = lax.axis_size("dp")
    bits = parts.bit_length() - 1
    t = lax.axis_index("tensor")
    dp = lax.axis_index("dp")
    bit_of = [(dp >> i) & 1 for i in range(bits)]
    info = jnp.stack([lengths[0], lengths[1], t, bit_of[0], bit_of[1]]).astype(jnp.int32)
    par = jnp.concatenate([out_bias, first_gain, first_shift, down_bias, second_gain, second_shift])
    par = par.reshape(6, d).astype(f32)
    w_t = jnp.transpose(qkv_weight, (1, 2, 0))
    pack, up_half, dn_half = prepare(info, out_weight, up_bias[None], up_weight, down_weight)
    pack2 = swap(pack, "tensor", 2)
    pack1 = swap(pack, "tensor", 1)
    u2a = swap(up_half, "tensor", 2)
    d2a = swap(dn_half, "tensor", 2)
    saved = []
    ctx = []
    for s in range(batch):
        q, k, v, lse, c, *cs = attend_fwd(s, info, inputs, w_t, qkv_bias, peers)
        saved.append((q, k, v, lse, c))
        if s == 0:
            *cs, pack1, pack2 = after(*cs, pack1, pack2)
        else:
            both = after(*cs, pack2, *ctx)
            cs, pack2, ctx = list(both[:peers]), both[peers], list(both[peers + 1 :])
        ctx += [cs[0]] + [swap(cs[j], "tensor", j) for j in range(1, peers)]
    pack3 = swap(pack2, "tensor", 1)
    packs = [pack, pack1, pack2, pack3]
    ctx[0], u2a = after(ctx[0], u2a)
    u2b = swap(u2a, "dp", 1)
    d2b = swap(d2a, "dp", 1)
    far_ctx = [whole(c) for c in ctx]
    far_packs = [whole(p) for p in packs]
    share = (inputs, ((batch, rows, d), lambda ref, info: ref.at[:, pl.ds(pl.multiple_of(info[2] * rows, rows), rows), :]))
    nv1, r1, low = call(
        "first_norm",
        first_norm_kernel,
        info,
        [share, par, *far_ctx, *far_packs],
        [[SDS((n, d), f32)], SDS((n, 1), f32), SDS((n, d), bf16)],
    )
    low2 = swap(low, "tensor", 1)
    pair = [SDS((2, n, units), bf16)]
    part = SDS((n, d), f32)
    act0, slope0, own, sib = call(
        "feed",
        feed_kernel,
        info,
        [low, low2, far_packs[0], whole(up_weight), whole(down_weight)],
        [pair, pair, part, part],
        width=width,
        far=False,
    )
    halves = [whole(x) for x in (u2a, u2b, d2a, d2b)]
    both = [pltpu.VMEM((d, units), bf16), pltpu.VMEM((units, d), bf16)]
    act1, slope1, own, sib = call(
        "feed",
        feed_kernel,
        info,
        [low, low2, far_packs[2], *halves, own, sib],
        [pair, pair, part, SDS((n, d), bf16)],
        both,
        width=width,
        far=True,
    )
    got = swap(sib, "tensor", 1)
    outputs, gsec, gs_low, small2 = call(
        "second_norm",
        second_norm_kernel,
        info,
        [whole(cotangent), par, whole(nv1), own, got],
        [[SDS((batch, rows, d), bf16)], [part], SDS((n, d), bf16), SDS((8, d), f32)],
    )
    gs_low2 = swap(gs_low, "tensor", 1)
    gh, own, sib, ub = call(
        "feed_back",
        feed_back_kernel,
        info,
        [gs_low, gs_low2, whole(slope0), whole(slope1), whole(up_weight), whole(down_weight), *halves],
        [[SDS((2, 2, n, units), bf16)], part, SDS((n, d), bf16), SDS((8, d), f32)],
        both,
    )
    got = swap(sib, "tensor", 1)
    block = units // parts
    downs = call(
        "down_grads",
        down_grads_kernel,
        info,
        [whole(act0), whole(act1), gs_low, gs_low2],
        [[SDS((parts // 2, block, d), bf16)]] * 4,
        [pltpu.VMEM((2, parts // 2, block, d), bf16)],
        parts=parts,
    )
    down_far_keep, down_far_send, down_keep, down_send = downs
    down_far_got = swap(down_far_send, "dp", 1)
    gfi, g0, g1, g2, g3, okeep, osend, small1 = call(
        "first_back",
        first_back_kernel,
        info,
        [par, whole(nv1), r1, own, got, whole(gsec), small2, *far_ctx, *far_packs],
        [
            [part],
            *[[SDS((batch, width, rows), bf16)]] * 4,
            *[[SDS((2, width + 8, d), bf16)]] * 2,
            SDS((8, d), f32),
        ],
        [pltpu.VMEM((n, d), bf16)],
    )
    gctx = [g0] + [swap(g, "tensor", j) for j, g in ((1, g1), (2, g2), (3, g3))]
    got_o = swap(osend, "tensor", 1)
    joint = block + width // parts
    cut = parts // 2 * joint
    up_far_keep, up_far_send, up_keep, up_send, small = call(
        "up_grads",
        up_grads_kernel,
        info,
        [low, low2, whole(gh), whole(okeep), whole(got_o), small1, ub],
        [
            [SDS((cut, d), bf16)],
            [SDS((cut + 16, d), bf16)],
            [SDS((cut, d), bf16)],
            [SDS((cut, d), bf16)],
            SDS((8, d), f32),
        ],
        [pltpu.VMEM((2, parts // 2, joint, d), bf16)],
        parts=parts,
        width=width,
    )
    up_far_got = swap(up_far_send, "dp", 2)
    *gctx, down_far_got, up_far_keep = after(*gctx, down_far_got, up_far_keep)
    down_far_sum = summed([down_far_keep, down_far_got]).astype(bf16)
    down_y = swap(down_far_sum, "tensor", 2)
    down_send, down_far_sum = after(down_send, down_far_sum)
    down_got = swap(down_send, "dp", 1)
    *gctx, down_far_sum, up_far_keep = after(*gctx, down_far_sum, up_far_keep)
    q, k, v, lse, c = saved[0]
    keep, send, dw, db = attend_bwd(0, info, inputs, w_t, q, k, v, lse, c, gctx, None, parts)
    near = swap(send, "tensor", 1)
    keep, down_got, up_far_got = after(keep, down_got, up_far_got)
    shape = ([2] * (bits - 1)) + [block, d]
    terms = [x.reshape(shape) for x in (down_keep, down_got, down_y)]
    down_terms, down_next = halve(terms, bits - 2, 2, bit_of[1])
    shape = ([2] * (bits - 1)) + [joint, d]
    small = small + pair_sum(up_far_got, cut, 8)
    terms = [x.reshape(shape) for x in (up_far_keep, up_far_got[:cut])]
    up_far_terms, up_far_next, small_x = halve_with(terms, bits - 2, small, "dp", 1, bit_of[0])
    up_send, up_far_next = after(up_send, up_far_next)
    up_got = swap(up_send, "dp", 2)
    in_sum = summed([keep[1], near[1]]).astype(bf16)
    far = swap(in_sum, "tensor", 2)
    first_terms = [keep[0], near[0], far]
    dw, down_next, up_far_next, in_sum, up_keep = after(dw, down_next, up_far_next, in_sum, up_keep)
    q, k, v, lse, c = saved[1]
    keep, send, w_keep, w_send, db = attend_bwd(1, info, inputs, w_t, q, k, v, lse, c, gctx, (dw, db), parts)
    near = swap(send, "tensor", 1)
    far = swap(summed([keep[1], near[1]]).astype(bf16), "tensor", 2)
    input_list = [
        (summed(x) + gfi[s * rows : (s + 1) * rows]).astype(bf16)
        for s, x in enumerate((first_terms, [keep[0], near[0], far]))
    ]
    order = [1, 0] + list(range(2, bits))
    row = 3 * (d // parts) // 2
    got = swap(w_send, "dp", 2)
    at = parts // 2 * row
    shape = ([2] * (bits - 1)) + [row, 2 * width]
    terms = [x.reshape(shape) for x in (w_keep, got[:at])]
    db = db + got[at : at + 1].astype(f32) + got[at + 1 : at + 2].astype(f32)
    for i in order[1:]:
        kept, sent, more = halve_with(terms, terms[0].ndim - 3, db, "dp", 1 << i, bit_of[i])
        terms, db = kept, db + more
    qkv_sum = summed(terms)
    qkv_sum = jnp.concatenate([qkv_sum[:, :width], qkv_sum[:, width:]], axis=0).reshape(3, -1, width)
    qkv_sum = jnp.transpose(qkv_sum, (1, 0, 2))
    db = db.reshape(2, width)
    for i in range(2, bits):
        down_terms, sent = halve(down_terms, bits - 1 - i, 1 << i, bit_of[i])
    down_sum = summed(down_terms)
    small = small + small_x
    small = jnp.concatenate([small[0:6], small[7:8], small[6:7]])
    send = summed(up_far_terms).astype(bf16)
    up_y = swap(with_rows(send, small), "tensor", 2)
    at = send.size // d
    small = jnp.concatenate([small[0:6], small[7:8], small[7:8]]) + pair_sum(up_y, at, 8)
    shape = ([2] * (bits - 1)) + [joint, d]
    terms, sent = halve([x.reshape(shape) for x in (up_keep, up_got)], bits - 2, 1, bit_of[0])
    terms.append(up_y[:at].reshape(send.shape))
    for i in range(2, bits):
        terms, sent, more = halve_with(terms, terms[0].ndim - 3, small, "dp", 1 << i, bit_of[i])
        small = small + more
    up_sum = summed(terms)
    mine = small
    return (
        outputs,
        jnp.stack(input_list, 0),
        qkv_sum,
        db,
        up_sum[block:],
        mine[0],
        mine[1],
        mine[2],
        up_sum[:block],
        mine[6],
        down_sum,
        mine[3],
        mine[4],
        mine[5],
    )


def pair_sum(array, at, n):
    return array[at : at + n].astype(f32) + array[at + n : at + 2 * n].astype(f32)


def with_rows(array, rows):
    flat = array.reshape(-1, array.shape[-1])
    high = rows.astype(bf16)
    low = (rows - high.astype(f32)).astype(bf16)
    return jnp.concatenate([flat, high, low], axis=0)


def halve_with(terms, axis, rows, name, bit, mine):
    other = [lax.dynamic_index_in_dim(t, 1 - mine, axis, keepdims=False) for t in terms]
    kept = [lax.dynamic_index_in_dim(t, mine, axis, keepdims=False) for t in terms]
    other = summed(other).astype(bf16)
    sent = with_rows(other, rows)
    got = swap(sent, name, bit)
    cut = other.size // other.shape[-1]
    return kept + [got[:cut].reshape(other.shape)], sent, pair_sum(got, cut, rows.shape[0])


def after(*values):
    return lax.optimization_barrier(values)


def solution(mesh):
    in_specs = (
        P("dp", None, None),
        P("dp", "tensor", None),
        P("dp"),
        P(None, None, "tensor"),
        P(None, "tensor"),
        P("tensor", None),
        P(),
        P(),
        P(),
        P(None, "tensor"),
        P("tensor"),
        P("tensor", None),
        P(),
        P(),
        P(),
    )
    out_specs = (
        P("dp", "tensor", None),
        P("dp", "tensor", None),
        P("dp", None, "tensor"),
        P(None, "tensor"),
        P(("tensor", "dp"), None),
        P(),
        P(),
        P(),
        P("dp", "tensor"),
        P("tensor"),
        P(("tensor", "dp"), None),
        P(),
        P(),
        P(),
    )
    return jax.shard_map(body, mesh=mesh, in_specs=in_specs, out_specs=out_specs, check_vma=False)
```

```python
import functools

import jax
import jax.numpy as jnp
from jax import lax
from jax.experimental import pallas as pl
from jax.experimental.pallas import tpu as pltpu
from jax.sharding import PartitionSpec as P

HEAD = 64
NT = (((1,), (1,)), ((), ()))
NN = (((1,), (0,)), ((), ()))
TN = (((0,), (0,)), ((), ()))
bf16 = jnp.bfloat16
f32 = jnp.float32
VM = pl.BlockSpec(memory_space=pltpu.VMEM)
SDS = jax.ShapeDtypeStruct
FWD_COST = (10**10, 1000)


def mm(a, b, dims=NN):
    return lax.dot_general(a, b, dims, preferred_element_type=f32)


class Fetch:
    def __init__(self, src, dst, sem):
        self.dst, self.copy = dst, pltpu.make_async_copy(src, dst, sem)
        self.copy.start()
        self.waiting = True

    def __call__(self):
        if self.waiting:
            self.copy.wait()
            self.waiting = False
        return self.dst


class Flush:
    def __init__(self, src, dst, sem):
        self.src, self.copy = src, pltpu.make_async_copy(src, dst, sem)
        self.started = False

    def start(self):
        if not self.started:
            self.copy.start()
        self.started = True


def call(name, body, info, ins, outs, scratch=(), vmem=58, cost=1000, **static):
    far_in = [i for i, a in enumerate(ins) if isinstance(a, tuple)]
    pinned = [i for i in far_in if len(ins[i]) == 2]
    far_out = [i for i, o in enumerate(outs) if isinstance(o, list)]
    arrays = [a[0] if isinstance(a, tuple) else a for a in ins]
    shapes = [o[0] if isinstance(o, list) else o for o in outs]
    picked = [a[1] if isinstance(a, tuple) else None for a in ins]
    n_in, n_out = len(ins), len(outs)

    def kernel(info_ref, *refs):
        in_refs, refs = refs[:n_in], refs[n_in:]
        out_refs, refs = refs[:n_out], refs[n_out:]
        sem, refs = refs[-1], refs[:-1]
        buffers, rest = refs[: len(far_in) + len(far_out)], refs[len(far_in) + len(far_out) :]
        args = list(in_refs)
        for j, i in enumerate(far_in):
            view = picked[i][1]
            args[i] = Fetch(view(in_refs[i], info_ref), buffers[j], sem.at[j])
        results = list(out_refs)
        flushes = []
        for j, i in enumerate(far_out):
            at = len(far_in) + j
            results[i] = Flush(buffers[at], out_refs[i], sem.at[at])
            flushes.append(results[i])
        body(info_ref, *args, *results, *rest, **static)
        for i in far_in:
            args[i]()
        for f in flushes:
            f.start()
        for f in flushes:
            f.copy.wait()

    hbm = pl.BlockSpec(memory_space=pltpu.HBM)
    buffers = [pltpu.VMEM(picked[i][0], arrays[i].dtype) for i in far_in]
    buffers += [pltpu.VMEM(shapes[i].shape, shapes[i].dtype) for i in far_out]
    return pl.pallas_call(
        kernel,
        out_shape=[pltpu.HBM(o.shape, o.dtype) if i in far_out else o for i, o in enumerate(shapes)],
        grid_spec=pltpu.PrefetchScalarGridSpec(
            num_scalar_prefetch=1,
            grid=(1,),
            in_specs=[hbm if i in pinned else pl.BlockSpec(memory_space=pl.ANY) if i in far_in else VM for i in range(n_in)],
            out_specs=[hbm if i in far_out else VM for i in range(n_out)],
            scratch_shapes=[*buffers, *scratch, pltpu.SemaphoreType.DMA((max(1, len(far_in) + len(far_out)),))],
        ),
        compiler_params=pltpu.CompilerParams(vmem_limit_bytes=vmem << 20),
        cost_estimate=pl.CostEstimate(flops=cost, bytes_accessed=1000, transcendentals=0),
        name=name,
    )(info, *[pltpu.with_memory_space_constraint(a, pltpu.HBM) if i in pinned else a for i, a in enumerate(arrays)])


def whole(a):
    return (a, (a.shape, lambda ref, info: ref))


def loose(a):
    return (*whole(a), None)


def prepare_kernel(info, out_in, bias, up_in, dn_in, pack, up_half, dn_half):
    for src, dst in ((up_in, up_half), (dn_in, dn_half)):
        dst.src[...] = src()[...]
        dst.start()
    out_w = out_in()
    width, d = out_w.shape
    pack.src[0:width, :] = out_w[...]
    pack.src[width : width + 8, :] = jnp.broadcast_to(bias[...], (8, d))


def prepare(info, out_w, bias, up, dn):
    width, d = out_w.shape
    half = up.shape[0] // 2
    view = lambda ref, info: ref.at[pl.ds(pl.multiple_of(info[3] * half, half), half)]
    ins = [whole(out_w), bias, (up, ((half, d), view)), (dn, ((half, d), view))]
    return call("prepare", prepare_kernel, info, ins, [[SDS((width + 8, d), bf16)]] + [[SDS((half, d), bf16)]] * 2)


def head_cols(a, h):
    lane = lax.broadcasted_iota(jnp.int32, a.shape, 1)
    return jnp.where((lane >= HEAD * h) & (lane < HEAD * (h + 1)), a, jnp.zeros_like(a))


def attend_fwd_kernel(info, x_ref, w_ref, b_ref, q_out, k_out, v_out, lse_out, c_out, *rest, which):
    outs, v_t = rest[:-1], rest[-1]
    length = info[which]
    me = info[2]
    q_ref, k_ref, v_ref, lse_ref, c_ref = (o.src for o in (q_out, k_out, v_out, lse_out, c_out))
    peers, width, block = c_ref.shape
    heads = width // HEAD
    w = w_ref()
    x = x_ref()[...]
    q = mm(x, w[0], NT) + b_ref[0:1, :].astype(f32)
    q_ref[...] = q.astype(bf16) * jnp.asarray(0.125, bf16)
    k_ref[...] = mm(x, w[1], NT).astype(bf16)
    v = (mm(x, w[2], NT) + b_ref[1:2, :].astype(f32)).astype(bf16)
    v_ref[...] = v
    v_t[...] = v.T
    for o in (q_out, k_out, v_out):
        o.start()

    def one_block(s, carry):
        qb = q_ref[pl.ds(pl.multiple_of(s * block, block), block), :]
        for h in range(heads):
            scores = mm(k_ref[...], head_cols(qb, h), NT)
            row = lax.broadcasted_iota(jnp.int32, scores.shape, 0)
            scores = jnp.where(row < length, scores, -1e30)
            top = jnp.max(scores, axis=0, keepdims=True)
            p = jnp.exp(scores - top)
            total = jnp.sum(p, axis=0, keepdims=True)
            rows = slice(HEAD * h, HEAD * (h + 1))
            c_ref[s, rows, :] = (mm(v_t[rows, :], p.astype(bf16)) * (1.0 / total)).astype(bf16)
            lse_ref[s, h : h + 1, :] = top + jnp.log(total)
        return carry

    lax.fori_loop(0, peers, one_block, 0)
    for k, out in enumerate(outs):
        out.src[...] = c_ref[me ^ k]


def attend_fwd(which, info, inputs, w_t, bias, peers):
    _, seq, d = inputs.shape
    width = w_t.shape[1]
    block = seq // peers
    outs = [[SDS((seq, width), bf16)]] * 3
    outs += [[SDS((peers, 8, block), f32)], [SDS((peers, width, block), bf16)]]
    outs += [[SDS((width, block), bf16)]] * peers
    return call(
        "attend_fwd",
        attend_fwd_kernel,
        info,
        [(inputs, ((seq, d), lambda ref, info: ref.at[which])), whole(w_t), bias],
        outs,
        [pltpu.VMEM((width, seq), bf16)],
        cost=FWD_COST[which],
        which=which,
    )


def attend_bwd_kernel(info, x_ref, w_ref, q_in, k_in, v_in, lse_in, c_in, *rest, which, first, parts):
    peers = 4
    gs, rest = rest[:peers], rest[peers:]
    if not first:
        pw_in, pb_ref = rest[:2]
        rest = rest[2:]
    if first:
        keep, send, dw_out, db_ref, dq_t, dk, dv, k_t, low, g_ref = rest
    else:
        keep, send, w_keep, w_send, db_ref, dq_t, dk, dv, k_t, low, g_ref, dw_scr, pair = rest
    length = info[which]
    me = info[2]
    k_ref, q_ref, v_ref = k_in(), q_in(), v_in()
    lse_ref, c_ref = lse_in(), c_in()
    _, width, block = c_ref.shape
    heads = width // HEAD
    k_t[...] = k_ref[...].T
    dk[...] = jnp.zeros_like(dk)
    dv[...] = jnp.zeros_like(dv)
    for k in range(peers):
        g_ref[me ^ k] = gs[k]()[...]

    def one_block(s, carry):
        at = pl.multiple_of(s * block, block)

        @pl.when(at >= length)
        def _():
            dq_t[:, pl.ds(at, block)] = jnp.zeros((width, block), f32)

        @pl.when(at < length)
        def _():
            qb = q_ref[pl.ds(at, block), :]
            g_t = g_ref[s]
            g = g_t.T
            prod_t = g_t.astype(f32) * c_ref[s].astype(f32)
            for h in range(heads):
                rows = slice(HEAD * h, HEAD * (h + 1))
                qh = head_cols(qb, h)
                gh = head_cols(g, h)
                scores = mm(k_ref[...], qh, NT)
                row = lax.broadcasted_iota(jnp.int32, scores.shape, 0)
                p = jnp.where(row < length, jnp.exp(scores - lse_ref[s, h : h + 1, :]), 0.0)
                dp = mm(v_ref[...], gh, NT)
                inner = jnp.sum(prod_t[rows], axis=0, keepdims=True)
                ds = (p * (dp - inner)).astype(bf16)
                dv[...] += mm(p.astype(bf16), gh)
                dk[...] += mm(ds, qh)
                dq_t[rows, pl.ds(at, block)] = mm(k_t[rows, :], ds) * 0.125

        return carry

    lax.fori_loop(0, peers, one_block, 0)
    low[0] = dq_t[...].T.astype(bf16)
    low[1] = dk[...].astype(bf16)
    low[2] = dv[...].astype(bf16)
    w = w_ref()
    for s in range(peers):
        at = pl.multiple_of((me ^ s) * block, block)
        total = sum(mm(low[i, pl.ds(at, block), :], w[i]) for i in range(3))
        (send if s % 2 else keep).src[s // 2] = total.astype(bf16)
    send.start()
    keep.start()
    db = jnp.concatenate([rowsum(low[i].astype(f32)) for i in (0, 2)], axis=1)
    db = db if first else db + pb_ref[...]
    db_ref[...] = db
    x_t = x_ref()[...].T
    if first:
        for i in range(3):
            dw_out.src[i] = mm(x_t, low[i])
        return
    for i in range(3):
        dw_scr[i] = mm(x_t, low[i]) + pw_in()[i]
    d = dw_scr.shape[1]
    rows = d // parts
    half = 3 * rows // 2
    for b in range(parts):
        flat = dw_scr[:, b * rows : (b + 1) * rows, :].reshape(3 * rows, width)
        flat = jnp.concatenate([flat[0:half], flat[half : 2 * half]], axis=1)
        at = ((b >> 2) * 2 + (b & 1)) * half
        pair[((b >> 1) & 1) ^ info[4], at : at + half, :] = flat.astype(bf16)
    n = parts // 2 * half
    w_send.src[0:n, :] = pair[1]
    high = db.astype(bf16)
    w_send.src[n : n + 8, :] = jnp.concatenate(
        [high, (db - high.astype(f32)).astype(bf16), jnp.zeros((6, 2 * width), bf16)], axis=0
    )
    w_send.start()
    w_keep.src[...] = pair[0]


def attend_bwd(which, info, inputs, w_t, q, k, v, lse, c, gs, prev, parts):
    _, seq, d = inputs.shape
    peers, width, block = c.shape
    outs = [[SDS((2, block, d), bf16)]] * 2
    n = 3 * d // 4
    outs += [[SDS((n, 2 * width), bf16)], [SDS((n + 8, 2 * width), bf16)]] if prev else [[SDS((3, d, width), f32)]]
    outs += [SDS((1, 2 * width), f32)]
    scratch = [
        pltpu.VMEM((width, seq), f32),
        pltpu.VMEM((seq, width), f32),
        pltpu.VMEM((seq, width), f32),
        pltpu.VMEM((width, seq), bf16),
        pltpu.VMEM((3, seq, width), bf16),
        pltpu.VMEM((peers, width, block), bf16),
    ]
    if prev:
        scratch += [pltpu.VMEM((3, d, width), f32), pltpu.VMEM((2, n, 2 * width), bf16)]
    ins = [(inputs, ((seq, d), lambda ref, info: ref.at[which])), whole(w_t)]
    ins += [whole(a) for a in (q, k, v, lse, c)]
    ins += [(g, ((width, block), lambda ref, info: ref.at[which]), None) for g in gs]
    if prev:
        ins += [whole(prev[0]), prev[1]]
    return call(
        "attend_bwd", attend_bwd_kernel, info, ins, outs, scratch, which=which, first=not prev, parts=parts
    )


def gelu_parts(h):
    t = 1.0 / (1.0 + (0.3275911 * 0.7071067811865476) * jnp.abs(h))
    poly = t * (0.127414796 + t * (-0.142248368 + t * (0.7107068705 + t * (-0.7265760135 + t * 0.5307027145))))
    bell = jnp.exp2((-0.5 * 1.4426950408889634) * (h * h))
    tail = poly * bell
    cum = jnp.where(h < 0, tail, 1.0 - tail)
    return h * cum, cum + h * (bell * 0.3989422804014327)


def norm_parts(v):
    center = v - jnp.mean(v, axis=1, keepdims=True)
    r = lax.rsqrt(jnp.mean(center * center, axis=1, keepdims=True) + 1e-12)
    return center * r, r


def norm_back(u, gain, nv, r):
    gu = u * gain
    return r * (gu - jnp.mean(gu, axis=1, keepdims=True) - nv * jnp.mean(gu * nv, axis=1, keepdims=True))


def rowsum(v):
    return jnp.sum(v, axis=0, keepdims=True)


def first_norm_kernel(info, x_in, par, *rest):
    cs, packs = rest[:8], rest[8:12]
    nv_out, r_ref, low = rest[12:]
    nv_ref = nv_out.src
    x_ref = x_in()
    packs = [p() for p in packs]
    rows = x_ref.shape[1]
    width = cs[0].dst.shape[0]
    for s in range(2):
        here = slice(s * rows, (s + 1) * rows)
        total = par[0:1, :] + x_ref[s].astype(f32)
        for k in range(4):
            total = total + mm(cs[4 * s + k]()[...], packs[k][0:width, :], TN)
        nv, r = norm_parts(total)
        nv_ref[here] = nv
        r_ref[here] = r
        low[here] = (nv * par[1:2, :] + par[2:3, :]).astype(bf16)


def feed_kernel(info, low, low2, pack, *rest, width, far):
    if far:
        u_a, u_b, d_a, d_b, p_own, p_sib, act_out, slope_out, own, sib, up, dn = rest
        half = u_a.dst.shape[0]
        assemble(info, up, u_a(), u_b(), half)
    else:
        u_in, d_in, act_out, slope_out, own, sib = rest
        up = u_in()
    act, slope = act_out.src, slope_out.src
    units = up.shape[1]
    bias = pack()
    step = 256
    for j, rows in enumerate((low, low2)):

        def chunk(n, carry):
            cols = pl.ds(pl.multiple_of(n * step, step), step)
            hidden = mm(rows[...], up[:, cols]) + bias[width : width + 1, cols].astype(f32)
            a, g = gelu_parts(hidden)
            act[j, :, cols] = a.astype(bf16)
            slope[j, :, cols] = g.astype(bf16)
            return carry

        lax.fori_loop(0, units // step, chunk, 0)
    act_out.start()
    slope_out.start()
    if far:
        assemble(info, dn, d_a(), d_b(), half)
        sib[...] = (p_sib[...] + mm(act[1], dn[...])).astype(bf16)
        own[...] = p_own[...] + mm(act[0], dn[...])
    else:
        dn = d_in()
        own[...] = mm(act[0], dn[...])
        sib[...] = mm(act[1], dn[...])


def assemble(info, dst, a, b, half):
    dst[pl.ds(pl.multiple_of(info[3] * half, half), half)] = a[...]
    dst[pl.ds(pl.multiple_of((1 - info[3]) * half, half), half)] = b[...]


def second_norm_kernel(info, cot_in, par, nv_in, own, got, outs, gsec_out, gs_low, small):
    cot, nv_ref, gsec = cot_in(), nv_in(), gsec_out.src
    batch, rows, d = cot.shape
    sums = [0.0] * 3
    for s in range(batch):
        here = slice(s * rows, (s + 1) * rows)
        total = own[here] + got[here].astype(f32) + par[3:4, :] + (nv_ref[here] * par[1:2, :] + par[2:3, :])
        nv, r = norm_parts(total)
        outs.src[s] = (nv * par[4:5, :] + par[5:6, :]).astype(bf16)
        at = info[2] * rows + lax.broadcasted_iota(jnp.int32, (rows, 1), 0)
        seed = jnp.where(at < info[s], cot[s].astype(f32), 0.0)
        g = norm_back(seed, par[4:5, :], nv, r)
        sums = [a + rowsum(b) for a, b in zip(sums, (g, seed * nv, seed))]
        gsec[here] = g
        gs_low[here] = g.astype(bf16)
    small[...] = jnp.concatenate([*sums, jnp.zeros((5, d), f32)], axis=0)


def feed_back_kernel(info, gs, gs2, slope0, slope1, up0, dn0, u_a, u_b, d_a, d_b, gh_out, own, sib, ub, up2, dn2):
    gh = gh_out.src
    half = u_a.dst.shape[0]
    units = up0.dst.shape[1]
    ub[...] = jnp.zeros_like(ub)
    step = 256
    for k, slope in enumerate((slope0(), slope1())):
        if k:
            assemble(info, dn2, d_a(), d_b(), half)
            dn = dn2
        else:
            dn = dn0()
        for j, rows in enumerate((gs, gs2)):

            def chunk(n, carry):
                cols = pl.ds(pl.multiple_of(n * step, step), step)
                ga = mm(rows[...], dn[cols, :], NT)
                h = (ga * slope[j, :, cols].astype(f32)).astype(bf16)
                gh[k, j, :, cols] = h
                ub[k : k + 1, cols] += rowsum(h.astype(f32))
                return carry

            lax.fori_loop(0, units // step, chunk, 0)
    gh_out.start()
    assemble(info, up2, u_a(), u_b(), half)
    up = up0()
    sib[...] = (mm(gh[0, 1], up[...], NT) + mm(gh[1, 1], up2[...], NT)).astype(bf16)
    own[...] = mm(gh[0, 0], up[...], NT) + mm(gh[1, 0], up2[...], NT)


def first_back_kernel(info, par, nv_in, r_ref, own, got, gsec_in, small2, *rest):
    cs, packs = rest[:8], rest[8:12]
    gfi, g0, g1, g2, g3, okeep, osend, small, ga_low = rest[12:]
    nv_ref, gsec = nv_in(), gsec_in()
    packs = [p() for p in packs]
    n, d = own.shape
    rows = n // 2
    width = cs[0].dst.shape[0]
    sums = [0.0] * 3
    for s in range(2):
        here = slice(s * rows, (s + 1) * rows)
        u = own[here] + got[here].astype(f32) + gsec[here]
        nv = nv_ref[here]
        g = norm_back(u, par[1:2, :], nv, r_ref[here])
        sums = [a + rowsum(b) for a, b in zip(sums, (g, u * nv, u))]
        gfi.src[here] = g
        low = g.astype(bf16)
        ga_low[here] = low
        for k, out in enumerate((g0, g1, g2, g3)):
            out.src[s] = mm(packs[k][0:width, :], low, NT).astype(bf16)
    for out in (g3, g2, g1, g0, gfi):
        out.start()
    for k in range(4):
        total = mm(cs[k]()[...], ga_low[0:rows, :]) + mm(cs[4 + k]()[...], ga_low[rows:n, :])
        (osend if k % 2 else okeep).src[k // 2, 0:width, :] = total.astype(bf16)
    both = jnp.concatenate([*sums, small2[0:3, :], jnp.zeros((2, d), f32)], axis=0)
    small[...] = both
    high = both.astype(bf16)
    osend.src[0, width : width + 8, :] = high
    osend.src[1, width : width + 8, :] = (both - high.astype(f32)).astype(bf16)


def down_grads_kernel(info, act0, act1, gs, gs2, far_keep, far_send, keep, send, scr, *, parts):
    units = act0.dst.shape[2]
    block = units // parts
    step = 384
    for act, mine, theirs in ((act1(), far_keep, far_send), (act0(), keep, send)):
        for m in range(0, units, step):
            cols = slice(m, m + step)
            total = mm(act[0, :, cols], gs[...], TN) + mm(act[1, :, cols], gs2[...], TN)
            total = total.astype(bf16)
            for i in range(step // block):
                b = m // block + i
                scr[(b & 1) ^ info[3], b >> 1] = total[i * block : (i + 1) * block]
        theirs.src[...] = scr[1]
        theirs.start()
        mine.src[...] = scr[0]
        mine.start()


def up_grads_kernel(
    info, low, low2, gh_in, okeep, ogot, small, ub, far_keep, far_send, keep, send, sums, scr, *, parts, width
):
    gh = gh_in()
    units = low.shape[1]
    block = units // parts
    extra = width // parts
    joint = block + extra
    n = parts // 2 * joint
    step = 384
    got = ogot()
    both = small[...] + got[0, width : width + 8, :].astype(f32) + got[1, width : width + 8, :].astype(f32)
    both = jnp.concatenate([both[0:6], ub[0:2, :]], axis=0)
    sums[...] = both
    high = both.astype(bf16)
    far_send.src[n : n + 8, :] = high
    far_send.src[n + 8 : n + 16, :] = (both - high.astype(f32)).astype(bf16)
    for k, mine, theirs in ((1, far_keep, far_send), (0, keep, send)):
        for m in range(0, units, step):
            cols = slice(m, m + step)
            total = mm(low[:, cols], gh[k, 0], TN) + mm(low2[:, cols], gh[k, 1], TN)
            total = total.astype(bf16)
            for i in range(step // block):
                b = m // block + i
                scr[((b >> 1) & 1) ^ info[4], (b >> 2) * 2 + (b & 1), 0:block, :] = total[i * block : (i + 1) * block]
        o = (okeep()[k, 0:width, :].astype(f32) + got[k, 0:width, :].astype(f32)).astype(bf16)
        for b in range(parts):
            at = (b >> 2) * 2 + (b & 1)
            scr[((b >> 1) & 1) ^ info[4], at, block:joint, :] = o[b * extra : (b + 1) * extra]
        for b in range(parts // 2):
            theirs.src[b * joint : (b + 1) * joint, :] = scr[1, b]
            mine.src[b * joint : (b + 1) * joint, :] = scr[0, b]
        theirs.start()
        mine.start()


def swap(x, axis, bit):
    size = lax.axis_size(axis)
    return lax.ppermute(x, axis, [(i, i ^ bit) for i in range(size)])


def summed(parts):
    return sum(p.astype(f32) for p in parts)


def spread(array, axis, parts):
    bits = parts.bit_length() - 1
    return array.reshape(*array.shape[:axis], *([2] * bits), array.shape[axis] // parts, *array.shape[axis + 1 :])


def halve(terms, axis, bit, mine):
    other = [lax.dynamic_index_in_dim(t, 1 - mine, axis, keepdims=False) for t in terms]
    kept = [lax.dynamic_index_in_dim(t, mine, axis, keepdims=False) for t in terms]
    other = summed(other).astype(bf16)
    return kept + [swap(other, "dp", bit)], other


def body(
    inputs,
    cotangent,
    lengths,
    qkv_weight,
    qkv_bias,
    out_weight,
    out_bias,
    first_gain,
    first_shift,
    up_weight,
    up_bias,
    down_weight,
    down_bias,
    second_gain,
    second_shift,
):
    batch, seq, d = inputs.shape
    rows = cotangent.shape[1]
    n = batch * rows
    width = out_weight.shape[0]
    units = up_weight.shape[1]
    peers = lax.axis_size("tensor")
    parts = lax.axis_size("dp")
    bits = parts.bit_length() - 1
    t = lax.axis_index("tensor")
    dp = lax.axis_index("dp")
    bit_of = [(dp >> i) & 1 for i in range(bits)]
    info = jnp.stack([lengths[0], lengths[1], t, bit_of[0], bit_of[1]]).astype(jnp.int32)
    par = jnp.concatenate([out_bias, first_gain, first_shift, down_bias, second_gain, second_shift])
    par = par.reshape(6, d).astype(f32)
    w_t = jnp.transpose(qkv_weight, (1, 2, 0))
    pack, up_half, dn_half = prepare(info, out_weight, up_bias[None], up_weight, down_weight)
    pack2 = swap(pack, "tensor", 2)
    pack1 = swap(pack, "tensor", 1)
    u2a = swap(up_half, "tensor", 2)
    d2a = swap(dn_half, "tensor", 2)
    saved = []
    ctx = []
    for s in range(batch):
        q, k, v, lse, c, *cs = attend_fwd(s, info, inputs, w_t, qkv_bias, peers)
        saved.append((q, k, v, lse, c))
        if s == 0:
            *cs, pack1, pack2 = after(*cs, pack1, pack2)
        else:
            both = after(*cs, pack2, *ctx)
            cs, pack2, ctx = list(both[:peers]), both[peers], list(both[peers + 1 :])
        ctx += [cs[0]] + [swap(cs[j], "tensor", j) for j in range(1, peers)]
    pack3 = swap(pack2, "tensor", 1)
    packs = [pack, pack1, pack2, pack3]
    ctx[0], u2a = after(ctx[0], u2a)
    u2b = swap(u2a, "dp", 1)
    d2b = swap(d2a, "dp", 1)
    far_ctx = [whole(c) if k % peers == 0 else loose(c) for k, c in enumerate(ctx)]
    far_packs = [whole(pack)] + [loose(p) for p in packs[1:]]
    share = (inputs, ((batch, rows, d), lambda ref, info: ref.at[:, pl.ds(pl.multiple_of(info[2] * rows, rows), rows), :]))
    nv1, r1, low = call(
        "first_norm",
        first_norm_kernel,
        info,
        [share, par, *far_ctx, *far_packs],
        [[SDS((n, d), f32)], SDS((n, 1), f32), SDS((n, d), bf16)],
    )
    low2 = swap(low, "tensor", 1)
    pair = [SDS((2, n, units), bf16)]
    part = SDS((n, d), f32)
    act0, slope0, own, sib = call(
        "feed",
        feed_kernel,
        info,
        [low, low2, far_packs[0], whole(up_weight), whole(down_weight)],
        [pair, pair, part, part],
        vmem=40,
        width=width,
        far=False,
    )
    halves = [loose(x) for x in (u2a, u2b, d2a, d2b)]
    both = [pltpu.VMEM((d, units), bf16), pltpu.VMEM((units, d), bf16)]
    act1, slope1, own, sib = call(
        "feed",
        feed_kernel,
        info,
        [low, low2, far_packs[2], *halves, own, sib],
        [pair, pair, part, SDS((n, d), bf16)],
        both,
        vmem=40,
        width=width,
        far=True,
    )
    got = swap(sib, "tensor", 1)
    outputs, gsec, gs_low, small2 = call(
        "second_norm",
        second_norm_kernel,
        info,
        [whole(cotangent), par, whole(nv1), own, got],
        [[SDS((batch, rows, d), bf16)], [part], SDS((n, d), bf16), SDS((8, d), f32)],
        vmem=40,
    )
    gs_low2 = swap(gs_low, "tensor", 1)
    gh, own, sib, ub = call(
        "feed_back",
        feed_back_kernel,
        info,
        [gs_low, gs_low2, whole(slope0), whole(slope1), whole(up_weight), whole(down_weight), *halves],
        [[SDS((2, 2, n, units), bf16)], part, SDS((n, d), bf16), SDS((8, d), f32)],
        both,
        vmem=40,
    )
    got = swap(sib, "tensor", 1)
    block = units // parts
    downs = call(
        "down_grads",
        down_grads_kernel,
        info,
        [whole(act0), whole(act1), gs_low, gs_low2],
        [[SDS((parts // 2, block, d), bf16)]] * 4,
        [pltpu.VMEM((2, parts // 2, block, d), bf16)],
        parts=parts,
    )
    down_far_keep, down_far_send, down_keep, down_send = downs
    down_far_got = swap(down_far_send, "dp", 1)
    gfi, g0, g1, g2, g3, okeep, osend, small1 = call(
        "first_back",
        first_back_kernel,
        info,
        [par, whole(nv1), r1, own, got, whole(gsec), small2, *far_ctx, *far_packs],
        [
            [part],
            *[[SDS((batch, width, rows), bf16)]] * 4,
            *[[SDS((2, width + 8, d), bf16)]] * 2,
            SDS((8, d), f32),
        ],
        [pltpu.VMEM((n, d), bf16)],
        vmem=40,
    )
    gctx = [g0] + [swap(g, "tensor", j) for j, g in ((1, g1), (2, g2), (3, g3))]
    got_o = swap(osend, "tensor", 1)
    joint = block + width // parts
    cut = parts // 2 * joint
    up_far_keep, up_far_send, up_keep, up_send, small = call(
        "up_grads",
        up_grads_kernel,
        info,
        [low, low2, whole(gh), whole(okeep), loose(got_o), small1, ub],
        [
            [SDS((cut, d), bf16)],
            [SDS((cut + 16, d), bf16)],
            [SDS((cut, d), bf16)],
            [SDS((cut, d), bf16)],
            SDS((8, d), f32),
        ],
        [pltpu.VMEM((2, parts // 2, joint, d), bf16)],
        parts=parts,
        width=width,
    )
    up_far_got = swap(up_far_send, "dp", 2)
    *gctx, down_far_got, up_far_keep = after(*gctx, down_far_got, up_far_keep)
    down_far_sum = summed([down_far_keep, down_far_got]).astype(bf16)
    down_y = swap(down_far_sum, "tensor", 2)
    down_send, down_far_sum = after(down_send, down_far_sum)
    down_got = swap(down_send, "dp", 1)
    *gctx, down_far_sum, up_far_keep = after(*gctx, down_far_sum, up_far_keep)
    q, k, v, lse, c = saved[0]
    keep, send, dw, db = attend_bwd(0, info, inputs, w_t, q, k, v, lse, c, gctx, None, parts)
    near = swap(send, "tensor", 1)
    keep, down_got, up_far_got = after(keep, down_got, up_far_got)
    shape = ([2] * (bits - 1)) + [block, d]
    terms = [x.reshape(shape) for x in (down_keep, down_got, down_y)]
    down_terms, down_next = halve(terms, bits - 2, 2, bit_of[1])
    shape = ([2] * (bits - 1)) + [joint, d]
    small = small + pair_sum(up_far_got, cut, 8)
    terms = [x.reshape(shape) for x in (up_far_keep, up_far_got[:cut])]
    up_far_terms, up_far_next, small_x = halve_with(terms, bits - 2, small, "dp", 1, bit_of[0])
    up_send, up_far_next = after(up_send, up_far_next)
    up_got = swap(up_send, "dp", 2)
    in_sum = summed([keep[1], near[1]]).astype(bf16)
    far = swap(in_sum, "tensor", 2)
    first_terms = [keep[0], near[0], far]
    dw, down_next, up_far_next, in_sum, up_keep = after(dw, down_next, up_far_next, in_sum, up_keep)
    q, k, v, lse, c = saved[1]
    keep, send, w_keep, w_send, db = attend_bwd(1, info, inputs, w_t, q, k, v, lse, c, gctx, (dw, db), parts)
    near = swap(send, "tensor", 1)
    far = swap(summed([keep[1], near[1]]).astype(bf16), "tensor", 2)
    input_list = [
        (summed(x) + gfi[s * rows : (s + 1) * rows]).astype(bf16)
        for s, x in enumerate((first_terms, [keep[0], near[0], far]))
    ]
    order = [1, 0] + list(range(2, bits))
    row = 3 * (d // parts) // 2
    got = swap(w_send, "dp", 2)
    at = parts // 2 * row
    shape = ([2] * (bits - 1)) + [row, 2 * width]
    terms = [x.reshape(shape) for x in (w_keep, got[:at])]
    db = db + got[at : at + 1].astype(f32) + got[at + 1 : at + 2].astype(f32)
    for i in order[1:]:
        kept, sent, more = halve_with(terms, terms[0].ndim - 3, db, "dp", 1 << i, bit_of[i])
        terms, db = kept, db + more
    qkv_sum = summed(terms)
    qkv_sum = jnp.concatenate([qkv_sum[:, :width], qkv_sum[:, width:]], axis=0).reshape(3, -1, width)
    qkv_sum = jnp.transpose(qkv_sum, (1, 0, 2))
    db = db.reshape(2, width)
    for i in range(2, bits):
        down_terms, sent = halve(down_terms, bits - 1 - i, 1 << i, bit_of[i])
    down_sum = summed(down_terms)
    small = small + small_x
    small = jnp.concatenate([small[0:6], small[7:8], small[6:7]])
    send = summed(up_far_terms).astype(bf16)
    up_y = swap(with_rows(send, small), "tensor", 2)
    at = send.size // d
    small = jnp.concatenate([small[0:6], small[7:8], small[7:8]]) + pair_sum(up_y, at, 8)
    shape = ([2] * (bits - 1)) + [joint, d]
    terms, sent = halve([x.reshape(shape) for x in (up_keep, up_got)], bits - 2, 1, bit_of[0])
    terms.append(up_y[:at].reshape(send.shape))
    for i in range(2, bits):
        terms, sent, more = halve_with(terms, terms[0].ndim - 3, small, "dp", 1 << i, bit_of[i])
        small = small + more
    up_sum = summed(terms)
    mine = small
    return (
        outputs,
        jnp.stack(input_list, 0),
        qkv_sum,
        db,
        up_sum[block:],
        mine[0],
        mine[1],
        mine[2],
        up_sum[:block],
        mine[6],
        down_sum,
        mine[3],
        mine[4],
        mine[5],
    )


def pair_sum(array, at, n):
    return array[at : at + n].astype(f32) + array[at + n : at + 2 * n].astype(f32)


def with_rows(array, rows):
    flat = array.reshape(-1, array.shape[-1])
    high = rows.astype(bf16)
    low = (rows - high.astype(f32)).astype(bf16)
    return jnp.concatenate([flat, high, low], axis=0)


def halve_with(terms, axis, rows, name, bit, mine):
    other = [lax.dynamic_index_in_dim(t, 1 - mine, axis, keepdims=False) for t in terms]
    kept = [lax.dynamic_index_in_dim(t, mine, axis, keepdims=False) for t in terms]
    other = summed(other).astype(bf16)
    sent = with_rows(other, rows)
    got = swap(sent, name, bit)
    cut = other.size // other.shape[-1]
    return kept + [got[:cut].reshape(other.shape)], sent, pair_sum(got, cut, rows.shape[0])


def after(*values):
    return lax.optimization_barrier(values)


def solution(mesh):
    in_specs = (
        P("dp", None, None),
        P("dp", "tensor", None),
        P("dp"),
        P(None, None, "tensor"),
        P(None, "tensor"),
        P("tensor", None),
        P(),
        P(),
        P(),
        P(None, "tensor"),
        P("tensor"),
        P("tensor", None),
        P(),
        P(),
        P(),
    )
    out_specs = (
        P("dp", "tensor", None),
        P("dp", "tensor", None),
        P("dp", None, "tensor"),
        P(None, "tensor"),
        P(("tensor", "dp"), None),
        P(),
        P(),
        P(),
        P("dp", "tensor"),
        P("tensor"),
        P(("tensor", "dp"), None),
        P(),
        P(),
        P(),
    )
    return jax.shard_map(body, mesh=mesh, in_specs=in_specs, out_specs=out_specs, check_vma=False)
```

```python
import functools

import jax
import jax.numpy as jnp
from jax import lax
from jax.experimental import pallas as pl
from jax.experimental.pallas import tpu as pltpu
from jax.sharding import PartitionSpec as P

HEAD = 64
WIDE, LANES = 192, 256
NT = (((1,), (1,)), ((), ()))
NN = (((1,), (0,)), ((), ()))
TN = (((0,), (0,)), ((), ()))
bf16 = jnp.bfloat16
f32 = jnp.float32
VM = pl.BlockSpec(memory_space=pltpu.VMEM)
SDS = jax.ShapeDtypeStruct
FWD_COST = (10**10, 1000)


def mm(a, b, dims=NN):
    return lax.dot_general(a, b, dims, preferred_element_type=f32)


class Fetch:
    def __init__(self, src, dst, sem):
        self.dst, self.copy = dst, pltpu.make_async_copy(src, dst, sem)
        self.copy.start()
        self.waiting = True

    def __call__(self):
        if self.waiting:
            self.copy.wait()
            self.waiting = False
        return self.dst


class Flush:
    def __init__(self, src, dst, sem):
        self.src, self.copy = src, pltpu.make_async_copy(src, dst, sem)
        self.started = False

    def start(self):
        if not self.started:
            self.copy.start()
        self.started = True


def call(name, body, info, ins, outs, scratch=(), vmem=58, cost=1000, **static):
    far_in = [i for i, a in enumerate(ins) if isinstance(a, tuple)]
    pinned = [i for i in far_in if len(ins[i]) == 2]
    far_out = [i for i, o in enumerate(outs) if isinstance(o, list)]
    arrays = [a[0] if isinstance(a, tuple) else a for a in ins]
    shapes = [o[0] if isinstance(o, list) else o for o in outs]
    picked = [a[1] if isinstance(a, tuple) else None for a in ins]
    n_in, n_out = len(ins), len(outs)

    def kernel(info_ref, *refs):
        in_refs, refs = refs[:n_in], refs[n_in:]
        out_refs, refs = refs[:n_out], refs[n_out:]
        sem, refs = refs[-1], refs[:-1]
        buffers, rest = refs[: len(far_in) + len(far_out)], refs[len(far_in) + len(far_out) :]
        args = list(in_refs)
        for j, i in enumerate(far_in):
            view = picked[i][1]
            args[i] = Fetch(view(in_refs[i], info_ref), buffers[j], sem.at[j])
        results = list(out_refs)
        flushes = []
        for j, i in enumerate(far_out):
            at = len(far_in) + j
            results[i] = Flush(buffers[at], out_refs[i], sem.at[at])
            flushes.append(results[i])
        body(info_ref, *args, *results, *rest, **static)
        for i in far_in:
            args[i]()
        for f in flushes:
            f.start()
        for f in flushes:
            f.copy.wait()

    hbm = pl.BlockSpec(memory_space=pltpu.HBM)
    buffers = [pltpu.VMEM(picked[i][0], arrays[i].dtype) for i in far_in]
    buffers += [pltpu.VMEM(shapes[i].shape, shapes[i].dtype) for i in far_out]
    return pl.pallas_call(
        kernel,
        out_shape=[pltpu.HBM(o.shape, o.dtype) if i in far_out else o for i, o in enumerate(shapes)],
        grid_spec=pltpu.PrefetchScalarGridSpec(
            num_scalar_prefetch=1,
            grid=(1,),
            in_specs=[hbm if i in pinned else pl.BlockSpec(memory_space=pl.ANY) if i in far_in else VM for i in range(n_in)],
            out_specs=[hbm if i in far_out else VM for i in range(n_out)],
            scratch_shapes=[*buffers, *scratch, pltpu.SemaphoreType.DMA((max(1, len(far_in) + len(far_out)),))],
        ),
        compiler_params=pltpu.CompilerParams(vmem_limit_bytes=vmem << 20),
        cost_estimate=pl.CostEstimate(flops=cost, bytes_accessed=1000, transcendentals=0),
        name=name,
    )(info, *[pltpu.with_memory_space_constraint(a, pltpu.HBM) if i in pinned else a for i, a in enumerate(arrays)])


def whole(a):
    return (a, (a.shape, lambda ref, info: ref))


def loose(a):
    return (*whole(a), None)


def prepare_kernel(info, out_in, bias, up_in, dn_in, pack, up_half, dn_half):
    for src, dst in ((up_in, up_half), (dn_in, dn_half)):
        dst.src[...] = src()[...]
        dst.start()
    out_w = out_in()
    width, d = out_w.shape
    pack.src[0:width, :] = out_w[...]
    pack.src[width : width + 8, :] = jnp.broadcast_to(bias[...], (8, d))


def prepare(info, out_w, bias, up, dn):
    width, d = out_w.shape
    half = up.shape[0] // 2
    view = lambda ref, info: ref.at[pl.ds(pl.multiple_of(info[3] * half, half), half)]
    view2 = lambda ref, info: ref.at[pl.ds(pl.multiple_of(info[4] * half, half), half)]
    ins = [whole(out_w), bias, (up, ((half, d), view)), (dn, ((half, d), view2))]
    return call("prepare", prepare_kernel, info, ins, [[SDS((width + 8, d), bf16)]] + [[SDS((half, d), bf16)]] * 2)


def head_cols(a, h, extra=()):
    lane = lax.broadcasted_iota(jnp.int32, a.shape, 1)
    out = jnp.where((lane >= HEAD * h) & (lane < HEAD * (h + 1)), a, jnp.zeros_like(a))
    for i, e in enumerate(extra):
        out = jnp.where(lane == WIDE + i, e, out)
    return out


def tail_cols(rows, values):
    lane = lax.broadcasted_iota(jnp.int32, (rows, LANES - WIDE), 1)
    out = jnp.zeros((rows, LANES - WIDE), f32)
    for i, v in enumerate(values):
        out = jnp.where(lane == i, v, out)
    return out.astype(bf16)


def attend_fwd_kernel(info, x_ref, w_ref, b_ref, q_out, k_out, v_out, lse_out, c_out, *rest, which):
    outs, v_t, s_all = rest[:-2], rest[-2], rest[-1]
    length = info[which]
    me = info[2]
    q_ref, k_ref, v_ref, lse_ref, c_ref = (o.src for o in (q_out, k_out, v_out, lse_out, c_out))
    peers, width, block = c_ref.shape
    heads = width // HEAD
    seq = k_ref.shape[0]
    w = w_ref()
    x = x_ref()[...]
    k_ref[:, 0:WIDE] = mm(x, w[1], NT).astype(bf16)
    row = lax.broadcasted_iota(jnp.int32, (seq, 1), 0)
    k_ref[:, WIDE:LANES] = tail_cols(seq, (jnp.where(row < length, 0.0, -1e30),))
    q = mm(x, w[0], NT) + b_ref[0:1, :].astype(f32)
    q_ref[:, 0:WIDE] = q.astype(bf16) * jnp.asarray(0.125, bf16)
    q_ref[:, WIDE:LANES] = tail_cols(seq, (1.0,))
    v = (mm(x, w[2], NT) + b_ref[1:2, :].astype(f32)).astype(bf16)
    v_ref[...] = v
    v_t[...] = v.T
    for o in (q_out, k_out, v_out):
        o.start()

    def one_block(s, carry):
        qb = q_ref[pl.ds(pl.multiple_of(s * 2 * block, 2 * block), 2 * block), :]
        one = jnp.ones_like(qb[:, 0:1])
        for h in range(heads):
            s_all[h] = mm(k_ref[...], head_cols(qb, h, (one,)), NT)
        for h in range(heads):
            top = jnp.max(s_all[h], axis=0, keepdims=True)
            p = jnp.exp(s_all[h] - top)
            total = jnp.sum(p, axis=0, keepdims=True)
            rows = slice(HEAD * h, HEAD * (h + 1))
            out = (mm(v_t[rows, :], p.astype(bf16)) * (1.0 / total)).astype(bf16)
            lse = top + jnp.log(total)
            for j in range(2):
                cols = slice(block * j, block * (j + 1))
                c_ref[2 * s + j, rows, :] = out[:, cols]
                lse_ref[2 * s + j, h : h + 1, :] = lse[:, cols]
        return carry

    lax.fori_loop(0, peers // 2, one_block, 0)
    for k, out in enumerate(outs):
        out.src[...] = c_ref[me ^ k]


def attend_fwd(which, info, inputs, w_t, bias, peers):
    _, seq, d = inputs.shape
    width = w_t.shape[1]
    block = seq // peers
    outs = [[SDS((seq, LANES), bf16)]] * 2 + [[SDS((seq, width), bf16)]]
    outs += [[SDS((peers, 8, block), f32)], [SDS((peers, width, block), bf16)]]
    outs += [[SDS((width, block), bf16)]] * peers
    return call(
        "attend_fwd",
        attend_fwd_kernel,
        info,
        [(inputs, ((seq, d), lambda ref, info: ref.at[which])), whole(w_t), bias],
        outs,
        [pltpu.VMEM((width, seq), bf16), pltpu.VMEM((width // HEAD, seq, 2 * block), f32)],
        cost=FWD_COST[which],
        which=which,
    )


def attend_bwd_kernel(info, x_ref, w_ref, q_in, k_in, v_in, lse_in, c_in, *rest, which, first, parts):
    peers = 4
    gs, rest = rest[:peers], rest[peers:]
    if not first:
        pw_in, pb_ref = rest[:2]
        rest = rest[2:]
    if first:
        keep, send, dw_out, db_ref, dq_t, dk, dv, k_t, low, g_ref = rest
    else:
        keep, send, w_keep, w_send, db_ref, dq_t, dk, dv, k_t, low, g_ref, dw_scr, pair = rest
    length = info[which]
    me = info[2]
    k_ref, q_ref, v_ref = k_in(), q_in(), v_in()
    lse_ref, c_ref = lse_in(), c_in()
    _, width, block = c_ref.shape
    heads = width // HEAD
    k_t[...] = k_ref[:, 0:WIDE].T
    dk[...] = jnp.zeros_like(dk)
    dv[...] = jnp.zeros_like(dv)
    for k in range(peers):
        g_ref[me ^ k] = gs[k]()[...]

    def one_block(s, carry):
        at = pl.multiple_of(s * block, block)

        @pl.when(at >= length)
        def _():
            dq_t[:, pl.ds(at, block)] = jnp.zeros((width, block), f32)

        @pl.when(at < length)
        def _():
            qb = q_ref[pl.ds(at, block), :]
            g_t = g_ref[s]
            g = g_t.T
            prod_t = g_t.astype(f32) * c_ref[s].astype(f32)
            for h in range(heads):
                rows = slice(HEAD * h, HEAD * (h + 1))
                qh = head_cols(qb, h)
                gh = head_cols(g, h)
                scores = mm(k_ref[...], qh, NT)
                row = lax.broadcasted_iota(jnp.int32, scores.shape, 0)
                p = jnp.where(row < length, jnp.exp(scores - lse_ref[s, h : h + 1, :]), 0.0)
                dp = mm(v_ref[...], gh, NT)
                inner = jnp.sum(prod_t[rows], axis=0, keepdims=True)
                ds = (p * (dp - inner)).astype(bf16)
                dv[...] += mm(p.astype(bf16), gh)
                dk[...] += mm(ds, qh)
                dq_t[rows, pl.ds(at, block)] = mm(k_t[rows, :], ds) * 0.125

        return carry

    lax.fori_loop(0, peers, one_block, 0)
    low[0] = dq_t[...].T.astype(bf16)
    low[1] = dk[:, 0:WIDE].astype(bf16)
    low[2] = dv[...].astype(bf16)
    w = w_ref()
    for s in range(peers):
        at = pl.multiple_of((me ^ s) * block, block)
        total = sum(mm(low[i, pl.ds(at, block), :], w[i]) for i in range(3))
        (send if s % 2 else keep).src[s // 2] = total.astype(bf16)
    send.start()
    keep.start()
    db = jnp.concatenate([rowsum(low[i].astype(f32)) for i in (0, 2)], axis=1)
    db = db if first else db + pb_ref[...]
    db_ref[...] = db
    x_t = x_ref()[...].T
    if first:
        for i in range(3):
            dw_out.src[i] = mm(x_t, low[i])
        return
    for i in range(3):
        dw_scr[i] = mm(x_t, low[i]) + pw_in()[i]
    d = dw_scr.shape[1]
    rows = d // parts
    half = 3 * rows // 2
    for b in range(parts):
        flat = dw_scr[:, b * rows : (b + 1) * rows, :].reshape(3 * rows, width)
        flat = jnp.concatenate([flat[0:half], flat[half : 2 * half]], axis=1)
        at = ((b >> 2) * 2 + (b & 1)) * half
        pair[((b >> 1) & 1) ^ info[4], at : at + half, :] = flat.astype(bf16)
    n = parts // 2 * half
    w_send.src[0:n, :] = pair[1]
    high = db.astype(bf16)
    w_send.src[n : n + 8, :] = jnp.concatenate(
        [high, (db - high.astype(f32)).astype(bf16), jnp.zeros((6, 2 * width), bf16)], axis=0
    )
    w_send.start()
    w_keep.src[...] = pair[0]


def attend_bwd(which, info, inputs, w_t, q, k, v, lse, c, gs, prev, parts):
    _, seq, d = inputs.shape
    peers, width, block = c.shape
    outs = [[SDS((2, block, d), bf16)]] * 2
    n = 3 * d // 4
    outs += [[SDS((n, 2 * width), bf16)], [SDS((n + 8, 2 * width), bf16)]] if prev else [[SDS((3, d, width), f32)]]
    outs += [SDS((1, 2 * width), f32)]
    scratch = [
        pltpu.VMEM((width, seq), f32),
        pltpu.VMEM((seq, LANES), f32),
        pltpu.VMEM((seq, width), f32),
        pltpu.VMEM((width, seq), bf16),
        pltpu.VMEM((3, seq, width), bf16),
        pltpu.VMEM((peers, width, block), bf16),
    ]
    if prev:
        scratch += [pltpu.VMEM((3, d, width), f32), pltpu.VMEM((2, n, 2 * width), bf16)]
    ins = [(inputs, ((seq, d), lambda ref, info: ref.at[which])), whole(w_t)]
    ins += [whole(a) for a in (q, k, v, lse, c)]
    ins += [(g, ((width, block), lambda ref, info: ref.at[which]), None) for g in gs]
    if prev:
        ins += [whole(prev[0]), prev[1]]
    return call(
        "attend_bwd", attend_bwd_kernel, info, ins, outs, scratch, which=which, first=not prev, parts=parts
    )


def gelu_parts(h):
    t = 1.0 / (1.0 + (0.3275911 * 0.7071067811865476) * jnp.abs(h))
    poly = t * (0.127414796 + t * (-0.142248368 + t * (0.7107068705 + t * (-0.7265760135 + t * 0.5307027145))))
    bell = jnp.exp2((-0.5 * 1.4426950408889634) * (h * h))
    tail = poly * bell
    cum = jnp.where(h < 0, tail, 1.0 - tail)
    return h * cum, cum + h * (bell * 0.3989422804014327)


def norm_parts(v):
    center = v - jnp.mean(v, axis=1, keepdims=True)
    r = lax.rsqrt(jnp.mean(center * center, axis=1, keepdims=True) + 1e-12)
    return center * r, r


def norm_back(u, gain, nv, r):
    gu = u * gain
    return r * (gu - jnp.mean(gu, axis=1, keepdims=True) - nv * jnp.mean(gu * nv, axis=1, keepdims=True))


def rowsum(v):
    return jnp.sum(v, axis=0, keepdims=True)


def first_norm_kernel(info, x_in, par, *rest):
    cs, packs = rest[:8], rest[8:12]
    nv_out, r_ref, low = rest[12:]
    nv_ref = nv_out.src
    x_ref = x_in()
    packs = [p() for p in packs]
    rows = x_ref.shape[1]
    width = cs[0].dst.shape[0]
    for s in range(2):
        here = slice(s * rows, (s + 1) * rows)
        total = par[0:1, :] + x_ref[s].astype(f32)
        for k in range(4):
            total = total + mm(cs[4 * s + k]()[...], packs[k][0:width, :], TN)
        nv, r = norm_parts(total)
        nv_ref[here] = nv
        r_ref[here] = r
        low[here] = (nv * par[1:2, :] + par[2:3, :]).astype(bf16)


def feed_kernel(info, low, low2, pack, *rest, width, far):
    if far:
        u_a, u_b, d_a, d_b, p_own, p_sib, act_out, slope_out, own, sib, up, dn = rest
        half = u_a.dst.shape[0]
        assemble(info[3], up, u_a(), u_b(), half)
    else:
        u_in, d_in, act_out, slope_out, own, sib = rest
        up = u_in()
    act, slope = act_out.src, slope_out.src
    units = up.shape[1]
    bias = pack()
    step = 256
    for j, rows in enumerate((low, low2)):

        def chunk(n, carry):
            cols = pl.ds(pl.multiple_of(n * step, step), step)
            hidden = mm(rows[...], up[:, cols]) + bias[width : width + 1, cols].astype(f32)
            a, g = gelu_parts(hidden)
            act[j, :, cols] = a.astype(bf16)
            slope[j, :, cols] = g.astype(bf16)
            return carry

        lax.fori_loop(0, units // step, chunk, 0)
    act_out.start()
    slope_out.start()
    if far:
        assemble(info[4], dn, d_a(), d_b(), half)
        sib[...] = (p_sib[...] + mm(act[1], dn[...])).astype(bf16)
        own[...] = p_own[...] + mm(act[0], dn[...])
    else:
        dn = d_in()
        own[...] = mm(act[0], dn[...])
        sib[...] = mm(act[1], dn[...])


def assemble(bit, dst, a, b, half):
    dst[pl.ds(pl.multiple_of(bit * half, half), half)] = a[...]
    dst[pl.ds(pl.multiple_of((1 - bit) * half, half), half)] = b[...]


def second_norm_kernel(info, cot_in, par, nv_in, own, got, outs, gsec_out, gs_low, small):
    cot, nv_ref, gsec = cot_in(), nv_in(), gsec_out.src
    batch, rows, d = cot.shape
    sums = [0.0] * 3
    for s in range(batch):
        here = slice(s * rows, (s + 1) * rows)
        total = own[here] + got[here].astype(f32) + par[3:4, :] + (nv_ref[here] * par[1:2, :] + par[2:3, :])
        nv, r = norm_parts(total)
        outs.src[s] = (nv * par[4:5, :] + par[5:6, :]).astype(bf16)
        at = info[2] * rows + lax.broadcasted_iota(jnp.int32, (rows, 1), 0)
        seed = jnp.where(at < info[s], cot[s].astype(f32), 0.0)
        g = norm_back(seed, par[4:5, :], nv, r)
        sums = [a + rowsum(b) for a, b in zip(sums, (g, seed * nv, seed))]
        gsec[here] = g
        gs_low[here] = g.astype(bf16)
    small[...] = jnp.concatenate([*sums, jnp.zeros((5, d), f32)], axis=0)


def feed_back_kernel(info, gs, gs2, slope0, slope1, up0, dn0, u_a, u_b, d_a, d_b, gh_out, own, sib, ub, up2, dn2):
    gh = gh_out.src
    half = u_a.dst.shape[0]
    units = up0.dst.shape[1]
    ub[...] = jnp.zeros_like(ub)
    step = 256
    for k, slope in enumerate((slope0(), slope1())):
        if k:
            assemble(info[4], dn2, d_a(), d_b(), half)
            dn = dn2
        else:
            dn = dn0()
        for j, rows in enumerate((gs, gs2)):

            def chunk(n, carry):
                cols = pl.ds(pl.multiple_of(n * step, step), step)
                ga = mm(rows[...], dn[cols, :], NT)
                h = (ga * slope[j, :, cols].astype(f32)).astype(bf16)
                gh[k, j, :, cols] = h
                ub[k : k + 1, cols] += rowsum(h.astype(f32))
                return carry

            lax.fori_loop(0, units // step, chunk, 0)
    gh_out.start()
    assemble(info[3], up2, u_a(), u_b(), half)
    up = up0()
    sib[...] = (mm(gh[0, 1], up[...], NT) + mm(gh[1, 1], up2[...], NT)).astype(bf16)
    own[...] = mm(gh[0, 0], up[...], NT) + mm(gh[1, 0], up2[...], NT)


def first_back_kernel(info, par, nv_in, r_ref, own, got, gsec_in, small2, *rest):
    cs, packs = rest[:8], rest[8:12]
    gfi, g0, g1, g2, g3, okeep, osend, small, ga_low = rest[12:]
    nv_ref, gsec = nv_in(), gsec_in()
    packs = [p() for p in packs]
    n, d = own.shape
    rows = n // 2
    width = cs[0].dst.shape[0]
    sums = [0.0] * 3
    for s in range(2):
        here = slice(s * rows, (s + 1) * rows)
        u = own[here] + got[here].astype(f32) + gsec[here]
        nv = nv_ref[here]
        g = norm_back(u, par[1:2, :], nv, r_ref[here])
        sums = [a + rowsum(b) for a, b in zip(sums, (g, u * nv, u))]
        gfi.src[here] = g
        low = g.astype(bf16)
        ga_low[here] = low
        for k, out in enumerate((g0, g1, g2, g3)):
            out.src[s] = mm(packs[k][0:width, :], low, NT).astype(bf16)
    for out in (g3, g2, g1, g0, gfi):
        out.start()
    for k in range(4):
        total = mm(cs[k]()[...], ga_low[0:rows, :]) + mm(cs[4 + k]()[...], ga_low[rows:n, :])
        (osend if k % 2 else okeep).src[k // 2, 0:width, :] = total.astype(bf16)
    both = jnp.concatenate([*sums, small2[0:3, :], jnp.zeros((2, d), f32)], axis=0)
    small[...] = both
    high = both.astype(bf16)
    osend.src[0, width : width + 8, :] = high
    osend.src[1, width : width + 8, :] = (both - high.astype(f32)).astype(bf16)


def down_grads_kernel(info, act0, act1, gs, gs2, far_keep, far_send, keep, send, scr, *, parts):
    units = act0.dst.shape[2]
    block = units // parts
    step = 384
    for act, mine, theirs in ((act1(), far_keep, far_send), (act0(), keep, send)):
        for m in range(0, units, step):
            cols = slice(m, m + step)
            total = mm(act[0, :, cols], gs[...], TN) + mm(act[1, :, cols], gs2[...], TN)
            total = total.astype(bf16)
            for i in range(step // block):
                b = m // block + i
                scr[(b & 1) ^ info[3], b >> 1] = total[i * block : (i + 1) * block]
        theirs.src[...] = scr[1]
        theirs.start()
        mine.src[...] = scr[0]
        mine.start()


def up_grads_kernel(
    info, low, low2, gh_in, okeep, ogot, small, ub, far_keep, far_send, keep, send, sums, scr, *, parts, width
):
    gh = gh_in()
    units = low.shape[1]
    block = units // parts
    extra = width // parts
    joint = block + extra
    n = parts // 2 * joint
    step = 384
    got = ogot()
    both = small[...] + got[0, width : width + 8, :].astype(f32) + got[1, width : width + 8, :].astype(f32)
    both = jnp.concatenate([both[0:6], ub[0:2, :]], axis=0)
    sums[...] = both
    high = both.astype(bf16)
    far_send.src[n : n + 8, :] = high
    far_send.src[n + 8 : n + 16, :] = (both - high.astype(f32)).astype(bf16)
    for k, mine, theirs in ((1, far_keep, far_send), (0, keep, send)):
        for m in range(0, units, step):
            cols = slice(m, m + step)
            total = mm(low[:, cols], gh[k, 0], TN) + mm(low2[:, cols], gh[k, 1], TN)
            total = total.astype(bf16)
            for i in range(step // block):
                b = m // block + i
                scr[((b >> 1) & 1) ^ info[4], (b >> 2) * 2 + (b & 1), 0:block, :] = total[i * block : (i + 1) * block]
        o = (okeep()[k, 0:width, :].astype(f32) + got[k, 0:width, :].astype(f32)).astype(bf16)
        for b in range(parts):
            at = (b >> 2) * 2 + (b & 1)
            scr[((b >> 1) & 1) ^ info[4], at, block:joint, :] = o[b * extra : (b + 1) * extra]
        for b in range(parts // 2):
            theirs.src[b * joint : (b + 1) * joint, :] = scr[1, b]
            mine.src[b * joint : (b + 1) * joint, :] = scr[0, b]
        theirs.start()
        mine.start()


def swap(x, axis, bit):
    size = lax.axis_size(axis)
    return lax.ppermute(x, axis, [(i, i ^ bit) for i in range(size)])


def summed(parts):
    return sum(p.astype(f32) for p in parts)


def spread(array, axis, parts):
    bits = parts.bit_length() - 1
    return array.reshape(*array.shape[:axis], *([2] * bits), array.shape[axis] // parts, *array.shape[axis + 1 :])


def halve(terms, axis, bit, mine):
    other = [lax.dynamic_index_in_dim(t, 1 - mine, axis, keepdims=False) for t in terms]
    kept = [lax.dynamic_index_in_dim(t, mine, axis, keepdims=False) for t in terms]
    other = summed(other).astype(bf16)
    return kept + [swap(other, "dp", bit)], other


def body(
    inputs,
    cotangent,
    lengths,
    qkv_weight,
    qkv_bias,
    out_weight,
    out_bias,
    first_gain,
    first_shift,
    up_weight,
    up_bias,
    down_weight,
    down_bias,
    second_gain,
    second_shift,
):
    batch, seq, d = inputs.shape
    rows = cotangent.shape[1]
    n = batch * rows
    width = out_weight.shape[0]
    units = up_weight.shape[1]
    peers = lax.axis_size("tensor")
    parts = lax.axis_size("dp")
    bits = parts.bit_length() - 1
    t = lax.axis_index("tensor")
    dp = lax.axis_index("dp")
    bit_of = [(dp >> i) & 1 for i in range(bits)]
    info = jnp.stack([lengths[0], lengths[1], t, bit_of[0], bit_of[1]]).astype(jnp.int32)
    par = jnp.concatenate([out_bias, first_gain, first_shift, down_bias, second_gain, second_shift])
    par = par.reshape(6, d).astype(f32)
    w_t = jnp.transpose(qkv_weight, (1, 2, 0))
    pack, up_half, dn_half = prepare(info, out_weight, up_bias[None], up_weight, down_weight)
    pack2 = swap(pack, "tensor", 2)
    pack1 = swap(pack, "tensor", 1)
    u2a = swap(up_half, "tensor", 2)
    d2a = swap(dn_half, "tensor", 2)
    saved = []
    ctx = []
    for s in range(batch):
        q, k, v, lse, c, *cs = attend_fwd(s, info, inputs, w_t, qkv_bias, peers)
        saved.append((q, k, v, lse, c))
        if s == 0:
            *cs, pack1, pack2 = after(*cs, pack1, pack2)
        else:
            both = after(*cs, pack2, *ctx)
            cs, pack2, ctx = list(both[:peers]), both[peers], list(both[peers + 1 :])
        ctx += [cs[0]] + [swap(cs[j], "tensor", j) for j in range(1, peers)]
    pack3 = swap(pack2, "tensor", 1)
    packs = [pack, pack1, pack2, pack3]
    ctx[0], u2a = after(ctx[0], u2a)
    u2b = swap(u2a, "dp", 1)
    d2b = swap(d2a, "dp", 2)
    far_ctx = [whole(c) if k % peers == 0 else loose(c) for k, c in enumerate(ctx)]
    far_packs = [whole(pack)] + [loose(p) for p in packs[1:]]
    share = (inputs, ((batch, rows, d), lambda ref, info: ref.at[:, pl.ds(pl.multiple_of(info[2] * rows, rows), rows), :]))
    nv1, r1, low = call(
        "first_norm",
        first_norm_kernel,
        info,
        [share, par, *far_ctx, *far_packs],
        [[SDS((n, d), f32)], SDS((n, 1), f32), SDS((n, d), bf16)],
    )
    low2 = swap(low, "tensor", 1)
    pair = [SDS((2, n, units), bf16)]
    part = SDS((n, d), f32)
    act0, slope0, own, sib = call(
        "feed",
        feed_kernel,
        info,
        [low, low2, far_packs[0], whole(up_weight), whole(down_weight)],
        [pair, pair, part, part],
        vmem=40,
        width=width,
        far=False,
    )
    halves = [loose(x) for x in (u2a, u2b, d2a, d2b)]
    both = [pltpu.VMEM((d, units), bf16), pltpu.VMEM((units, d), bf16)]
    act1, slope1, own, sib = call(
        "feed",
        feed_kernel,
        info,
        [low, low2, far_packs[2], *halves, own, sib],
        [pair, pair, part, SDS((n, d), bf16)],
        both,
        vmem=40,
        width=width,
        far=True,
    )
    got = swap(sib, "tensor", 1)
    outputs, gsec, gs_low, small2 = call(
        "second_norm",
        second_norm_kernel,
        info,
        [whole(cotangent), par, whole(nv1), own, got],
        [[SDS((batch, rows, d), bf16)], [part], SDS((n, d), bf16), SDS((8, d), f32)],
        vmem=40,
    )
    gs_low2 = swap(gs_low, "tensor", 1)
    gh, own, sib, ub = call(
        "feed_back",
        feed_back_kernel,
        info,
        [gs_low, gs_low2, whole(slope0), whole(slope1), whole(up_weight), whole(down_weight), *halves],
        [[SDS((2, 2, n, units), bf16)], part, SDS((n, d), bf16), SDS((8, d), f32)],
        both,
        vmem=40,
    )
    got = swap(sib, "tensor", 1)
    block = units // parts
    downs = call(
        "down_grads",
        down_grads_kernel,
        info,
        [whole(act0), whole(act1), gs_low, gs_low2],
        [[SDS((parts // 2, block, d), bf16)]] * 4,
        [pltpu.VMEM((2, parts // 2, block, d), bf16)],
        parts=parts,
    )
    down_far_keep, down_far_send, down_keep, down_send = downs
    down_far_got = swap(down_far_send, "dp", 1)
    gfi, g0, g1, g2, g3, okeep, osend, small1 = call(
        "first_back",
        first_back_kernel,
        info,
        [par, whole(nv1), r1, own, got, whole(gsec), small2, *far_ctx, *far_packs],
        [
            [part],
            *[[SDS((batch, width, rows), bf16)]] * 4,
            *[[SDS((2, width + 8, d), bf16)]] * 2,
            SDS((8, d), f32),
        ],
        [pltpu.VMEM((n, d), bf16)],
        vmem=40,
    )
    gctx = [g0] + [swap(g, "tensor", j) for j, g in ((1, g1), (2, g2), (3, g3))]
    got_o = swap(osend, "tensor", 1)
    joint = block + width // parts
    cut = parts // 2 * joint
    up_far_keep, up_far_send, up_keep, up_send, small = call(
        "up_grads",
        up_grads_kernel,
        info,
        [low, low2, whole(gh), whole(okeep), loose(got_o), small1, ub],
        [
            [SDS((cut, d), bf16)],
            [SDS((cut + 16, d), bf16)],
            [SDS((cut, d), bf16)],
            [SDS((cut, d), bf16)],
            SDS((8, d), f32),
        ],
        [pltpu.VMEM((2, parts // 2, joint, d), bf16)],
        parts=parts,
        width=width,
    )
    up_far_got = swap(up_far_send, "dp", 2)
    *gctx, down_far_got, up_far_keep = after(*gctx, down_far_got, up_far_keep)
    down_far_sum = summed([down_far_keep, down_far_got]).astype(bf16)
    down_y = swap(down_far_sum, "tensor", 2)
    down_send, down_far_sum = after(down_send, down_far_sum)
    down_got = swap(down_send, "dp", 1)
    *gctx, down_far_sum, up_far_keep = after(*gctx, down_far_sum, up_far_keep)
    q, k, v, lse, c = saved[0]
    keep, send, dw, db = attend_bwd(0, info, inputs, w_t, q, k, v, lse, c, gctx, None, parts)
    near = swap(send, "tensor", 1)
    keep, down_got, up_far_got = after(keep, down_got, up_far_got)
    shape = ([2] * (bits - 1)) + [block, d]
    terms = [x.reshape(shape) for x in (down_keep, down_got, down_y)]
    down_terms, down_next = halve(terms, bits - 2, 2, bit_of[1])
    shape = ([2] * (bits - 1)) + [joint, d]
    small = small + pair_sum(up_far_got, cut, 8)
    terms = [x.reshape(shape) for x in (up_far_keep, up_far_got[:cut])]
    up_far_terms, up_far_next, small_x = halve_with(terms, bits - 2, small, "dp", 1, bit_of[0])
    up_send, up_far_next = after(up_send, up_far_next)
    up_got = swap(up_send, "dp", 2)
    in_sum = summed([keep[1], near[1]]).astype(bf16)
    far = swap(in_sum, "tensor", 2)
    first_terms = [keep[0], near[0], far]
    dw, down_next, up_far_next, in_sum, up_keep = after(dw, down_next, up_far_next, in_sum, up_keep)
    q, k, v, lse, c = saved[1]
    keep, send, w_keep, w_send, db = attend_bwd(1, info, inputs, w_t, q, k, v, lse, c, gctx, (dw, db), parts)
    near = swap(send, "tensor", 1)
    in_sum = summed([keep[1], near[1]]).astype(bf16)
    far = swap(in_sum, "tensor", 2)
    input_list = [
        (summed(x) + gfi[s * rows : (s + 1) * rows]).astype(bf16)
        for s, x in enumerate((first_terms, [keep[0], near[0], far]))
    ]
    for i in range(2, bits):
        down_terms, sent = halve(down_terms, bits - 1 - i, 1 << i, bit_of[i])
    down_sum = summed(down_terms)
    small = small + small_x
    small = jnp.concatenate([small[0:6], small[7:8], small[6:7]])
    send = summed(up_far_terms).astype(bf16)
    up_y_sent = with_rows(send, small)
    up_y = swap(up_y_sent, "tensor", 2)
    at = send.size // d
    small = jnp.concatenate([small[0:6], small[7:8], small[7:8]]) + pair_sum(up_y, at, 8)
    shape = ([2] * (bits - 1)) + [joint, d]
    terms, up_next = halve([x.reshape(shape) for x in (up_keep, up_got)], bits - 2, 1, bit_of[0])
    terms.append(up_y[:at].reshape(send.shape))
    for i in range(2, bits):
        terms, sent, more = halve_with(terms, terms[0].ndim - 3, small, "dp", 1 << i, bit_of[i])
        small = small + more
    up_sum = summed(terms)
    mine = small
    order = [1, 0] + list(range(2, bits))
    row = 3 * (d // parts) // 2
    got = swap(w_send, "dp", 2)
    got, in_sum, up_next, up_y_sent = after(got, in_sum, up_next, up_y_sent)
    at = parts // 2 * row
    shape = ([2] * (bits - 1)) + [row, 2 * width]
    terms = [x.reshape(shape) for x in (w_keep, got[:at])]
    db = db + got[at : at + 1].astype(f32) + got[at + 1 : at + 2].astype(f32)
    for i in order[1:]:
        kept, sent, more = halve_with(terms, terms[0].ndim - 3, db, "dp", 1 << i, bit_of[i])
        terms, db = kept, db + more
    qkv_sum = summed(terms)
    qkv_sum = jnp.concatenate([qkv_sum[:, :width], qkv_sum[:, width:]], axis=0).reshape(3, -1, width)
    qkv_sum = jnp.transpose(qkv_sum, (1, 0, 2))
    db = db.reshape(2, width)
    return (
        outputs,
        jnp.stack(input_list, 0),
        qkv_sum,
        db,
        up_sum[block:],
        mine[0],
        mine[1],
        mine[2],
        up_sum[:block],
        mine[6],
        down_sum,
        mine[3],
        mine[4],
        mine[5],
    )


def pair_sum(array, at, n):
    return array[at : at + n].astype(f32) + array[at + n : at + 2 * n].astype(f32)


def with_rows(array, rows):
    flat = array.reshape(-1, array.shape[-1])
    high = rows.astype(bf16)
    low = (rows - high.astype(f32)).astype(bf16)
    return jnp.concatenate([flat, high, low], axis=0)


def halve_with(terms, axis, rows, name, bit, mine):
    other = [lax.dynamic_index_in_dim(t, 1 - mine, axis, keepdims=False) for t in terms]
    kept = [lax.dynamic_index_in_dim(t, mine, axis, keepdims=False) for t in terms]
    other = summed(other).astype(bf16)
    sent = with_rows(other, rows)
    got = swap(sent, name, bit)
    cut = other.size // other.shape[-1]
    return kept + [got[:cut].reshape(other.shape)], sent, pair_sum(got, cut, rows.shape[0])


def after(*values):
    return lax.optimization_barrier(values)


def solution(mesh):
    in_specs = (
        P("dp", None, None),
        P("dp", "tensor", None),
        P("dp"),
        P(None, None, "tensor"),
        P(None, "tensor"),
        P("tensor", None),
        P(),
        P(),
        P(),
        P(None, "tensor"),
        P("tensor"),
        P("tensor", None),
        P(),
        P(),
        P(),
    )
    out_specs = (
        P("dp", "tensor", None),
        P("dp", "tensor", None),
        P("dp", None, "tensor"),
        P(None, "tensor"),
        P(("tensor", "dp"), None),
        P(),
        P(),
        P(),
        P("dp", "tensor"),
        P("tensor"),
        P(("tensor", "dp"), None),
        P(),
        P(),
        P(),
    )
    return jax.shard_map(body, mesh=mesh, in_specs=in_specs, out_specs=out_specs, check_vma=False)
```

```python
import functools

import jax
import jax.numpy as jnp
from jax import lax
from jax.experimental import pallas as pl
from jax.experimental.pallas import tpu as pltpu
from jax.sharding import PartitionSpec as P

HEAD = 64
WIDE, LANES = 192, 256
NEAR = 30
NT = (((1,), (1,)), ((), ()))
NN = (((1,), (0,)), ((), ()))
TN = (((0,), (0,)), ((), ()))
bf16 = jnp.bfloat16
f32 = jnp.float32
VM = pl.BlockSpec(memory_space=pltpu.VMEM)
SDS = jax.ShapeDtypeStruct
FWD_COST = (10**10, 1000)


def mm(a, b, dims=NN):
    return lax.dot_general(a, b, dims, preferred_element_type=f32)


class Fetch:
    def __init__(self, src, dst, sem):
        self.dst, self.copy = dst, pltpu.make_async_copy(src, dst, sem)
        self.copy.start()
        self.waiting = True

    def __call__(self):
        if self.waiting:
            self.copy.wait()
            self.waiting = False
        return self.dst


class Flush:
    def __init__(self, src, dst, sem):
        self.src, self.copy = src, pltpu.make_async_copy(src, dst, sem)
        self.started = False

    def start(self):
        if not self.started:
            self.copy.start()
        self.started = True


def call(name, body, info, ins, outs, scratch=(), vmem=58, cost=1000, **static):
    far_in = [i for i, a in enumerate(ins) if isinstance(a, tuple)]
    pinned = [i for i in far_in if len(ins[i]) == 2]
    far_out = [i for i, o in enumerate(outs) if isinstance(o, list)]
    arrays = [a[0] if isinstance(a, tuple) else a for a in ins]
    shapes = [o[0] if isinstance(o, list) else o for o in outs]
    picked = [a[1] if isinstance(a, tuple) else None for a in ins]
    n_in, n_out = len(ins), len(outs)

    def kernel(lengths_ref, *refs):
        dp = lax.axis_index("dp")
        info_ref = (lengths_ref[0], lengths_ref[1], lax.axis_index("tensor"), dp & 1, (dp >> 1) & 1)
        in_refs, refs = refs[:n_in], refs[n_in:]
        out_refs, refs = refs[:n_out], refs[n_out:]
        sem, refs = refs[-1], refs[:-1]
        buffers, rest = refs[: len(far_in) + len(far_out)], refs[len(far_in) + len(far_out) :]
        args = list(in_refs)
        for j, i in enumerate(far_in):
            view = picked[i][1]
            args[i] = Fetch(view(in_refs[i], info_ref), buffers[j], sem.at[j])
        results = list(out_refs)
        flushes = []
        for j, i in enumerate(far_out):
            at = len(far_in) + j
            results[i] = Flush(buffers[at], out_refs[i], sem.at[at])
            flushes.append(results[i])
        body(info_ref, *args, *results, *rest, **static)
        for i in far_in:
            args[i]()
        for f in flushes:
            f.start()
        for f in flushes:
            f.copy.wait()

    hbm = pl.BlockSpec(memory_space=pltpu.HBM)
    buffers = [pltpu.VMEM(picked[i][0], arrays[i].dtype) for i in far_in]
    buffers += [pltpu.VMEM(shapes[i].shape, shapes[i].dtype) for i in far_out]
    return pl.pallas_call(
        kernel,
        out_shape=[pltpu.HBM(o.shape, o.dtype) if i in far_out else o for i, o in enumerate(shapes)],
        grid_spec=pltpu.PrefetchScalarGridSpec(
            num_scalar_prefetch=1,
            grid=(1,),
            in_specs=[hbm if i in pinned else pl.BlockSpec(memory_space=pl.ANY) if i in far_in else VM for i in range(n_in)],
            out_specs=[hbm if i in far_out else VM for i in range(n_out)],
            scratch_shapes=[*buffers, *scratch, pltpu.SemaphoreType.DMA((max(1, len(far_in) + len(far_out)),))],
        ),
        compiler_params=pltpu.CompilerParams(vmem_limit_bytes=vmem << 20),
        cost_estimate=pl.CostEstimate(flops=cost, bytes_accessed=1000, transcendentals=0),
        name=name,
    )(info, *[pltpu.with_memory_space_constraint(a, pltpu.HBM) if i in pinned else a for i, a in enumerate(arrays)])


def ref(x):
    return x() if isinstance(x, Fetch) else x.src if isinstance(x, Flush) else x


def whole(a):
    return (a, (a.shape, lambda ref, info: ref))


def loose(a):
    return (*whole(a), None)


def prepare_kernel(info, out_in, bias, up_in, dn_in, pack, up_half, dn_half):
    for src, dst in ((up_in, up_half), (dn_in, dn_half)):
        dst.src[...] = src()[...]
        dst.start()
    out_w = out_in()
    width, d = out_w.shape
    pack.src[0:width, :] = out_w[...]
    pack.src[width : width + 8, :] = jnp.broadcast_to(bias[...], (8, d))


def prepare(info, out_w, bias, up, dn):
    width, d = out_w.shape
    half = up.shape[0] // 2
    view = lambda ref, info: ref.at[pl.ds(pl.multiple_of(info[3] * half, half), half)]
    view2 = lambda ref, info: ref.at[pl.ds(pl.multiple_of(info[4] * half, half), half)]
    ins = [whole(out_w), bias, (up, ((half, d), view)), (dn, ((half, d), view2))]
    return call("prepare", prepare_kernel, info, ins, [[SDS((width + 8, d), bf16)]] + [[SDS((half, d), bf16)]] * 2)


def head_cols(a, h, extra=()):
    lane = lax.broadcasted_iota(jnp.int32, a.shape, 1)
    out = jnp.where((lane >= HEAD * h) & (lane < HEAD * (h + 1)), a, jnp.zeros_like(a))
    for i, e in enumerate(extra):
        out = jnp.where(lane == WIDE + i, e, out)
    return out


def tail_cols(rows, values):
    lane = lax.broadcasted_iota(jnp.int32, (rows, LANES - WIDE), 1)
    out = jnp.zeros((rows, LANES - WIDE), f32)
    for i, v in enumerate(values):
        out = jnp.where(lane == i, v, out)
    return out.astype(bf16)


def attend_fwd_kernel(info, x_ref, w_ref, b_ref, q_out, k_out, v_out, lse_out, c_out, *rest, which):
    outs, v_t, s_all = rest[:-2], rest[-2], rest[-1]
    length = info[which]
    me = info[2]
    q_ref, k_ref, v_ref, lse_ref, c_ref = (o.src for o in (q_out, k_out, v_out, lse_out, c_out))
    peers, width, block = c_ref.shape
    heads = width // HEAD
    seq = k_ref.shape[0]
    w = w_ref()
    x = x_ref()[...]
    k_ref[:, 0:WIDE] = mm(x, w[1], NT).astype(bf16)
    row = lax.broadcasted_iota(jnp.int32, (seq, 1), 0)
    k_ref[:, WIDE:LANES] = tail_cols(seq, (jnp.where(row < length, 0.0, -1e30),))
    q = mm(x, w[0], NT) + b_ref[0:1, :].astype(f32)
    q_ref[:, 0:WIDE] = q.astype(bf16) * jnp.asarray(0.125, bf16)
    q_ref[:, WIDE:LANES] = tail_cols(seq, (1.0,))
    v = (mm(x, w[2], NT) + b_ref[1:2, :].astype(f32)).astype(bf16)
    v_ref[...] = v
    v_t[...] = v.T
    for o in (q_out, k_out, v_out):
        o.start()

    def one_block(s, carry):
        qb = q_ref[pl.ds(pl.multiple_of(s * 2 * block, 2 * block), 2 * block), :]
        one = jnp.ones_like(qb[:, 0:1])
        for h in range(heads):
            s_all[h] = mm(k_ref[...], head_cols(qb, h, (one,)), NT)
        for h in range(heads):
            top = jnp.max(s_all[h], axis=0, keepdims=True)
            p = jnp.exp(s_all[h] - top)
            total = jnp.sum(p, axis=0, keepdims=True)
            rows = slice(HEAD * h, HEAD * (h + 1))
            out = (mm(v_t[rows, :], p.astype(bf16)) * (1.0 / total)).astype(bf16)
            lse = top + jnp.log(total)
            for j in range(2):
                cols = slice(block * j, block * (j + 1))
                c_ref[2 * s + j, rows, :] = out[:, cols]
                lse_ref[2 * s + j, h : h + 1, :] = lse[:, cols]
        return carry

    lax.fori_loop(0, peers // 2, one_block, 0)
    for k, out in enumerate(outs):
        out.src[...] = c_ref[me ^ k]


def attend_fwd(which, info, inputs, w_t, bias, peers):
    _, seq, d = inputs.shape
    width = w_t.shape[1]
    block = seq // peers
    outs = [[SDS((seq, LANES), bf16)]] * 2 + [[SDS((seq, width), bf16)]]
    outs += [[SDS((peers, 8, block), f32)], [SDS((peers, width, block), bf16)]]
    outs += [[SDS((width, block), bf16)]] * peers
    return call(
        "attend_fwd",
        attend_fwd_kernel,
        info,
        [(inputs, ((seq, d), lambda ref, info: ref.at[which])), whole(w_t), bias],
        outs,
        [pltpu.VMEM((width, seq), bf16), pltpu.VMEM((width // HEAD, seq, 2 * block), f32)],
        cost=FWD_COST[which],
        which=which,
    )


def attend_bwd_kernel(info, x_ref, w_ref, q_in, k_in, v_in, lse_in, c_in, *rest, which, first, parts):
    peers = 4
    gs, rest = rest[:peers], rest[peers:]
    if not first:
        pw_in, pb_ref = rest[:2]
        rest = rest[2:]
    if first:
        keep, send, dw_out, db_ref, dq_t, dk, dv, k_t, low, g_ref = rest
    else:
        keep, send, w_keep, w_send, db_ref, dq_t, dk, dv, k_t, low, g_ref, dw_scr, pair = rest
    length = info[which]
    me = info[2]
    k_ref, q_ref, v_ref = k_in(), q_in(), v_in()
    lse_ref, c_ref = lse_in(), c_in()
    _, width, block = c_ref.shape
    heads = width // HEAD
    k_t[...] = k_ref[:, 0:WIDE].T
    dk[...] = jnp.zeros_like(dk)
    dv[...] = jnp.zeros_like(dv)
    for k in range(peers):
        g_ref[me ^ k] = gs[k]()[...]

    def one_block(s, carry):
        at = pl.multiple_of(s * block, block)

        @pl.when(at >= length)
        def _():
            dq_t[:, pl.ds(at, block)] = jnp.zeros((width, block), f32)

        @pl.when(at < length)
        def _():
            qb = q_ref[pl.ds(at, block), :]
            g_t = g_ref[s]
            g = g_t.T
            prod_t = g_t.astype(f32) * c_ref[s].astype(f32)
            for h in range(heads):
                rows = slice(HEAD * h, HEAD * (h + 1))
                qh = head_cols(qb, h)
                gh = head_cols(g, h)
                scores = mm(k_ref[...], qh, NT)
                row = lax.broadcasted_iota(jnp.int32, scores.shape, 0)
                p = jnp.where(row < length, jnp.exp(scores - lse_ref[s, h : h + 1, :]), 0.0)
                dp = mm(v_ref[...], gh, NT)
                inner = jnp.sum(prod_t[rows], axis=0, keepdims=True)
                ds = (p * (dp - inner)).astype(bf16)
                dv[...] += mm(p.astype(bf16), gh)
                dk[...] += mm(ds, qh)
                dq_t[rows, pl.ds(at, block)] = mm(k_t[rows, :], ds) * 0.125

        return carry

    lax.fori_loop(0, peers, one_block, 0)
    low[0] = dq_t[...].T.astype(bf16)
    low[1] = dk[:, 0:WIDE].astype(bf16)
    low[2] = dv[...].astype(bf16)
    w = w_ref()
    for s in range(peers):
        at = pl.multiple_of((me ^ s) * block, block)
        total = sum(mm(low[i, pl.ds(at, block), :], w[i]) for i in range(3))
        (send if s % 2 else keep).src[s // 2] = total.astype(bf16)
    send.start()
    keep.start()
    db = jnp.concatenate([rowsum(low[i].astype(f32)) for i in (0, 2)], axis=1)
    db = db if first else db + pb_ref[...]
    db_ref[...] = db
    x_t = x_ref()[...].T
    if first:
        for i in range(3):
            dw_out.src[i] = mm(x_t, low[i])
        return
    for i in range(3):
        dw_scr[i] = mm(x_t, low[i]) + pw_in()[i]
    d = dw_scr.shape[1]
    rows = d // parts
    half = 3 * rows // 2
    for b in range(parts):
        flat = dw_scr[:, b * rows : (b + 1) * rows, :].reshape(3 * rows, width)
        flat = jnp.concatenate([flat[0:half], flat[half : 2 * half]], axis=1)
        at = ((b >> 2) * 2 + (b & 1)) * half
        pair[((b >> 1) & 1) ^ info[4], at : at + half, :] = flat.astype(bf16)
    n = parts // 2 * half
    w_send.src[0:n, :] = pair[1]
    high = db.astype(bf16)
    w_send.src[n : n + 8, :] = jnp.concatenate(
        [high, (db - high.astype(f32)).astype(bf16), jnp.zeros((6, 2 * width), bf16)], axis=0
    )
    w_send.start()
    w_keep.src[...] = pair[0]


def attend_bwd(which, info, inputs, w_t, q, k, v, lse, c, gs, prev, parts):
    _, seq, d = inputs.shape
    peers, width, block = c.shape
    outs = [[SDS((2, block, d), bf16)]] * 2
    n = 3 * d // 4
    outs += [[SDS((n, 2 * width), bf16)], [SDS((n + 8, 2 * width), bf16)]] if prev else [[SDS((3, d, width), f32)]]
    outs += [SDS((1, 2 * width), f32)]
    scratch = [
        pltpu.VMEM((width, seq), f32),
        pltpu.VMEM((seq, LANES), f32),
        pltpu.VMEM((seq, width), f32),
        pltpu.VMEM((width, seq), bf16),
        pltpu.VMEM((3, seq, width), bf16),
        pltpu.VMEM((peers, width, block), bf16),
    ]
    if prev:
        scratch += [pltpu.VMEM((3, d, width), f32), pltpu.VMEM((2, n, 2 * width), bf16)]
    ins = [(inputs, ((seq, d), lambda ref, info: ref.at[which])), whole(w_t)]
    ins += [whole(a) for a in (q, k, v, lse, c)]
    ins += [(g, ((width, block), lambda ref, info: ref.at[which]), None) for g in gs]
    if prev:
        ins += [whole(prev[0]), prev[1]]
    return call(
        "attend_bwd", attend_bwd_kernel, info, ins, outs, scratch, which=which, first=not prev, parts=parts
    )


def gelu_parts(h):
    t = 1.0 / (1.0 + (0.3275911 * 0.7071067811865476) * jnp.abs(h))
    poly = t * (0.127414796 + t * (-0.142248368 + t * (0.7107068705 + t * (-0.7265760135 + t * 0.5307027145))))
    bell = jnp.exp2((-0.5 * 1.4426950408889634) * (h * h))
    tail = poly * bell
    cum = jnp.where(h < 0, tail, 1.0 - tail)
    return h * cum, cum + h * (bell * 0.3989422804014327)


def norm_parts(v):
    center = v - jnp.mean(v, axis=1, keepdims=True)
    r = lax.rsqrt(jnp.mean(center * center, axis=1, keepdims=True) + 1e-12)
    return center * r, r


def norm_back(u, gain, nv, r):
    gu = u * gain
    return r * (gu - jnp.mean(gu, axis=1, keepdims=True) - nv * jnp.mean(gu * nv, axis=1, keepdims=True))


def rowsum(v):
    return jnp.sum(v, axis=0, keepdims=True)


def first_norm_kernel(info, x_in, par, *rest):
    cs, packs = rest[:8], rest[8:12]
    nv_ref, r_ref, low = rest[12:]
    x_ref = x_in()
    packs = [p() for p in packs]
    rows = x_ref.shape[1]
    width = cs[0].dst.shape[0]
    for s in range(2):
        here = slice(s * rows, (s + 1) * rows)
        total = par[0:1, :] + x_ref[s].astype(f32)
        for k in range(4):
            total = total + mm(cs[4 * s + k]()[...], packs[k][0:width, :], TN)
        nv, r = norm_parts(total)
        nv_ref[here] = nv
        r_ref[here] = r
        low[here] = (nv * par[1:2, :] + par[2:3, :]).astype(bf16)


def feed_kernel(info, low, low2, pack, *rest, width, far):
    if far:
        u_a, u_b, d_a, d_b, p_own, p_sib, act_out, slope_out, own, sib, up, dn = rest
        half = u_a.dst.shape[0]
        assemble(info[3], up, u_a(), u_b(), half)
    else:
        u_in, d_in, act_out, slope_out, own, sib = rest
        up = u_in()
    act, slope = ref(act_out), ref(slope_out)
    units = up.shape[1]
    bias = pack()
    step = 256
    for j, rows in enumerate((low, low2)):

        def chunk(n, carry):
            cols = pl.ds(pl.multiple_of(n * step, step), step)
            hidden = mm(rows[...], up[:, cols]) + bias[width : width + 1, cols].astype(f32)
            a, g = gelu_parts(hidden)
            act[j, :, cols] = a.astype(bf16)
            slope[j, :, cols] = g.astype(bf16)
            return carry

        lax.fori_loop(0, units // step, chunk, 0)
    if far:
        assemble(info[4], dn, d_a(), d_b(), half)
        sib[...] = (p_sib[...] + mm(act[1], dn[...])).astype(bf16)
        own[...] = p_own[...] + mm(act[0], dn[...])
    else:
        dn = d_in()
        own[...] = mm(act[0], dn[...])
        sib[...] = mm(act[1], dn[...])


def assemble(bit, dst, a, b, half):
    dst[pl.ds(pl.multiple_of(bit * half, half), half)] = a[...]
    dst[pl.ds(pl.multiple_of((1 - bit) * half, half), half)] = b[...]


def second_norm_kernel(info, cot_in, par, nv_in, own, got, outs, gsec_out, gs_low, small):
    cot, nv_ref, gsec = cot_in(), ref(nv_in), ref(gsec_out)
    batch, rows, d = cot.shape
    sums = [0.0] * 3
    for s in range(batch):
        here = slice(s * rows, (s + 1) * rows)
        total = own[here] + got[here].astype(f32) + par[3:4, :] + (nv_ref[here] * par[1:2, :] + par[2:3, :])
        nv, r = norm_parts(total)
        outs.src[s] = (nv * par[4:5, :] + par[5:6, :]).astype(bf16)
        at = info[2] * rows + lax.broadcasted_iota(jnp.int32, (rows, 1), 0)
        seed = jnp.where(at < info[s], cot[s].astype(f32), 0.0)
        g = norm_back(seed, par[4:5, :], nv, r)
        sums = [a + rowsum(b) for a, b in zip(sums, (g, seed * nv, seed))]
        gsec[here] = g
        gs_low[here] = g.astype(bf16)
    small[...] = jnp.concatenate([*sums, jnp.zeros((5, d), f32)], axis=0)


def feed_back_kernel(info, gs, gs2, slope0, slope1, up0, dn0, u_a, u_b, d_a, d_b, gh_out, own, sib, ub, up2, dn2):
    gh = ref(gh_out)
    half = u_a.dst.shape[0]
    units = up0.dst.shape[1]
    ub[...] = jnp.zeros_like(ub)
    step = 256
    for k, slope in enumerate((ref(slope0), ref(slope1))):
        if k:
            assemble(info[4], dn2, d_a(), d_b(), half)
            dn = dn2
        else:
            dn = dn0()
        for j, rows in enumerate((gs, gs2)):

            def chunk(n, carry):
                cols = pl.ds(pl.multiple_of(n * step, step), step)
                ga = mm(rows[...], dn[cols, :], NT)
                h = (ga * slope[j, :, cols].astype(f32)).astype(bf16)
                gh[k, j, :, cols] = h
                ub[k : k + 1, cols] += rowsum(h.astype(f32))
                return carry

            lax.fori_loop(0, units // step, chunk, 0)
    assemble(info[3], up2, u_a(), u_b(), half)
    up = up0()
    sib[...] = (mm(gh[0, 1], up[...], NT) + mm(gh[1, 1], up2[...], NT)).astype(bf16)
    own[...] = mm(gh[0, 0], up[...], NT) + mm(gh[1, 0], up2[...], NT)


def first_back_kernel(info, par, nv_in, r_ref, own, got, gsec_in, small2, *rest):
    cs, packs = rest[:8], rest[8:12]
    gfi, g0, g1, g2, g3, okeep, osend, small, ga_low = rest[12:]
    nv_ref, gsec = ref(nv_in), ref(gsec_in)
    packs = [p() for p in packs]
    n, d = own.shape
    rows = n // 2
    width = cs[0].dst.shape[0]
    sums = [0.0] * 3
    for s in range(2):
        here = slice(s * rows, (s + 1) * rows)
        u = own[here] + got[here].astype(f32) + gsec[here]
        nv = nv_ref[here]
        g = norm_back(u, par[1:2, :], nv, r_ref[here])
        sums = [a + rowsum(b) for a, b in zip(sums, (g, u * nv, u))]
        gfi.src[here] = g
        low = g.astype(bf16)
        ga_low[here] = low
        for k, out in enumerate((g0, g1, g2, g3)):
            out.src[s] = mm(packs[k][0:width, :], low, NT).astype(bf16)
    for out in (g3, g2, g1, g0, gfi):
        out.start()
    for k in range(4):
        total = mm(cs[k]()[...], ga_low[0:rows, :]) + mm(cs[4 + k]()[...], ga_low[rows:n, :])
        (osend if k % 2 else okeep).src[k // 2, 0:width, :] = total.astype(bf16)
    both = jnp.concatenate([*sums, small2[0:3, :], jnp.zeros((2, d), f32)], axis=0)
    small[...] = both
    high = both.astype(bf16)
    osend.src[0, width : width + 8, :] = high
    osend.src[1, width : width + 8, :] = (both - high.astype(f32)).astype(bf16)


def down_grads_kernel(info, act0, act1, gs, gs2, far_keep, far_send, keep, send, scr, *, parts):
    units = act0.shape[2]
    block = units // parts
    step = 384
    for act, mine, theirs in ((act1, far_keep, far_send), (act0, keep, send)):
        for m in range(0, units, step):
            cols = slice(m, m + step)
            total = mm(act[0, :, cols], gs[...], TN) + mm(act[1, :, cols], gs2[...], TN)
            total = total.astype(bf16)
            for i in range(step // block):
                b = m // block + i
                scr[(b & 1) ^ info[3], b >> 1] = total[i * block : (i + 1) * block]
        theirs.src[...] = scr[1]
        theirs.start()
        mine.src[...] = scr[0]
        mine.start()


def up_grads_kernel(
    info, low, low2, gh_in, okeep, ogot, small, ub, far_keep, far_send, keep, send, sums, scr, *, parts, width
):
    gh = ref(gh_in)
    units = low.shape[1]
    block = units // parts
    extra = width // parts
    joint = block + extra
    n = parts // 2 * joint
    step = 384
    got = ogot()
    both = small[...] + got[0, width : width + 8, :].astype(f32) + got[1, width : width + 8, :].astype(f32)
    both = jnp.concatenate([both[0:6], ub[0:2, :]], axis=0)
    sums[...] = both
    high = both.astype(bf16)
    far_send.src[n : n + 8, :] = high
    far_send.src[n + 8 : n + 16, :] = (both - high.astype(f32)).astype(bf16)
    for k, mine, theirs in ((1, far_keep, far_send), (0, keep, send)):
        for m in range(0, units, step):
            cols = slice(m, m + step)
            total = mm(low[:, cols], gh[k, 0], TN) + mm(low2[:, cols], gh[k, 1], TN)
            total = total.astype(bf16)
            for i in range(step // block):
                b = m // block + i
                scr[((b >> 1) & 1) ^ info[4], (b >> 2) * 2 + (b & 1), 0:block, :] = total[i * block : (i + 1) * block]
        o = (okeep()[k, 0:width, :].astype(f32) + got[k, 0:width, :].astype(f32)).astype(bf16)
        for b in range(parts):
            at = (b >> 2) * 2 + (b & 1)
            scr[((b >> 1) & 1) ^ info[4], at, block:joint, :] = o[b * extra : (b + 1) * extra]
        for b in range(parts // 2):
            theirs.src[b * joint : (b + 1) * joint, :] = scr[1, b]
            mine.src[b * joint : (b + 1) * joint, :] = scr[0, b]
        theirs.start()
        mine.start()


def swap(x, axis, bit):
    size = lax.axis_size(axis)
    return lax.ppermute(x, axis, [(i, i ^ bit) for i in range(size)])


def summed(parts):
    return sum(p.astype(f32) for p in parts)


def spread(array, axis, parts):
    bits = parts.bit_length() - 1
    return array.reshape(*array.shape[:axis], *([2] * bits), array.shape[axis] // parts, *array.shape[axis + 1 :])


def halve(terms, axis, bit, mine):
    other = [lax.dynamic_index_in_dim(t, 1 - mine, axis, keepdims=False) for t in terms]
    kept = [lax.dynamic_index_in_dim(t, mine, axis, keepdims=False) for t in terms]
    other = summed(other).astype(bf16)
    return kept + [swap(other, "dp", bit)], other


def body(
    inputs,
    cotangent,
    lengths,
    qkv_weight,
    qkv_bias,
    out_weight,
    out_bias,
    first_gain,
    first_shift,
    up_weight,
    up_bias,
    down_weight,
    down_bias,
    second_gain,
    second_shift,
):
    batch, seq, d = inputs.shape
    rows = cotangent.shape[1]
    n = batch * rows
    width = out_weight.shape[0]
    units = up_weight.shape[1]
    peers = lax.axis_size("tensor")
    parts = lax.axis_size("dp")
    bits = parts.bit_length() - 1
    t = lax.axis_index("tensor")
    dp = lax.axis_index("dp")
    bit_of = [(dp >> i) & 1 for i in range(bits)]
    info = lengths
    par = jnp.concatenate([out_bias, first_gain, first_shift, down_bias, second_gain, second_shift])
    par = par.reshape(6, d).astype(f32)
    w_t = jnp.transpose(qkv_weight, (1, 2, 0))
    pack, up_half, dn_half = prepare(info, out_weight, up_bias[None], up_weight, down_weight)
    pack2 = swap(pack, "tensor", 2)
    pack1 = swap(pack, "tensor", 1)
    u2a = swap(up_half, "tensor", 2)
    saved = []
    ctx = []
    for s in range(batch):
        q, k, v, lse, c, *cs = attend_fwd(s, info, inputs, w_t, qkv_bias, peers)
        saved.append((q, k, v, lse, c))
        if s == 0:
            *cs, pack1, pack2 = after(*cs, pack1, pack2)
        else:
            both = after(*cs, pack2, dn_half, *ctx)
            cs, pack2, dn_half, ctx = list(both[:peers]), both[peers], both[peers + 1], list(both[peers + 2 :])
        ctx += [cs[0]] + [swap(cs[j], "tensor", j) for j in range(1, peers)]
    d2a = swap(dn_half, "tensor", 2)
    pack3 = swap(pack2, "tensor", 1)
    packs = [pack, pack1, pack2, pack3]
    ctx[0], u2a = after(ctx[0], u2a)
    u2b = swap(u2a, "dp", 1)
    d2b = swap(d2a, "dp", 2)
    far_ctx = [whole(c) if k % peers == 0 else loose(c) for k, c in enumerate(ctx)]
    far_packs = [whole(pack)] + [loose(p) for p in packs[1:]]
    share = (inputs, ((batch, rows, d), lambda ref, info: ref.at[:, pl.ds(pl.multiple_of(info[2] * rows, rows), rows), :]))
    nv1, r1, low = call(
        "first_norm",
        first_norm_kernel,
        info,
        [share, par, *far_ctx, *far_packs],
        [SDS((n, d), f32), SDS((n, 1), f32), SDS((n, d), bf16)],
        vmem=NEAR,
    )
    low2 = swap(low, "tensor", 1)
    pair = SDS((2, n, units), bf16)
    part = SDS((n, d), f32)
    act0, slope0, own, sib = call(
        "feed",
        feed_kernel,
        info,
        [low, low2, far_packs[0], whole(up_weight), whole(down_weight)],
        [pair, pair, part, part],
        vmem=NEAR,
        width=width,
        far=False,
    )
    halves = [loose(x) for x in (u2a, u2b, d2a, d2b)]
    both = [pltpu.VMEM((d, units), bf16), pltpu.VMEM((units, d), bf16)]
    act1, slope1, own, sib = call(
        "feed",
        feed_kernel,
        info,
        [low, low2, far_packs[2], *halves, own, sib],
        [pair, pair, part, SDS((n, d), bf16)],
        both,
        vmem=NEAR,
        width=width,
        far=True,
    )
    got = swap(sib, "tensor", 1)
    outputs, gsec, gs_low, small2 = call(
        "second_norm",
        second_norm_kernel,
        info,
        [whole(cotangent), par, nv1, own, got],
        [[SDS((batch, rows, d), bf16)], part, SDS((n, d), bf16), SDS((8, d), f32)],
        vmem=NEAR,
    )
    gs_low2 = swap(gs_low, "tensor", 1)
    gh, own, sib, ub = call(
        "feed_back",
        feed_back_kernel,
        info,
        [gs_low, gs_low2, slope0, slope1, whole(up_weight), whole(down_weight), *halves],
        [SDS((2, 2, n, units), bf16), part, SDS((n, d), bf16), SDS((8, d), f32)],
        both,
        vmem=NEAR,
    )
    got = swap(sib, "tensor", 1)
    block = units // parts
    downs = call(
        "down_grads",
        down_grads_kernel,
        info,
        [act0, act1, gs_low, gs_low2],
        [[SDS((parts // 2, block, d), bf16)]] * 4,
        [pltpu.VMEM((2, parts // 2, block, d), bf16)],
        vmem=NEAR,
        parts=parts,
    )
    down_far_keep, down_far_send, down_keep, down_send = downs
    down_far_got = swap(down_far_send, "dp", 1)
    gfi, g0, g1, g2, g3, okeep, osend, small1 = call(
        "first_back",
        first_back_kernel,
        info,
        [par, nv1, r1, own, got, gsec, small2, *far_ctx, *far_packs],
        [
            [part],
            *[[SDS((batch, width, rows), bf16)]] * 4,
            *[[SDS((2, width + 8, d), bf16)]] * 2,
            SDS((8, d), f32),
        ],
        [pltpu.VMEM((n, d), bf16)],
        vmem=NEAR,
    )
    gctx = [g0] + [swap(g, "tensor", j) for j, g in ((1, g1), (2, g2), (3, g3))]
    got_o = swap(osend, "tensor", 1)
    joint = block + width // parts
    cut = parts // 2 * joint
    up_far_keep, up_far_send, up_keep, up_send, small = call(
        "up_grads",
        up_grads_kernel,
        info,
        [low, low2, gh, whole(okeep), loose(got_o), small1, ub],
        [
            [SDS((cut, d), bf16)],
            [SDS((cut + 16, d), bf16)],
            [SDS((cut, d), bf16)],
            [SDS((cut, d), bf16)],
            SDS((8, d), f32),
        ],
        [pltpu.VMEM((2, parts // 2, joint, d), bf16)],
        vmem=NEAR,
        parts=parts,
        width=width,
    )
    up_far_got = swap(up_far_send, "dp", 2)
    *gctx, down_far_got, up_far_keep = after(*gctx, down_far_got, up_far_keep)
    down_far_sum = summed([down_far_keep, down_far_got]).astype(bf16)
    down_y = swap(down_far_sum, "tensor", 2)
    down_send, down_far_sum = after(down_send, down_far_sum)
    down_got = swap(down_send, "dp", 1)
    *gctx, down_far_sum, up_far_keep = after(*gctx, down_far_sum, up_far_keep)
    q, k, v, lse, c = saved[0]
    keep, send, dw, db = attend_bwd(0, info, inputs, w_t, q, k, v, lse, c, gctx, None, parts)
    near = swap(send, "tensor", 1)
    keep, down_got, up_far_got = after(keep, down_got, up_far_got)
    shape = ([2] * (bits - 1)) + [block, d]
    terms = [x.reshape(shape) for x in (down_keep, down_got, down_y)]
    down_terms, down_next = halve(terms, bits - 2, 2, bit_of[1])
    shape = ([2] * (bits - 1)) + [joint, d]
    small = small + pair_sum(up_far_got, cut, 8)
    terms = [x.reshape(shape) for x in (up_far_keep, up_far_got[:cut])]
    up_far_terms, up_far_next, small_x = halve_with(terms, bits - 2, small, "dp", 1, bit_of[0])
    up_send, up_far_next = after(up_send, up_far_next)
    up_got = swap(up_send, "dp", 2)
    in_sum = summed([keep[1], near[1]]).astype(bf16)
    far = swap(in_sum, "tensor", 2)
    first_terms = [keep[0], near[0], far]
    dw, down_next, up_far_next, in_sum, up_keep = after(dw, down_next, up_far_next, in_sum, up_keep)
    q, k, v, lse, c = saved[1]
    keep, send, w_keep, w_send, db = attend_bwd(1, info, inputs, w_t, q, k, v, lse, c, gctx, (dw, db), parts)
    near = swap(send, "tensor", 1)
    in_sum = summed([keep[1], near[1]]).astype(bf16)
    last_terms = [keep[0], near[0], swap(in_sum, "tensor", 2)]
    small = small + small_x
    small = jnp.concatenate([small[0:6], small[7:8], small[6:7]])
    send = summed(up_far_terms).astype(bf16)
    up_y_sent = with_rows(send, small)
    up_y = swap(up_y_sent, "tensor", 2)
    at = send.size // d
    small = jnp.concatenate([small[0:6], small[7:8], small[7:8]]) + pair_sum(up_y, at, 8)
    shape = ([2] * (bits - 1)) + [joint, d]
    terms, up_next = halve([x.reshape(shape) for x in (up_keep, up_got)], bits - 2, 1, bit_of[0])
    terms.append(up_y[:at].reshape(send.shape))
    for i in range(2, bits):
        terms, sent, more = halve_with(terms, terms[0].ndim - 3, small, "dp", 1 << i, bit_of[i])
        small = small + more
    up_sum = summed(terms)
    mine = small
    order = [1, 0] + list(range(2, bits))
    row = 3 * (d // parts) // 2
    w_send, far0 = after(w_send, first_terms[2])
    first_terms[2] = far0
    got = swap(w_send, "dp", 2)
    got, in_sum, up_next, up_y_sent = after(got, in_sum, up_next, up_y_sent)
    got, *down_terms = after(got, *down_terms)
    for i in range(2, bits):
        down_terms, sent = halve(down_terms, bits - 1 - i, 1 << i, bit_of[i])
    down_sum = summed(down_terms)
    at = parts // 2 * row
    shape = ([2] * (bits - 1)) + [row, 2 * width]
    terms = [x.reshape(shape) for x in (w_keep, got[:at])]
    db = db + got[at : at + 1].astype(f32) + got[at + 1 : at + 2].astype(f32)
    for i in order[1:]:
        kept, sent, more = halve_with(terms, terms[0].ndim - 3, db, "dp", 1 << i, bit_of[i])
        terms, db = kept, db + more
    qkv_sum = summed(terms)
    qkv_sum = jnp.concatenate([qkv_sum[:, :width], qkv_sum[:, width:]], axis=0).reshape(3, -1, width)
    qkv_sum = jnp.transpose(qkv_sum, (1, 0, 2))
    db = db.reshape(2, width)
    input_list = [
        (summed(x) + gfi[s * rows : (s + 1) * rows]).astype(bf16)
        for s, x in enumerate((first_terms, last_terms))
    ]
    return (
        outputs,
        jnp.stack(input_list, 0),
        qkv_sum,
        db,
        up_sum[block:],
        mine[0],
        mine[1],
        mine[2],
        up_sum[:block],
        mine[6],
        down_sum,
        mine[3],
        mine[4],
        mine[5],
    )


def pair_sum(array, at, n):
    return array[at : at + n].astype(f32) + array[at + n : at + 2 * n].astype(f32)


def with_rows(array, rows):
    flat = array.reshape(-1, array.shape[-1])
    high = rows.astype(bf16)
    low = (rows - high.astype(f32)).astype(bf16)
    return jnp.concatenate([flat, high, low], axis=0)


def halve_with(terms, axis, rows, name, bit, mine):
    other = [lax.dynamic_index_in_dim(t, 1 - mine, axis, keepdims=False) for t in terms]
    kept = [lax.dynamic_index_in_dim(t, mine, axis, keepdims=False) for t in terms]
    other = summed(other).astype(bf16)
    sent = with_rows(other, rows)
    got = swap(sent, name, bit)
    cut = other.size // other.shape[-1]
    return kept + [got[:cut].reshape(other.shape)], sent, pair_sum(got, cut, rows.shape[0])


def after(*values):
    return lax.optimization_barrier(values)


def solution(mesh):
    in_specs = (
        P("dp", None, None),
        P("dp", "tensor", None),
        P("dp"),
        P(None, None, "tensor"),
        P(None, "tensor"),
        P("tensor", None),
        P(),
        P(),
        P(),
        P(None, "tensor"),
        P("tensor"),
        P("tensor", None),
        P(),
        P(),
        P(),
    )
    out_specs = (
        P("dp", "tensor", None),
        P("dp", "tensor", None),
        P("dp", None, "tensor"),
        P(None, "tensor"),
        P(("tensor", "dp"), None),
        P(),
        P(),
        P(),
        P("dp", "tensor"),
        P("tensor"),
        P(("tensor", "dp"), None),
        P(),
        P(),
        P(),
    )
    return jax.shard_map(body, mesh=mesh, in_specs=in_specs, out_specs=out_specs, check_vma=False)
```

```python
import functools

import jax
import jax.numpy as jnp
from jax import lax
from jax.experimental import pallas as pl
from jax.experimental.pallas import tpu as pltpu
from jax.sharding import PartitionSpec as P

HEAD = 64
WIDE, LANES = 192, 256
NEAR = 30
NT = (((1,), (1,)), ((), ()))
NN = (((1,), (0,)), ((), ()))
TN = (((0,), (0,)), ((), ()))
bf16 = jnp.bfloat16
f32 = jnp.float32
VM = pl.BlockSpec(memory_space=pltpu.VMEM)
SDS = jax.ShapeDtypeStruct
FWD_COST = (10**10, 1000)


def mm(a, b, dims=NN):
    return lax.dot_general(a, b, dims, preferred_element_type=f32)


class Fetch:
    def __init__(self, src, dst, sem):
        self.dst, self.copy = dst, pltpu.make_async_copy(src, dst, sem)
        self.copy.start()
        self.waiting = True

    def __call__(self):
        if self.waiting:
            self.copy.wait()
            self.waiting = False
        return self.dst


class Flush:
    def __init__(self, src, dst, sem):
        self.src, self.copy = src, pltpu.make_async_copy(src, dst, sem)
        self.started = False

    def start(self):
        if not self.started:
            self.copy.start()
        self.started = True


def call(name, body, info, ins, outs, scratch=(), vmem=58, cost=1000, **static):
    far_in = [i for i, a in enumerate(ins) if isinstance(a, tuple)]
    pinned = [i for i in far_in if len(ins[i]) == 2]
    far_out = [i for i, o in enumerate(outs) if isinstance(o, list)]
    arrays = [a[0] if isinstance(a, tuple) else a for a in ins]
    shapes = [o[0] if isinstance(o, list) else o for o in outs]
    picked = [a[1] if isinstance(a, tuple) else None for a in ins]
    n_in, n_out = len(ins), len(outs)

    def kernel(lengths_ref, *refs):
        dp = lax.axis_index("dp")
        info_ref = (lengths_ref[0], lengths_ref[1], lax.axis_index("tensor"), dp & 1, (dp >> 1) & 1)
        in_refs, refs = refs[:n_in], refs[n_in:]
        out_refs, refs = refs[:n_out], refs[n_out:]
        sem, refs = refs[-1], refs[:-1]
        buffers, rest = refs[: len(far_in) + len(far_out)], refs[len(far_in) + len(far_out) :]
        args = list(in_refs)
        for j, i in enumerate(far_in):
            view = picked[i][1]
            args[i] = Fetch(view(in_refs[i], info_ref), buffers[j], sem.at[j])
        results = list(out_refs)
        flushes = []
        for j, i in enumerate(far_out):
            at = len(far_in) + j
            results[i] = Flush(buffers[at], out_refs[i], sem.at[at])
            flushes.append(results[i])
        body(info_ref, *args, *results, *rest, **static)
        for i in far_in:
            args[i]()
        for f in flushes:
            f.start()
        for f in flushes:
            f.copy.wait()

    hbm = pl.BlockSpec(memory_space=pltpu.HBM)
    buffers = [pltpu.VMEM(picked[i][0], arrays[i].dtype) for i in far_in]
    buffers += [pltpu.VMEM(shapes[i].shape, shapes[i].dtype) for i in far_out]
    return pl.pallas_call(
        kernel,
        out_shape=[pltpu.HBM(o.shape, o.dtype) if i in far_out else o for i, o in enumerate(shapes)],
        grid_spec=pltpu.PrefetchScalarGridSpec(
            num_scalar_prefetch=1,
            grid=(1,),
            in_specs=[hbm if i in pinned else pl.BlockSpec(memory_space=pl.ANY) if i in far_in else VM for i in range(n_in)],
            out_specs=[hbm if i in far_out else VM for i in range(n_out)],
            scratch_shapes=[*buffers, *scratch, pltpu.SemaphoreType.DMA((max(1, len(far_in) + len(far_out)),))],
        ),
        compiler_params=pltpu.CompilerParams(vmem_limit_bytes=vmem << 20),
        cost_estimate=pl.CostEstimate(flops=cost, bytes_accessed=1000, transcendentals=0),
        name=name,
    )(info, *[pltpu.with_memory_space_constraint(a, pltpu.HBM) if i in pinned else a for i, a in enumerate(arrays)])


def ref(x):
    return x() if isinstance(x, Fetch) else x.src if isinstance(x, Flush) else x


def whole(a):
    return (a, (a.shape, lambda ref, info: ref))


def loose(a):
    return (*whole(a), None)


def prepare_kernel(info, out_in, bias, up_in, dn_in, pack, up_half, dn_half):
    for src, dst in ((up_in, up_half), (dn_in, dn_half)):
        dst.src[...] = src()[...]
        dst.start()
    out_w = out_in()
    width, d = out_w.shape
    pack.src[0:width, :] = out_w[...]
    pack.src[width : width + 8, :] = jnp.broadcast_to(bias[...], (8, d))


def prepare(info, out_w, bias, up, dn):
    width, d = out_w.shape
    half = up.shape[0] // 2
    view = lambda ref, info: ref.at[pl.ds(pl.multiple_of(info[3] * half, half), half)]
    view2 = lambda ref, info: ref.at[pl.ds(pl.multiple_of(info[4] * half, half), half)]
    ins = [whole(out_w), bias, (up, ((half, d), view)), (dn, ((half, d), view2))]
    return call("prepare", prepare_kernel, info, ins, [[SDS((width + 8, d), bf16)]] + [[SDS((half, d), bf16)]] * 2)


def head_cols(a, h, extra=()):
    lane = lax.broadcasted_iota(jnp.int32, a.shape, 1)
    out = jnp.where((lane >= HEAD * h) & (lane < HEAD * (h + 1)), a, jnp.zeros_like(a))
    for i, e in enumerate(extra):
        out = jnp.where(lane == WIDE + i, e, out)
    return out


def tail_cols(rows, values):
    lane = lax.broadcasted_iota(jnp.int32, (rows, LANES - WIDE), 1)
    out = jnp.zeros((rows, LANES - WIDE), f32)
    for i, v in enumerate(values):
        out = jnp.where(lane == i, v, out)
    return out.astype(bf16)


def attend_fwd_kernel(info, x_ref, w_ref, b_ref, q_out, k_out, v_out, lse_out, c_out, *rest, which):
    outs, v_t, s_all = rest[:-2], rest[-2], rest[-1]
    length = info[which]
    me = info[2]
    q_ref, k_ref, v_ref, lse_ref, c_ref = (o.src for o in (q_out, k_out, v_out, lse_out, c_out))
    peers, width, block = c_ref.shape
    heads = width // HEAD
    seq = k_ref.shape[0]
    w = w_ref()
    x = x_ref()[...]
    k_ref[:, 0:WIDE] = mm(x, w[1], NT).astype(bf16)
    row = lax.broadcasted_iota(jnp.int32, (seq, 1), 0)
    k_ref[:, WIDE:LANES] = tail_cols(seq, (jnp.where(row < length, 0.0, -1e30),))
    q = mm(x, w[0], NT) + b_ref[0:1, :].astype(f32)
    q_ref[:, 0:WIDE] = q.astype(bf16) * jnp.asarray(0.125, bf16)
    q_ref[:, WIDE:LANES] = tail_cols(seq, (1.0,))
    v = (mm(x, w[2], NT) + b_ref[1:2, :].astype(f32)).astype(bf16)
    v_ref[...] = v
    v_t[...] = v.T
    for o in (q_out, k_out, v_out):
        o.start()

    def one_block(s, carry):
        qb = q_ref[pl.ds(pl.multiple_of(s * 2 * block, 2 * block), 2 * block), :]
        one = jnp.ones_like(qb[:, 0:1])
        for h in range(heads):
            s_all[h] = mm(k_ref[...], head_cols(qb, h, (one,)), NT)
        for h in range(heads):
            top = jnp.max(s_all[h], axis=0, keepdims=True)
            p = jnp.exp(s_all[h] - top)
            total = jnp.sum(p, axis=0, keepdims=True)
            rows = slice(HEAD * h, HEAD * (h + 1))
            out = (mm(v_t[rows, :], p.astype(bf16)) * (1.0 / total)).astype(bf16)
            lse = top + jnp.log(total)
            for j in range(2):
                cols = slice(block * j, block * (j + 1))
                c_ref[2 * s + j, rows, :] = out[:, cols]
                lse_ref[2 * s + j, h : h + 1, :] = lse[:, cols]
        return carry

    lax.fori_loop(0, peers // 2, one_block, 0)
    for k, out in enumerate(outs):
        out.src[...] = c_ref[me ^ k]


def attend_fwd(which, info, inputs, w_t, bias, peers):
    _, seq, d = inputs.shape
    width = w_t.shape[1]
    block = seq // peers
    outs = [[SDS((seq, LANES), bf16)]] * 2 + [[SDS((seq, width), bf16)]]
    outs += [[SDS((peers, 8, block), f32)], [SDS((peers, width, block), bf16)]]
    outs += [[SDS((width, block), bf16)]] * peers
    return call(
        "attend_fwd",
        attend_fwd_kernel,
        info,
        [(inputs, ((seq, d), lambda ref, info: ref.at[which])), whole(w_t), bias],
        outs,
        [pltpu.VMEM((width, seq), bf16), pltpu.VMEM((width // HEAD, seq, 2 * block), f32)],
        cost=FWD_COST[which],
        which=which,
    )


def attend_bwd_kernel(info, x_ref, w_ref, q_in, k_in, v_in, lse_in, c_in, *rest, which, first, parts):
    peers = 4
    gs, rest = rest[:peers], rest[peers:]
    if not first:
        pw_in, pb_ref = rest[:2]
        rest = rest[2:]
    if first:
        keep, send, dw_out, db_ref, dq_t, dk, dv, k_t, low, g_ref = rest
    else:
        keep, send, w_keep, w_send, db_ref, dq_t, dk, dv, k_t, low, g_ref, dw_scr, pair = rest
    length = info[which]
    me = info[2]
    k_ref, q_ref, v_ref = k_in(), q_in(), v_in()
    lse_ref, c_ref = lse_in(), c_in()
    _, width, block = c_ref.shape
    heads = width // HEAD
    k_t[...] = k_ref[:, 0:WIDE].T
    dk[...] = jnp.zeros_like(dk)
    dv[...] = jnp.zeros_like(dv)
    for k in range(peers):
        g_ref[me ^ k] = gs[k]()[...]

    def one_block(s, carry):
        at = pl.multiple_of(s * block, block)

        @pl.when(at >= length)
        def _():
            dq_t[:, pl.ds(at, block)] = jnp.zeros((width, block), f32)

        @pl.when(at < length)
        def _():
            qb = q_ref[pl.ds(at, block), :]
            g_t = g_ref[s]
            g = g_t.T
            prod_t = g_t.astype(f32) * c_ref[s].astype(f32)
            for h in range(heads):
                rows = slice(HEAD * h, HEAD * (h + 1))
                qh = head_cols(qb, h)
                gh = head_cols(g, h)
                scores = mm(k_ref[...], qh, NT)
                row = lax.broadcasted_iota(jnp.int32, scores.shape, 0)
                p = jnp.where(row < length, jnp.exp(scores - lse_ref[s, h : h + 1, :]), 0.0)
                dp = mm(v_ref[...], gh, NT)
                inner = jnp.sum(prod_t[rows], axis=0, keepdims=True)
                ds = (p * (dp - inner)).astype(bf16)
                dv[...] += mm(p.astype(bf16), gh)
                dk[...] += mm(ds, qh)
                dq_t[rows, pl.ds(at, block)] = mm(k_t[rows, :], ds) * 0.125

        return carry

    lax.fori_loop(0, peers, one_block, 0)
    low[0] = dq_t[...].T.astype(bf16)
    low[1] = dk[:, 0:WIDE].astype(bf16)
    low[2] = dv[...].astype(bf16)
    w = w_ref()
    for s in range(peers):
        at = pl.multiple_of((me ^ s) * block, block)
        total = sum(mm(low[i, pl.ds(at, block), :], w[i]) for i in range(3))
        (send if s % 2 else keep).src[s // 2] = total.astype(bf16)
    send.start()
    keep.start()
    db = jnp.concatenate([rowsum(low[i].astype(f32)) for i in (0, 2)], axis=1)
    db = db if first else db + pb_ref[...]
    db_ref[...] = db
    x_t = x_ref()[...].T
    if first:
        for i in range(3):
            dw_out.src[i] = mm(x_t, low[i])
        return
    for i in range(3):
        dw_scr[i] = mm(x_t, low[i]) + pw_in()[i]
    d = dw_scr.shape[1]
    rows = d // parts
    half = 3 * rows // 2
    for b in range(parts):
        flat = dw_scr[:, b * rows : (b + 1) * rows, :].reshape(3 * rows, width)
        flat = jnp.concatenate([flat[0:half], flat[half : 2 * half]], axis=1)
        at = ((b >> 2) * 2 + (b & 1)) * half
        pair[((b >> 1) & 1) ^ info[4], at : at + half, :] = flat.astype(bf16)
    n = parts // 2 * half
    w_send.src[0:n, :] = pair[1]
    high = db.astype(bf16)
    w_send.src[n : n + 8, :] = jnp.concatenate(
        [high, (db - high.astype(f32)).astype(bf16), jnp.zeros((6, 2 * width), bf16)], axis=0
    )
    w_send.start()
    w_keep.src[...] = pair[0]


def attend_bwd(which, info, inputs, w_t, q, k, v, lse, c, gs, prev, parts):
    _, seq, d = inputs.shape
    peers, width, block = c.shape
    outs = [[SDS((2, block, d), bf16)]] * 2
    n = 3 * d // 4
    outs += [[SDS((n, 2 * width), bf16)], [SDS((n + 8, 2 * width), bf16)]] if prev else [[SDS((3, d, width), f32)]]
    outs += [SDS((1, 2 * width), f32)]
    scratch = [
        pltpu.VMEM((width, seq), f32),
        pltpu.VMEM((seq, LANES), f32),
        pltpu.VMEM((seq, width), f32),
        pltpu.VMEM((width, seq), bf16),
        pltpu.VMEM((3, seq, width), bf16),
        pltpu.VMEM((peers, width, block), bf16),
    ]
    if prev:
        scratch += [pltpu.VMEM((3, d, width), f32), pltpu.VMEM((2, n, 2 * width), bf16)]
    ins = [(inputs, ((seq, d), lambda ref, info: ref.at[which])), whole(w_t)]
    ins += [whole(a) for a in (q, k, v, lse, c)]
    ins += [(g, ((width, block), lambda ref, info: ref.at[which]), None) for g in gs]
    if prev:
        ins += [whole(prev[0]), prev[1]]
    return call(
        "attend_bwd", attend_bwd_kernel, info, ins, outs, scratch, which=which, first=not prev, parts=parts
    )


def gelu_parts(h):
    t = 1.0 / (1.0 + (0.3275911 * 0.7071067811865476) * jnp.abs(h))
    poly = t * (0.127414796 + t * (-0.142248368 + t * (0.7107068705 + t * (-0.7265760135 + t * 0.5307027145))))
    bell = jnp.exp2((-0.5 * 1.4426950408889634) * (h * h))
    tail = poly * bell
    cum = jnp.where(h < 0, tail, 1.0 - tail)
    return h * cum, cum + h * (bell * 0.3989422804014327)


def norm_parts(v):
    center = v - jnp.mean(v, axis=1, keepdims=True)
    r = lax.rsqrt(jnp.mean(center * center, axis=1, keepdims=True) + 1e-12)
    return center * r, r


def norm_back(u, gain, nv, r):
    gu = u * gain
    return r * (gu - jnp.mean(gu, axis=1, keepdims=True) - nv * jnp.mean(gu * nv, axis=1, keepdims=True))


def rowsum(v):
    return jnp.sum(v, axis=0, keepdims=True)


def first_norm_kernel(info, x_in, par, *rest):
    cs, packs = rest[:8], rest[8:12]
    nv_ref, r_ref, low = rest[12:]
    x_ref = x_in()
    packs = [p() for p in packs]
    rows = x_ref.shape[1]
    width = cs[0].dst.shape[0]
    for s in range(2):
        here = slice(s * rows, (s + 1) * rows)
        total = par[0:1, :] + x_ref[s].astype(f32)
        for k in range(4):
            total = total + mm(cs[4 * s + k]()[...], packs[k][0:width, :], TN)
        nv, r = norm_parts(total)
        nv_ref[here] = nv
        r_ref[here] = r
        low[here] = (nv * par[1:2, :] + par[2:3, :]).astype(bf16)


def feed_kernel(info, low, low2, pack, *rest, width, far):
    if far:
        u_a, u_b, d_a, d_b, p_own, p_sib, act_out, slope_out, own, sib, up, dn = rest
        half = u_a.dst.shape[0]
        assemble(info[3], up, u_a(), u_b(), half)
    else:
        u_in, d_in, act_out, slope_out, own, sib = rest
        up = u_in()
    act, slope = ref(act_out), ref(slope_out)
    units = up.shape[1]
    bias = pack()
    step = 256
    for j, rows in enumerate((low, low2)):

        def chunk(n, carry):
            cols = pl.ds(pl.multiple_of(n * step, step), step)
            hidden = mm(rows[...], up[:, cols]) + bias[width : width + 1, cols].astype(f32)
            a, g = gelu_parts(hidden)
            act[j, :, cols] = a.astype(bf16)
            slope[j, :, cols] = g.astype(bf16)
            return carry

        lax.fori_loop(0, units // step, chunk, 0)
    if far:
        assemble(info[4], dn, d_a(), d_b(), half)
        sib[...] = (p_sib[...] + mm(act[1], dn[...])).astype(bf16)
        own[...] = p_own[...] + mm(act[0], dn[...])
    else:
        dn = d_in()
        own[...] = mm(act[0], dn[...])
        sib[...] = mm(act[1], dn[...])


def assemble(bit, dst, a, b, half):
    dst[pl.ds(pl.multiple_of(bit * half, half), half)] = a[...]
    dst[pl.ds(pl.multiple_of((1 - bit) * half, half), half)] = b[...]


def second_norm_kernel(info, cot_in, par, nv_in, own, got, outs, gsec_out, gs_low, small):
    cot, nv_ref, gsec = cot_in(), ref(nv_in), ref(gsec_out)
    batch, rows, d = cot.shape
    sums = [0.0] * 3
    for s in range(batch):
        here = slice(s * rows, (s + 1) * rows)
        total = own[here] + got[here].astype(f32) + par[3:4, :] + (nv_ref[here] * par[1:2, :] + par[2:3, :])
        nv, r = norm_parts(total)
        outs.src[s] = (nv * par[4:5, :] + par[5:6, :]).astype(bf16)
        at = info[2] * rows + lax.broadcasted_iota(jnp.int32, (rows, 1), 0)
        seed = jnp.where(at < info[s], cot[s].astype(f32), 0.0)
        g = norm_back(seed, par[4:5, :], nv, r)
        sums = [a + rowsum(b) for a, b in zip(sums, (g, seed * nv, seed))]
        gsec[here] = g
        gs_low[here] = g.astype(bf16)
    small[...] = jnp.concatenate([*sums, jnp.zeros((5, d), f32)], axis=0)


def feed_back_kernel(info, gs, gs2, slope0, slope1, up0, dn0, u_a, u_b, d_a, d_b, gh_out, own, sib, ub, up2, dn2):
    gh = ref(gh_out)
    half = u_a.dst.shape[0]
    units = up0.dst.shape[1]
    ub[...] = jnp.zeros_like(ub)
    step = 256
    for k, slope in enumerate((ref(slope0), ref(slope1))):
        if k:
            assemble(info[4], dn2, d_a(), d_b(), half)
            dn = dn2
        else:
            dn = dn0()
        for j, rows in enumerate((gs, gs2)):

            def chunk(n, carry):
                cols = pl.ds(pl.multiple_of(n * step, step), step)
                ga = mm(rows[...], dn[cols, :], NT)
                h = (ga * slope[j, :, cols].astype(f32)).astype(bf16)
                gh[k, j, :, cols] = h
                ub[k : k + 1, cols] += rowsum(h.astype(f32))
                return carry

            lax.fori_loop(0, units // step, chunk, 0)
    assemble(info[3], up2, u_a(), u_b(), half)
    up = up0()
    sib[...] = (mm(gh[0, 1], up[...], NT) + mm(gh[1, 1], up2[...], NT)).astype(bf16)
    own[...] = mm(gh[0, 0], up[...], NT) + mm(gh[1, 0], up2[...], NT)


def first_back_kernel(info, par, nv_in, r_ref, own, got, gsec_in, small2, *rest):
    cs, packs = rest[:8], rest[8:12]
    gfi, g0, g1, g2, g3, okeep, osend, small, ga_low = rest[12:]
    nv_ref, gsec = ref(nv_in), ref(gsec_in)
    packs = [p() for p in packs]
    n, d = own.shape
    rows = n // 2
    width = cs[0].dst.shape[0]
    sums = [0.0] * 3
    for s in range(2):
        here = slice(s * rows, (s + 1) * rows)
        u = own[here] + got[here].astype(f32) + gsec[here]
        nv = nv_ref[here]
        g = norm_back(u, par[1:2, :], nv, r_ref[here])
        sums = [a + rowsum(b) for a, b in zip(sums, (g, u * nv, u))]
        gfi.src[here] = g
        low = g.astype(bf16)
        ga_low[here] = low
        for k, out in enumerate((g0, g1, g2, g3)):
            out.src[s] = mm(packs[k][0:width, :], low, NT).astype(bf16)
    for out in (g3, g2, g1, g0, gfi):
        out.start()
    for k in range(4):
        total = mm(cs[k]()[...], ga_low[0:rows, :]) + mm(cs[4 + k]()[...], ga_low[rows:n, :])
        (osend if k % 2 else okeep).src[k // 2, 0:width, :] = total.astype(bf16)
    both = jnp.concatenate([*sums, small2[0:3, :], jnp.zeros((2, d), f32)], axis=0)
    small[...] = both
    high = both.astype(bf16)
    osend.src[0, width : width + 8, :] = high
    osend.src[1, width : width + 8, :] = (both - high.astype(f32)).astype(bf16)


def down_grads_kernel(info, act0, act1, gs, gs2, far_keep, far_send, keep, send, scr, *, parts):
    units = act0.shape[2]
    block = units // parts
    step = 384
    for act, mine, theirs in ((act1, far_keep, far_send), (act0, keep, send)):
        for m in range(0, units, step):
            cols = slice(m, m + step)
            total = mm(act[0, :, cols], gs[...], TN) + mm(act[1, :, cols], gs2[...], TN)
            total = total.astype(bf16)
            for i in range(step // block):
                b = m // block + i
                scr[(b & 1) ^ info[3], b >> 1] = total[i * block : (i + 1) * block]
        theirs.src[...] = scr[1]
        theirs.start()
        mine.src[...] = scr[0]
        mine.start()


def up_grads_kernel(
    info, low, low2, gh_in, okeep, ogot, small, ub, far_keep, far_send, keep, send, sums, scr, *, parts, width
):
    gh = ref(gh_in)
    units = low.shape[1]
    block = units // parts
    extra = width // parts
    joint = block + extra
    n = parts // 2 * joint
    step = 384
    got = ogot()
    both = small[...] + got[0, width : width + 8, :].astype(f32) + got[1, width : width + 8, :].astype(f32)
    both = jnp.concatenate([both[0:6], ub[0:2, :]], axis=0)
    sums[...] = both
    high = both.astype(bf16)
    far_send.src[n : n + 8, :] = high
    far_send.src[n + 8 : n + 16, :] = (both - high.astype(f32)).astype(bf16)
    for k, mine, theirs in ((1, far_keep, far_send), (0, keep, send)):
        for m in range(0, units, step):
            cols = slice(m, m + step)
            total = mm(low[:, cols], gh[k, 0], TN) + mm(low2[:, cols], gh[k, 1], TN)
            total = total.astype(bf16)
            for i in range(step // block):
                b = m // block + i
                scr[((b >> 1) & 1) ^ info[4], (b >> 2) * 2 + (b & 1), 0:block, :] = total[i * block : (i + 1) * block]
        o = (okeep()[k, 0:width, :].astype(f32) + got[k, 0:width, :].astype(f32)).astype(bf16)
        for b in range(parts):
            at = (b >> 2) * 2 + (b & 1)
            scr[((b >> 1) & 1) ^ info[4], at, block:joint, :] = o[b * extra : (b + 1) * extra]
        for b in range(parts // 2):
            theirs.src[b * joint : (b + 1) * joint, :] = scr[1, b]
            mine.src[b * joint : (b + 1) * joint, :] = scr[0, b]
        theirs.start()
        mine.start()


def swap(x, axis, bit):
    size = lax.axis_size(axis)
    return lax.ppermute(x, axis, [(i, i ^ bit) for i in range(size)])


def summed(parts):
    return sum(p.astype(f32) for p in parts)


def spread(array, axis, parts):
    bits = parts.bit_length() - 1
    return array.reshape(*array.shape[:axis], *([2] * bits), array.shape[axis] // parts, *array.shape[axis + 1 :])


def halve_sum(terms, axis, mine):
    other = [lax.dynamic_index_in_dim(t, 1 - mine, axis, keepdims=False) for t in terms]
    kept = [lax.dynamic_index_in_dim(t, mine, axis, keepdims=False) for t in terms]
    return kept, summed(other).astype(bf16)


def halve(terms, axis, bit, mine):
    other = [lax.dynamic_index_in_dim(t, 1 - mine, axis, keepdims=False) for t in terms]
    kept = [lax.dynamic_index_in_dim(t, mine, axis, keepdims=False) for t in terms]
    other = summed(other).astype(bf16)
    return kept + [swap(other, "dp", bit)], other


def body(
    inputs,
    cotangent,
    lengths,
    qkv_weight,
    qkv_bias,
    out_weight,
    out_bias,
    first_gain,
    first_shift,
    up_weight,
    up_bias,
    down_weight,
    down_bias,
    second_gain,
    second_shift,
):
    batch, seq, d = inputs.shape
    rows = cotangent.shape[1]
    n = batch * rows
    width = out_weight.shape[0]
    units = up_weight.shape[1]
    peers = lax.axis_size("tensor")
    parts = lax.axis_size("dp")
    bits = parts.bit_length() - 1
    t = lax.axis_index("tensor")
    dp = lax.axis_index("dp")
    bit_of = [(dp >> i) & 1 for i in range(bits)]
    info = lengths
    par = jnp.concatenate([out_bias, first_gain, first_shift, down_bias, second_gain, second_shift])
    par = par.reshape(6, d).astype(f32)
    w_t = jnp.transpose(qkv_weight, (1, 2, 0))
    pack, up_half, dn_half = prepare(info, out_weight, up_bias[None], up_weight, down_weight)
    pack2 = swap(pack, "tensor", 2)
    pack1 = swap(pack, "tensor", 1)
    u2a = swap(up_half, "tensor", 2)
    saved = []
    ctx = []
    for s in range(batch):
        q, k, v, lse, c, *cs = attend_fwd(s, info, inputs, w_t, qkv_bias, peers)
        saved.append((q, k, v, lse, c))
        if s == 0:
            *cs, pack1, pack2 = after(*cs, pack1, pack2)
        else:
            both = after(*cs, pack2, u2a, *ctx)
            cs, pack2, u2a, ctx = list(both[:peers]), both[peers], both[peers + 1], list(both[peers + 2 :])
        ctx += [cs[0]] + [swap(cs[j], "tensor", j) for j in range(1, peers)]
    *ctx, dn_half = after(*ctx, dn_half)
    d2a = swap(dn_half, "tensor", 2)
    pack3 = swap(pack2, "tensor", 1)
    packs = [pack, pack1, pack2, pack3]
    u2b = swap(u2a, "dp", 1)
    d2b = swap(d2a, "dp", 2)
    far_ctx = [whole(c) if k % peers == 0 else loose(c) for k, c in enumerate(ctx)]
    far_packs = [whole(pack)] + [loose(p) for p in packs[1:]]
    share = (inputs, ((batch, rows, d), lambda ref, info: ref.at[:, pl.ds(pl.multiple_of(info[2] * rows, rows), rows), :]))
    nv1, r1, low = call(
        "first_norm",
        first_norm_kernel,
        info,
        [share, par, *far_ctx, *far_packs],
        [SDS((n, d), f32), SDS((n, 1), f32), SDS((n, d), bf16)],
        vmem=NEAR,
    )
    low2 = swap(low, "tensor", 1)
    pair = SDS((2, n, units), bf16)
    part = SDS((n, d), f32)
    act0, slope0, own, sib = call(
        "feed",
        feed_kernel,
        info,
        [low, low2, far_packs[0], whole(up_weight), whole(down_weight)],
        [pair, pair, part, part],
        vmem=NEAR,
        width=width,
        far=False,
    )
    halves = [loose(x) for x in (u2a, u2b, d2a, d2b)]
    both = [pltpu.VMEM((d, units), bf16), pltpu.VMEM((units, d), bf16)]
    act1, slope1, own, sib = call(
        "feed",
        feed_kernel,
        info,
        [low, low2, far_packs[2], *halves, own, sib],
        [pair, pair, part, SDS((n, d), bf16)],
        both,
        vmem=NEAR,
        width=width,
        far=True,
    )
    got = swap(sib, "tensor", 1)
    outputs, gsec, gs_low, small2 = call(
        "second_norm",
        second_norm_kernel,
        info,
        [whole(cotangent), par, nv1, own, got],
        [[SDS((batch, rows, d), bf16)], part, SDS((n, d), bf16), SDS((8, d), f32)],
        vmem=NEAR,
    )
    gs_low2 = swap(gs_low, "tensor", 1)
    gh, own, sib, ub = call(
        "feed_back",
        feed_back_kernel,
        info,
        [gs_low, gs_low2, slope0, slope1, whole(up_weight), whole(down_weight), *halves],
        [SDS((2, 2, n, units), bf16), part, SDS((n, d), bf16), SDS((8, d), f32)],
        both,
        vmem=NEAR,
    )
    got = swap(sib, "tensor", 1)
    block = units // parts
    downs = call(
        "down_grads",
        down_grads_kernel,
        info,
        [act0, act1, gs_low, gs_low2],
        [[SDS((parts // 2, block, d), bf16)]] * 4,
        [pltpu.VMEM((2, parts // 2, block, d), bf16)],
        vmem=NEAR,
        parts=parts,
    )
    down_far_keep, down_far_send, down_keep, down_send = downs
    down_far_got = swap(down_far_send, "dp", 1)
    gfi, g0, g1, g2, g3, okeep, osend, small1 = call(
        "first_back",
        first_back_kernel,
        info,
        [par, nv1, r1, own, got, gsec, small2, *far_ctx, *far_packs],
        [
            [part],
            *[[SDS((batch, width, rows), bf16)]] * 4,
            *[[SDS((2, width + 8, d), bf16)]] * 2,
            SDS((8, d), f32),
        ],
        [pltpu.VMEM((n, d), bf16)],
        vmem=NEAR,
    )
    gctx = [g0] + [swap(g, "tensor", j) for j, g in ((1, g1), (2, g2), (3, g3))]
    got_o = swap(osend, "tensor", 1)
    joint = block + width // parts
    cut = parts // 2 * joint
    up_far_keep, up_far_send, up_keep, up_send, small = call(
        "up_grads",
        up_grads_kernel,
        info,
        [low, low2, gh, whole(okeep), loose(got_o), small1, ub],
        [
            [SDS((cut, d), bf16)],
            [SDS((cut + 16, d), bf16)],
            [SDS((cut, d), bf16)],
            [SDS((cut, d), bf16)],
            SDS((8, d), f32),
        ],
        [pltpu.VMEM((2, parts // 2, joint, d), bf16)],
        vmem=NEAR,
        parts=parts,
        width=width,
    )
    *gctx, up_far_send = after(*gctx, up_far_send)
    down_far_sum = summed([down_far_keep, down_far_got]).astype(bf16)
    q, k, v, lse, c = saved[0]
    *gctx, down_far_sum, up_far_keep = after(*gctx, down_far_sum, up_far_keep)
    up_far_got = swap(up_far_send, "dp", 2)
    down_y = swap(down_far_sum, "tensor", 2)
    down_got = swap(down_send, "dp", 1)
    keep, send, dw, db = attend_bwd(0, info, inputs, w_t, q, k, v, lse, c, gctx, None, parts)
    send, up_far_got, down_y, down_got = after(send, up_far_got, down_y, down_got)
    near = swap(send, "tensor", 1)
    shape = ([2] * (bits - 1)) + [block, d]
    down_terms = [x.reshape(shape) for x in (down_keep, down_got, down_y)]
    down_kept, down_next = halve_sum(down_terms, bits - 2, bit_of[1])
    shape = ([2] * (bits - 1)) + [joint, d]
    small = small + pair_sum(up_far_got, cut, 8)
    terms = [x.reshape(shape) for x in (up_far_keep, up_far_got[:cut])]
    up_far_kept, up_far_next = halve_sum(terms, bits - 2, bit_of[0])
    up_far_rows = with_rows(up_far_next, small)
    in_sum = summed([keep[1], near[1]]).astype(bf16)
    dw, down_next, up_far_rows, in_sum, up_send, up_keep = after(dw, down_next, up_far_rows, in_sum, up_send, up_keep)
    first_terms = [keep[0], near[0]]
    q, k, v, lse, c = saved[1]
    up_got = swap(up_send, "dp", 2)
    down_more = swap(down_next, "dp", 2)
    up_more = swap(up_far_rows, "dp", 1)
    first_far = swap(in_sum, "tensor", 2)
    keep, send, w_keep, w_send, db = attend_bwd(1, info, inputs, w_t, q, k, v, lse, c, gctx, (dw, db), parts)
    w_send, send, up_got, down_more, up_more, first_far = after(w_send, send, up_got, down_more, up_more, first_far)
    first_terms.append(first_far)
    down_terms = down_kept + [down_more]
    near = swap(send, "tensor", 1)
    in_sum = summed([keep[1], near[1]]).astype(bf16)
    last_terms = [keep[0], near[0], swap(in_sum, "tensor", 2)]
    order = [1, 0] + list(range(2, bits))
    row = 3 * (d // parts) // 2
    got = swap(w_send, "dp", 2)
    got, in_sum = after(got, in_sum)
    got, up_got, up_more, *down_terms = after(got, up_got, up_more, *down_terms)
    at = up_far_next.size // d
    up_far_terms = up_far_kept + [up_more[:at].reshape(up_far_next.shape)]
    small_x = pair_sum(up_more, at, 8)
    small = small + small_x
    small = jnp.concatenate([small[0:6], small[7:8], small[6:7]])
    send = summed(up_far_terms).astype(bf16)
    up_y_sent = with_rows(send, small)
    up_y = swap(up_y_sent, "tensor", 2)
    at = send.size // d
    small = jnp.concatenate([small[0:6], small[7:8], small[7:8]]) + pair_sum(up_y, at, 8)
    shape = ([2] * (bits - 1)) + [joint, d]
    terms, up_next = halve([x.reshape(shape) for x in (up_keep, up_got)], bits - 2, 1, bit_of[0])
    terms.append(up_y[:at].reshape(send.shape))
    for i in range(2, bits):
        terms, sent, more = halve_with(terms, terms[0].ndim - 3, small, "dp", 1 << i, bit_of[i])
        small = small + more
    up_sum = summed(terms)
    mine = small
    for i in range(2, bits):
        down_terms, sent = halve(down_terms, bits - 1 - i, 1 << i, bit_of[i])
    down_sum = summed(down_terms)
    at = parts // 2 * row
    shape = ([2] * (bits - 1)) + [row, 2 * width]
    terms = [x.reshape(shape) for x in (w_keep, got[:at])]
    db = db + got[at : at + 1].astype(f32) + got[at + 1 : at + 2].astype(f32)
    for i in order[1:]:
        kept, sent, more = halve_with(terms, terms[0].ndim - 3, db, "dp", 1 << i, bit_of[i])
        terms, db = kept, db + more
    qkv_sum = summed(terms)
    qkv_sum = jnp.concatenate([qkv_sum[:, :width], qkv_sum[:, width:]], axis=0).reshape(3, -1, width)
    qkv_sum = jnp.transpose(qkv_sum, (1, 0, 2))
    db = db.reshape(2, width)
    input_list = [
        (summed(x) + gfi[s * rows : (s + 1) * rows]).astype(bf16)
        for s, x in enumerate((first_terms, last_terms))
    ]
    return (
        outputs,
        jnp.stack(input_list, 0),
        qkv_sum,
        db,
        up_sum[block:],
        mine[0],
        mine[1],
        mine[2],
        up_sum[:block],
        mine[6],
        down_sum,
        mine[3],
        mine[4],
        mine[5],
    )


def pair_sum(array, at, n):
    return array[at : at + n].astype(f32) + array[at + n : at + 2 * n].astype(f32)


def with_rows(array, rows):
    flat = array.reshape(-1, array.shape[-1])
    high = rows.astype(bf16)
    low = (rows - high.astype(f32)).astype(bf16)
    return jnp.concatenate([flat, high, low], axis=0)


def halve_with(terms, axis, rows, name, bit, mine):
    other = [lax.dynamic_index_in_dim(t, 1 - mine, axis, keepdims=False) for t in terms]
    kept = [lax.dynamic_index_in_dim(t, mine, axis, keepdims=False) for t in terms]
    other = summed(other).astype(bf16)
    sent = with_rows(other, rows)
    got = swap(sent, name, bit)
    cut = other.size // other.shape[-1]
    return kept + [got[:cut].reshape(other.shape)], sent, pair_sum(got, cut, rows.shape[0])


def after(*values):
    return lax.optimization_barrier(values)


def solution(mesh):
    in_specs = (
        P("dp", None, None),
        P("dp", "tensor", None),
        P("dp"),
        P(None, None, "tensor"),
        P(None, "tensor"),
        P("tensor", None),
        P(),
        P(),
        P(),
        P(None, "tensor"),
        P("tensor"),
        P("tensor", None),
        P(),
        P(),
        P(),
    )
    out_specs = (
        P("dp", "tensor", None),
        P("dp", "tensor", None),
        P("dp", None, "tensor"),
        P(None, "tensor"),
        P(("tensor", "dp"), None),
        P(),
        P(),
        P(),
        P("dp", "tensor"),
        P("tensor"),
        P(("tensor", "dp"), None),
        P(),
        P(),
        P(),
    )
    return jax.shard_map(body, mesh=mesh, in_specs=in_specs, out_specs=out_specs, check_vma=False)
```

```python
import functools

import jax
import jax.numpy as jnp
from jax import lax
from jax.experimental import pallas as pl
from jax.experimental.pallas import tpu as pltpu
from jax.sharding import PartitionSpec as P

HEAD = 64
WIDE, LANES = 192, 256
NEAR = 30
NT = (((1,), (1,)), ((), ()))
NN = (((1,), (0,)), ((), ()))
TN = (((0,), (0,)), ((), ()))
bf16 = jnp.bfloat16
f32 = jnp.float32
VM = pl.BlockSpec(memory_space=pltpu.VMEM)
SDS = jax.ShapeDtypeStruct


def mm(a, b, dims=NN):
    return lax.dot_general(a, b, dims, preferred_element_type=f32)


class Fetch:
    def __init__(self, src, dst, sem):
        self.dst, self.copy = dst, pltpu.make_async_copy(src, dst, sem)
        self.copy.start()
        self.waiting = True

    def __call__(self):
        if self.waiting:
            self.copy.wait()
            self.waiting = False
        return self.dst


class Flush:
    def __init__(self, src, dst, sem):
        self.src, self.copy = src, pltpu.make_async_copy(src, dst, sem)
        self.started = False

    def start(self):
        if not self.started:
            self.copy.start()
        self.started = True


def call(name, body, info, ins, outs, scratch=(), vmem=58, which=0, **static):
    far_in = [i for i, a in enumerate(ins) if isinstance(a, tuple)]
    pinned = [i for i in far_in if len(ins[i]) == 2]
    far_out = [i for i, o in enumerate(outs) if isinstance(o, list)]
    raw_in = [i for i, a in enumerate(ins) if isinstance(a, Raw)]
    raw_out = [i for i, o in enumerate(outs) if isinstance(o, Raw)]
    pinned += raw_in
    arrays = [a[0] if isinstance(a, tuple) else a.value if isinstance(a, Raw) else a for a in ins]
    shapes = [o[0] if isinstance(o, list) else o.value if isinstance(o, Raw) else o for o in outs]
    picked = [a[1] if isinstance(a, tuple) else None for a in ins]
    n_in, n_out = len(ins), len(outs)

    def kernel(lengths_ref, which_ref, *refs):
        dp = lax.axis_index("dp")
        at = which_ref[0]
        info_ref = (lengths_ref[0], lengths_ref[1], lax.axis_index("tensor"), dp & 1, (dp >> 1) & 1, at, lengths_ref[at], lengths_ref)
        in_refs, refs = refs[:n_in], refs[n_in:]
        out_refs, refs = refs[:n_out], refs[n_out:]
        sem, refs = refs[-1], refs[:-1]
        buffers, rest = refs[: len(far_in) + len(far_out)], refs[len(far_in) + len(far_out) :]
        args = list(in_refs)
        for j, i in enumerate(far_in):
            view = picked[i][1]
            args[i] = Fetch(view(in_refs[i], info_ref), buffers[j], sem.at[j])
        results = list(out_refs)
        flushes = []
        for j, i in enumerate(far_out):
            at = len(far_in) + j
            results[i] = Flush(buffers[at], out_refs[i], sem.at[at])
            flushes.append(results[i])
        body(info_ref, *args, *results, *rest, **static)
        for i in far_in:
            args[i]()
        for f in flushes:
            f.start()
        for f in flushes:
            f.copy.wait()

    hbm = pl.BlockSpec(memory_space=pltpu.HBM)
    buffers = [pltpu.VMEM(picked[i][0], arrays[i].dtype) for i in far_in]
    buffers += [pltpu.VMEM(shapes[i].shape, shapes[i].dtype) for i in far_out]
    return pl.pallas_call(
        kernel,
        out_shape=[pltpu.HBM(o.shape, o.dtype) if i in far_out + raw_out else o for i, o in enumerate(shapes)],
        grid_spec=pltpu.PrefetchScalarGridSpec(
            num_scalar_prefetch=2,
            grid=(1,),
            in_specs=[hbm if i in pinned else pl.BlockSpec(memory_space=pl.ANY) if i in far_in else VM for i in range(n_in)],
            out_specs=[hbm if i in far_out + raw_out else VM for i in range(n_out)],
            scratch_shapes=[*buffers, *scratch, pltpu.SemaphoreType.DMA((max(1, len(far_in) + len(far_out)),))],
        ),
        compiler_params=pltpu.CompilerParams(vmem_limit_bytes=vmem << 20),
        cost_estimate=pl.CostEstimate(flops=1000, bytes_accessed=1000, transcendentals=0),
        name=name,
    )(info, jnp.full((1,), which, jnp.int32), *[pltpu.with_memory_space_constraint(a, pltpu.HBM) if i in pinned else a for i, a in enumerate(arrays)])


class Raw:
    def __init__(self, value):
        self.value = value


def ref(x):
    return x() if isinstance(x, Fetch) else x.src if isinstance(x, Flush) else x


def whole(a):
    return (a, (a.shape, lambda ref, info: ref))


def loose(a):
    return (*whole(a), None)


def prepare_kernel(info, out_in, bias, up_in, dn_in, pack, up_half, dn_half):
    for src, dst in ((up_in, up_half), (dn_in, dn_half)):
        dst.src[...] = src()[...]
        dst.start()
    out_w = out_in()
    width, d = out_w.shape
    pack.src[0:width, :] = out_w[...]
    pack.src[width : width + 8, :] = jnp.broadcast_to(bias[...], (8, d))


def prepare(info, out_w, bias, up, dn):
    width, d = out_w.shape
    half = up.shape[0] // 2
    view = lambda ref, info: ref.at[pl.ds(pl.multiple_of(info[3] * half, half), half)]
    view2 = lambda ref, info: ref.at[pl.ds(pl.multiple_of(info[4] * half, half), half)]
    ins = [whole(out_w), bias, (up, ((half, d), view)), (dn, ((half, d), view2))]
    return call("prepare", prepare_kernel, info, ins, [[SDS((width + 8, d), bf16)]] + [[SDS((half, d), bf16)]] * 2)


def head_cols(a, h, extra=()):
    lane = lax.broadcasted_iota(jnp.int32, a.shape, 1)
    out = jnp.where((lane >= HEAD * h) & (lane < HEAD * (h + 1)), a, jnp.zeros_like(a))
    for i, e in enumerate(extra):
        out = jnp.where(lane == WIDE + i, e, out)
    return out


def tail_cols(rows, values):
    lane = lax.broadcasted_iota(jnp.int32, (rows, LANES - WIDE), 1)
    out = jnp.zeros((rows, LANES - WIDE), f32)
    for i, v in enumerate(values):
        out = jnp.where(lane == i, v, out)
    return out.astype(bf16)


def attend_fwd_kernel(info, x_hbm, w_ref, b_ref, *rest):
    far, outs = rest[:5], rest[5:9]
    x_all, *near, v_t, s_all, sem_in, sem_out = rest[9:]
    q_all, k_all, v_all, lse_all, c_all = near
    me = info[2]
    batch, peers, width, block = c_all.shape
    seq = peers * block
    heads = width // HEAD

    def fetch(s):
        return pltpu.make_async_copy(x_hbm.at[s], x_all.at[s], sem_in.at[s])

    def flush(s, i):
        return pltpu.make_async_copy(near[i].at[s], far[i].at[s], sem_out.at[s, i])

    for s in range(batch):
        fetch(s).start()
    w = w_ref()

    def one_sequence(s, carry):
        length = info[7][s]
        fetch(s).wait()
        x = x_all[s]
        k_all[s, :, 0:WIDE] = mm(x, w[1], NT).astype(bf16)
        row = lax.broadcasted_iota(jnp.int32, (seq, 1), 0)
        k_all[s, :, WIDE:LANES] = tail_cols(seq, (jnp.where(row < length, 0.0, -1e30),))
        q = mm(x, w[0], NT) + b_ref[0:1, :].astype(f32)
        q_all[s, :, 0:WIDE] = q.astype(bf16) * jnp.asarray(0.125, bf16)
        q_all[s, :, WIDE:LANES] = tail_cols(seq, (1.0,))
        v = (mm(x, w[2], NT) + b_ref[1:2, :].astype(f32)).astype(bf16)
        v_all[s] = v
        v_t[...] = v.T
        for i in range(3):
            flush(s, i).start()

        def two_blocks(n, carry):
            qb = q_all[s, pl.ds(pl.multiple_of(n * 2 * block, 2 * block), 2 * block), :]
            one = jnp.ones_like(qb[:, 0:1])
            for h in range(heads):
                s_all[h] = mm(k_all[s], head_cols(qb, h, (one,)), NT)
            for h in range(heads):
                top = jnp.max(s_all[h], axis=0, keepdims=True)
                p = jnp.exp(s_all[h] - top)
                total = jnp.sum(p, axis=0, keepdims=True)
                rows = slice(HEAD * h, HEAD * (h + 1))
                out = (mm(v_t[rows, :], p.astype(bf16)) * (1.0 / total)).astype(bf16)
                lse = top + jnp.log(total)
                for j in range(2):
                    cols = slice(block * j, block * (j + 1))
                    c_all[s, 2 * n + j, rows, :] = out[:, cols]
                    lse_all[s, 2 * n + j, h : h + 1, :] = lse[:, cols]
            return carry

        lax.fori_loop(0, peers // 2, two_blocks, 0)
        for i in range(3, 5):
            flush(s, i).start()
        for k, out in enumerate(outs):
            out.src[s] = c_all[s, me ^ k]
        return carry

    lax.fori_loop(0, batch, one_sequence, 0)
    for out in outs:
        out.start()
    for s in range(batch):
        for i in range(5):
            flush(s, i).wait()


def attend_fwd(info, inputs, w_t, bias, peers):
    batch, seq, d = inputs.shape
    width = w_t.shape[1]
    block = seq // peers
    far = [SDS((batch, seq, LANES), bf16)] * 2 + [SDS((batch, seq, width), bf16)]
    far += [SDS((batch, peers, 8, block), f32), SDS((batch, peers, width, block), bf16)]
    scratch = [pltpu.VMEM(inputs.shape, bf16), *[pltpu.VMEM(o.shape, o.dtype) for o in far]]
    scratch += [pltpu.VMEM((width, seq), bf16), pltpu.VMEM((width // HEAD, seq, 2 * block), f32)]
    scratch += [pltpu.SemaphoreType.DMA((batch,)), pltpu.SemaphoreType.DMA((batch, 5))]
    return call(
        "attend_fwd",
        attend_fwd_kernel,
        info,
        [Raw(inputs), whole(w_t), bias],
        [Raw(o) for o in far] + [[SDS((batch, width, block), bf16)]] * peers,
        scratch,
    )


def of_sequence(a):
    return (a, (a.shape[1:], lambda ref, info: ref.at[info[5]]))


def attend_bwd_kernel(info, x_ref, q_in, k_in, v_in, lse_in, c_in, *rest):
    w_ref = x_ref
    peers = 4
    gs, rest = rest[:peers], rest[peers:]
    keep, send, low_out, db_ref, dq_t, dk, dv, k_t, g_ref = rest
    low = low_out.src
    length = info[6]
    me = info[2]
    k_ref, q_ref, v_ref = k_in(), q_in(), v_in()
    lse_ref, c_ref = lse_in(), c_in()
    _, width, block = c_ref.shape
    heads = width // HEAD
    k_t[...] = k_ref[:, 0:WIDE].T
    dk[...] = jnp.zeros_like(dk)
    dv[...] = jnp.zeros_like(dv)
    for k in range(peers):
        g_ref[me ^ k] = gs[k]()[...]

    def one_block(s, carry):
        at = pl.multiple_of(s * block, block)

        @pl.when(at >= length)
        def _():
            dq_t[:, pl.ds(at, block)] = jnp.zeros((width, block), f32)

        @pl.when(at < length)
        def _():
            qb = q_ref[pl.ds(at, block), :]
            g_t = g_ref[s]
            g = g_t.T
            prod_t = g_t.astype(f32) * c_ref[s].astype(f32)
            for h in range(heads):
                rows = slice(HEAD * h, HEAD * (h + 1))
                qh = head_cols(qb, h)
                gh = head_cols(g, h)
                scores = mm(k_ref[...], qh, NT)
                row = lax.broadcasted_iota(jnp.int32, scores.shape, 0)
                p = jnp.where(row < length, jnp.exp(scores - lse_ref[s, h : h + 1, :]), 0.0)
                dp = mm(v_ref[...], gh, NT)
                inner = jnp.sum(prod_t[rows], axis=0, keepdims=True)
                ds = (p * (dp - inner)).astype(bf16)
                dv[...] += mm(p.astype(bf16), gh)
                dk[...] += mm(ds, qh)
                dq_t[rows, pl.ds(at, block)] = mm(k_t[rows, :], ds) * 0.125

        return carry

    lax.fori_loop(0, peers, one_block, 0)
    low[0] = dq_t[...].T.astype(bf16)
    low[1] = dk[:, 0:WIDE].astype(bf16)
    low[2] = dv[...].astype(bf16)
    w = w_ref()
    for s in range(peers):
        at = pl.multiple_of((me ^ s) * block, block)
        total = sum(mm(low[i, pl.ds(at, block), :], w[i]) for i in range(3))
        (send if s % 2 else keep).src[s // 2] = total.astype(bf16)
    send.start()
    keep.start()
    db_ref[...] = jnp.concatenate([rowsum(low[i].astype(f32)) for i in (0, 2)], axis=1)


def attend_bwd(which, info, w_t, q, k, v, lse, c, gs, d):
    _, peers, width, block = c.shape
    seq = peers * block
    outs = [[SDS((2, block, d), bf16)]] * 2 + [[SDS((3, seq, width), bf16)], SDS((1, 2 * width), f32)]
    scratch = [
        pltpu.VMEM((width, seq), f32),
        pltpu.VMEM((seq, LANES), f32),
        pltpu.VMEM((seq, width), f32),
        pltpu.VMEM((width, seq), bf16),
        pltpu.VMEM((peers, width, block), bf16),
    ]
    ins = [whole(w_t)] + [of_sequence(a) for a in (q, k, v, lse, c)]
    ins += [(g, ((width, block), lambda ref, info: ref.at[info[5]]), None) for g in gs]
    return call("attend_bwd", attend_bwd_kernel, info, ins, outs, scratch, which=which)


def project_grads_kernel(info, x_in, low0, low1, db0, db1, keep, send, db_ref, dw, *, parts):
    lows = (low0(), low1())
    x = x_in()
    _, d, width = dw.shape
    step = 256
    for i in range(3):
        for m in range(0, d, step):
            cols = slice(m, m + step)
            dw[i, cols, :] = mm(x[0, :, cols], lows[0][i], TN) + mm(x[1, :, cols], lows[1][i], TN)
    rows = d // parts
    half = 3 * rows // 2
    for b in range(parts):
        flat = dw[:, b * rows : (b + 1) * rows, :].reshape(3 * rows, width)
        flat = jnp.concatenate([flat[0:half], flat[half : 2 * half]], axis=1).astype(bf16)
        at = ((b >> 2) * 2 + (b & 1)) * half
        mine = ((b >> 1) & 1) == info[4]

        @pl.when(mine)
        def _():
            keep.src[at : at + half, :] = flat

        @pl.when(jnp.logical_not(mine))
        def _():
            send.src[at : at + half, :] = flat

    db = db0[...] + db1[...]
    db_ref[...] = db
    high = db.astype(bf16)
    n = keep.src.shape[0]
    send.src[n : n + 8, :] = jnp.concatenate(
        [high, (db - high.astype(f32)).astype(bf16), jnp.zeros((6, 2 * width), bf16)], axis=0
    )
    send.start()


def gelu_parts(h):
    t = 1.0 / (1.0 + (0.3275911 * 0.7071067811865476) * jnp.abs(h))
    poly = t * (0.127414796 + t * (-0.142248368 + t * (0.7107068705 + t * (-0.7265760135 + t * 0.5307027145))))
    bell = jnp.exp2((-0.5 * 1.4426950408889634) * (h * h))
    tail = poly * bell
    cum = jnp.where(h < 0, tail, 1.0 - tail)
    return h * cum, cum + h * (bell * 0.3989422804014327)


def norm_parts(v):
    center = v - jnp.mean(v, axis=1, keepdims=True)
    r = lax.rsqrt(jnp.mean(center * center, axis=1, keepdims=True) + 1e-12)
    return center * r, r


def norm_back(u, gain, nv, r):
    gu = u * gain
    return r * (gu - jnp.mean(gu, axis=1, keepdims=True) - nv * jnp.mean(gu * nv, axis=1, keepdims=True))


def rowsum(v):
    return jnp.sum(v, axis=0, keepdims=True)


def first_norm_kernel(info, x_in, par, *rest):
    nv_ref, r_ref, low = rest[8:]
    cs, packs = [c() for c in rest[:4]], [p() for p in rest[4:8]]
    x_ref = x_in()
    batch, rows = x_ref.shape[:2]
    width = cs[0].shape[1]

    def one_sequence(s, carry):
        here = pl.ds(pl.multiple_of(s * rows, rows), rows)
        total = par[0:1, :] + x_ref[s].astype(f32)
        for k in range(4):
            total = total + mm(cs[k][s], packs[k][0:width, :], TN)
        nv, r = norm_parts(total)
        nv_ref[here, :] = nv
        r_ref[here, :] = r
        low[here, :] = (nv * par[1:2, :] + par[2:3, :]).astype(bf16)
        return carry

    lax.fori_loop(0, batch, one_sequence, 0)


def feed_kernel(info, low, low2, pack, *rest, width, far):
    if far:
        u_a, u_b, d_a, d_b, p_own, p_sib, act_out, slope_out, own, sib, both, up, dn = rest
        half = u_a.dst.shape[0]
        assemble(info[3], up, u_a(), u_b(), half)
    else:
        u_in, d_in, act_out, slope_out, own, sib, both = rest
        up = u_in()
    act, slope = ref(act_out), ref(slope_out)
    units = up.shape[1]
    bias = pack()
    step = 256
    both[0] = low[...]
    both[1] = low2[...]

    def side(j, carry):
        def chunk(n, carry):
            cols = pl.ds(pl.multiple_of(n * step, step), step)
            hidden = mm(both[j], up[:, cols]) + bias[width : width + 1, cols].astype(f32)
            a, g = gelu_parts(hidden)
            act[j, :, cols] = a.astype(bf16)
            slope[j, :, cols] = g.astype(bf16)
            return carry

        return lax.fori_loop(0, units // step, chunk, carry)

    lax.fori_loop(0, 2, side, 0)
    if far:
        assemble(info[4], dn, d_a(), d_b(), half)
        sib[...] = (p_sib[...] + mm(act[1], dn[...])).astype(bf16)
        own[...] = p_own[...] + mm(act[0], dn[...])
    else:
        dn = d_in()
        own[...] = mm(act[0], dn[...])
        sib[...] = mm(act[1], dn[...])


def assemble(bit, dst, a, b, half):
    dst[pl.ds(pl.multiple_of(bit * half, half), half)] = a[...]
    dst[pl.ds(pl.multiple_of((1 - bit) * half, half), half)] = b[...]


def second_norm_kernel(info, cot_in, par, nv_in, own, got, outs, gsec_out, gs_low, small):
    cot, nv_ref, gsec = cot_in(), ref(nv_in), ref(gsec_out)
    batch, rows, d = cot.shape

    def one_sequence(s, sums):
        here = pl.ds(pl.multiple_of(s * rows, rows), rows)
        total = own[here, :] + got[here, :].astype(f32) + par[3:4, :] + (nv_ref[here, :] * par[1:2, :] + par[2:3, :])
        nv, r = norm_parts(total)
        outs.src[s] = (nv * par[4:5, :] + par[5:6, :]).astype(bf16)
        at = info[2] * rows + lax.broadcasted_iota(jnp.int32, (rows, 1), 0)
        seed = jnp.where(at < info[7][s], cot[s].astype(f32), 0.0)
        g = norm_back(seed, par[4:5, :], nv, r)
        gsec[here, :] = g
        gs_low[here, :] = g.astype(bf16)
        return tuple(a + rowsum(b) for a, b in zip(sums, (g, seed * nv, seed)))

    sums = lax.fori_loop(0, batch, one_sequence, (jnp.zeros((1, d), f32),) * 3)
    small[...] = jnp.concatenate([*sums, jnp.zeros((5, d), f32)], axis=0)


def feed_back_kernel(info, gs, gs2, slope0, slope1, up0, dn0, u_a, u_b, d_a, d_b, gh_out, own, sib, ub, sides, up2, dn2):
    gh = ref(gh_out)
    half = u_a.dst.shape[0]
    units = up0.dst.shape[1]
    ub[...] = jnp.zeros_like(ub)
    sides[0] = gs[...]
    sides[1] = gs2[...]
    step = 256
    for k, slope in enumerate((ref(slope0), ref(slope1))):
        if k:
            assemble(info[4], dn2, d_a(), d_b(), half)
            dn = dn2
        else:
            dn = dn0()

        def side(j, carry):
            def chunk(n, carry):
                cols = pl.ds(pl.multiple_of(n * step, step), step)
                ga = mm(sides[j], dn[cols, :], NT)
                h = (ga * slope[j, :, cols].astype(f32)).astype(bf16)
                gh[k, j, :, cols] = h
                ub[k : k + 1, cols] += rowsum(h.astype(f32))
                return carry

            return lax.fori_loop(0, units // step, chunk, carry)

        lax.fori_loop(0, 2, side, 0)
    assemble(info[3], up2, u_a(), u_b(), half)
    up = up0()
    sib[...] = (mm(gh[0, 1], up[...], NT) + mm(gh[1, 1], up2[...], NT)).astype(bf16)
    own[...] = mm(gh[0, 0], up[...], NT) + mm(gh[1, 0], up2[...], NT)


def first_back_kernel(info, par, nv_in, r_ref, own, got, gsec_in, small2, *rest):
    cs, packs = [c() for c in rest[:4]], rest[4:8]
    gfi, g0, g1, g2, g3, okeep, osend, small, ga_low = rest[8:]
    nv_ref, gsec = ref(nv_in), ref(gsec_in)
    packs = [p() for p in packs]
    n, d = own.shape
    rows = n // 2
    width = cs[0].shape[1]

    def one_sequence(s, sums):
        here = pl.ds(pl.multiple_of(s * rows, rows), rows)
        u = own[here, :] + got[here, :].astype(f32) + gsec[here, :]
        nv = nv_ref[here, :]
        g = norm_back(u, par[1:2, :], nv, r_ref[here, :])
        gfi.src[here, :] = g
        low = g.astype(bf16)
        ga_low[here, :] = low
        for k, out in enumerate((g0, g1, g2, g3)):
            out.src[s] = mm(packs[k][0:width, :], low, NT).astype(bf16)
        return tuple(a + rowsum(b) for a, b in zip(sums, (g, u * nv, u)))

    sums = lax.fori_loop(0, 2, one_sequence, (jnp.zeros((1, d), f32),) * 3)
    for out in (g3, g2, g1, g0, gfi):
        out.start()
    for k in range(4):
        total = mm(cs[k][0], ga_low[0:rows, :]) + mm(cs[k][1], ga_low[rows:n, :])
        (osend if k % 2 else okeep).src[k // 2, 0:width, :] = total.astype(bf16)
    both = jnp.concatenate([*sums, small2[0:3, :], jnp.zeros((2, d), f32)], axis=0)
    small[...] = both
    high = both.astype(bf16)
    osend.src[0, width : width + 8, :] = high
    osend.src[1, width : width + 8, :] = (both - high.astype(f32)).astype(bf16)


def down_grads_kernel(info, act0, act1, gs, gs2, far_keep, far_send, keep, send, scr, *, parts):
    units = act0.shape[2]
    block = units // parts
    step = 384
    for act, mine, theirs in ((act1, far_keep, far_send), (act0, keep, send)):

        def chunk(m, carry):
            cols = pl.ds(pl.multiple_of(m * step, step), step)
            total = mm(act[0, :, cols], gs[...], TN) + mm(act[1, :, cols], gs2[...], TN)
            total = total.astype(bf16)
            for i in range(step // block):
                scr[(i & 1) ^ info[3], m * (step // block // 2) + (i >> 1)] = total[i * block : (i + 1) * block]
            return carry

        lax.fori_loop(0, units // step, chunk, 0)
        theirs.src[...] = scr[1]
        theirs.start()
        mine.src[...] = scr[0]
        mine.start()


def up_grads_kernel(
    info, low, low2, gh_in, okeep, ogot, small, ub, far_keep, far_send, keep, send, sums, scr, *, parts, width
):
    gh = ref(gh_in)
    units = low.shape[1]
    block = units // parts
    extra = width // parts
    joint = block + extra
    n = parts // 2 * joint
    step = 384
    got = ogot()
    both = small[...] + got[0, width : width + 8, :].astype(f32) + got[1, width : width + 8, :].astype(f32)
    both = jnp.concatenate([both[0:6], ub[0:2, :]], axis=0)
    sums[...] = both
    high = both.astype(bf16)
    far_send.src[n : n + 8, :] = high
    far_send.src[n + 8 : n + 16, :] = (both - high.astype(f32)).astype(bf16)
    for k, mine, theirs in ((1, far_keep, far_send), (0, keep, send)):

        def chunk(m, carry):
            cols = pl.ds(pl.multiple_of(m * step, step), step)
            total = mm(low[:, cols], gh[k, 0], TN) + mm(low2[:, cols], gh[k, 1], TN)
            total = total.astype(bf16)
            for i in range(step // block):
                at = (m * (step // block // 4) + (i >> 2)) * 2 + (i & 1)
                scr[((i >> 1) & 1) ^ info[4], at, 0:block, :] = total[i * block : (i + 1) * block]
            return carry

        lax.fori_loop(0, units // step, chunk, 0)
        o = (okeep()[k, 0:width, :].astype(f32) + got[k, 0:width, :].astype(f32)).astype(bf16)
        for b in range(parts):
            at = (b >> 2) * 2 + (b & 1)
            scr[((b >> 1) & 1) ^ info[4], at, block:joint, :] = o[b * extra : (b + 1) * extra]
        for b in range(parts // 2):
            theirs.src[b * joint : (b + 1) * joint, :] = scr[1, b]
            mine.src[b * joint : (b + 1) * joint, :] = scr[0, b]
        theirs.start()
        mine.start()


def swap(x, axis, bit):
    size = lax.axis_size(axis)
    return lax.ppermute(x, axis, [(i, i ^ bit) for i in range(size)])


def summed(parts):
    return sum(p.astype(f32) for p in parts)


def spread(array, axis, parts):
    bits = parts.bit_length() - 1
    return array.reshape(*array.shape[:axis], *([2] * bits), array.shape[axis] // parts, *array.shape[axis + 1 :])


def halve_sum(terms, axis, mine):
    other = [lax.dynamic_index_in_dim(t, 1 - mine, axis, keepdims=False) for t in terms]
    kept = [lax.dynamic_index_in_dim(t, mine, axis, keepdims=False) for t in terms]
    return kept, summed(other).astype(bf16)


def halve(terms, axis, bit, mine):
    other = [lax.dynamic_index_in_dim(t, 1 - mine, axis, keepdims=False) for t in terms]
    kept = [lax.dynamic_index_in_dim(t, mine, axis, keepdims=False) for t in terms]
    other = summed(other).astype(bf16)
    return kept + [swap(other, "dp", bit)], other


def body(
    inputs,
    cotangent,
    lengths,
    qkv_weight,
    qkv_bias,
    out_weight,
    out_bias,
    first_gain,
    first_shift,
    up_weight,
    up_bias,
    down_weight,
    down_bias,
    second_gain,
    second_shift,
):
    batch, seq, d = inputs.shape
    rows = cotangent.shape[1]
    n = batch * rows
    width = out_weight.shape[0]
    units = up_weight.shape[1]
    peers = lax.axis_size("tensor")
    parts = lax.axis_size("dp")
    bits = parts.bit_length() - 1
    t = lax.axis_index("tensor")
    dp = lax.axis_index("dp")
    bit_of = [(dp >> i) & 1 for i in range(bits)]
    info = lengths
    par = jnp.concatenate([out_bias, first_gain, first_shift, down_bias, second_gain, second_shift])
    par = par.reshape(6, d).astype(f32)
    w_t = jnp.transpose(qkv_weight, (1, 2, 0))
    pack, up_half, dn_half = prepare(info, out_weight, up_bias[None], up_weight, down_weight)
    pack2 = swap(pack, "tensor", 2)
    pack1 = swap(pack, "tensor", 1)
    u2a = swap(up_half, "tensor", 2)
    q, k, v, lse, c, *cs = attend_fwd(info, inputs, w_t, qkv_bias, peers)
    saved = (q, k, v, lse, c)
    *cs, pack1, pack2, u2a = after(*cs, pack1, pack2, u2a)
    ctx = [cs[0]] + [swap(cs[j], "tensor", j) for j in range(1, peers)]
    pack3 = swap(pack2, "tensor", 1)
    *ctx, pack3, dn_half = after(*ctx, pack3, dn_half)
    d2a = swap(dn_half, "tensor", 2)
    packs = [pack, pack1, pack2, pack3]
    u2b = swap(u2a, "dp", 1)
    d2b = swap(d2a, "dp", 2)
    far_ctx = [whole(ctx[0])] + [loose(x) for x in ctx[1:]]
    far_packs = [whole(pack)] + [loose(p) for p in packs[1:]]
    share = (inputs, ((batch, rows, d), lambda ref, info: ref.at[:, pl.ds(pl.multiple_of(info[2] * rows, rows), rows), :]))
    nv1, r1, low = call(
        "first_norm",
        first_norm_kernel,
        info,
        [share, par, *far_ctx, *far_packs],
        [SDS((n, d), f32), SDS((n, 1), f32), SDS((n, d), bf16)],
        vmem=NEAR,
    )
    low2 = swap(low, "tensor", 1)
    pair = SDS((2, n, units), bf16)
    part = SDS((n, d), f32)
    sides = pltpu.VMEM((2, n, d), bf16)
    act0, slope0, own, sib = call(
        "feed",
        feed_kernel,
        info,
        [low, low2, far_packs[0], whole(up_weight), whole(down_weight)],
        [pair, pair, part, part],
        [sides],
        vmem=NEAR,
        width=width,
        far=False,
    )
    halves = [loose(x) for x in (u2a, u2b, d2a, d2b)]
    both = [pltpu.VMEM((d, units), bf16), pltpu.VMEM((units, d), bf16)]
    act1, slope1, own, sib = call(
        "feed",
        feed_kernel,
        info,
        [low, low2, far_packs[2], *halves, own, sib],
        [pair, pair, part, SDS((n, d), bf16)],
        [sides, *both],
        vmem=NEAR,
        width=width,
        far=True,
    )
    got = swap(sib, "tensor", 1)
    outputs, gsec, gs_low, small2 = call(
        "second_norm",
        second_norm_kernel,
        info,
        [whole(cotangent), par, nv1, own, got],
        [[SDS((batch, rows, d), bf16)], part, SDS((n, d), bf16), SDS((8, d), f32)],
        vmem=NEAR,
    )
    gs_low2 = swap(gs_low, "tensor", 1)
    gh, own, sib, ub = call(
        "feed_back",
        feed_back_kernel,
        info,
        [gs_low, gs_low2, slope0, slope1, whole(up_weight), whole(down_weight), *halves],
        [SDS((2, 2, n, units), bf16), part, SDS((n, d), bf16), SDS((8, d), f32)],
        [sides, *both],
        vmem=NEAR,
    )
    got = swap(sib, "tensor", 1)
    block = units // parts
    downs = call(
        "down_grads",
        down_grads_kernel,
        info,
        [act0, act1, gs_low, gs_low2],
        [[SDS((parts // 2, block, d), bf16)]] * 4,
        [pltpu.VMEM((2, parts // 2, block, d), bf16)],
        vmem=NEAR,
        parts=parts,
    )
    down_far_keep, down_far_send, down_keep, down_send = downs
    down_far_got = swap(down_far_send, "dp", 1)
    gfi, g0, g1, g2, g3, okeep, osend, small1 = call(
        "first_back",
        first_back_kernel,
        info,
        [par, nv1, r1, own, got, gsec, small2, *far_ctx, *far_packs],
        [
            [part],
            *[[SDS((batch, width, rows), bf16)]] * 4,
            *[[SDS((2, width + 8, d), bf16)]] * 2,
            SDS((8, d), f32),
        ],
        [pltpu.VMEM((n, d), bf16)],
        vmem=NEAR,
    )
    gctx = [g0] + [swap(g, "tensor", j) for j, g in ((1, g1), (2, g2), (3, g3))]
    got_o = swap(osend, "tensor", 1)
    joint = block + width // parts
    cut = parts // 2 * joint
    up_far_keep, up_far_send, up_keep, up_send, small = call(
        "up_grads",
        up_grads_kernel,
        info,
        [low, low2, gh, whole(okeep), loose(got_o), small1, ub],
        [
            [SDS((cut, d), bf16)],
            [SDS((cut + 16, d), bf16)],
            [SDS((cut, d), bf16)],
            [SDS((cut, d), bf16)],
            SDS((8, d), f32),
        ],
        [pltpu.VMEM((2, parts // 2, joint, d), bf16)],
        vmem=NEAR,
        parts=parts,
        width=width,
    )
    *gctx, up_far_send = after(*gctx, up_far_send)
    down_far_sum = summed([down_far_keep, down_far_got]).astype(bf16)
    *gctx, down_far_sum, up_far_keep = after(*gctx, down_far_sum, up_far_keep)
    up_far_got = swap(up_far_send, "dp", 2)
    down_y = swap(down_far_sum, "tensor", 2)
    down_got = swap(down_send, "dp", 1)
    lows, biases, terms_of = [], [], []
    for s in range(batch):
        keep, send, low_grads, db = attend_bwd(s, info, w_t, *saved, gctx, d)
        if s == 0:
            send, up_far_got, down_y, down_got = after(send, up_far_got, down_y, down_got)
        else:
            send, low_grads, up_got, up_more, far = after(send, low_grads, up_got, up_more, far)
            terms_of[0].append(far)
        near = swap(send, "tensor", 1)
        in_sum = summed([keep[1], near[1]]).astype(bf16)
        terms_of.append([keep[0], near[0]])
        lows.append(low_grads)
        biases.append(db)
        if s:
            continue
        shape = ([2] * (bits - 1)) + [block, d]
        down_terms = [x.reshape(shape) for x in (down_keep, down_got, down_y)]
        down_kept, down_next = halve_sum(down_terms, bits - 2, bit_of[1])
        shape = ([2] * (bits - 1)) + [joint, d]
        small = small + pair_sum(up_far_got, cut, 8)
        terms = [x.reshape(shape) for x in (up_far_keep, up_far_got[:cut])]
        up_far_kept, up_far_next = halve_sum(terms, bits - 2, bit_of[0])
        up_far_rows = with_rows(up_far_next, small)
        tied = after(down_next, up_far_rows, in_sum, up_send, *gctx)
        (down_next, up_far_rows, in_sum, up_send), gctx = tied[:4], tied[4:]
        up_got = swap(up_send, "dp", 2)
        down_more = swap(down_next, "dp", 2)
        up_more = swap(up_far_rows, "dp", 1)
        far = swap(in_sum, "tensor", 2)
    terms_of[1].append(swap(in_sum, "tensor", 2))
    first_terms, last_terms = terms_of
    m = 3 * d // 4
    w_keep, w_send, db = call(
        "project_grads",
        project_grads_kernel,
        info,
        [whole(inputs), *[whole(a) for a in lows], *biases],
        [[SDS((m, 2 * width), bf16)], [SDS((m + 8, 2 * width), bf16)], SDS((1, 2 * width), f32)],
        [pltpu.VMEM((3, d, width), f32)],
        parts=parts,
    )
    w_send, down_more = after(w_send, down_more)
    down_terms = down_kept + [down_more]
    order = [1, 0] + list(range(2, bits))
    row = 3 * (d // parts) // 2
    got = swap(w_send, "dp", 2)
    got, in_sum = after(got, in_sum)
    got, up_got, up_more, *down_terms = after(got, up_got, up_more, *down_terms)
    at = up_far_next.size // d
    up_far_terms = up_far_kept + [up_more[:at].reshape(up_far_next.shape)]
    small_x = pair_sum(up_more, at, 8)
    small = small + small_x
    small = jnp.concatenate([small[0:6], small[7:8], small[6:7]])
    send = summed(up_far_terms).astype(bf16)
    up_y_sent = with_rows(send, small)
    up_y = swap(up_y_sent, "tensor", 2)
    at = send.size // d
    small = jnp.concatenate([small[0:6], small[7:8], small[7:8]]) + pair_sum(up_y, at, 8)
    shape = ([2] * (bits - 1)) + [joint, d]
    terms, up_next = halve([x.reshape(shape) for x in (up_keep, up_got)], bits - 2, 1, bit_of[0])
    terms.append(up_y[:at].reshape(send.shape))
    for i in range(2, bits):
        terms, sent, more = halve_with(terms, terms[0].ndim - 3, small, "dp", 1 << i, bit_of[i])
        small = small + more
    up_sum = summed(terms)
    mine = small
    for i in range(2, bits):
        down_terms, sent = halve(down_terms, bits - 1 - i, 1 << i, bit_of[i])
    down_sum = summed(down_terms)
    at = parts // 2 * row
    shape = ([2] * (bits - 1)) + [row, 2 * width]
    terms = [x.reshape(shape) for x in (w_keep, got[:at])]
    db = db + got[at : at + 1].astype(f32) + got[at + 1 : at + 2].astype(f32)
    for i in order[1:]:
        kept, sent, more = halve_with(terms, terms[0].ndim - 3, db, "dp", 1 << i, bit_of[i])
        terms, db = kept, db + more
    qkv_sum = summed(terms)
    qkv_sum = jnp.concatenate([qkv_sum[:, :width], qkv_sum[:, width:]], axis=0).reshape(3, -1, width)
    qkv_sum = jnp.transpose(qkv_sum, (1, 0, 2))
    db = db.reshape(2, width)
    input_list = [
        (summed(x) + gfi[s * rows : (s + 1) * rows]).astype(bf16)
        for s, x in enumerate((first_terms, last_terms))
    ]
    return (
        outputs,
        jnp.stack(input_list, 0),
        qkv_sum,
        db,
        up_sum[block:],
        mine[0],
        mine[1],
        mine[2],
        up_sum[:block],
        mine[6],
        down_sum,
        mine[3],
        mine[4],
        mine[5],
    )


def pair_sum(array, at, n):
    return array[at : at + n].astype(f32) + array[at + n : at + 2 * n].astype(f32)


def with_rows(array, rows):
    flat = array.reshape(-1, array.shape[-1])
    high = rows.astype(bf16)
    low = (rows - high.astype(f32)).astype(bf16)
    return jnp.concatenate([flat, high, low], axis=0)


def halve_with(terms, axis, rows, name, bit, mine):
    other = [lax.dynamic_index_in_dim(t, 1 - mine, axis, keepdims=False) for t in terms]
    kept = [lax.dynamic_index_in_dim(t, mine, axis, keepdims=False) for t in terms]
    other = summed(other).astype(bf16)
    sent = with_rows(other, rows)
    got = swap(sent, name, bit)
    cut = other.size // other.shape[-1]
    return kept + [got[:cut].reshape(other.shape)], sent, pair_sum(got, cut, rows.shape[0])


def after(*values):
    return lax.optimization_barrier(values)


def solution(mesh):
    in_specs = (
        P("dp", None, None),
        P("dp", "tensor", None),
        P("dp"),
        P(None, None, "tensor"),
        P(None, "tensor"),
        P("tensor", None),
        P(),
        P(),
        P(),
        P(None, "tensor"),
        P("tensor"),
        P("tensor", None),
        P(),
        P(),
        P(),
    )
    out_specs = (
        P("dp", "tensor", None),
        P("dp", "tensor", None),
        P("dp", None, "tensor"),
        P(None, "tensor"),
        P(("tensor", "dp"), None),
        P(),
        P(),
        P(),
        P("dp", "tensor"),
        P("tensor"),
        P(("tensor", "dp"), None),
        P(),
        P(),
        P(),
    )
    return jax.shard_map(body, mesh=mesh, in_specs=in_specs, out_specs=out_specs, check_vma=False)
```

```python
import functools

import jax
import jax.numpy as jnp
from jax import lax
from jax.experimental import pallas as pl
from jax.experimental.pallas import tpu as pltpu
from jax.sharding import PartitionSpec as P

HEAD = 64
WIDE, LANES = 192, 256
NEAR = 30
NT = (((1,), (1,)), ((), ()))
NN = (((1,), (0,)), ((), ()))
TN = (((0,), (0,)), ((), ()))
bf16 = jnp.bfloat16
f32 = jnp.float32
VM = pl.BlockSpec(memory_space=pltpu.VMEM)
SDS = jax.ShapeDtypeStruct


def mm(a, b, dims=NN):
    return lax.dot_general(a, b, dims, preferred_element_type=f32)


class Fetch:
    def __init__(self, src, dst, sem):
        self.dst, self.copy = dst, pltpu.make_async_copy(src, dst, sem)
        self.copy.start()
        self.waiting = True

    def __call__(self):
        if self.waiting:
            self.copy.wait()
            self.waiting = False
        return self.dst


class Flush:
    def __init__(self, src, dst, sem):
        self.src, self.copy = src, pltpu.make_async_copy(src, dst, sem)
        self.started = False

    def start(self):
        if not self.started:
            self.copy.start()
        self.started = True


def call(name, body, info, ins, outs, scratch=(), vmem=58, which=0, **static):
    far_in = [i for i, a in enumerate(ins) if isinstance(a, tuple)]
    pinned = [i for i in far_in if len(ins[i]) == 2]
    far_out = [i for i, o in enumerate(outs) if isinstance(o, list)]
    raw_in = [i for i, a in enumerate(ins) if isinstance(a, Raw)]
    raw_out = [i for i, o in enumerate(outs) if isinstance(o, Raw)]
    pinned += raw_in
    arrays = [a[0] if isinstance(a, tuple) else a.value if isinstance(a, Raw) else a for a in ins]
    shapes = [o[0] if isinstance(o, list) else o.value if isinstance(o, Raw) else o for o in outs]
    picked = [a[1] if isinstance(a, tuple) else None for a in ins]
    n_in, n_out = len(ins), len(outs)

    def kernel(lengths_ref, which_ref, *refs):
        dp = lax.axis_index("dp")
        at = which_ref[0]
        info_ref = (lengths_ref[0], lengths_ref[1], lax.axis_index("tensor"), dp & 1, (dp >> 1) & 1, at, lengths_ref[at], lengths_ref)
        in_refs, refs = refs[:n_in], refs[n_in:]
        out_refs, refs = refs[:n_out], refs[n_out:]
        sem, refs = refs[-1], refs[:-1]
        buffers, rest = refs[: len(far_in) + len(far_out)], refs[len(far_in) + len(far_out) :]
        args = list(in_refs)
        for j, i in enumerate(far_in):
            view = picked[i][1]
            args[i] = Fetch(view(in_refs[i], info_ref), buffers[j], sem.at[j])
        results = list(out_refs)
        flushes = []
        for j, i in enumerate(far_out):
            at = len(far_in) + j
            results[i] = Flush(buffers[at], out_refs[i], sem.at[at])
            flushes.append(results[i])
        body(info_ref, *args, *results, *rest, **static)
        for i in far_in:
            args[i]()
        for f in flushes:
            f.start()
        for f in flushes:
            f.copy.wait()

    hbm = pl.BlockSpec(memory_space=pltpu.HBM)
    buffers = [pltpu.VMEM(picked[i][0], arrays[i].dtype) for i in far_in]
    buffers += [pltpu.VMEM(shapes[i].shape, shapes[i].dtype) for i in far_out]
    return pl.pallas_call(
        kernel,
        out_shape=[pltpu.HBM(o.shape, o.dtype) if i in far_out + raw_out else o for i, o in enumerate(shapes)],
        grid_spec=pltpu.PrefetchScalarGridSpec(
            num_scalar_prefetch=2,
            grid=(1,),
            in_specs=[hbm if i in pinned else pl.BlockSpec(memory_space=pl.ANY) if i in far_in else VM for i in range(n_in)],
            out_specs=[hbm if i in far_out + raw_out else VM for i in range(n_out)],
            scratch_shapes=[*buffers, *scratch, pltpu.SemaphoreType.DMA((max(1, len(far_in) + len(far_out)),))],
        ),
        compiler_params=pltpu.CompilerParams(vmem_limit_bytes=vmem << 20),
        cost_estimate=pl.CostEstimate(flops=1000, bytes_accessed=1000, transcendentals=0),
        name=name,
    )(info, jnp.full((1,), which, jnp.int32), *[pltpu.with_memory_space_constraint(a, pltpu.HBM) if i in pinned else a for i, a in enumerate(arrays)])


class Raw:
    def __init__(self, value):
        self.value = value


def ref(x):
    return x() if isinstance(x, Fetch) else x.src if isinstance(x, Flush) else x


def whole(a):
    return (a, (a.shape, lambda ref, info: ref))


def loose(a):
    return (*whole(a), None)


def prepare_kernel(info, out_in, bias, up_in, dn_in, pack, up_half, dn_half):
    for src, dst in ((up_in, up_half), (dn_in, dn_half)):
        dst.src[...] = src()[...]
        dst.start()
    out_w = out_in()
    width, d = out_w.shape
    pack.src[0:width, :] = out_w[...]
    pack.src[width : width + 8, :] = jnp.broadcast_to(bias[...], (8, d))


def prepare(info, out_w, bias, up, dn):
    width, d = out_w.shape
    half = up.shape[0] // 2
    view = lambda ref, info: ref.at[pl.ds(pl.multiple_of(info[3] * half, half), half)]
    view2 = lambda ref, info: ref.at[pl.ds(pl.multiple_of(info[4] * half, half), half)]
    ins = [whole(out_w), bias, (up, ((half, d), view)), (dn, ((half, d), view2))]
    return call("prepare", prepare_kernel, info, ins, [[SDS((width + 8, d), bf16)]] + [[SDS((half, d), bf16)]] * 2)


def head_cols(a, h, extra=()):
    lane = lax.broadcasted_iota(jnp.int32, a.shape, 1)
    out = jnp.where((lane >= HEAD * h) & (lane < HEAD * (h + 1)), a, jnp.zeros_like(a))
    for i, e in enumerate(extra):
        out = jnp.where(lane == WIDE + i, e, out)
    return out


def tail_cols(rows, values):
    lane = lax.broadcasted_iota(jnp.int32, (rows, LANES - WIDE), 1)
    out = jnp.zeros((rows, LANES - WIDE), f32)
    for i, v in enumerate(values):
        out = jnp.where(lane == i, v, out)
    return out.astype(bf16)


def attend_fwd_kernel(info, x_hbm, w_ref, b_ref, *rest):
    far, outs = rest[:5], rest[5:9]
    x_all, *near, v_t, s_all, sem_in, sem_out = rest[9:]
    q_all, k_all, v_all, lse_all, c_all = near
    me = info[2]
    batch, peers, width, block = c_all.shape
    seq = peers * block
    heads = width // HEAD

    def fetch(s):
        return pltpu.make_async_copy(x_hbm.at[s], x_all.at[s], sem_in.at[s])

    def flush(s, i):
        return pltpu.make_async_copy(near[i].at[s], far[i].at[s], sem_out.at[s, i])

    for s in range(batch):
        fetch(s).start()
    w = w_ref()

    def one_sequence(s, carry):
        length = info[7][s]
        fetch(s).wait()
        x = x_all[s]
        k_all[s, :, 0:WIDE] = mm(x, w[1], NT).astype(bf16)
        row = lax.broadcasted_iota(jnp.int32, (seq, 1), 0)
        k_all[s, :, WIDE:LANES] = tail_cols(seq, (jnp.where(row < length, 0.0, -1e30),))
        q = mm(x, w[0], NT) + b_ref[0:1, :].astype(f32)
        q_all[s, :, 0:WIDE] = q.astype(bf16) * jnp.asarray(0.125, bf16)
        q_all[s, :, WIDE:LANES] = tail_cols(seq, (1.0,))
        v = (mm(x, w[2], NT) + b_ref[1:2, :].astype(f32)).astype(bf16)
        v_all[s] = v
        v_t[...] = v.T
        for i in range(3):
            flush(s, i).start()

        def two_blocks(n, carry):
            qb = q_all[s, pl.ds(pl.multiple_of(n * 2 * block, 2 * block), 2 * block), :]
            one = jnp.ones_like(qb[:, 0:1])
            for h in range(heads):
                s_all[h] = mm(k_all[s], head_cols(qb, h, (one,)), NT)
            for h in range(heads):
                top = jnp.max(s_all[h], axis=0, keepdims=True)
                p = jnp.exp(s_all[h] - top)
                total = jnp.sum(p, axis=0, keepdims=True)
                rows = slice(HEAD * h, HEAD * (h + 1))
                out = (mm(v_t[rows, :], p.astype(bf16)) * (1.0 / total)).astype(bf16)
                lse = top + jnp.log(total)
                for j in range(2):
                    cols = slice(block * j, block * (j + 1))
                    c_all[s, 2 * n + j, rows, :] = out[:, cols]
                    lse_all[s, 2 * n + j, h : h + 1, :] = lse[:, cols]
            return carry

        lax.fori_loop(0, peers // 2, two_blocks, 0)
        for i in range(3, 5):
            flush(s, i).start()
        for k, out in enumerate(outs):
            out.src[s] = c_all[s, me ^ k]
        return carry

    lax.fori_loop(0, batch, one_sequence, 0)
    for out in outs:
        out.start()
    for s in range(batch):
        for i in range(5):
            flush(s, i).wait()


def attend_fwd(info, inputs, w_t, bias, peers):
    batch, seq, d = inputs.shape
    width = w_t.shape[1]
    block = seq // peers
    far = [SDS((batch, seq, LANES), bf16)] * 2 + [SDS((batch, seq, width), bf16)]
    far += [SDS((batch, peers, 8, block), f32), SDS((batch, peers, width, block), bf16)]
    scratch = [pltpu.VMEM(inputs.shape, bf16), *[pltpu.VMEM(o.shape, o.dtype) for o in far]]
    scratch += [pltpu.VMEM((width, seq), bf16), pltpu.VMEM((width // HEAD, seq, 2 * block), f32)]
    scratch += [pltpu.SemaphoreType.DMA((batch,)), pltpu.SemaphoreType.DMA((batch, 5))]
    return call(
        "attend_fwd",
        attend_fwd_kernel,
        info,
        [Raw(inputs), whole(w_t), bias],
        [Raw(o) for o in far] + [[SDS((batch, width, block), bf16)]] * peers,
        scratch,
    )


def of_sequence(a):
    return (a, (a.shape[1:], lambda ref, info: ref.at[info[5]]))


def attend_bwd_kernel(info, x_ref, q_in, k_in, v_in, lse_in, c_in, *rest):
    w_ref = x_ref
    peers = 4
    gs, rest = rest[:peers], rest[peers:]
    keep, send, low_out, db_ref, dq_t, dk, dv, k_t, g_ref = rest
    low = low_out.src
    length = info[6]
    me = info[2]
    k_ref, q_ref, v_ref = k_in(), q_in(), v_in()
    lse_ref, c_ref = lse_in(), c_in()
    _, width, block = c_ref.shape
    heads = width // HEAD
    k_t[...] = k_ref[:, 0:WIDE].T
    dk[...] = jnp.zeros_like(dk)
    dv[...] = jnp.zeros_like(dv)
    for k in range(peers):
        g_ref[me ^ k] = gs[k]()[...]

    def one_block(s, carry):
        at = pl.multiple_of(s * block, block)

        @pl.when(at >= length)
        def _():
            dq_t[:, pl.ds(at, block)] = jnp.zeros((width, block), f32)

        @pl.when(at < length)
        def _():
            qb = q_ref[pl.ds(at, block), :]
            g_t = g_ref[s]
            g = g_t.T
            prod_t = g_t.astype(f32) * c_ref[s].astype(f32)
            for h in range(heads):
                rows = slice(HEAD * h, HEAD * (h + 1))
                qh = head_cols(qb, h)
                gh = head_cols(g, h)
                scores = mm(k_ref[...], qh, NT)
                row = lax.broadcasted_iota(jnp.int32, scores.shape, 0)
                p = jnp.where(row < length, jnp.exp(scores - lse_ref[s, h : h + 1, :]), 0.0)
                dp = mm(v_ref[...], gh, NT)
                inner = jnp.sum(prod_t[rows], axis=0, keepdims=True)
                ds = (p * (dp - inner)).astype(bf16)
                dv[...] += mm(p.astype(bf16), gh)
                dk[...] += mm(ds, qh)
                dq_t[rows, pl.ds(at, block)] = mm(k_t[rows, :], ds) * 0.125

        return carry

    lax.fori_loop(0, peers, one_block, 0)
    low[0] = dq_t[...].T.astype(bf16)
    low[1] = dk[:, 0:WIDE].astype(bf16)
    low[2] = dv[...].astype(bf16)
    w = w_ref()
    for s in range(peers):
        at = pl.multiple_of((me ^ s) * block, block)
        total = sum(mm(low[i, pl.ds(at, block), :], w[i]) for i in range(3))
        (send if s % 2 else keep).src[s // 2] = total.astype(bf16)
    send.start()
    keep.start()
    db_ref[...] = jnp.concatenate([rowsum(low[i].astype(f32)) for i in (0, 2)], axis=1)


def attend_bwd(which, info, w_t, q, k, v, lse, c, gs, d):
    _, peers, width, block = c.shape
    seq = peers * block
    outs = [[SDS((2, block, d), bf16)]] * 2 + [[SDS((3, seq, width), bf16)], SDS((1, 2 * width), f32)]
    scratch = [
        pltpu.VMEM((width, seq), f32),
        pltpu.VMEM((seq, LANES), f32),
        pltpu.VMEM((seq, width), f32),
        pltpu.VMEM((width, seq), bf16),
        pltpu.VMEM((peers, width, block), bf16),
    ]
    ins = [whole(w_t)] + [of_sequence(a) for a in (q, k, v, lse, c)]
    ins += [(g, ((width, block), lambda ref, info: ref.at[info[5]]), None) for g in gs]
    return call("attend_bwd", attend_bwd_kernel, info, ins, outs, scratch, which=which)


def project_grads_kernel(info, x_in, low0, low1, db0, db1, keep, send, db_ref, dw, pair, *, parts):
    x = x_in()
    lows = (low0(), low1())
    _, d, width = dw.shape
    step = 256

    def chunk(m, carry):
        cols = pl.ds(pl.multiple_of(m * step, step), step)
        x_t = (x[0, :, cols].T, x[1, :, cols].T)
        for i in range(3):
            dw[i, cols, :] = mm(x_t[0], lows[0][i]) + mm(x_t[1], lows[1][i])
        return carry

    lax.fori_loop(0, d // step, chunk, 0)
    rows = d // parts
    half = 3 * rows // 2
    for b in range(parts):
        flat = dw[:, b * rows : (b + 1) * rows, :].reshape(3 * rows, width)
        flat = jnp.concatenate([flat[0:half], flat[half : 2 * half]], axis=1).astype(bf16)
        pair[(b & 1) ^ info[3], (b >> 1) * half : (b // 2 + 1) * half, :] = flat
    n = keep.src.shape[0]
    send.src[0:n, :] = pair[1]
    keep.src[...] = pair[0]
    db = db0[...] + db1[...]
    db_ref[...] = db
    high = db.astype(bf16)
    send.src[n : n + 8, :] = jnp.concatenate(
        [high, (db - high.astype(f32)).astype(bf16), jnp.zeros((6, 2 * width), bf16)], axis=0
    )
    send.start()


def gelu_parts(h):
    t = 1.0 / (1.0 + (0.3275911 * 0.7071067811865476) * jnp.abs(h))
    poly = t * (0.127414796 + t * (-0.142248368 + t * (0.7107068705 + t * (-0.7265760135 + t * 0.5307027145))))
    bell = jnp.exp2((-0.5 * 1.4426950408889634) * (h * h))
    tail = poly * bell
    cum = jnp.where(h < 0, tail, 1.0 - tail)
    return h * cum, cum + h * (bell * 0.3989422804014327)


def norm_parts(v):
    center = v - jnp.mean(v, axis=1, keepdims=True)
    r = lax.rsqrt(jnp.mean(center * center, axis=1, keepdims=True) + 1e-12)
    return center * r, r


def norm_back(u, gain, nv, r):
    gu = u * gain
    return r * (gu - jnp.mean(gu, axis=1, keepdims=True) - nv * jnp.mean(gu * nv, axis=1, keepdims=True))


def rowsum(v):
    return jnp.sum(v, axis=0, keepdims=True)


def first_norm_kernel(info, x_in, par, *rest):
    nv_ref, r_ref, low = rest[8:]
    cs, packs = [c() for c in rest[:4]], [p() for p in rest[4:8]]
    x_ref = x_in()
    batch, rows = x_ref.shape[:2]
    width = cs[0].shape[1]

    def one_sequence(s, carry):
        here = pl.ds(pl.multiple_of(s * rows, rows), rows)
        total = par[0:1, :] + x_ref[s].astype(f32)
        for k in range(4):
            total = total + mm(cs[k][s], packs[k][0:width, :], TN)
        nv, r = norm_parts(total)
        nv_ref[here, :] = nv
        r_ref[here, :] = r
        low[here, :] = (nv * par[1:2, :] + par[2:3, :]).astype(bf16)
        return carry

    lax.fori_loop(0, batch, one_sequence, 0)


def feed_kernel(info, low, low2, pack, *rest, width, far):
    if far:
        u_a, u_b, d_a, d_b, p_own, p_sib, act_out, slope_out, own, sib, both, up, dn = rest
        half = u_a.dst.shape[0]
        assemble(info[3], up, u_a(), u_b(), half)
    else:
        u_in, d_in, act_out, slope_out, own, sib, both = rest
        up = u_in()
    act, slope = ref(act_out), ref(slope_out)
    units = up.shape[1]
    bias = pack()
    step = 256
    both[0] = low[...]
    both[1] = low2[...]

    def side(j, carry):
        def chunk(n, carry):
            cols = pl.ds(pl.multiple_of(n * step, step), step)
            hidden = mm(both[j], up[:, cols]) + bias[width : width + 1, cols].astype(f32)
            a, g = gelu_parts(hidden)
            act[j, :, cols] = a.astype(bf16)
            slope[j, :, cols] = g.astype(bf16)
            return carry

        return lax.fori_loop(0, units // step, chunk, carry)

    lax.fori_loop(0, 2, side, 0)
    if far:
        assemble(info[4], dn, d_a(), d_b(), half)
        sib[...] = (p_sib[...] + mm(act[1], dn[...])).astype(bf16)
        own[...] = p_own[...] + mm(act[0], dn[...])
    else:
        dn = d_in()
        own[...] = mm(act[0], dn[...])
        sib[...] = mm(act[1], dn[...])


def assemble(bit, dst, a, b, half):
    dst[pl.ds(pl.multiple_of(bit * half, half), half)] = a[...]
    dst[pl.ds(pl.multiple_of((1 - bit) * half, half), half)] = b[...]


def second_norm_kernel(info, cot_in, par, nv_in, own, got, outs, gsec_out, gs_low, small):
    cot, nv_ref, gsec = cot_in(), ref(nv_in), ref(gsec_out)
    batch, rows, d = cot.shape

    def one_sequence(s, sums):
        here = pl.ds(pl.multiple_of(s * rows, rows), rows)
        total = own[here, :] + got[here, :].astype(f32) + par[3:4, :] + (nv_ref[here, :] * par[1:2, :] + par[2:3, :])
        nv, r = norm_parts(total)
        outs.src[s] = (nv * par[4:5, :] + par[5:6, :]).astype(bf16)
        at = info[2] * rows + lax.broadcasted_iota(jnp.int32, (rows, 1), 0)
        seed = jnp.where(at < info[7][s], cot[s].astype(f32), 0.0)
        g = norm_back(seed, par[4:5, :], nv, r)
        gsec[here, :] = g
        gs_low[here, :] = g.astype(bf16)
        return tuple(a + rowsum(b) for a, b in zip(sums, (g, seed * nv, seed)))

    sums = lax.fori_loop(0, batch, one_sequence, (jnp.zeros((1, d), f32),) * 3)
    small[...] = jnp.concatenate([*sums, jnp.zeros((5, d), f32)], axis=0)


def feed_back_kernel(info, gs, gs2, slope0, slope1, up0, dn0, u_a, u_b, d_a, d_b, gh_out, own, sib, ub, sides, up2, dn2):
    gh = ref(gh_out)
    half = u_a.dst.shape[0]
    units = up0.dst.shape[1]
    ub[...] = jnp.zeros_like(ub)
    sides[0] = gs[...]
    sides[1] = gs2[...]
    step = 256
    for k, slope in enumerate((ref(slope0), ref(slope1))):
        if k:
            assemble(info[4], dn2, d_a(), d_b(), half)
            dn = dn2
        else:
            dn = dn0()

        def side(j, carry):
            def chunk(n, carry):
                cols = pl.ds(pl.multiple_of(n * step, step), step)
                ga = mm(sides[j], dn[cols, :], NT)
                h = (ga * slope[j, :, cols].astype(f32)).astype(bf16)
                gh[k, j, :, cols] = h
                ub[k : k + 1, cols] += rowsum(h.astype(f32))
                return carry

            return lax.fori_loop(0, units // step, chunk, carry)

        lax.fori_loop(0, 2, side, 0)
    assemble(info[3], up2, u_a(), u_b(), half)
    up = up0()
    sib[...] = (mm(gh[0, 1], up[...], NT) + mm(gh[1, 1], up2[...], NT)).astype(bf16)
    own[...] = mm(gh[0, 0], up[...], NT) + mm(gh[1, 0], up2[...], NT)


def first_back_kernel(info, par, nv_in, r_ref, own, got, gsec_in, small2, *rest):
    cs, packs = [c() for c in rest[:4]], rest[4:8]
    gfi, g0, g1, g2, g3, okeep, osend, small, ga_low = rest[8:]
    nv_ref, gsec = ref(nv_in), ref(gsec_in)
    packs = [p() for p in packs]
    n, d = own.shape
    rows = n // 2
    width = cs[0].shape[1]

    def one_sequence(s, sums):
        here = pl.ds(pl.multiple_of(s * rows, rows), rows)
        u = own[here, :] + got[here, :].astype(f32) + gsec[here, :]
        nv = nv_ref[here, :]
        g = norm_back(u, par[1:2, :], nv, r_ref[here, :])
        gfi.src[here, :] = g
        low = g.astype(bf16)
        ga_low[here, :] = low
        for k, out in enumerate((g0, g1, g2, g3)):
            out.src[s] = mm(packs[k][0:width, :], low, NT).astype(bf16)
        return tuple(a + rowsum(b) for a, b in zip(sums, (g, u * nv, u)))

    sums = lax.fori_loop(0, 2, one_sequence, (jnp.zeros((1, d), f32),) * 3)
    for out in (g3, g2, g1, g0, gfi):
        out.start()
    for k in range(4):
        total = mm(cs[k][0], ga_low[0:rows, :]) + mm(cs[k][1], ga_low[rows:n, :])
        (osend if k % 2 else okeep).src[k // 2, 0:width, :] = total.astype(bf16)
    both = jnp.concatenate([*sums, small2[0:3, :], jnp.zeros((2, d), f32)], axis=0)
    small[...] = both
    high = both.astype(bf16)
    osend.src[0, width : width + 8, :] = high
    osend.src[1, width : width + 8, :] = (both - high.astype(f32)).astype(bf16)


def down_grads_kernel(info, act0, act1, gs, gs2, far_keep, keep, send, scr, *, parts):
    units = act0.shape[2]
    block = units // parts
    step = 384
    for k, (act, mine) in enumerate(((act1, far_keep), (act0, keep))):

        def chunk(m, carry):
            cols = pl.ds(pl.multiple_of(m * step, step), step)
            total = mm(act[0, :, cols], gs[...], TN) + mm(act[1, :, cols], gs2[...], TN)
            total = total.astype(bf16)
            for i in range(step // block):
                scr[(i & 1) ^ info[3], m * (step // block // 2) + (i >> 1)] = total[i * block : (i + 1) * block]
            return carry

        lax.fori_loop(0, units // step, chunk, 0)
        send.src[k] = scr[1]
        mine.src[...] = scr[0]
    send.start()


def up_grads_kernel(
    info, low, low2, gh_in, okeep, ogot, small, ub, far_keep, far_send, keep, send, sums, scr, *, parts, width
):
    gh = ref(gh_in)
    units = low.shape[1]
    block = units // parts
    extra = width // parts
    joint = block + extra
    n = parts // 2 * joint
    step = 384
    got = ogot()
    both = small[...] + got[0, width : width + 8, :].astype(f32) + got[1, width : width + 8, :].astype(f32)
    both = jnp.concatenate([both[0:6], ub[0:2, :]], axis=0)
    sums[...] = both
    high = both.astype(bf16)
    far_send.src[n : n + 8, :] = high
    far_send.src[n + 8 : n + 16, :] = (both - high.astype(f32)).astype(bf16)
    for k, mine, theirs in ((1, far_keep, far_send), (0, keep, send)):

        def chunk(m, carry):
            cols = pl.ds(pl.multiple_of(m * step, step), step)
            total = mm(low[:, cols], gh[k, 0], TN) + mm(low2[:, cols], gh[k, 1], TN)
            total = total.astype(bf16)
            for i in range(step // block):
                at = (m * (step // block // 4) + (i >> 2)) * 2 + (i & 1)
                scr[((i >> 1) & 1) ^ info[4], at, 0:block, :] = total[i * block : (i + 1) * block]
            return carry

        lax.fori_loop(0, units // step, chunk, 0)
        o = (okeep()[k, 0:width, :].astype(f32) + got[k, 0:width, :].astype(f32)).astype(bf16)
        for b in range(parts):
            at = (b >> 2) * 2 + (b & 1)
            scr[((b >> 1) & 1) ^ info[4], at, block:joint, :] = o[b * extra : (b + 1) * extra]
        for b in range(parts // 2):
            theirs.src[b * joint : (b + 1) * joint, :] = scr[1, b]
            mine.src[b * joint : (b + 1) * joint, :] = scr[0, b]
        theirs.start()
        mine.start()


def swap(x, axis, bit):
    size = lax.axis_size(axis)
    return lax.ppermute(x, axis, [(i, i ^ bit) for i in range(size)])


def summed(parts):
    return sum(p.astype(f32) for p in parts)


def spread(array, axis, parts):
    bits = parts.bit_length() - 1
    return array.reshape(*array.shape[:axis], *([2] * bits), array.shape[axis] // parts, *array.shape[axis + 1 :])


def halve_sum(terms, axis, mine):
    other = [lax.dynamic_index_in_dim(t, 1 - mine, axis, keepdims=False) for t in terms]
    kept = [lax.dynamic_index_in_dim(t, mine, axis, keepdims=False) for t in terms]
    return kept, summed(other).astype(bf16)


def halve(terms, axis, bit, mine):
    other = [lax.dynamic_index_in_dim(t, 1 - mine, axis, keepdims=False) for t in terms]
    kept = [lax.dynamic_index_in_dim(t, mine, axis, keepdims=False) for t in terms]
    other = summed(other).astype(bf16)
    return kept + [swap(other, "dp", bit)], other


def body(
    inputs,
    cotangent,
    lengths,
    qkv_weight,
    qkv_bias,
    out_weight,
    out_bias,
    first_gain,
    first_shift,
    up_weight,
    up_bias,
    down_weight,
    down_bias,
    second_gain,
    second_shift,
):
    batch, seq, d = inputs.shape
    rows = cotangent.shape[1]
    n = batch * rows
    width = out_weight.shape[0]
    units = up_weight.shape[1]
    peers = lax.axis_size("tensor")
    parts = lax.axis_size("dp")
    bits = parts.bit_length() - 1
    t = lax.axis_index("tensor")
    dp = lax.axis_index("dp")
    bit_of = [(dp >> i) & 1 for i in range(bits)]
    info = lengths
    par = jnp.concatenate([out_bias, first_gain, first_shift, down_bias, second_gain, second_shift])
    par = par.reshape(6, d).astype(f32)
    w_t = jnp.transpose(qkv_weight, (1, 2, 0))
    pack, up_half, dn_half = prepare(info, out_weight, up_bias[None], up_weight, down_weight)
    pack2 = swap(pack, "tensor", 2)
    pack1 = swap(pack, "tensor", 1)
    u2a = swap(up_half, "tensor", 2)
    q, k, v, lse, c, *cs = attend_fwd(info, inputs, w_t, qkv_bias, peers)
    saved = (q, k, v, lse, c)
    *cs, pack1, pack2, u2a = after(*cs, pack1, pack2, u2a)
    ctx = [cs[0]] + [swap(cs[j], "tensor", j) for j in range(1, peers)]
    pack3 = swap(pack2, "tensor", 1)
    *ctx, pack3, dn_half = after(*ctx, pack3, dn_half)
    d2a = swap(dn_half, "tensor", 2)
    packs = [pack, pack1, pack2, pack3]
    u2b = swap(u2a, "dp", 1)
    d2b = swap(d2a, "dp", 2)
    far_ctx = [whole(ctx[0])] + [loose(x) for x in ctx[1:]]
    far_packs = [whole(pack)] + [loose(p) for p in packs[1:]]
    share = (inputs, ((batch, rows, d), lambda ref, info: ref.at[:, pl.ds(pl.multiple_of(info[2] * rows, rows), rows), :]))
    nv1, r1, low = call(
        "first_norm",
        first_norm_kernel,
        info,
        [share, par, *far_ctx, *far_packs],
        [SDS((n, d), f32), SDS((n, 1), f32), SDS((n, d), bf16)],
        vmem=NEAR,
    )
    low2 = swap(low, "tensor", 1)
    pair = SDS((2, n, units), bf16)
    part = SDS((n, d), f32)
    sides = pltpu.VMEM((2, n, d), bf16)
    act0, slope0, own, sib = call(
        "feed",
        feed_kernel,
        info,
        [low, low2, far_packs[0], whole(up_weight), whole(down_weight)],
        [pair, pair, part, part],
        [sides],
        vmem=NEAR,
        width=width,
        far=False,
    )
    halves = [loose(x) for x in (u2a, u2b, d2a, d2b)]
    both = [pltpu.VMEM((d, units), bf16), pltpu.VMEM((units, d), bf16)]
    act1, slope1, own, sib = call(
        "feed",
        feed_kernel,
        info,
        [low, low2, far_packs[2], *halves, own, sib],
        [pair, pair, part, SDS((n, d), bf16)],
        [sides, *both],
        vmem=NEAR,
        width=width,
        far=True,
    )
    got = swap(sib, "tensor", 1)
    outputs, gsec, gs_low, small2 = call(
        "second_norm",
        second_norm_kernel,
        info,
        [whole(cotangent), par, nv1, own, got],
        [[SDS((batch, rows, d), bf16)], part, SDS((n, d), bf16), SDS((8, d), f32)],
        vmem=NEAR,
    )
    gs_low2 = swap(gs_low, "tensor", 1)
    gh, own, sib, ub = call(
        "feed_back",
        feed_back_kernel,
        info,
        [gs_low, gs_low2, slope0, slope1, whole(up_weight), whole(down_weight), *halves],
        [SDS((2, 2, n, units), bf16), part, SDS((n, d), bf16), SDS((8, d), f32)],
        [sides, *both],
        vmem=NEAR,
    )
    got = swap(sib, "tensor", 1)
    block = units // parts
    half_shape = (parts // 2, block, d)
    down_far_keep, down_keep, down_send = call(
        "down_grads",
        down_grads_kernel,
        info,
        [act0, act1, gs_low, gs_low2],
        [[SDS(half_shape, bf16)], [SDS(half_shape, bf16)], [SDS((2, *half_shape), bf16)]],
        [pltpu.VMEM((2, *half_shape), bf16)],
        vmem=NEAR,
        parts=parts,
    )
    down_got = swap(down_send, "dp", 1)
    gfi, g0, g1, g2, g3, okeep, osend, small1 = call(
        "first_back",
        first_back_kernel,
        info,
        [par, nv1, r1, own, got, gsec, small2, *far_ctx, *far_packs],
        [
            [part],
            *[[SDS((batch, width, rows), bf16)]] * 4,
            *[[SDS((2, width + 8, d), bf16)]] * 2,
            SDS((8, d), f32),
        ],
        [pltpu.VMEM((n, d), bf16)],
        vmem=NEAR,
    )
    gctx = [g0] + [swap(g, "tensor", j) for j, g in ((1, g1), (2, g2), (3, g3))]
    got_o = swap(osend, "tensor", 1)
    joint = block + width // parts
    cut = parts // 2 * joint
    up_far_keep, up_far_send, up_keep, up_send, small = call(
        "up_grads",
        up_grads_kernel,
        info,
        [low, low2, gh, whole(okeep), loose(got_o), small1, ub],
        [
            [SDS((cut, d), bf16)],
            [SDS((cut + 16, d), bf16)],
            [SDS((cut, d), bf16)],
            [SDS((cut, d), bf16)],
            SDS((8, d), f32),
        ],
        [pltpu.VMEM((2, parts // 2, joint, d), bf16)],
        vmem=NEAR,
        parts=parts,
        width=width,
    )
    *gctx, up_far_send = after(*gctx, up_far_send)
    up_far_got = swap(up_far_send, "dp", 2)
    *gctx, up_far_keep = after(*gctx, up_far_keep)
    lows, biases, terms_of = [], [], []
    for s in range(batch):
        keep, send, low_grads, db = attend_bwd(s, info, w_t, *saved, gctx, d)
        biases.append(db)
        if s == 0:
            send, up_far_got, down_got = after(send, up_far_got, down_got)
        else:
            send, low_grads, down_y, up_got, up_more, far = after(send, low_grads, down_y, up_got, up_more, far)
            terms_of[0].append(far)
        near = swap(send, "tensor", 1)
        in_sum = summed([keep[1], near[1]]).astype(bf16)
        terms_of.append([keep[0], near[0]])
        if s == 0:
            lows.append(low_grads)
            down_sum = summed([down_far_keep, down_got[0]]).astype(bf16)
            shape = ([2] * (bits - 1)) + [joint, d]
            small = small + pair_sum(up_far_got, cut, 8)
            terms = [x.reshape(shape) for x in (up_far_keep, up_far_got[:cut])]
            up_far_kept, up_far_next = halve_sum(terms, bits - 2, bit_of[0])
            up_far_rows = with_rows(up_far_next, small)
            tied = after(down_sum, up_far_rows, in_sum, up_send, *gctx)
            (down_sum, up_far_rows, in_sum, up_send), gctx = tied[:4], tied[4:]
            down_y = swap(down_sum, "tensor", 2)
            up_got = swap(up_send, "dp", 2)
            up_more = swap(up_far_rows, "dp", 1)
            far = swap(in_sum, "tensor", 2)
    shape = ([2] * (bits - 1)) + [block, d]
    down_terms = [x.reshape(shape) for x in (down_keep, down_got[1], down_y)]
    down_kept, down_next = halve_sum(down_terms, bits - 2, bit_of[1])
    at = up_far_next.size // d
    small = small + pair_sum(up_more, at, 8)
    small = jnp.concatenate([small[0:6], small[7:8], small[6:7]])
    up_y_next = summed(up_far_kept + [up_more[:at].reshape(up_far_next.shape)]).astype(bf16)
    up_y_rows = with_rows(up_y_next, small)
    shape = ([2] * (bits - 1)) + [joint, d]
    up_kept, up_next = halve_sum([x.reshape(shape) for x in (up_keep, up_got)], bits - 2, bit_of[0])
    low_grads, down_next, up_y_rows, up_next = after(low_grads, down_next, up_y_rows, up_next)
    lows.append(low_grads)
    down_more = swap(down_next, "dp", 2)
    up_y = swap(up_y_rows, "tensor", 2)
    up_more = swap(up_next, "dp", 1)
    m = 3 * d // 4
    w_keep, w_send, db = call(
        "project_grads",
        project_grads_kernel,
        info,
        [whole(inputs), *[whole(a) for a in lows], *biases],
        [[SDS((m, 2 * width), bf16)], [SDS((m + 8, 2 * width), bf16)], SDS((1, 2 * width), f32)],
        [pltpu.VMEM((3, d, width), f32), pltpu.VMEM((2, m, 2 * width), bf16)],
        parts=parts,
    )
    w_send, down_more, up_y, up_more = after(w_send, down_more, up_y, up_more)
    down_more, up_y, up_more, in_sum = after(down_more, up_y, up_more, in_sum)
    got = swap(w_send, "dp", 1)
    got, far = after(got, swap(in_sum, "tensor", 2))
    terms_of[1].append(far)
    down_terms = down_kept + [down_more]
    for i in range(2, bits):
        down_terms, sent = halve(down_terms, bits - 1 - i, 1 << i, bit_of[i])
    down_sum = summed(down_terms)
    at = up_y_next.size // d
    small = jnp.concatenate([small[0:6], small[7:8], small[7:8]]) + pair_sum(up_y, at, 8)
    terms = up_kept + [up_more, up_y[:at].reshape(up_y_next.shape)]
    for i in range(2, bits):
        terms, sent, more = halve_with(terms, terms[0].ndim - 3, small, "dp", 1 << i, bit_of[i])
        small = small + more
    up_sum = summed(terms)
    mine = small
    row = 3 * (d // parts) // 2
    at = parts // 2 * row
    shape = ([2] * (bits - 1)) + [row, 2 * width]
    terms = [x.reshape(shape) for x in (w_keep, got[:at])]
    db = db + got[at : at + 1].astype(f32) + got[at + 1 : at + 2].astype(f32)
    for i in range(1, bits):
        kept, sent, more = halve_with(terms, terms[0].ndim - 3, db, "dp", 1 << i, bit_of[i])
        terms, db = kept, db + more
    qkv_sum = summed(terms)
    qkv_sum = jnp.concatenate([qkv_sum[:, :width], qkv_sum[:, width:]], axis=0).reshape(3, -1, width)
    qkv_sum = jnp.transpose(qkv_sum, (1, 0, 2))
    db = db.reshape(2, width)
    input_list = [
        (summed(x) + gfi[s * rows : (s + 1) * rows]).astype(bf16)
        for s, x in enumerate(terms_of)
    ]
    return (
        outputs,
        jnp.stack(input_list, 0),
        qkv_sum,
        db,
        up_sum[block:],
        mine[0],
        mine[1],
        mine[2],
        up_sum[:block],
        mine[6],
        down_sum,
        mine[3],
        mine[4],
        mine[5],
    )


def pair_sum(array, at, n):
    return array[at : at + n].astype(f32) + array[at + n : at + 2 * n].astype(f32)


def with_rows(array, rows):
    flat = array.reshape(-1, array.shape[-1])
    high = rows.astype(bf16)
    low = (rows - high.astype(f32)).astype(bf16)
    return jnp.concatenate([flat, high, low], axis=0)


def halve_with(terms, axis, rows, name, bit, mine):
    other = [lax.dynamic_index_in_dim(t, 1 - mine, axis, keepdims=False) for t in terms]
    kept = [lax.dynamic_index_in_dim(t, mine, axis, keepdims=False) for t in terms]
    other = summed(other).astype(bf16)
    sent = with_rows(other, rows)
    got = swap(sent, name, bit)
    cut = other.size // other.shape[-1]
    return kept + [got[:cut].reshape(other.shape)], sent, pair_sum(got, cut, rows.shape[0])


def after(*values):
    return lax.optimization_barrier(values)


def solution(mesh):
    in_specs = (
        P("dp", None, None),
        P("dp", "tensor", None),
        P("dp"),
        P(None, None, "tensor"),
        P(None, "tensor"),
        P("tensor", None),
        P(),
        P(),
        P(),
        P(None, "tensor"),
        P("tensor"),
        P("tensor", None),
        P(),
        P(),
        P(),
    )
    out_specs = (
        P("dp", "tensor", None),
        P("dp", "tensor", None),
        P("dp", None, "tensor"),
        P(None, "tensor"),
        P(("tensor", "dp"), None),
        P(),
        P(),
        P(),
        P("dp", "tensor"),
        P("tensor"),
        P(("tensor", "dp"), None),
        P(),
        P(),
        P(),
    )
    return jax.shard_map(body, mesh=mesh, in_specs=in_specs, out_specs=out_specs, check_vma=False)
```

```python
import functools

import jax
import jax.numpy as jnp
from jax import lax
from jax.experimental import pallas as pl
from jax.experimental.pallas import tpu as pltpu
from jax.sharding import PartitionSpec as P

HEAD = 64
WIDE, LANES = 192, 256
NEAR = 30
NT = (((1,), (1,)), ((), ()))
NN = (((1,), (0,)), ((), ()))
TN = (((0,), (0,)), ((), ()))
bf16 = jnp.bfloat16
f32 = jnp.float32
VM = pl.BlockSpec(memory_space=pltpu.VMEM)
SDS = jax.ShapeDtypeStruct


def mm(a, b, dims=NN):
    return lax.dot_general(a, b, dims, preferred_element_type=f32)


class Fetch:
    def __init__(self, src, dst, sem):
        self.dst, self.copy = dst, pltpu.make_async_copy(src, dst, sem)
        self.copy.start()
        self.waiting = True

    def __call__(self):
        if self.waiting:
            self.copy.wait()
            self.waiting = False
        return self.dst


class Flush:
    def __init__(self, src, dst, sem):
        self.src, self.copy = src, pltpu.make_async_copy(src, dst, sem)
        self.started = False

    def start(self):
        if not self.started:
            self.copy.start()
        self.started = True


def call(name, body, info, ins, outs, scratch=(), vmem=58, which=0, cost=1000, **static):
    far_in = [i for i, a in enumerate(ins) if isinstance(a, tuple)]
    pinned = [i for i in far_in if len(ins[i]) == 2]
    far_out = [i for i, o in enumerate(outs) if isinstance(o, list)]
    raw_in = [i for i, a in enumerate(ins) if isinstance(a, Raw)]
    raw_out = [i for i, o in enumerate(outs) if isinstance(o, Raw)]
    pinned += raw_in
    arrays = [a[0] if isinstance(a, tuple) else a.value if isinstance(a, Raw) else a for a in ins]
    shapes = [o[0] if isinstance(o, list) else o.value if isinstance(o, Raw) else o for o in outs]
    picked = [a[1] if isinstance(a, tuple) else None for a in ins]
    n_in, n_out = len(ins), len(outs)

    def kernel(lengths_ref, which_ref, *refs):
        dp = lax.axis_index("dp")
        at = which_ref[0]
        info_ref = (lengths_ref[0], lengths_ref[1], lax.axis_index("tensor"), dp & 1, (dp >> 1) & 1, at, lengths_ref[at], lengths_ref)
        in_refs, refs = refs[:n_in], refs[n_in:]
        out_refs, refs = refs[:n_out], refs[n_out:]
        sem, refs = refs[-1], refs[:-1]
        buffers, rest = refs[: len(far_in) + len(far_out)], refs[len(far_in) + len(far_out) :]
        args = list(in_refs)
        for j, i in enumerate(far_in):
            view = picked[i][1]
            args[i] = Fetch(view(in_refs[i], info_ref), buffers[j], sem.at[j])
        results = list(out_refs)
        flushes = []
        for j, i in enumerate(far_out):
            at = len(far_in) + j
            results[i] = Flush(buffers[at], out_refs[i], sem.at[at])
            flushes.append(results[i])
        body(info_ref, *args, *results, *rest, **static)
        for i in far_in:
            args[i]()
        for f in flushes:
            f.start()
        for f in flushes:
            f.copy.wait()

    hbm = pl.BlockSpec(memory_space=pltpu.HBM)
    buffers = [pltpu.VMEM(picked[i][0], arrays[i].dtype) for i in far_in]
    buffers += [pltpu.VMEM(shapes[i].shape, shapes[i].dtype) for i in far_out]
    return pl.pallas_call(
        kernel,
        out_shape=[pltpu.HBM(o.shape, o.dtype) if i in far_out + raw_out else o for i, o in enumerate(shapes)],
        grid_spec=pltpu.PrefetchScalarGridSpec(
            num_scalar_prefetch=2,
            grid=(1,),
            in_specs=[hbm if i in pinned else pl.BlockSpec(memory_space=pl.ANY) if i in far_in else VM for i in range(n_in)],
            out_specs=[hbm if i in far_out + raw_out else VM for i in range(n_out)],
            scratch_shapes=[*buffers, *scratch, pltpu.SemaphoreType.DMA((max(1, len(far_in) + len(far_out)),))],
        ),
        compiler_params=pltpu.CompilerParams(vmem_limit_bytes=vmem << 20),
        cost_estimate=pl.CostEstimate(flops=cost, bytes_accessed=1000, transcendentals=0),
        name=name,
    )(info, jnp.full((1,), which, jnp.int32), *[pltpu.with_memory_space_constraint(a, pltpu.HBM) if i in pinned else a for i, a in enumerate(arrays)])


class Raw:
    def __init__(self, value):
        self.value = value


def ref(x):
    return x() if isinstance(x, Fetch) else x.src if isinstance(x, Flush) else x


def whole(a):
    return (a, (a.shape, lambda ref, info: ref))


def loose(a):
    return (*whole(a), None)


def prepare_kernel(info, out_in, bias, up_in, dn_in, pack, up_half, dn_half):
    for src, dst in ((up_in, up_half), (dn_in, dn_half)):
        dst.src[...] = src()[...]
        dst.start()
    out_w = out_in()
    width, d = out_w.shape
    pack.src[0:width, :] = out_w[...]
    pack.src[width : width + 8, :] = jnp.broadcast_to(bias[...], (8, d))


def prepare(info, out_w, bias, up, dn):
    width, d = out_w.shape
    part = up.shape[0] // 4
    view = lambda ref, info: ref.at[pl.ds(pl.multiple_of((2 * info[3] + info[4]) * part, part), part)]
    ins = [whole(out_w), bias, (up, ((part, d), view)), (dn, ((part, d), view))]
    return call("prepare", prepare_kernel, info, ins, [[SDS((width + 8, d), bf16)]] + [[SDS((part, d), bf16)]] * 2)


def head_cols(a, h, extra=()):
    lane = lax.broadcasted_iota(jnp.int32, a.shape, 1)
    out = jnp.where((lane >= HEAD * h) & (lane < HEAD * (h + 1)), a, jnp.zeros_like(a))
    for i, e in enumerate(extra):
        out = jnp.where(lane == WIDE + i, e, out)
    return out


def tail_cols(rows, values):
    lane = lax.broadcasted_iota(jnp.int32, (rows, LANES - WIDE), 1)
    out = jnp.zeros((rows, LANES - WIDE), f32)
    for i, v in enumerate(values):
        out = jnp.where(lane == i, v, out)
    return out.astype(bf16)


def attend_fwd_kernel(info, x_hbm, w_ref, b_ref, *rest):
    far, outs = rest[:5], rest[5:9]
    x_all, *near, v_t, s_all, sem_in, sem_out = rest[9:]
    q_all, k_all, v_all, lse_all, c_all = near
    me = info[2]
    batch, peers, width, block = c_all.shape
    seq = peers * block
    heads = width // HEAD

    def fetch(s):
        return pltpu.make_async_copy(x_hbm.at[s], x_all.at[s], sem_in.at[s])

    def flush(s, i):
        return pltpu.make_async_copy(near[i].at[s], far[i].at[s], sem_out.at[s, i])

    for s in range(batch):
        fetch(s).start()
    w = w_ref()

    def one_sequence(s, carry):
        length = info[7][s]
        fetch(s).wait()
        x = x_all[s]
        k_all[s, :, 0:WIDE] = mm(x, w[1], NT).astype(bf16)
        row = lax.broadcasted_iota(jnp.int32, (seq, 1), 0)
        k_all[s, :, WIDE:LANES] = tail_cols(seq, (jnp.where(row < length, 0.0, -1e30),))
        q = mm(x, w[0], NT) + b_ref[0:1, :].astype(f32)
        q_all[s, :, 0:WIDE] = q.astype(bf16) * jnp.asarray(0.125, bf16)
        q_all[s, :, WIDE:LANES] = tail_cols(seq, (1.0,))
        v = (mm(x, w[2], NT) + b_ref[1:2, :].astype(f32)).astype(bf16)
        v_all[s] = v
        v_t[...] = v.T
        for i in range(3):
            flush(s, i).start()

        def two_blocks(n, carry):
            qb = q_all[s, pl.ds(pl.multiple_of(n * 2 * block, 2 * block), 2 * block), :]
            one = jnp.ones_like(qb[:, 0:1])
            for h in range(heads):
                s_all[h] = mm(k_all[s], head_cols(qb, h, (one,)), NT)
            for h in range(heads):
                top = jnp.max(s_all[h], axis=0, keepdims=True)
                p = jnp.exp(s_all[h] - top)
                total = jnp.sum(p, axis=0, keepdims=True)
                rows = slice(HEAD * h, HEAD * (h + 1))
                out = (mm(v_t[rows, :], p.astype(bf16)) * (1.0 / total)).astype(bf16)
                lse = top + jnp.log(total)
                for j in range(2):
                    cols = slice(block * j, block * (j + 1))
                    c_all[s, 2 * n + j, rows, :] = out[:, cols]
                    lse_all[s, 2 * n + j, h : h + 1, :] = lse[:, cols]
            return carry

        lax.fori_loop(0, peers // 2, two_blocks, 0)
        for i in range(3, 5):
            flush(s, i).start()
        for k, out in enumerate(outs):
            out.src[s] = c_all[s, me ^ k]
        return carry

    lax.fori_loop(0, batch, one_sequence, 0)
    for out in outs:
        out.start()
    for s in range(batch):
        for i in range(5):
            flush(s, i).wait()


def attend_fwd(info, inputs, w_t, bias, peers):
    batch, seq, d = inputs.shape
    width = w_t.shape[1]
    block = seq // peers
    far = [SDS((batch, seq, LANES), bf16)] * 2 + [SDS((batch, seq, width), bf16)]
    far += [SDS((batch, peers, 8, block), f32), SDS((batch, peers, width, block), bf16)]
    scratch = [pltpu.VMEM(inputs.shape, bf16), *[pltpu.VMEM(o.shape, o.dtype) for o in far]]
    scratch += [pltpu.VMEM((width, seq), bf16), pltpu.VMEM((width // HEAD, seq, 2 * block), f32)]
    scratch += [pltpu.SemaphoreType.DMA((batch,)), pltpu.SemaphoreType.DMA((batch, 5))]
    return call(
        "attend_fwd",
        attend_fwd_kernel,
        info,
        [Raw(inputs), whole(w_t), bias],
        [Raw(o) for o in far] + [[SDS((batch, width, block), bf16)]] * peers,
        scratch,
    )


def nth(at, ref, info):
    return ref.at[at]


def of_sequence(a):
    return (a, (a.shape[1:], lambda ref, info: ref.at[info[5]]))


def attend_bwd_kernel(info, x_ref, q_in, k_in, v_in, lse_in, c_in, *rest):
    w_ref = x_ref
    peers = 4
    gs, rest = rest[:peers], rest[peers:]
    keep, send, low_out, db_ref, dq_t, dk, dv, k_t, g_ref = rest
    low = low_out.src
    length = info[6]
    me = info[2]
    k_ref, q_ref, v_ref = k_in(), q_in(), v_in()
    lse_ref, c_ref = lse_in(), c_in()
    _, width, block = c_ref.shape
    heads = width // HEAD
    k_t[...] = k_ref[:, 0:WIDE].T
    dk[...] = jnp.zeros_like(dk)
    dv[...] = jnp.zeros_like(dv)
    for k in range(peers):
        g_ref[me ^ k] = gs[k]()[...]

    def one_block(s, carry):
        at = pl.multiple_of(s * block, block)

        @pl.when(at >= length)
        def _():
            dq_t[:, pl.ds(at, block)] = jnp.zeros((width, block), f32)

        @pl.when(at < length)
        def _():
            qb = q_ref[pl.ds(at, block), :]
            g_t = g_ref[s]
            g = g_t.T
            prod_t = g_t.astype(f32) * c_ref[s].astype(f32)
            for h in range(heads):
                rows = slice(HEAD * h, HEAD * (h + 1))
                qh = head_cols(qb, h)
                gh = head_cols(g, h)
                scores = mm(k_ref[...], qh, NT)
                row = lax.broadcasted_iota(jnp.int32, scores.shape, 0)
                p = jnp.where(row < length, jnp.exp(scores - lse_ref[s, h : h + 1, :]), 0.0)
                dp = mm(v_ref[...], gh, NT)
                inner = jnp.sum(prod_t[rows], axis=0, keepdims=True)
                ds = (p * (dp - inner)).astype(bf16)
                dv[...] += mm(p.astype(bf16), gh)
                dk[...] += mm(ds, qh)
                dq_t[rows, pl.ds(at, block)] = mm(k_t[rows, :], ds) * 0.125

        return carry

    lax.fori_loop(0, peers, one_block, 0)
    low[0] = dq_t[...].T.astype(bf16)
    low[1] = dk[:, 0:WIDE].astype(bf16)
    low[2] = dv[...].astype(bf16)
    w = w_ref()
    for s in range(peers):
        at = pl.multiple_of((me ^ s) * block, block)
        total = sum(mm(low[i, pl.ds(at, block), :], w[i]) for i in range(3))
        (send if s % 2 else keep).src[s // 2] = total.astype(bf16)
    send.start()
    keep.start()
    db_ref[...] = jnp.concatenate([rowsum(low[i].astype(f32)) for i in (0, 2)], axis=1)


def attend_bwd(which, info, w_t, q, k, v, lse, c, gs, d):
    _, peers, width, block = c.shape
    seq = peers * block
    outs = [[SDS((2, block, d), bf16)]] * 2 + [[SDS((3, seq, width), bf16)], SDS((1, 2 * width), f32)]
    scratch = [
        pltpu.VMEM((width, seq), f32),
        pltpu.VMEM((seq, LANES), f32),
        pltpu.VMEM((seq, width), f32),
        pltpu.VMEM((width, seq), bf16),
        pltpu.VMEM((peers, width, block), bf16),
    ]
    ins = [whole(w_t)] + [of_sequence(a) for a in (q, k, v, lse, c)]
    ins += [(g, ((width, block), lambda ref, info: ref.at[info[5]]), None) for g in gs]
    return call("attend_bwd", attend_bwd_kernel, info, ins, outs, scratch, which=which, cost=10**10)


def project_grads_kernel(info, x0, x1, low0, low1, db0, db1, keep, send, db_ref, dw, pair, *, parts):
    lows = (low0(), low1())
    x = (x0(), x1())
    _, d, width = dw.shape
    step = 256

    def chunk(m, carry):
        cols = pl.ds(pl.multiple_of(m * step, step), step)
        x_t = (x[0][:, cols].T, x[1][:, cols].T)
        for i in range(3):
            dw[i, cols, :] = mm(x_t[0], lows[0][i]) + mm(x_t[1], lows[1][i])
        return carry

    lax.fori_loop(0, d // step, chunk, 0)
    rows = d // parts
    half = 3 * rows // 2
    for b in range(parts):
        flat = dw[:, b * rows : (b + 1) * rows, :].reshape(3 * rows, width)
        flat = jnp.concatenate([flat[0:half], flat[half : 2 * half]], axis=1).astype(bf16)
        pair[(b & 1) ^ info[3], (b >> 1) * half : (b // 2 + 1) * half, :] = flat
    n = keep.src.shape[0]
    send.src[0:n, :] = pair[1]
    keep.src[...] = pair[0]
    db = db0[...] + db1[...]
    db_ref[...] = db
    high = db.astype(bf16)
    send.src[n : n + 8, :] = jnp.concatenate(
        [high, (db - high.astype(f32)).astype(bf16), jnp.zeros((6, 2 * width), bf16)], axis=0
    )
    send.start()


def gelu_parts(h):
    t = 1.0 / (1.0 + (0.3275911 * 0.7071067811865476) * jnp.abs(h))
    poly = t * (0.127414796 + t * (-0.142248368 + t * (0.7107068705 + t * (-0.7265760135 + t * 0.5307027145))))
    bell = jnp.exp2((-0.5 * 1.4426950408889634) * (h * h))
    tail = poly * bell
    cum = jnp.where(h < 0, tail, 1.0 - tail)
    return h * cum, cum + h * (bell * 0.3989422804014327)


def norm_parts(v):
    center = v - jnp.mean(v, axis=1, keepdims=True)
    r = lax.rsqrt(jnp.mean(center * center, axis=1, keepdims=True) + 1e-12)
    return center * r, r


def norm_back(u, gain, nv, r):
    gu = u * gain
    return r * (gu - jnp.mean(gu, axis=1, keepdims=True) - nv * jnp.mean(gu * nv, axis=1, keepdims=True))


def rowsum(v):
    return jnp.sum(v, axis=0, keepdims=True)


def first_norm_kernel(info, x_in, par, *rest):
    nv_ref, r_ref, low = rest[8:]
    cs, packs = [c() for c in rest[:4]], [p() for p in rest[4:8]]
    x_ref = x_in()
    batch, rows = x_ref.shape[:2]
    width = cs[0].shape[1]

    def one_sequence(s, carry):
        here = pl.ds(pl.multiple_of(s * rows, rows), rows)
        total = par[0:1, :] + x_ref[s].astype(f32)
        for k in range(4):
            total = total + mm(cs[k][s], packs[k][0:width, :], TN)
        nv, r = norm_parts(total)
        nv_ref[here, :] = nv
        r_ref[here, :] = r
        low[here, :] = (nv * par[1:2, :] + par[2:3, :]).astype(bf16)
        return carry

    lax.fori_loop(0, batch, one_sequence, 0)


def feed_kernel(info, low, low2, pack, *rest, width, far):
    if far:
        u_a, u_b, d_a, d_b, p_own, p_sib, act_out, slope_out, own, sib, both, up, dn = rest
        assemble(info[3], info[4], up, u_a(), u_b(), False)
    else:
        u_in, d_in, act_out, slope_out, own, sib, both = rest
        up = u_in()
    act, slope = ref(act_out), ref(slope_out)
    units = up.shape[1]
    bias = pack()
    step = 256
    both[0] = low[...]
    both[1] = low2[...]

    def side(j, carry):
        def chunk(n, carry):
            cols = pl.ds(pl.multiple_of(n * step, step), step)
            hidden = mm(both[j], up[:, cols]) + bias[width : width + 1, cols].astype(f32)
            a, g = gelu_parts(hidden)
            act[j, :, cols] = a.astype(bf16)
            slope[j, :, cols] = g.astype(bf16)
            return carry

        return lax.fori_loop(0, units // step, chunk, carry)

    lax.fori_loop(0, 2, side, 0)
    if far:
        assemble(info[3], info[4], dn, d_a(), d_b(), True)
        sib[...] = (p_sib[...] + mm(act[1], dn[...])).astype(bf16)
        own[...] = p_own[...] + mm(act[0], dn[...])
    else:
        dn = d_in()
        own[...] = mm(act[0], dn[...])
        sib[...] = mm(act[1], dn[...])


def assemble(x, z, dst, a, b, z_first):
    part = a.shape[0] // 2
    for src, other in ((a, 0), (b, 1)):
        for i in range(2):
            flips = (other, i) if z_first else (i, other)
            at = 2 * (x ^ flips[0]) + (z ^ flips[1])
            dst[pl.ds(pl.multiple_of(at * part, part), part)] = src[i * part : (i + 1) * part]


def second_norm_kernel(info, cot_in, par, nv_in, own, got, outs, gsec_out, gs_low, small):
    cot, nv_ref, gsec = cot_in(), ref(nv_in), ref(gsec_out)
    batch, rows, d = cot.shape

    def one_sequence(s, sums):
        here = pl.ds(pl.multiple_of(s * rows, rows), rows)
        total = own[here, :] + got[here, :].astype(f32) + par[3:4, :] + (nv_ref[here, :] * par[1:2, :] + par[2:3, :])
        nv, r = norm_parts(total)
        outs.src[s] = (nv * par[4:5, :] + par[5:6, :]).astype(bf16)
        at = info[2] * rows + lax.broadcasted_iota(jnp.int32, (rows, 1), 0)
        seed = jnp.where(at < info[7][s], cot[s].astype(f32), 0.0)
        g = norm_back(seed, par[4:5, :], nv, r)
        gsec[here, :] = g
        gs_low[here, :] = g.astype(bf16)
        return tuple(a + rowsum(b) for a, b in zip(sums, (g, seed * nv, seed)))

    sums = lax.fori_loop(0, batch, one_sequence, (jnp.zeros((1, d), f32),) * 3)
    small[...] = jnp.concatenate([*sums, jnp.zeros((5, d), f32)], axis=0)


def feed_back_kernel(info, gs, gs2, slope0, slope1, up0, dn0, u_a, u_b, d_a, d_b, gh_out, own, sib, ub, sides, up2, dn2):
    gh = ref(gh_out)
    units = up0.dst.shape[1]
    ub[...] = jnp.zeros_like(ub)
    sides[0] = gs[...]
    sides[1] = gs2[...]
    step = 256
    for k, slope in enumerate((ref(slope0), ref(slope1))):
        if k:
            assemble(info[3], info[4], dn2, d_a(), d_b(), True)
            dn = dn2
        else:
            dn = dn0()

        def side(j, carry):
            def chunk(n, carry):
                cols = pl.ds(pl.multiple_of(n * step, step), step)
                ga = mm(sides[j], dn[cols, :], NT)
                h = (ga * slope[j, :, cols].astype(f32)).astype(bf16)
                gh[k, j, :, cols] = h
                ub[k : k + 1, cols] += rowsum(h.astype(f32))
                return carry

            return lax.fori_loop(0, units // step, chunk, carry)

        lax.fori_loop(0, 2, side, 0)
    assemble(info[3], info[4], up2, u_a(), u_b(), False)
    up = up0()
    sib[...] = (mm(gh[0, 1], up[...], NT) + mm(gh[1, 1], up2[...], NT)).astype(bf16)
    own[...] = mm(gh[0, 0], up[...], NT) + mm(gh[1, 0], up2[...], NT)


def first_back_kernel(info, par, nv_in, r_ref, own, got, gsec_in, small2, *rest):
    cs, packs = [c() for c in rest[:4]], rest[4:8]
    gfi, g0, g1, g2, g3, okeep, osend, small, ga_low = rest[8:]
    nv_ref, gsec = ref(nv_in), ref(gsec_in)
    packs = [p() for p in packs]
    n, d = own.shape
    rows = n // 2
    width = cs[0].shape[1]

    def one_sequence(s, sums):
        here = pl.ds(pl.multiple_of(s * rows, rows), rows)
        u = own[here, :] + got[here, :].astype(f32) + gsec[here, :]
        nv = nv_ref[here, :]
        g = norm_back(u, par[1:2, :], nv, r_ref[here, :])
        gfi.src[here, :] = g
        low = g.astype(bf16)
        ga_low[here, :] = low
        for k, out in enumerate((g0, g1, g2, g3)):
            out.src[s] = mm(packs[k][0:width, :], low, NT).astype(bf16)
        return tuple(a + rowsum(b) for a, b in zip(sums, (g, u * nv, u)))

    sums = lax.fori_loop(0, 2, one_sequence, (jnp.zeros((1, d), f32),) * 3)
    for out in (g3, g2, g1, g0, gfi):
        out.start()
    for k in range(4):
        total = mm(cs[k][0], ga_low[0:rows, :]) + mm(cs[k][1], ga_low[rows:n, :])
        (osend if k % 2 else okeep).src[k // 2, 0:width, :] = total.astype(bf16)
    both = jnp.concatenate([*sums, small2[0:3, :], jnp.zeros((2, d), f32)], axis=0)
    small[...] = both
    high = both.astype(bf16)
    osend.src[0, width : width + 8, :] = high
    osend.src[1, width : width + 8, :] = (both - high.astype(f32)).astype(bf16)


def down_grads_kernel(info, act0, act1, gs, gs2, far_keep, keep, send, scr, *, parts):
    units = act0.shape[2]
    block = units // parts
    step = 384
    for k, (act, mine) in enumerate(((act1, far_keep), (act0, keep))):

        def chunk(m, carry):
            cols = pl.ds(pl.multiple_of(m * step, step), step)
            total = mm(act[0, :, cols], gs[...], TN) + mm(act[1, :, cols], gs2[...], TN)
            total = total.astype(bf16)
            for i in range(step // block):
                scr[(i & 1) ^ info[3], m * (step // block // 2) + (i >> 1)] = total[i * block : (i + 1) * block]
            return carry

        lax.fori_loop(0, units // step, chunk, 0)
        send.src[k] = scr[1]
        mine.src[...] = scr[0]
    send.start()


def up_grads_kernel(
    info, low, low2, gh_in, okeep, ogot, small, ub, far_keep, far_send, keep, send, sums, scr, *, parts, width
):
    gh = ref(gh_in)
    units = low.shape[1]
    block = units // parts
    extra = width // parts
    joint = block + extra
    n = parts // 2 * joint
    step = 384
    got = ogot()
    both = small[...] + got[0, width : width + 8, :].astype(f32) + got[1, width : width + 8, :].astype(f32)
    both = jnp.concatenate([both[0:6], ub[0:2, :]], axis=0)
    sums[...] = both
    high = both.astype(bf16)
    far_send.src[n : n + 8, :] = high
    far_send.src[n + 8 : n + 16, :] = (both - high.astype(f32)).astype(bf16)
    for k, mine, theirs in ((1, far_keep, far_send), (0, keep, send)):

        def chunk(m, carry):
            cols = pl.ds(pl.multiple_of(m * step, step), step)
            total = mm(low[:, cols], gh[k, 0], TN) + mm(low2[:, cols], gh[k, 1], TN)
            total = total.astype(bf16)
            for i in range(step // block):
                at = (m * (step // block // 4) + (i >> 2)) * 2 + (i & 1)
                scr[((i >> 1) & 1) ^ info[4], at, 0:block, :] = total[i * block : (i + 1) * block]
            return carry

        lax.fori_loop(0, units // step, chunk, 0)
        o = (okeep()[k, 0:width, :].astype(f32) + got[k, 0:width, :].astype(f32)).astype(bf16)
        for b in range(parts):
            at = (b >> 2) * 2 + (b & 1)
            scr[((b >> 1) & 1) ^ info[4], at, block:joint, :] = o[b * extra : (b + 1) * extra]
        for b in range(parts // 2):
            theirs.src[b * joint : (b + 1) * joint, :] = scr[1, b]
            mine.src[b * joint : (b + 1) * joint, :] = scr[0, b]
        theirs.start()
        mine.start()


def swap(x, axis, bit):
    size = lax.axis_size(axis)
    return lax.ppermute(x, axis, [(i, i ^ bit) for i in range(size)])


def summed(parts):
    return sum(p.astype(f32) for p in parts)


def spread(array, axis, parts):
    bits = parts.bit_length() - 1
    return array.reshape(*array.shape[:axis], *([2] * bits), array.shape[axis] // parts, *array.shape[axis + 1 :])


def halve_sum(terms, axis, mine):
    other = [lax.dynamic_index_in_dim(t, 1 - mine, axis, keepdims=False) for t in terms]
    kept = [lax.dynamic_index_in_dim(t, mine, axis, keepdims=False) for t in terms]
    return kept, summed(other).astype(bf16)


def halve(terms, axis, bit, mine):
    other = [lax.dynamic_index_in_dim(t, 1 - mine, axis, keepdims=False) for t in terms]
    kept = [lax.dynamic_index_in_dim(t, mine, axis, keepdims=False) for t in terms]
    other = summed(other).astype(bf16)
    return kept + [swap(other, "dp", bit)], other


def body(
    inputs,
    cotangent,
    lengths,
    qkv_weight,
    qkv_bias,
    out_weight,
    out_bias,
    first_gain,
    first_shift,
    up_weight,
    up_bias,
    down_weight,
    down_bias,
    second_gain,
    second_shift,
):
    batch, seq, d = inputs.shape
    rows = cotangent.shape[1]
    n = batch * rows
    width = out_weight.shape[0]
    units = up_weight.shape[1]
    peers = lax.axis_size("tensor")
    parts = lax.axis_size("dp")
    bits = parts.bit_length() - 1
    t = lax.axis_index("tensor")
    dp = lax.axis_index("dp")
    bit_of = [(dp >> i) & 1 for i in range(bits)]
    info = lengths
    par = jnp.concatenate([out_bias, first_gain, first_shift, down_bias, second_gain, second_shift])
    par = par.reshape(6, d).astype(f32)
    w_t = jnp.transpose(qkv_weight, (1, 2, 0))
    pack, u_part, d_part = prepare(info, out_weight, up_bias[None], up_weight, down_weight)
    pack2 = swap(pack, "tensor", 2)
    pack1 = swap(pack, "tensor", 1)
    u_part = swap(u_part, "tensor", 2)
    d_part = swap(d_part, "tensor", 2)
    q, k, v, lse, c, *cs = attend_fwd(info, inputs, w_t, qkv_bias, peers)
    saved = (q, k, v, lse, c)
    *cs, pack1, pack2, u_part, d_part = after(*cs, pack1, pack2, u_part, d_part)
    ctx = [cs[0]] + [swap(cs[j], "tensor", j) for j in range(1, peers)]
    u2a = jnp.concatenate([u_part, swap(u_part, "dp", 1)])
    d2a = jnp.concatenate([d_part, swap(d_part, "dp", 2)])
    *ctx, pack2, u2a, d2a = after(*ctx, pack2, u2a, d2a)
    pack3 = swap(pack2, "tensor", 1)
    packs = [pack, pack1, pack2, pack3]
    u2b = swap(u2a, "dp", 2)
    d2b = swap(d2a, "dp", 1)
    far_ctx = [whole(ctx[0])] + [loose(x) for x in ctx[1:]]
    far_packs = [whole(pack)] + [loose(p) for p in packs[1:]]
    share = (inputs, ((batch, rows, d), lambda ref, info: ref.at[:, pl.ds(pl.multiple_of(info[2] * rows, rows), rows), :]))
    nv1, r1, low = call(
        "first_norm",
        first_norm_kernel,
        info,
        [share, par, *far_ctx, *far_packs],
        [SDS((n, d), f32), SDS((n, 1), f32), SDS((n, d), bf16)],
        vmem=NEAR,
    )
    low2 = swap(low, "tensor", 1)
    pair = SDS((2, n, units), bf16)
    part = SDS((n, d), f32)
    sides = pltpu.VMEM((2, n, d), bf16)
    act0, slope0, own, sib = call(
        "feed",
        feed_kernel,
        info,
        [low, low2, far_packs[0], whole(up_weight), whole(down_weight)],
        [pair, pair, part, part],
        [sides],
        vmem=NEAR,
        width=width,
        far=False,
    )
    halves = [loose(x) for x in (u2a, u2b, d2a, d2b)]
    both = [pltpu.VMEM((d, units), bf16), pltpu.VMEM((units, d), bf16)]
    act1, slope1, own, sib = call(
        "feed",
        feed_kernel,
        info,
        [low, low2, far_packs[2], *halves, own, sib],
        [pair, pair, part, SDS((n, d), bf16)],
        [sides, *both],
        vmem=NEAR,
        width=width,
        far=True,
    )
    got = swap(sib, "tensor", 1)
    outputs, gsec, gs_low, small2 = call(
        "second_norm",
        second_norm_kernel,
        info,
        [whole(cotangent), par, nv1, own, got],
        [[SDS((batch, rows, d), bf16)], part, SDS((n, d), bf16), SDS((8, d), f32)],
        vmem=NEAR,
    )
    gs_low2 = swap(gs_low, "tensor", 1)
    gh, own, sib, ub = call(
        "feed_back",
        feed_back_kernel,
        info,
        [gs_low, gs_low2, slope0, slope1, whole(up_weight), whole(down_weight), *halves],
        [SDS((2, 2, n, units), bf16), part, SDS((n, d), bf16), SDS((8, d), f32)],
        [sides, *both],
        vmem=NEAR,
    )
    got = swap(sib, "tensor", 1)
    block = units // parts
    half_shape = (parts // 2, block, d)
    down_far_keep, down_keep, down_send = call(
        "down_grads",
        down_grads_kernel,
        info,
        [act0, act1, gs_low, gs_low2],
        [[SDS(half_shape, bf16)], [SDS(half_shape, bf16)], [SDS((2, *half_shape), bf16)]],
        [pltpu.VMEM((2, *half_shape), bf16)],
        vmem=NEAR,
        parts=parts,
    )
    down_got = swap(down_send, "dp", 1)
    gfi, g0, g1, g2, g3, okeep, osend, small1 = call(
        "first_back",
        first_back_kernel,
        info,
        [par, nv1, r1, own, got, gsec, small2, *far_ctx, *far_packs],
        [
            [part],
            *[[SDS((batch, width, rows), bf16)]] * 4,
            *[[SDS((2, width + 8, d), bf16)]] * 2,
            SDS((8, d), f32),
        ],
        [pltpu.VMEM((n, d), bf16)],
        vmem=NEAR,
    )
    gctx = [g0] + [swap(g, "tensor", j) for j, g in ((1, g1), (2, g2), (3, g3))]
    got_o = swap(osend, "tensor", 1)
    joint = block + width // parts
    cut = parts // 2 * joint
    up_far_keep, up_far_send, up_keep, up_send, small = call(
        "up_grads",
        up_grads_kernel,
        info,
        [low, low2, gh, whole(okeep), loose(got_o), small1, ub],
        [
            [SDS((cut, d), bf16)],
            [SDS((cut + 16, d), bf16)],
            [SDS((cut, d), bf16)],
            [SDS((cut, d), bf16)],
            SDS((8, d), f32),
        ],
        [pltpu.VMEM((2, parts // 2, joint, d), bf16)],
        vmem=NEAR,
        parts=parts,
        width=width,
    )
    *gctx, up_far_send = after(*gctx, up_far_send)
    up_far_got = swap(up_far_send, "dp", 2)
    *gctx, up_far_keep = after(*gctx, up_far_keep)
    lows, biases, terms_of = [], [], []
    for s in range(batch):
        keep, send, low_grads, db = attend_bwd(s, info, w_t, *saved, gctx, d)
        biases.append(db)
        if s == 0:
            send, up_far_got, down_got = after(send, up_far_got, down_got)
        else:
            send, low_grads, down_y, up_got, up_more, far = after(send, low_grads, down_y, up_got, up_more, far)
            terms_of[0].append(far)
        near = swap(send, "tensor", 1)
        in_sum = summed([keep[1], near[1]]).astype(bf16)
        terms_of.append([keep[0], near[0]])
        if s == 0:
            lows.append(low_grads)
            down_sum = summed([down_far_keep, down_got[0]]).astype(bf16)
            shape = ([2] * (bits - 1)) + [joint, d]
            small = small + pair_sum(up_far_got, cut, 8)
            terms = [x.reshape(shape) for x in (up_far_keep, up_far_got[:cut])]
            up_far_kept, up_far_next = halve_sum(terms, bits - 2, bit_of[0])
            up_far_rows = with_rows(up_far_next, small)
            tied = after(down_sum, up_far_rows, in_sum, up_send, *gctx)
            (down_sum, up_far_rows, in_sum, up_send), gctx = tied[:4], tied[4:]
            down_y = swap(down_sum, "tensor", 2)
            up_got = swap(up_send, "dp", 2)
            up_more = swap(up_far_rows, "dp", 1)
            far = swap(in_sum, "tensor", 2)
    shape = ([2] * (bits - 1)) + [block, d]
    down_terms = [x.reshape(shape) for x in (down_keep, down_got[1], down_y)]
    down_kept, down_next = halve_sum(down_terms, bits - 2, bit_of[1])
    at = up_far_next.size // d
    small = small + pair_sum(up_more, at, 8)
    small = jnp.concatenate([small[0:6], small[7:8], small[6:7]])
    up_y_next = summed(up_far_kept + [up_more[:at].reshape(up_far_next.shape)]).astype(bf16)
    up_y_rows = with_rows(up_y_next, small)
    shape = ([2] * (bits - 1)) + [joint, d]
    up_kept, up_next = halve_sum([x.reshape(shape) for x in (up_keep, up_got)], bits - 2, bit_of[0])
    low_grads, down_next, up_y_rows, up_next = after(low_grads, down_next, up_y_rows, up_next)
    lows.append(low_grads)
    down_more = swap(down_next, "dp", 2)
    up_y = swap(up_y_rows, "tensor", 2)
    up_more = swap(up_next, "dp", 1)
    m = 3 * d // 4
    w_keep, w_send, db = call(
        "project_grads",
        project_grads_kernel,
        info,
        [*[(inputs, (inputs.shape[1:], functools.partial(nth, at))) for at in range(batch)], *[whole(a) for a in lows], *biases],
        [[SDS((m, 2 * width), bf16)], [SDS((m + 8, 2 * width), bf16)], SDS((1, 2 * width), f32)],
        [pltpu.VMEM((3, d, width), f32), pltpu.VMEM((2, m, 2 * width), bf16)],
        parts=parts,
    )
    w_send, down_more, up_y, up_more = after(w_send, down_more, up_y, up_more)
    down_more, up_y, up_more, in_sum = after(down_more, up_y, up_more, in_sum)
    got = swap(w_send, "dp", 1)
    got, far = after(got, swap(in_sum, "tensor", 2))
    terms_of[1].append(far)
    down_terms = down_kept + [down_more]
    at = up_y_next.size // d
    small = jnp.concatenate([small[0:6], small[7:8], small[7:8]]) + pair_sum(up_y, at, 8)
    up_terms = up_kept + [up_more, up_y[:at].reshape(up_y_next.shape)]
    for i in range(2, bits):
        down_terms, sent = halve_sum(down_terms, bits - 1 - i, bit_of[i])
        down_got = swap(sent, "dp", 1 << i)
        up_terms, sent = halve_sum(up_terms, bits - 1 - i, bit_of[i])
        up_got = swap(with_rows(sent, small), "dp", 1 << i)
        if i == bits - 1:
            break
        down_terms, up_terms, small = with_received(down_terms, down_got, up_terms, up_got, sent, small)
    row = 3 * (d // parts) // 2
    at = parts // 2 * row
    shape = ([2] * (bits - 1)) + [row, 2 * width]
    terms = [x.reshape(shape) for x in (w_keep, got[:at])]
    db = db + got[at : at + 1].astype(f32) + got[at + 1 : at + 2].astype(f32)
    for i in range(1, bits):
        kept, rows_sent, more = halve_with(terms, terms[0].ndim - 3, db, "dp", 1 << i, bit_of[i])
        if i == 1:
            kept[-1], down_got, up_got = after(kept[-1], down_got, up_got)
        terms, db = kept, db + more
    down_terms, up_terms, small = with_received(down_terms, down_got, up_terms, up_got, sent, small)
    down_sum = summed(down_terms)
    up_sum = summed(up_terms)
    mine = small
    qkv_sum = summed(terms)
    qkv_sum = jnp.concatenate([qkv_sum[:, :width], qkv_sum[:, width:]], axis=0).reshape(3, -1, width)
    qkv_sum = jnp.transpose(qkv_sum, (1, 0, 2))
    db = db.reshape(2, width)
    input_list = [
        (summed(x) + gfi[s * rows : (s + 1) * rows]).astype(bf16)
        for s, x in enumerate(terms_of)
    ]
    return (
        outputs,
        jnp.stack(input_list, 0),
        qkv_sum,
        db,
        up_sum[block:],
        mine[0],
        mine[1],
        mine[2],
        up_sum[:block],
        mine[6],
        down_sum,
        mine[3],
        mine[4],
        mine[5],
    )


def pair_sum(array, at, n):
    return array[at : at + n].astype(f32) + array[at + n : at + 2 * n].astype(f32)


def with_rows(array, rows):
    flat = array.reshape(-1, array.shape[-1])
    high = rows.astype(bf16)
    low = (rows - high.astype(f32)).astype(bf16)
    return jnp.concatenate([flat, high, low], axis=0)


def halve_with(terms, axis, rows, name, bit, mine):
    other = [lax.dynamic_index_in_dim(t, 1 - mine, axis, keepdims=False) for t in terms]
    kept = [lax.dynamic_index_in_dim(t, mine, axis, keepdims=False) for t in terms]
    other = summed(other).astype(bf16)
    sent = with_rows(other, rows)
    got = swap(sent, name, bit)
    cut = other.size // other.shape[-1]
    return kept + [got[:cut].reshape(other.shape)], sent, pair_sum(got, cut, rows.shape[0])


def with_received(down_terms, down_got, up_terms, up_got, sent, small):
    at = sent.size // sent.shape[-1]
    small = small + pair_sum(up_got, at, small.shape[0])
    return down_terms + [down_got], up_terms + [up_got[:at].reshape(sent.shape)], small


def after(*values):
    return lax.optimization_barrier(values)


def solution(mesh):
    in_specs = (
        P("dp", None, None),
        P("dp", "tensor", None),
        P("dp"),
        P(None, None, "tensor"),
        P(None, "tensor"),
        P("tensor", None),
        P(),
        P(),
        P(),
        P(None, "tensor"),
        P("tensor"),
        P("tensor", None),
        P(),
        P(),
        P(),
    )
    out_specs = (
        P("dp", "tensor", None),
        P("dp", "tensor", None),
        P("dp", None, "tensor"),
        P(None, "tensor"),
        P(("tensor", "dp"), None),
        P(),
        P(),
        P(),
        P("dp", "tensor"),
        P("tensor"),
        P(("tensor", "dp"), None),
        P(),
        P(),
        P(),
    )
    return jax.shard_map(body, mesh=mesh, in_specs=in_specs, out_specs=out_specs, check_vma=False)
```

```python
import functools

import jax
import jax.numpy as jnp
from jax import lax
from jax.experimental import pallas as pl
from jax.experimental.pallas import tpu as pltpu
from jax.sharding import PartitionSpec as P

HEAD = 64
WIDE, LANES = 192, 256
NEAR = 30
NT = (((1,), (1,)), ((), ()))
NN = (((1,), (0,)), ((), ()))
TN = (((0,), (0,)), ((), ()))
bf16 = jnp.bfloat16
f32 = jnp.float32
VM = pl.BlockSpec(memory_space=pltpu.VMEM)
SDS = jax.ShapeDtypeStruct


def mm(a, b, dims=NN):
    return lax.dot_general(a, b, dims, preferred_element_type=f32)


class Fetch:
    def __init__(self, src, dst, sem):
        self.dst, self.copy = dst, pltpu.make_async_copy(src, dst, sem)
        self.copy.start()
        self.waiting = True

    def __call__(self):
        if self.waiting:
            self.copy.wait()
            self.waiting = False
        return self.dst


class Flush:
    def __init__(self, src, dst, sem):
        self.src, self.copy = src, pltpu.make_async_copy(src, dst, sem)
        self.started = False

    def start(self):
        if not self.started:
            self.copy.start()
        self.started = True


def call(name, body, info, ins, outs, scratch=(), vmem=58, which=0, cost=1000, **static):
    far_in = [i for i, a in enumerate(ins) if isinstance(a, tuple)]
    pinned = [i for i in far_in if len(ins[i]) == 2]
    far_out = [i for i, o in enumerate(outs) if isinstance(o, list)]
    raw_in = [i for i, a in enumerate(ins) if isinstance(a, Raw)]
    raw_out = [i for i, o in enumerate(outs) if isinstance(o, Raw)]
    pinned += raw_in
    arrays = [a[0] if isinstance(a, tuple) else a.value if isinstance(a, Raw) else a for a in ins]
    shapes = [o[0] if isinstance(o, list) else o.value if isinstance(o, Raw) else o for o in outs]
    picked = [a[1] if isinstance(a, tuple) else None for a in ins]
    n_in, n_out = len(ins), len(outs)

    def kernel(lengths_ref, which_ref, *refs):
        dp = lax.axis_index("dp")
        at = which_ref[0]
        info_ref = (lengths_ref[0], lengths_ref[1], lax.axis_index("tensor"), dp & 1, (dp >> 1) & 1, at, lengths_ref[at], lengths_ref)
        in_refs, refs = refs[:n_in], refs[n_in:]
        out_refs, refs = refs[:n_out], refs[n_out:]
        sem, refs = refs[-1], refs[:-1]
        buffers, rest = refs[: len(far_in) + len(far_out)], refs[len(far_in) + len(far_out) :]
        args = list(in_refs)
        for j, i in enumerate(far_in):
            view = picked[i][1]
            args[i] = Fetch(view(in_refs[i], info_ref), buffers[j], sem.at[j])
        results = list(out_refs)
        flushes = []
        for j, i in enumerate(far_out):
            at = len(far_in) + j
            results[i] = Flush(buffers[at], out_refs[i], sem.at[at])
            flushes.append(results[i])
        body(info_ref, *args, *results, *rest, **static)
        for i in far_in:
            args[i]()
        for f in flushes:
            f.start()
        for f in flushes:
            f.copy.wait()

    hbm = pl.BlockSpec(memory_space=pltpu.HBM)
    buffers = [pltpu.VMEM(picked[i][0], arrays[i].dtype) for i in far_in]
    buffers += [pltpu.VMEM(shapes[i].shape, shapes[i].dtype) for i in far_out]
    return pl.pallas_call(
        kernel,
        out_shape=[pltpu.HBM(o.shape, o.dtype) if i in far_out + raw_out else o for i, o in enumerate(shapes)],
        grid_spec=pltpu.PrefetchScalarGridSpec(
            num_scalar_prefetch=2,
            grid=(1,),
            in_specs=[hbm if i in pinned else pl.BlockSpec(memory_space=pl.ANY) if i in far_in else VM for i in range(n_in)],
            out_specs=[hbm if i in far_out + raw_out else VM for i in range(n_out)],
            scratch_shapes=[*buffers, *scratch, pltpu.SemaphoreType.DMA((max(1, len(far_in) + len(far_out)),))],
        ),
        compiler_params=pltpu.CompilerParams(vmem_limit_bytes=vmem << 20),
        cost_estimate=pl.CostEstimate(flops=cost, bytes_accessed=1000, transcendentals=0),
        name=name,
    )(info, jnp.full((1,), which, jnp.int32), *[pltpu.with_memory_space_constraint(a, pltpu.HBM) if i in pinned else a for i, a in enumerate(arrays)])


class Raw:
    def __init__(self, value):
        self.value = value


def ref(x):
    return x() if isinstance(x, Fetch) else x.src if isinstance(x, Flush) else x


def whole(a):
    return (a, (a.shape, lambda ref, info: ref))


def loose(a):
    return (*whole(a), None)


def prepare_kernel(info, out_in, bias, up_in, dn_in, pack, up_half, dn_half):
    for src, dst in ((up_in, up_half), (dn_in, dn_half)):
        dst.src[...] = src()[...]
        dst.start()
    out_w = out_in()
    width, d = out_w.shape
    pack.src[0:width, :] = out_w[...]
    pack.src[width : width + 8, :] = jnp.broadcast_to(bias[...].reshape(1, d), (8, d))


def prepare(info, out_w, bias, up, dn):
    width, d = out_w.shape
    part = up.shape[0] // 4
    view = lambda ref, info: ref.at[pl.ds(pl.multiple_of((2 * info[3] + info[4]) * part, part), part)]
    ins = [whole(out_w), bias, (up, ((part, d), view)), (dn, ((part, d), view))]
    return call("prepare", prepare_kernel, info, ins, [[SDS((width + 8, d), bf16)]] + [[SDS((part, d), bf16)]] * 2)


def head_cols(a, h, extra=()):
    lane = lax.broadcasted_iota(jnp.int32, a.shape, 1)
    out = jnp.where((lane >= HEAD * h) & (lane < HEAD * (h + 1)), a, jnp.zeros_like(a))
    for i, e in enumerate(extra):
        out = jnp.where(lane == WIDE + i, e, out)
    return out


def tail_cols(rows, values):
    lane = lax.broadcasted_iota(jnp.int32, (rows, LANES - WIDE), 1)
    out = jnp.zeros((rows, LANES - WIDE), f32)
    for i, v in enumerate(values):
        out = jnp.where(lane == i, v, out)
    return out.astype(bf16)


def attend_fwd_kernel(info, x_hbm, w_ref, b_ref, *rest):
    far, outs = rest[:5], rest[5:9]
    x_all, *near, v_t, s_all, sem_in, sem_out = rest[9:]
    q_all, k_all, v_all, lse_all, c_all = near
    me = info[2]
    batch, peers, width, block = c_all.shape
    seq = peers * block
    heads = width // HEAD

    def fetch(s):
        return pltpu.make_async_copy(x_hbm.at[s], x_all.at[s], sem_in.at[s])

    def flush(s, i):
        return pltpu.make_async_copy(near[i].at[s], far[i].at[s], sem_out.at[s, i])

    for s in range(batch):
        fetch(s).start()
    w = w_ref()

    def one_sequence(s, carry):
        length = info[7][s]
        fetch(s).wait()
        x = x_all[s]
        k_all[s, :, 0:WIDE] = mm(x, w[1], NT).astype(bf16)
        row = lax.broadcasted_iota(jnp.int32, (seq, 1), 0)
        k_all[s, :, WIDE:LANES] = tail_cols(seq, (jnp.where(row < length, 0.0, -1e30),))
        q = mm(x, w[0], NT) + b_ref[0:1, :].astype(f32)
        q_all[s, :, 0:WIDE] = q.astype(bf16) * jnp.asarray(0.125, bf16)
        q_all[s, :, WIDE:LANES] = tail_cols(seq, (1.0,))
        v = (mm(x, w[2], NT) + b_ref[1:2, :].astype(f32)).astype(bf16)
        v_all[s] = v
        v_t[...] = v.T
        for i in range(3):
            flush(s, i).start()

        def two_blocks(n, carry):
            qb = q_all[s, pl.ds(pl.multiple_of(n * 2 * block, 2 * block), 2 * block), :]
            one = jnp.ones_like(qb[:, 0:1])
            for h in range(heads):
                s_all[h] = mm(k_all[s], head_cols(qb, h, (one,)), NT)
            for h in range(heads):
                top = jnp.max(s_all[h], axis=0, keepdims=True)
                p = jnp.exp(s_all[h] - top)
                total = jnp.sum(p, axis=0, keepdims=True)
                rows = slice(HEAD * h, HEAD * (h + 1))
                out = (mm(v_t[rows, :], p.astype(bf16)) * (1.0 / total)).astype(bf16)
                lse = top + jnp.log(total)
                for j in range(2):
                    cols = slice(block * j, block * (j + 1))
                    c_all[s, 2 * n + j, rows, :] = out[:, cols]
                    lse_all[s, 2 * n + j, h : h + 1, :] = lse[:, cols]
            return carry

        lax.fori_loop(0, peers // 2, two_blocks, 0)
        for i in range(3, 5):
            flush(s, i).start()
        for k, out in enumerate(outs):
            out.src[s] = c_all[s, me ^ k]
        return carry

    lax.fori_loop(0, batch, one_sequence, 0)
    for out in outs:
        out.start()
    for s in range(batch):
        for i in range(5):
            flush(s, i).wait()


def attend_fwd(info, inputs, w_t, bias, peers):
    batch, seq, d = inputs.shape
    width = w_t.shape[1]
    block = seq // peers
    far = [SDS((batch, seq, LANES), bf16)] * 2 + [SDS((batch, seq, width), bf16)]
    far += [SDS((batch, peers, 8, block), f32), SDS((batch, peers, width, block), bf16)]
    scratch = [pltpu.VMEM(inputs.shape, bf16), *[pltpu.VMEM(o.shape, o.dtype) for o in far]]
    scratch += [pltpu.VMEM((width, seq), bf16), pltpu.VMEM((width // HEAD, seq, 2 * block), f32)]
    scratch += [pltpu.SemaphoreType.DMA((batch,)), pltpu.SemaphoreType.DMA((batch, 5))]
    return call(
        "attend_fwd",
        attend_fwd_kernel,
        info,
        [Raw(inputs), whole(w_t), bias],
        [Raw(o) for o in far] + [[SDS((batch, width, block), bf16)]] * peers,
        scratch,
    )


def nth(at, ref, info):
    return ref.at[at]


def of_sequence(a):
    return (a, (a.shape[1:], lambda ref, info: ref.at[info[5]]))


def attend_bwd_kernel(info, x_ref, q_in, k_in, v_in, lse_in, c_in, *rest):
    w_ref = x_ref
    peers = 4
    gs, rest = rest[:peers], rest[peers:]
    keep, send, low_out, db_ref, dq_t, dk, dv, k_t, g_ref = rest
    low = low_out.src
    length = info[6]
    me = info[2]
    k_ref, q_ref, v_ref = k_in(), q_in(), v_in()
    lse_ref, c_ref = lse_in(), c_in()
    _, width, block = c_ref.shape
    heads = width // HEAD
    k_t[...] = k_ref[:, 0:WIDE].T
    dk[...] = jnp.zeros_like(dk)
    dv[...] = jnp.zeros_like(dv)
    for k in range(peers):
        g_ref[me ^ k] = gs[k]()[...]

    def one_block(s, carry):
        at = pl.multiple_of(s * block, block)

        @pl.when(at >= length)
        def _():
            dq_t[:, pl.ds(at, block)] = jnp.zeros((width, block), f32)

        @pl.when(at < length)
        def _():
            qb = q_ref[pl.ds(at, block), :]
            g_t = g_ref[s]
            g = g_t.T
            prod_t = g_t.astype(f32) * c_ref[s].astype(f32)
            for h in range(heads):
                rows = slice(HEAD * h, HEAD * (h + 1))
                qh = head_cols(qb, h)
                gh = head_cols(g, h)
                scores = mm(k_ref[...], qh, NT)
                row = lax.broadcasted_iota(jnp.int32, scores.shape, 0)
                p = jnp.where(row < length, jnp.exp(scores - lse_ref[s, h : h + 1, :]), 0.0)
                dp = mm(v_ref[...], gh, NT)
                inner = jnp.sum(prod_t[rows], axis=0, keepdims=True)
                ds = (p * (dp - inner)).astype(bf16)
                dv[...] += mm(p.astype(bf16), gh)
                dk[...] += mm(ds, qh)
                dq_t[rows, pl.ds(at, block)] = mm(k_t[rows, :], ds) * 0.125

        return carry

    lax.fori_loop(0, peers, one_block, 0)
    low[0] = dq_t[...].T.astype(bf16)
    low[1] = dk[:, 0:WIDE].astype(bf16)
    low[2] = dv[...].astype(bf16)
    w = w_ref()
    for s in range(peers):
        at = pl.multiple_of((me ^ s) * block, block)
        total = sum(mm(low[i, pl.ds(at, block), :], w[i]) for i in range(3))
        (send if s % 2 else keep).src[s // 2] = total.astype(bf16)
    send.start()
    keep.start()
    db_ref[...] = jnp.concatenate([rowsum(low[i].astype(f32)) for i in (0, 2)], axis=1)


def attend_bwd(which, info, w_t, q, k, v, lse, c, gs, d):
    _, peers, width, block = c.shape
    seq = peers * block
    outs = [[SDS((2, block, d), bf16)]] * 2 + [[SDS((3, seq, width), bf16)], SDS((1, 2 * width), f32)]
    scratch = [
        pltpu.VMEM((width, seq), f32),
        pltpu.VMEM((seq, LANES), f32),
        pltpu.VMEM((seq, width), f32),
        pltpu.VMEM((width, seq), bf16),
        pltpu.VMEM((peers, width, block), bf16),
    ]
    ins = [whole(w_t)] + [of_sequence(a) for a in (q, k, v, lse, c)]
    ins += [(g, ((width, block), lambda ref, info: ref.at[info[5]]), None) for g in gs]
    return call("attend_bwd", attend_bwd_kernel, info, ins, outs, scratch, which=which, cost=10**10)


def project_grads_kernel(info, x0, low0, x1, low1, db0, db1, keep, send, db_ref, dw, acc, pair, *, parts):
    _, d, width = dw.shape
    x, low = x0(), low0()
    for i in range(3):
        acc[i] = mm(low[i].T, x[...])
    x, low = x1(), low1()
    for i in range(3):
        dw[i] = (acc[i] + mm(low[i].T, x[...])).T
    rows = d // parts
    half = 3 * rows // 2
    for b in range(parts):
        flat = dw[:, b * rows : (b + 1) * rows, :].reshape(3 * rows, width)
        flat = jnp.concatenate([flat[0:half], flat[half : 2 * half]], axis=1).astype(bf16)
        pair[(b & 1) ^ info[3], (b >> 1) * half : (b // 2 + 1) * half, :] = flat
    n = keep.src.shape[0]
    send.src[0:n, :] = pair[1]
    keep.src[...] = pair[0]
    db = db0[...] + db1[...]
    db_ref[...] = db
    high = db.astype(bf16)
    send.src[n : n + 8, :] = jnp.concatenate(
        [high, (db - high.astype(f32)).astype(bf16), jnp.zeros((6, 2 * width), bf16)], axis=0
    )
    send.start()


def gelu_parts(h):
    t = 1.0 / (1.0 + (0.3275911 * 0.7071067811865476) * jnp.abs(h))
    poly = t * (0.127414796 + t * (-0.142248368 + t * (0.7107068705 + t * (-0.7265760135 + t * 0.5307027145))))
    bell = jnp.exp2((-0.5 * 1.4426950408889634) * (h * h))
    tail = poly * bell
    cum = jnp.where(h < 0, tail, 1.0 - tail)
    return h * cum, cum + h * (bell * 0.3989422804014327)


def norm_parts(v):
    center = v - jnp.mean(v, axis=1, keepdims=True)
    r = lax.rsqrt(jnp.mean(center * center, axis=1, keepdims=True) + 1e-12)
    return center * r, r


def norm_back(u, gain, nv, r):
    gu = u * gain
    return r * (gu - jnp.mean(gu, axis=1, keepdims=True) - nv * jnp.mean(gu * nv, axis=1, keepdims=True))


def rowsum(v):
    return jnp.sum(v, axis=0, keepdims=True)


def first_norm_kernel(info, x_in, par, *rest):
    nv_ref, r_ref, low0, low1, low = rest[8:]
    cs, packs = [c() for c in rest[:4]], [p() for p in rest[4:8]]
    x_ref = x_in()
    batch, rows = x_ref.shape[:2]
    width = cs[0].shape[1]

    def one_sequence(s, carry):
        here = pl.ds(pl.multiple_of(s * rows, rows), rows)
        total = par[0:1, :] + x_ref[s].astype(f32)
        for k in range(4):
            total = total + mm(cs[k][s], packs[k][0:width, :], TN)
        nv, r = norm_parts(total)
        nv_ref[here, :] = nv
        r_ref[here, :] = r
        low[s] = (nv * par[1:2, :] + par[2:3, :]).astype(bf16)
        return carry

    lax.fori_loop(0, batch, one_sequence, 0)
    low0[...] = low[0]
    low1[...] = low[1]


def feed_kernel(info, *rest, width, far):
    low, (pack, *rest) = rest[:4], rest[4:]
    if far:
        u_a, u_b, d_a, d_b, p_own, p_sib, act_out, slope_out, own, sib, both, up, dn = rest
        assemble(info[3], info[4], up, u_a(), u_b(), False)
    else:
        u_in, d_in, act_out, slope_out, own, sib, both = rest
        up = u_in()
    act, slope = ref(act_out), ref(slope_out)
    units = up.shape[1]
    bias = pack()
    step = 256
    n = low[0].shape[0]
    for i, x in enumerate(low):
        both[i // 2, (i % 2) * n : (i % 2 + 1) * n, :] = x[...]

    def side(j, carry):
        def chunk(n, carry):
            cols = pl.ds(pl.multiple_of(n * step, step), step)
            hidden = mm(both[j], up[:, cols]) + bias[width : width + 1, cols].astype(f32)
            a, g = gelu_parts(hidden)
            act[j, :, cols] = a.astype(bf16)
            slope[j, :, cols] = g.astype(bf16)
            return carry

        return lax.fori_loop(0, units // step, chunk, carry)

    lax.fori_loop(0, 2, side, 0)
    if far:
        assemble(info[3], info[4], dn, d_a(), d_b(), True)
        sib[...] = (p_sib[...] + mm(act[1], dn[...])).astype(bf16)
        own[...] = p_own[...] + mm(act[0], dn[...])
    else:
        dn = d_in()
        own[...] = mm(act[0], dn[...])
        sib[...] = mm(act[1], dn[...])


def assemble(x, z, dst, a, b, z_first):
    part = a.shape[0] // 2
    for src, other in ((a, 0), (b, 1)):
        for i in range(2):
            flips = (other, i) if z_first else (i, other)
            at = 2 * (x ^ flips[0]) + (z ^ flips[1])
            dst[pl.ds(pl.multiple_of(at * part, part), part)] = src[i * part : (i + 1) * part]


def second_norm_kernel(info, cot_in, par, nv_in, own, got, outs, gsec_out, gs_low, small):
    cot, nv_ref, gsec = cot_in(), ref(nv_in), ref(gsec_out)
    batch, rows, d = cot.shape

    def one_sequence(s, sums):
        here = pl.ds(pl.multiple_of(s * rows, rows), rows)
        total = own[here, :] + got[here, :].astype(f32) + par[3:4, :] + (nv_ref[here, :] * par[1:2, :] + par[2:3, :])
        nv, r = norm_parts(total)
        outs.src[s] = (nv * par[4:5, :] + par[5:6, :]).astype(bf16)
        at = info[2] * rows + lax.broadcasted_iota(jnp.int32, (rows, 1), 0)
        seed = jnp.where(at < info[7][s], cot[s].astype(f32), 0.0)
        g = norm_back(seed, par[4:5, :], nv, r)
        gsec[here, :] = g
        gs_low[here, :] = g.astype(bf16)
        return tuple(a + rowsum(b) for a, b in zip(sums, (g, seed * nv, seed)))

    sums = lax.fori_loop(0, batch, one_sequence, (jnp.zeros((1, d), f32),) * 3)
    small[...] = jnp.concatenate([*sums, jnp.zeros((5, d), f32)], axis=0)


def feed_back_kernel(info, gs, gs2, slope0, slope1, up0, dn0, u_a, u_b, d_a, d_b, gh_out, own, sib, ub, sides, up2, dn2):
    gh = ref(gh_out)
    units = up0.dst.shape[1]
    ub[...] = jnp.zeros_like(ub)
    sides[0] = gs[...]
    sides[1] = gs2[...]
    step = 256
    for k, slope in enumerate((ref(slope0), ref(slope1))):
        if k:
            assemble(info[3], info[4], dn2, d_a(), d_b(), True)
            dn = dn2
        else:
            dn = dn0()

        def side(j, carry):
            def chunk(n, carry):
                cols = pl.ds(pl.multiple_of(n * step, step), step)
                ga = mm(sides[j], dn[cols, :], NT)
                h = (ga * slope[j, :, cols].astype(f32)).astype(bf16)
                gh[k, j, :, cols] = h
                ub[k : k + 1, cols] += rowsum(h.astype(f32))
                return carry

            return lax.fori_loop(0, units // step, chunk, carry)

        lax.fori_loop(0, 2, side, 0)
    assemble(info[3], info[4], up2, u_a(), u_b(), False)
    up = up0()
    sib[...] = (mm(gh[0, 1], up[...], NT) + mm(gh[1, 1], up2[...], NT)).astype(bf16)
    own[...] = mm(gh[0, 0], up[...], NT) + mm(gh[1, 0], up2[...], NT)


def first_back_kernel(info, par, nv_in, r_ref, own, got, gsec_in, small2, *rest):
    cs, packs = [c() for c in rest[:4]], rest[4:8]
    gfi, g0, g1, g2, g3, okeep, osend, small, ga_low = rest[8:]
    nv_ref, gsec = ref(nv_in), ref(gsec_in)
    packs = [p() for p in packs]
    n, d = own.shape
    rows = n // 2
    width = cs[0].shape[1]

    def one_sequence(s, sums):
        here = pl.ds(pl.multiple_of(s * rows, rows), rows)
        u = own[here, :] + got[here, :].astype(f32) + gsec[here, :]
        nv = nv_ref[here, :]
        g = norm_back(u, par[1:2, :], nv, r_ref[here, :])
        gfi.src[here, :] = g
        low = g.astype(bf16)
        ga_low[here, :] = low
        for k, out in enumerate((g0, g1, g2, g3)):
            out.src[s] = mm(packs[k][0:width, :], low, NT).astype(bf16)
        return tuple(a + rowsum(b) for a, b in zip(sums, (g, u * nv, u)))

    sums = lax.fori_loop(0, 2, one_sequence, (jnp.zeros((1, d), f32),) * 3)
    for out in (g3, g2, g1, g0, gfi):
        out.start()
    for k in range(4):
        total = mm(cs[k][0], ga_low[0:rows, :]) + mm(cs[k][1], ga_low[rows:n, :])
        (osend if k % 2 else okeep).src[k // 2, 0:width, :] = total.astype(bf16)
    both = jnp.concatenate([*sums, small2[0:3, :], jnp.zeros((2, d), f32)], axis=0)
    small[...] = both
    high = both.astype(bf16)
    osend.src[0, width : width + 8, :] = high
    osend.src[1, width : width + 8, :] = (both - high.astype(f32)).astype(bf16)


def down_grads_kernel(info, act0, act1, gs, gs2, far_keep, keep, send, scr, *, parts):
    units = act0.shape[2]
    block = units // parts
    step = 384
    for k, (act, mine) in enumerate(((act1, far_keep), (act0, keep))):

        def chunk(m, carry):
            cols = pl.ds(pl.multiple_of(m * step, step), step)
            total = mm(act[0, :, cols], gs[...], TN) + mm(act[1, :, cols], gs2[...], TN)
            total = total.astype(bf16)
            for i in range(step // block):
                scr[(i & 1) ^ info[3], m * (step // block // 2) + (i >> 1)] = total[i * block : (i + 1) * block]
            return carry

        lax.fori_loop(0, units // step, chunk, 0)
        send.src[k] = scr[1]
        mine.src[...] = scr[0]
    send.start()


def up_grads_kernel(info, *rest, parts, width):
    lows, (gh_in, okeep, ogot, small, ub, far_keep, far_send, keep, send, sums, scr, both_low) = rest[:4], rest[4:]
    n = lows[0].shape[0]
    for i, x in enumerate(lows):
        both_low[i // 2, (i % 2) * n : (i % 2 + 1) * n, :] = x[...]
    low, low2 = both_low.at[0], both_low.at[1]
    gh = ref(gh_in)
    units = low.shape[1]
    block = units // parts
    extra = width // parts
    joint = block + extra
    n = parts // 2 * joint
    step = 384
    got = ogot()
    both = small[...] + got[0, width : width + 8, :].astype(f32) + got[1, width : width + 8, :].astype(f32)
    both = jnp.concatenate([both[0:6], ub[0:2, :]], axis=0)
    sums[...] = both
    high = both.astype(bf16)
    far_send.src[n : n + 8, :] = high
    far_send.src[n + 8 : n + 16, :] = (both - high.astype(f32)).astype(bf16)
    for k, mine, theirs in ((1, far_keep, far_send), (0, keep, send)):

        def chunk(m, carry):
            cols = pl.ds(pl.multiple_of(m * step, step), step)
            total = mm(low[:, cols], gh[k, 0], TN) + mm(low2[:, cols], gh[k, 1], TN)
            total = total.astype(bf16)
            for i in range(step // block):
                at = (m * (step // block // 4) + (i >> 2)) * 2 + (i & 1)
                scr[((i >> 1) & 1) ^ info[4], at, 0:block, :] = total[i * block : (i + 1) * block]
            return carry

        lax.fori_loop(0, units // step, chunk, 0)
        o = (okeep()[k, 0:width, :].astype(f32) + got[k, 0:width, :].astype(f32)).astype(bf16)
        for b in range(parts):
            at = (b >> 2) * 2 + (b & 1)
            scr[((b >> 1) & 1) ^ info[4], at, block:joint, :] = o[b * extra : (b + 1) * extra]
        for b in range(parts // 2):
            theirs.src[b * joint : (b + 1) * joint, :] = scr[1, b]
            mine.src[b * joint : (b + 1) * joint, :] = scr[0, b]
        theirs.start()
        mine.start()


def swap(x, axis, bit):
    size = lax.axis_size(axis)
    return lax.ppermute(x, axis, [(i, i ^ bit) for i in range(size)])


def summed(parts):
    return sum(p.astype(f32) for p in parts)


def spread(array, axis, parts):
    bits = parts.bit_length() - 1
    return array.reshape(*array.shape[:axis], *([2] * bits), array.shape[axis] // parts, *array.shape[axis + 1 :])


def halve_sum(terms, axis, mine):
    other = [lax.dynamic_index_in_dim(t, 1 - mine, axis, keepdims=False) for t in terms]
    kept = [lax.dynamic_index_in_dim(t, mine, axis, keepdims=False) for t in terms]
    return kept, summed(other).astype(bf16)


def halve(terms, axis, bit, mine):
    other = [lax.dynamic_index_in_dim(t, 1 - mine, axis, keepdims=False) for t in terms]
    kept = [lax.dynamic_index_in_dim(t, mine, axis, keepdims=False) for t in terms]
    other = summed(other).astype(bf16)
    return kept + [swap(other, "dp", bit)], other


def body(
    inputs,
    cotangent,
    lengths,
    qkv_weight,
    qkv_bias,
    out_weight,
    out_bias,
    first_gain,
    first_shift,
    up_weight,
    up_bias,
    down_weight,
    down_bias,
    second_gain,
    second_shift,
):
    batch, seq, d = inputs.shape
    rows = cotangent.shape[1]
    n = batch * rows
    width = out_weight.shape[0]
    units = up_weight.shape[1]
    peers = lax.axis_size("tensor")
    parts = lax.axis_size("dp")
    bits = parts.bit_length() - 1
    t = lax.axis_index("tensor")
    dp = lax.axis_index("dp")
    bit_of = [(dp >> i) & 1 for i in range(bits)]
    info = lengths
    par = jnp.concatenate([out_bias, first_gain, first_shift, down_bias, second_gain, second_shift])
    par = par.reshape(6, d).astype(f32)
    w_t = jnp.transpose(qkv_weight, (1, 2, 0))
    pack, u_part, d_part = prepare(info, out_weight, up_bias, up_weight, down_weight)
    pack2 = swap(pack, "tensor", 2)
    pack1 = swap(pack, "tensor", 1)
    u_part = swap(u_part, "tensor", 2)
    d_part = swap(d_part, "tensor", 2)
    q, k, v, lse, c, *cs = attend_fwd(info, inputs, w_t, qkv_bias, peers)
    saved = (q, k, v, lse, c)
    *cs, pack1, pack2, u_part, d_part = after(*cs, pack1, pack2, u_part, d_part)
    ctx = [cs[0]] + [swap(cs[j], "tensor", j) for j in range(1, peers)]
    u_next, d_next = swap(u_part, "dp", 1), swap(d_part, "dp", 2)
    *ctx, u_next, d_next = after(*ctx, u_next, d_next)
    u2a = jnp.concatenate([u_part, u_next])
    d2a = jnp.concatenate([d_part, d_next])
    pack2, u2a, d2a = after(pack2, u2a, d2a)
    pack3 = swap(pack2, "tensor", 1)
    packs = [pack, pack1, pack2, pack3]
    u2b = swap(u2a, "dp", 2)
    d2b = swap(d2a, "dp", 1)
    far_ctx = [whole(ctx[0])] + [loose(x) for x in ctx[1:]]
    far_packs = [whole(pack)] + [loose(p) for p in packs[1:]]
    share = (inputs, ((batch, rows, d), lambda ref, info: ref.at[:, pl.ds(pl.multiple_of(info[2] * rows, rows), rows), :]))
    nv1, r1, *low = call(
        "first_norm",
        first_norm_kernel,
        info,
        [share, par, *far_ctx, *far_packs],
        [SDS((n, d), f32), SDS((n, 1), f32), SDS((rows, d), bf16), SDS((rows, d), bf16)],
        [pltpu.VMEM((batch, rows, d), bf16)],
        vmem=NEAR,
    )
    low2 = [swap(x, "tensor", 1) for x in low]
    pair = SDS((2, n, units), bf16)
    part = SDS((n, d), f32)
    sides = pltpu.VMEM((2, n, d), bf16)
    act0, slope0, own, sib = call(
        "feed",
        feed_kernel,
        info,
        [*low, *low2, far_packs[0], whole(up_weight), whole(down_weight)],
        [pair, pair, part, part],
        [sides],
        vmem=NEAR,
        width=width,
        far=False,
    )
    halves = [loose(x) for x in (u2a, u2b, d2a, d2b)]
    both = [pltpu.VMEM((d, units), bf16), pltpu.VMEM((units, d), bf16)]
    act1, slope1, own, sib = call(
        "feed",
        feed_kernel,
        info,
        [*low, *low2, far_packs[2], *halves, own, sib],
        [pair, pair, part, SDS((n, d), bf16)],
        [sides, *both],
        vmem=NEAR,
        width=width,
        far=True,
    )
    got = swap(sib, "tensor", 1)
    outputs, gsec, gs_low, small2 = call(
        "second_norm",
        second_norm_kernel,
        info,
        [whole(cotangent), par, nv1, own, got],
        [[SDS((batch, rows, d), bf16)], part, SDS((n, d), bf16), SDS((8, d), f32)],
        vmem=NEAR,
    )
    gs_low2 = swap(gs_low, "tensor", 1)
    gh, own, sib, ub = call(
        "feed_back",
        feed_back_kernel,
        info,
        [gs_low, gs_low2, slope0, slope1, whole(up_weight), whole(down_weight), *halves],
        [SDS((2, 2, n, units), bf16), part, SDS((n, d), bf16), SDS((8, d), f32)],
        [sides, *both],
        vmem=NEAR,
    )
    got = swap(sib, "tensor", 1)
    block = units // parts
    half_shape = (parts // 2, block, d)
    down_far_keep, down_keep, down_send = call(
        "down_grads",
        down_grads_kernel,
        info,
        [act0, act1, gs_low, gs_low2],
        [[SDS(half_shape, bf16)], [SDS(half_shape, bf16)], [SDS((2, *half_shape), bf16)]],
        [pltpu.VMEM((2, *half_shape), bf16)],
        vmem=NEAR,
        parts=parts,
    )
    down_got = swap(down_send, "dp", 1)
    gfi, g0, g1, g2, g3, okeep, osend, small1 = call(
        "first_back",
        first_back_kernel,
        info,
        [par, nv1, r1, own, got, gsec, small2, *far_ctx, *far_packs],
        [
            [part],
            *[[SDS((batch, width, rows), bf16)]] * 4,
            *[[SDS((2, width + 8, d), bf16)]] * 2,
            SDS((8, d), f32),
        ],
        [pltpu.VMEM((n, d), bf16)],
        vmem=NEAR,
    )
    gctx = [g0] + [swap(g, "tensor", j) for j, g in ((1, g1), (2, g2), (3, g3))]
    got_o = swap(osend, "tensor", 1)
    joint = block + width // parts
    cut = parts // 2 * joint
    up_far_keep, up_far_send, up_keep, up_send, small = call(
        "up_grads",
        up_grads_kernel,
        info,
        [*low, *low2, gh, whole(okeep), loose(got_o), small1, ub],
        [
            [SDS((cut, d), bf16)],
            [SDS((cut + 16, d), bf16)],
            [SDS((cut, d), bf16)],
            [SDS((cut, d), bf16)],
            SDS((8, d), f32),
        ],
        [pltpu.VMEM((2, parts // 2, joint, d), bf16), sides],
        vmem=NEAR,
        parts=parts,
        width=width,
    )
    *gctx, up_far_send = after(*gctx, up_far_send)
    up_far_got = swap(up_far_send, "dp", 2)
    *gctx, up_far_keep = after(*gctx, up_far_keep)
    lows, biases, terms_of = [], [], []
    for s in range(batch):
        keep, send, low_grads, db = attend_bwd(s, info, w_t, *saved, gctx, d)
        biases.append(db)
        if s == 0:
            send, up_far_got, down_got = after(send, up_far_got, down_got)
        else:
            send, low_grads, down_y, up_got, up_more, far = after(send, low_grads, down_y, up_got, up_more, far)
            terms_of[0].append(far)
        near = swap(send, "tensor", 1)
        in_sum = summed([keep[1], near[1]]).astype(bf16)
        terms_of.append([keep[0], near[0]])
        if s == 0:
            lows.append(low_grads)
            down_sum = summed([down_far_keep, down_got[0]]).astype(bf16)
            shape = ([2] * (bits - 1)) + [joint, d]
            small = small + pair_sum(up_far_got, cut, 8)
            terms = [x.reshape(shape) for x in (up_far_keep, up_far_got[:cut])]
            up_far_kept, up_far_next = halve_sum(terms, bits - 2, bit_of[0])
            up_far_rows = with_rows(up_far_next, small)
            tied = after(down_sum, up_far_rows, in_sum, up_send, *gctx)
            (down_sum, up_far_rows, in_sum, up_send), gctx = tied[:4], tied[4:]
            down_y = swap(down_sum, "tensor", 2)
            up_got = swap(up_send, "dp", 2)
            up_more = swap(up_far_rows, "dp", 1)
            far = swap(in_sum, "tensor", 2)
    shape = ([2] * (bits - 1)) + [block, d]
    down_terms = [x.reshape(shape) for x in (down_keep, down_got[1], down_y)]
    down_kept, down_next = halve_sum(down_terms, bits - 2, bit_of[1])
    at = up_far_next.size // d
    small = small + pair_sum(up_more, at, 8)
    small = jnp.concatenate([small[0:6], small[7:8], small[6:7]])
    up_y_next = summed(up_far_kept + [up_more[:at].reshape(up_far_next.shape)]).astype(bf16)
    up_y_rows = with_rows(up_y_next, small)
    shape = ([2] * (bits - 1)) + [joint, d]
    up_kept, up_next = halve_sum([x.reshape(shape) for x in (up_keep, up_got)], bits - 2, bit_of[0])
    low_grads, down_next, up_y_rows, up_next = after(low_grads, down_next, up_y_rows, up_next)
    lows.append(low_grads)
    down_more = swap(down_next, "dp", 2)
    up_y = swap(up_y_rows, "tensor", 2)
    up_more = swap(up_next, "dp", 1)
    m = 3 * d // 4
    operands = []
    for s in range(batch):
        operands += [(inputs, (inputs.shape[1:], functools.partial(nth, s))), whole(lows[s])]
    w_keep, w_send, db = call(
        "project_grads",
        project_grads_kernel,
        info,
        [*operands, *biases],
        [[SDS((m, 2 * width), bf16)], [SDS((m + 8, 2 * width), bf16)], SDS((1, 2 * width), f32)],
        [pltpu.VMEM((3, d, width), f32), pltpu.VMEM((3, width, d), f32), pltpu.VMEM((2, m, 2 * width), bf16)],
        parts=parts,
    )
    w_send, down_more, up_y, up_more = after(w_send, down_more, up_y, up_more)
    down_more, up_y, up_more, in_sum = after(down_more, up_y, up_more, in_sum)
    got = swap(w_send, "dp", 1)
    got, in_sum = after(got, in_sum)
    terms_of[1].append(swap(in_sum, "tensor", 2))
    down_terms = down_kept + [down_more]
    at = up_y_next.size // d
    small = jnp.concatenate([small[0:6], small[7:8], small[7:8]]) + pair_sum(up_y, at, 8)
    up_terms = up_kept + [up_more, up_y[:at].reshape(up_y_next.shape)]
    for i in range(2, bits):
        down_terms, sent = halve_sum(down_terms, bits - 1 - i, bit_of[i])
        down_got = swap(sent, "dp", 1 << i)
        up_terms, sent = halve_sum(up_terms, bits - 1 - i, bit_of[i])
        up_got = swap(with_rows(sent, small), "dp", 1 << i)
        if i == bits - 1:
            break
        down_terms, up_terms, small = with_received(down_terms, down_got, up_terms, up_got, sent, small)
    row = 3 * (d // parts) // 2
    at = parts // 2 * row
    shape = ([2] * (bits - 1)) + [row, 2 * width]
    terms = [x.reshape(shape) for x in (w_keep, got[:at])]
    db = db + got[at : at + 1].astype(f32) + got[at + 1 : at + 2].astype(f32)
    for i in range(1, bits):
        kept, rows_sent, more = halve_with(terms, terms[0].ndim - 3, db, "dp", 1 << i, bit_of[i])
        if i == 1:
            kept[-1], down_got, up_got = after(kept[-1], down_got, up_got)
        terms, db = kept, db + more
    down_terms, up_terms, small = with_received(down_terms, down_got, up_terms, up_got, sent, small)
    down_sum = summed(down_terms)
    up_sum = summed(up_terms)
    mine = small
    qkv_sum = summed(terms)
    qkv_sum = jnp.concatenate([qkv_sum[:, :width], qkv_sum[:, width:]], axis=0).reshape(3, -1, width)
    qkv_sum = jnp.transpose(qkv_sum, (1, 0, 2))
    db = db.reshape(2, width)
    input_list = [
        (summed(x) + gfi[s * rows : (s + 1) * rows]).astype(bf16)
        for s, x in enumerate(terms_of)
    ]
    return (
        outputs,
        jnp.stack(input_list, 0),
        qkv_sum,
        db,
        up_sum[block:],
        mine[0],
        mine[1],
        mine[2],
        up_sum[:block],
        mine[6],
        down_sum,
        mine[3],
        mine[4],
        mine[5],
    )


def pair_sum(array, at, n):
    return array[at : at + n].astype(f32) + array[at + n : at + 2 * n].astype(f32)


def with_rows(array, rows):
    flat = array.reshape(-1, array.shape[-1])
    high = rows.astype(bf16)
    low = (rows - high.astype(f32)).astype(bf16)
    return jnp.concatenate([flat, high, low], axis=0)


def halve_with(terms, axis, rows, name, bit, mine):
    other = [lax.dynamic_index_in_dim(t, 1 - mine, axis, keepdims=False) for t in terms]
    kept = [lax.dynamic_index_in_dim(t, mine, axis, keepdims=False) for t in terms]
    other = summed(other).astype(bf16)
    sent = with_rows(other, rows)
    got = swap(sent, name, bit)
    cut = other.size // other.shape[-1]
    return kept + [got[:cut].reshape(other.shape)], sent, pair_sum(got, cut, rows.shape[0])


def with_received(down_terms, down_got, up_terms, up_got, sent, small):
    at = sent.size // sent.shape[-1]
    small = small + pair_sum(up_got, at, small.shape[0])
    return down_terms + [down_got], up_terms + [up_got[:at].reshape(sent.shape)], small


def after(*values):
    return lax.optimization_barrier(values)


def solution(mesh):
    in_specs = (
        P("dp", None, None),
        P("dp", "tensor", None),
        P("dp"),
        P(None, None, "tensor"),
        P(None, "tensor"),
        P("tensor", None),
        P(),
        P(),
        P(),
        P(None, "tensor"),
        P("tensor"),
        P("tensor", None),
        P(),
        P(),
        P(),
    )
    out_specs = (
        P("dp", "tensor", None),
        P("dp", "tensor", None),
        P("dp", None, "tensor"),
        P(None, "tensor"),
        P(("tensor", "dp"), None),
        P(),
        P(),
        P(),
        P("dp", "tensor"),
        P("tensor"),
        P(("tensor", "dp"), None),
        P(),
        P(),
        P(),
    )
    return jax.shard_map(body, mesh=mesh, in_specs=in_specs, out_specs=out_specs, check_vma=False)
```

```python
import functools

import jax
import jax.numpy as jnp
from jax import lax
from jax.experimental import pallas as pl
from jax.experimental.pallas import tpu as pltpu
from jax.sharding import PartitionSpec as P

HEAD = 64
WIDE, LANES = 192, 256
NEAR = 30
NT = (((1,), (1,)), ((), ()))
NN = (((1,), (0,)), ((), ()))
TN = (((0,), (0,)), ((), ()))
bf16 = jnp.bfloat16
f32 = jnp.float32
VM = pl.BlockSpec(memory_space=pltpu.VMEM)
SDS = jax.ShapeDtypeStruct


def mm(a, b, dims=NN):
    return lax.dot_general(a, b, dims, preferred_element_type=f32)


class Fetch:
    def __init__(self, src, dst, sem):
        self.dst, self.copy = dst, pltpu.make_async_copy(src, dst, sem)
        self.copy.start()
        self.waiting = True

    def __call__(self):
        if self.waiting:
            self.copy.wait()
            self.waiting = False
        return self.dst


class Pieces:
    def __init__(self, copies, dst):
        self.copies, self.dst = copies, dst
        for c in copies:
            c.start()

    def __call__(self):
        for c in self.copies:
            c.wait()
        self.copies = []
        return self.dst


def pieces(info, a, b, dst, sem, z_first):
    part = a.shape[0] // 2
    copies = []
    for src, other in ((a, 0), (b, 1)):
        for i in range(2):
            flips = (other, i) if z_first else (i, other)
            at = 2 * (info[3] ^ flips[0]) + (info[4] ^ flips[1])
            rows = pl.ds(pl.multiple_of(at * part, part), part)
            copies.append(pltpu.make_async_copy(src.at[pl.ds(i * part, part)], dst.at[rows], sem.at[len(copies)]))
    return Pieces(copies, dst)


class Flush:
    def __init__(self, src, dst, sem):
        self.src, self.copy = src, pltpu.make_async_copy(src, dst, sem)
        self.started = False

    def start(self):
        if not self.started:
            self.copy.start()
        self.started = True


def call(name, body, info, ins, outs, scratch=(), vmem=58, which=0, cost=1000, **static):
    far_in = [i for i, a in enumerate(ins) if isinstance(a, tuple)]
    pinned = [i for i in far_in if len(ins[i]) == 2]
    far_out = [i for i, o in enumerate(outs) if isinstance(o, list)]
    raw_in = [i for i, a in enumerate(ins) if isinstance(a, Raw)]
    raw_out = [i for i, o in enumerate(outs) if isinstance(o, Raw)]
    pinned += [i for i in raw_in if ins[i].pinned]
    any_in = far_in + raw_in
    arrays = [a[0] if isinstance(a, tuple) else a.value if isinstance(a, Raw) else a for a in ins]
    shapes = [o[0] if isinstance(o, list) else o.value if isinstance(o, Raw) else o for o in outs]
    picked = [a[1] if isinstance(a, tuple) else None for a in ins]
    n_in, n_out = len(ins), len(outs)

    def kernel(lengths_ref, which_ref, *refs):
        dp = lax.axis_index("dp")
        at = which_ref[0]
        info_ref = (lengths_ref[0], lengths_ref[1], lax.axis_index("tensor"), dp & 1, (dp >> 1) & 1, at, lengths_ref[at], lengths_ref)
        in_refs, refs = refs[:n_in], refs[n_in:]
        out_refs, refs = refs[:n_out], refs[n_out:]
        sem, refs = refs[-1], refs[:-1]
        buffers, rest = refs[: len(far_in) + len(far_out)], refs[len(far_in) + len(far_out) :]
        args = list(in_refs)
        for j, i in enumerate(far_in):
            view = picked[i][1]
            args[i] = Fetch(view(in_refs[i], info_ref), buffers[j], sem.at[j])
        results = list(out_refs)
        flushes = []
        for j, i in enumerate(far_out):
            at = len(far_in) + j
            results[i] = Flush(buffers[at], out_refs[i], sem.at[at])
            flushes.append(results[i])
        body(info_ref, *args, *results, *rest, **static)
        for i in far_in:
            args[i]()
        for f in flushes:
            f.start()
        for f in flushes:
            f.copy.wait()

    hbm = pl.BlockSpec(memory_space=pltpu.HBM)
    buffers = [pltpu.VMEM(picked[i][0], arrays[i].dtype) for i in far_in]
    buffers += [pltpu.VMEM(shapes[i].shape, shapes[i].dtype) for i in far_out]
    return pl.pallas_call(
        kernel,
        out_shape=[pltpu.HBM(o.shape, o.dtype) if i in far_out + raw_out else o for i, o in enumerate(shapes)],
        grid_spec=pltpu.PrefetchScalarGridSpec(
            num_scalar_prefetch=2,
            grid=(1,),
            in_specs=[hbm if i in pinned else pl.BlockSpec(memory_space=pl.ANY) if i in any_in else VM for i in range(n_in)],
            out_specs=[hbm if i in far_out + raw_out else VM for i in range(n_out)],
            scratch_shapes=[*buffers, *scratch, pltpu.SemaphoreType.DMA((max(1, len(far_in) + len(far_out)),))],
        ),
        compiler_params=pltpu.CompilerParams(vmem_limit_bytes=vmem << 20),
        cost_estimate=pl.CostEstimate(flops=cost, bytes_accessed=1000, transcendentals=0),
        name=name,
    )(info, jnp.full((1,), which, jnp.int32), *[pltpu.with_memory_space_constraint(a, pltpu.HBM) if i in pinned else a for i, a in enumerate(arrays)])


class Raw:
    def __init__(self, value, pinned=True):
        self.value, self.pinned = value, pinned


def ref(x):
    return x() if isinstance(x, Fetch) else x.src if isinstance(x, Flush) else x


def whole(a):
    return (a, (a.shape, lambda ref, info: ref))


def loose(a):
    return (*whole(a), None)


def prepare_kernel(info, out_in, bias, up_in, dn_in, pack, up_half, dn_half):
    for src, dst in ((up_in, up_half), (dn_in, dn_half)):
        dst.src[...] = src()[...]
        dst.start()
    out_w = out_in()
    width, d = out_w.shape
    pack.src[0:width, :] = out_w[...]
    pack.src[width : width + 8, :] = jnp.broadcast_to(bias[...].reshape(1, d), (8, d))


def prepare(info, out_w, bias, up, dn):
    width, d = out_w.shape
    part = up.shape[0] // 4
    view = lambda ref, info: ref.at[pl.ds(pl.multiple_of((2 * info[3] + info[4]) * part, part), part)]
    ins = [whole(out_w), bias, (up, ((part, d), view)), (dn, ((part, d), view))]
    return call("prepare", prepare_kernel, info, ins, [[SDS((width + 8, d), bf16)]] + [[SDS((part, d), bf16)]] * 2)


def head_cols(a, h, extra=()):
    lane = lax.broadcasted_iota(jnp.int32, a.shape, 1)
    out = jnp.where((lane >= HEAD * h) & (lane < HEAD * (h + 1)), a, jnp.zeros_like(a))
    for i, e in enumerate(extra):
        out = jnp.where(lane == WIDE + i, e, out)
    return out


def tail_cols(rows, values):
    lane = lax.broadcasted_iota(jnp.int32, (rows, LANES - WIDE), 1)
    out = jnp.zeros((rows, LANES - WIDE), f32)
    for i, v in enumerate(values):
        out = jnp.where(lane == i, v, out)
    return out.astype(bf16)


def attend_fwd_kernel(info, x_hbm, w_ref, b_ref, *rest):
    far, outs = rest[:5], rest[5:9]
    x_all, *near, v_t, s_all, sem_in, sem_out = rest[9:]
    q_all, k_all, v_all, lse_all, c_all = near
    me = info[2]
    batch, peers, width, block = c_all.shape
    seq = peers * block
    heads = width // HEAD

    def fetch(s):
        return pltpu.make_async_copy(x_hbm.at[s], x_all.at[s], sem_in.at[s])

    def flush(s, i):
        return pltpu.make_async_copy(near[i].at[s], far[i].at[s], sem_out.at[s, i])

    for s in range(batch):
        fetch(s).start()
    w = w_ref()

    def one_sequence(s, carry):
        length = info[7][s]
        fetch(s).wait()
        x = x_all[s]
        k_all[s, :, 0:WIDE] = mm(x, w[1], NT).astype(bf16)
        row = lax.broadcasted_iota(jnp.int32, (seq, 1), 0)
        k_all[s, :, WIDE:LANES] = tail_cols(seq, (jnp.where(row < length, 0.0, -1e30),))
        q = mm(x, w[0], NT) + b_ref[0:1, :].astype(f32)
        q_all[s, :, 0:WIDE] = q.astype(bf16) * jnp.asarray(0.125, bf16)
        q_all[s, :, WIDE:LANES] = tail_cols(seq, (1.0,))
        v = (mm(x, w[2], NT) + b_ref[1:2, :].astype(f32)).astype(bf16)
        v_all[s] = v
        v_t[...] = v.T
        for i in range(3):
            flush(s, i).start()

        def two_blocks(n, carry):
            qb = q_all[s, pl.ds(pl.multiple_of(n * 2 * block, 2 * block), 2 * block), :]
            one = jnp.ones_like(qb[:, 0:1])
            for h in range(heads):
                s_all[h] = mm(k_all[s], head_cols(qb, h, (one,)), NT)
            for h in range(heads):
                top = jnp.max(s_all[h], axis=0, keepdims=True)
                p = jnp.exp(s_all[h] - top)
                total = jnp.sum(p, axis=0, keepdims=True)
                rows = slice(HEAD * h, HEAD * (h + 1))
                out = (mm(v_t[rows, :], p.astype(bf16)) * (1.0 / total)).astype(bf16)
                lse = top + jnp.log(total)
                for j in range(2):
                    cols = slice(block * j, block * (j + 1))
                    c_all[s, 2 * n + j, rows, :] = out[:, cols]
                    lse_all[s, 2 * n + j, h : h + 1, :] = lse[:, cols]
            return carry

        lax.fori_loop(0, peers // 2, two_blocks, 0)
        for i in range(3, 5):
            flush(s, i).start()
        for k, out in enumerate(outs):
            out.src[s] = c_all[s, me ^ k]
        return carry

    lax.fori_loop(0, batch, one_sequence, 0)
    for out in outs:
        out.start()
    for s in range(batch):
        for i in range(5):
            flush(s, i).wait()


def attend_fwd(info, inputs, w_t, bias, peers):
    batch, seq, d = inputs.shape
    width = w_t.shape[1]
    block = seq // peers
    far = [SDS((batch, seq, LANES), bf16)] * 2 + [SDS((batch, seq, width), bf16)]
    far += [SDS((batch, peers, 8, block), f32), SDS((batch, peers, width, block), bf16)]
    scratch = [pltpu.VMEM(inputs.shape, bf16), *[pltpu.VMEM(o.shape, o.dtype) for o in far]]
    scratch += [pltpu.VMEM((width, seq), bf16), pltpu.VMEM((width // HEAD, seq, 2 * block), f32)]
    scratch += [pltpu.SemaphoreType.DMA((batch,)), pltpu.SemaphoreType.DMA((batch, 5))]
    return call(
        "attend_fwd",
        attend_fwd_kernel,
        info,
        [Raw(inputs), whole(w_t), bias],
        [Raw(o) for o in far] + [[SDS((batch, width, block), bf16)]] * peers,
        scratch,
    )


def nth(at, ref, info):
    return ref.at[at]


def of_sequence(a):
    return (a, (a.shape[1:], lambda ref, info: ref.at[info[5]]))


def attend_bwd_kernel(info, x_ref, q_in, k_in, v_in, lse_in, c_in, *rest):
    w_ref = x_ref
    peers = 4
    gs, rest = rest[:peers], rest[peers:]
    keep, send, low_out, db_ref, dq_t, dk, dv, k_t, g_ref = rest
    low = low_out.src
    length = info[6]
    me = info[2]
    k_ref, q_ref, v_ref = k_in(), q_in(), v_in()
    lse_ref, c_ref = lse_in(), c_in()
    _, width, block = c_ref.shape
    heads = width // HEAD
    k_t[...] = k_ref[:, 0:WIDE].T
    dk[...] = jnp.zeros_like(dk)
    dv[...] = jnp.zeros_like(dv)
    for k in range(peers):
        g_ref[me ^ k] = gs[k]()[...]

    def one_block(s, carry):
        at = pl.multiple_of(s * block, block)

        @pl.when(at >= length)
        def _():
            dq_t[:, pl.ds(at, block)] = jnp.zeros((width, block), f32)

        @pl.when(at < length)
        def _():
            qb = q_ref[pl.ds(at, block), :]
            g_t = g_ref[s]
            g = g_t.T
            prod_t = g_t.astype(f32) * c_ref[s].astype(f32)
            for h in range(heads):
                rows = slice(HEAD * h, HEAD * (h + 1))
                qh = head_cols(qb, h)
                gh = head_cols(g, h)
                scores = mm(k_ref[...], qh, NT)
                row = lax.broadcasted_iota(jnp.int32, scores.shape, 0)
                p = jnp.where(row < length, jnp.exp(scores - lse_ref[s, h : h + 1, :]), 0.0)
                dp = mm(v_ref[...], gh, NT)
                inner = jnp.sum(prod_t[rows], axis=0, keepdims=True)
                ds = (p * (dp - inner)).astype(bf16)
                dv[...] += mm(p.astype(bf16), gh)
                dk[...] += mm(ds, qh)
                dq_t[rows, pl.ds(at, block)] = mm(k_t[rows, :], ds) * 0.125

        return carry

    lax.fori_loop(0, peers, one_block, 0)
    low[0] = dq_t[...].T.astype(bf16)
    low[1] = dk[:, 0:WIDE].astype(bf16)
    low[2] = dv[...].astype(bf16)
    w = w_ref()
    for s in range(peers):
        at = pl.multiple_of((me ^ s) * block, block)
        total = sum(mm(low[i, pl.ds(at, block), :], w[i]) for i in range(3))
        (send if s % 2 else keep).src[s // 2] = total.astype(bf16)
    send.start()
    keep.start()
    db_ref[...] = jnp.concatenate([rowsum(low[i].astype(f32)) for i in (0, 2)], axis=1)


def attend_bwd(which, info, w_t, q, k, v, lse, c, gs, d):
    _, peers, width, block = c.shape
    seq = peers * block
    outs = [[SDS((2, block, d), bf16)]] * 2 + [[SDS((3, seq, width), bf16)], SDS((1, 2 * width), f32)]
    scratch = [
        pltpu.VMEM((width, seq), f32),
        pltpu.VMEM((seq, LANES), f32),
        pltpu.VMEM((seq, width), f32),
        pltpu.VMEM((width, seq), bf16),
        pltpu.VMEM((peers, width, block), bf16),
    ]
    ins = [whole(w_t)] + [of_sequence(a) for a in (q, k, v, lse, c)]
    ins += [(g, ((width, block), lambda ref, info: ref.at[info[5]]), None) for g in gs]
    return call("attend_bwd", attend_bwd_kernel, info, ins, outs, scratch, which=which, cost=2 * 10**10)


def project_grads_kernel(info, x0, low0, x1, low1, db0, db1, keep, send, db_ref, dw, acc, pair, *, parts):
    _, d, width = dw.shape
    x, low = x0(), low0()
    for i in range(3):
        acc[i] = mm(low[i].T, x[...])
    x, low = x1(), low1()
    for i in range(3):
        dw[i] = (acc[i] + mm(low[i].T, x[...])).T
    rows = d // parts
    half = 3 * rows // 2
    for b in range(parts):
        flat = dw[:, b * rows : (b + 1) * rows, :].reshape(3 * rows, width)
        flat = jnp.concatenate([flat[0:half], flat[half : 2 * half]], axis=1).astype(bf16)
        pair[(b & 1) ^ info[3], (b >> 1) * half : (b // 2 + 1) * half, :] = flat
    n = keep.src.shape[0]
    send.src[0:n, :] = pair[1]
    keep.src[...] = pair[0]
    db = db0[...] + db1[...]
    db_ref[...] = db
    high = db.astype(bf16)
    send.src[n : n + 8, :] = jnp.concatenate(
        [high, (db - high.astype(f32)).astype(bf16), jnp.zeros((6, 2 * width), bf16)], axis=0
    )
    send.start()


def gelu_parts(h):
    den = 1.0 + (0.3275911 * 0.7071067811865476) * jnp.abs(h)
    t = pl.reciprocal(den, approx=True)
    t = t * (2.0 - den * t)
    t = t * (2.0 - den * t)
    poly = t * (0.127414796 + t * (-0.142248368 + t * (0.7107068705 + t * (-0.7265760135 + t * 0.5307027145))))
    bell = jnp.exp2((-0.5 * 1.4426950408889634) * (h * h))
    tail = poly * bell
    cum = jnp.where(h < 0, tail, 1.0 - tail)
    return h * cum, cum + h * (bell * 0.3989422804014327)


def norm_parts(v):
    center = v - jnp.mean(v, axis=1, keepdims=True)
    r = lax.rsqrt(jnp.mean(center * center, axis=1, keepdims=True) + 1e-12)
    return center * r, r


def norm_back(u, gain, nv, r):
    gu = u * gain
    return r * (gu - jnp.mean(gu, axis=1, keepdims=True) - nv * jnp.mean(gu * nv, axis=1, keepdims=True))


def rowsum(v):
    return jnp.sum(v, axis=0, keepdims=True)


def first_norm_kernel(info, x_in, par, *rest):
    nv_ref, r_ref, low0, low1, low = rest[8:]
    cs, packs = [c() for c in rest[:4]], [p() for p in rest[4:8]]
    x_ref = x_in()
    batch, rows = x_ref.shape[:2]
    width = cs[0].shape[1]

    def one_sequence(s, carry):
        here = pl.ds(pl.multiple_of(s * rows, rows), rows)
        total = par[0:1, :] + x_ref[s].astype(f32)
        for k in range(4):
            total = total + mm(cs[k][s], packs[k][0:width, :], TN)
        nv, r = norm_parts(total)
        nv_ref[here, :] = nv
        r_ref[here, :] = r
        low[s] = (nv * par[1:2, :] + par[2:3, :]).astype(bf16)
        return carry

    lax.fori_loop(0, batch, one_sequence, 0)
    low0[...] = low[0]
    low1[...] = low[1]


def feed_kernel(info, *rest, width, far):
    low, (pack, *rest) = rest[:4], rest[4:]
    if far:
        u_a, u_b, d_a, d_b, p_own, p_sib, act_out, slope_out, own, sib, both, up, dn, sem = rest
        up = pieces(info, u_a, u_b, up, sem.at[0], False)
        dn = pieces(info, d_a, d_b, dn, sem.at[1], True)
        up = up()
    else:
        u_in, d_in, act_out, slope_out, own, sib, both = rest
        up = u_in()
    act, slope = ref(act_out), ref(slope_out)
    units = up.shape[1]
    bias = pack()
    step = 256
    n = low[0].shape[0]
    for i, x in enumerate(low):
        both[i // 2, (i % 2) * n : (i % 2 + 1) * n, :] = x[...]

    def side(j, carry):
        def chunk(n, carry):
            cols = pl.ds(pl.multiple_of(n * step, step), step)
            hidden = mm(both[j], up[:, cols]) + bias[width : width + 1, cols].astype(f32)
            a, g = gelu_parts(hidden)
            act[j, :, cols] = a.astype(bf16)
            slope[j, :, cols] = g.astype(bf16)
            return carry

        return lax.fori_loop(0, units // step, chunk, carry)

    lax.fori_loop(0, 2, side, 0)
    if far:
        dn = dn()
        sib[...] = (p_sib[...] + mm(act[1], dn[...])).astype(bf16)
        own[...] = p_own[...] + mm(act[0], dn[...])
    else:
        dn = d_in()
        own[...] = mm(act[0], dn[...])
        sib[...] = mm(act[1], dn[...])


def second_norm_kernel(info, cot_in, par, nv_in, own, got, outs, gsec_out, gs_low, small):
    cot, nv_ref, gsec = cot_in(), ref(nv_in), ref(gsec_out)
    batch, rows, d = cot.shape

    def one_sequence(s, sums):
        here = pl.ds(pl.multiple_of(s * rows, rows), rows)
        total = own[here, :] + got[here, :].astype(f32) + par[3:4, :] + (nv_ref[here, :] * par[1:2, :] + par[2:3, :])
        nv, r = norm_parts(total)
        outs.src[s] = (nv * par[4:5, :] + par[5:6, :]).astype(bf16)
        at = info[2] * rows + lax.broadcasted_iota(jnp.int32, (rows, 1), 0)
        seed = jnp.where(at < info[7][s], cot[s].astype(f32), 0.0)
        g = norm_back(seed, par[4:5, :], nv, r)
        gsec[here, :] = g
        gs_low[here, :] = g.astype(bf16)
        return tuple(a + rowsum(b) for a, b in zip(sums, (g, seed * nv, seed)))

    sums = lax.fori_loop(0, batch, one_sequence, (jnp.zeros((1, d), f32),) * 3)
    small[...] = jnp.concatenate([*sums, jnp.zeros((5, d), f32)], axis=0)


def feed_back_kernel(info, gs, gs2, slope0, slope1, up0, dn0, u_a, u_b, d_a, d_b, gh_out, own, sib, ub, sides, up2, dn2, sem):
    gh = ref(gh_out)
    units = up0.dst.shape[1]
    dn2 = pieces(info, d_a, d_b, dn2, sem.at[1], True)
    up2 = pieces(info, u_a, u_b, up2, sem.at[0], False)
    ub[...] = jnp.zeros_like(ub)
    sides[0] = gs[...]
    sides[1] = gs2[...]
    step = 256
    for k, slope in enumerate((ref(slope0), ref(slope1))):
        if k:
            dn = dn2()
        else:
            dn = dn0()

        def side(j, carry):
            def chunk(n, carry):
                cols = pl.ds(pl.multiple_of(n * step, step), step)
                ga = mm(sides[j], dn[cols, :], NT)
                h = (ga * slope[j, :, cols].astype(f32)).astype(bf16)
                gh[k, j, :, cols] = h
                ub[k : k + 1, cols] += rowsum(h.astype(f32))
                return carry

            return lax.fori_loop(0, units // step, chunk, carry)

        lax.fori_loop(0, 2, side, 0)
    up2 = up2()
    up = up0()
    sib[...] = (mm(gh[0, 1], up[...], NT) + mm(gh[1, 1], up2[...], NT)).astype(bf16)
    own[...] = mm(gh[0, 0], up[...], NT) + mm(gh[1, 0], up2[...], NT)


def first_back_kernel(info, par, nv_in, r_ref, own, got, gsec_in, small2, *rest):
    cs, packs = [c() for c in rest[:4]], rest[4:8]
    gfi, g0, g1, g2, g3, okeep, osend, small, ga_low = rest[8:]
    nv_ref, gsec = ref(nv_in), ref(gsec_in)
    packs = [p() for p in packs]
    n, d = own.shape
    rows = n // 2
    width = cs[0].shape[1]

    def one_sequence(s, sums):
        here = pl.ds(pl.multiple_of(s * rows, rows), rows)
        u = own[here, :] + got[here, :].astype(f32) + gsec[here, :]
        nv = nv_ref[here, :]
        g = norm_back(u, par[1:2, :], nv, r_ref[here, :])
        gfi.src[here, :] = g
        low = g.astype(bf16)
        ga_low[here, :] = low
        for k, out in enumerate((g0, g1, g2, g3)):
            out.src[s] = mm(packs[k][0:width, :], low, NT).astype(bf16)
        return tuple(a + rowsum(b) for a, b in zip(sums, (g, u * nv, u)))

    sums = lax.fori_loop(0, 2, one_sequence, (jnp.zeros((1, d), f32),) * 3)
    for out in (g3, g2, g1, g0, gfi):
        out.start()
    for k in range(4):
        total = mm(cs[k][0], ga_low[0:rows, :]) + mm(cs[k][1], ga_low[rows:n, :])
        (osend if k % 2 else okeep).src[k // 2, 0:width, :] = total.astype(bf16)
    both = jnp.concatenate([*sums, small2[0:3, :], jnp.zeros((2, d), f32)], axis=0)
    small[...] = both
    high = both.astype(bf16)
    osend.src[0, width : width + 8, :] = high
    osend.src[1, width : width + 8, :] = (both - high.astype(f32)).astype(bf16)


def down_grads_kernel(info, act0, act1, gs, gs2, far_keep, keep, send, scr, *, parts):
    units = act0.shape[2]
    block = units // parts
    step = 384
    for k, (act, mine) in enumerate(((act1, far_keep), (act0, keep))):

        def chunk(m, carry):
            cols = pl.ds(pl.multiple_of(m * step, step), step)
            total = mm(act[0, :, cols], gs[...], TN) + mm(act[1, :, cols], gs2[...], TN)
            total = total.astype(bf16)
            for i in range(step // block):
                scr[(i & 1) ^ info[3], m * (step // block // 2) + (i >> 1)] = total[i * block : (i + 1) * block]
            return carry

        lax.fori_loop(0, units // step, chunk, 0)
        send.src[k] = scr[1]
        mine.src[...] = scr[0]
    send.start()


def up_grads_kernel(info, *rest, parts, width):
    lows, (gh_in, okeep, ogot, small, ub, far_keep, far_send, keep, send, sums, scr, both_low) = rest[:4], rest[4:]
    n = lows[0].shape[0]
    for i, x in enumerate(lows):
        both_low[i // 2, (i % 2) * n : (i % 2 + 1) * n, :] = x[...]
    low, low2 = both_low.at[0], both_low.at[1]
    gh = ref(gh_in)
    units = low.shape[1]
    block = units // parts
    extra = width // parts
    joint = block + extra
    n = parts // 2 * joint
    step = 384
    got = ogot()
    both = small[...] + got[0, width : width + 8, :].astype(f32) + got[1, width : width + 8, :].astype(f32)
    both = jnp.concatenate([both[0:6], ub[0:2, :]], axis=0)
    sums[...] = both
    high = both.astype(bf16)
    far_send.src[n : n + 8, :] = high
    far_send.src[n + 8 : n + 16, :] = (both - high.astype(f32)).astype(bf16)
    for k, mine, theirs in ((1, far_keep, far_send), (0, keep, send)):

        def chunk(m, carry):
            cols = pl.ds(pl.multiple_of(m * step, step), step)
            total = mm(low[:, cols], gh[k, 0], TN) + mm(low2[:, cols], gh[k, 1], TN)
            total = total.astype(bf16)
            for i in range(step // block):
                at = (m * (step // block // 4) + (i >> 2)) * 2 + (i & 1)
                scr[((i >> 1) & 1) ^ info[4], at, 0:block, :] = total[i * block : (i + 1) * block]
            return carry

        lax.fori_loop(0, units // step, chunk, 0)
        o = (okeep()[k, 0:width, :].astype(f32) + got[k, 0:width, :].astype(f32)).astype(bf16)
        for b in range(parts):
            at = (b >> 2) * 2 + (b & 1)
            scr[((b >> 1) & 1) ^ info[4], at, block:joint, :] = o[b * extra : (b + 1) * extra]
        for b in range(parts // 2):
            theirs.src[b * joint : (b + 1) * joint, :] = scr[1, b]
            mine.src[b * joint : (b + 1) * joint, :] = scr[0, b]
        theirs.start()
        mine.start()


def swap(x, axis, bit):
    size = lax.axis_size(axis)
    return lax.ppermute(x, axis, [(i, i ^ bit) for i in range(size)])


def summed(parts):
    return sum(p.astype(f32) for p in parts)


def spread(array, axis, parts):
    bits = parts.bit_length() - 1
    return array.reshape(*array.shape[:axis], *([2] * bits), array.shape[axis] // parts, *array.shape[axis + 1 :])


def halve_sum(terms, axis, mine):
    other = [lax.dynamic_index_in_dim(t, 1 - mine, axis, keepdims=False) for t in terms]
    kept = [lax.dynamic_index_in_dim(t, mine, axis, keepdims=False) for t in terms]
    return kept, summed(other).astype(bf16)


def halve(terms, axis, bit, mine):
    other = [lax.dynamic_index_in_dim(t, 1 - mine, axis, keepdims=False) for t in terms]
    kept = [lax.dynamic_index_in_dim(t, mine, axis, keepdims=False) for t in terms]
    other = summed(other).astype(bf16)
    return kept + [swap(other, "dp", bit)], other


def body(
    inputs,
    cotangent,
    lengths,
    qkv_weight,
    qkv_bias,
    out_weight,
    out_bias,
    first_gain,
    first_shift,
    up_weight,
    up_bias,
    down_weight,
    down_bias,
    second_gain,
    second_shift,
):
    batch, seq, d = inputs.shape
    rows = cotangent.shape[1]
    n = batch * rows
    width = out_weight.shape[0]
    units = up_weight.shape[1]
    peers = lax.axis_size("tensor")
    parts = lax.axis_size("dp")
    bits = parts.bit_length() - 1
    t = lax.axis_index("tensor")
    dp = lax.axis_index("dp")
    bit_of = [(dp >> i) & 1 for i in range(bits)]
    info = lengths
    par = jnp.concatenate([out_bias, first_gain, first_shift, down_bias, second_gain, second_shift])
    par = par.reshape(6, d).astype(f32)
    w_t = jnp.transpose(qkv_weight, (1, 2, 0))
    pack, u_part, d_part = prepare(info, out_weight, up_bias, up_weight, down_weight)
    pack2 = swap(pack, "tensor", 2)
    pack1 = swap(pack, "tensor", 1)
    u_part = swap(u_part, "tensor", 2)
    d_part = swap(d_part, "tensor", 2)
    q, k, v, lse, c, *cs = attend_fwd(info, inputs, w_t, qkv_bias, peers)
    saved = (q, k, v, lse, c)
    *cs, pack1, pack2, u_part, d_part = after(*cs, pack1, pack2, u_part, d_part)
    ctx = [cs[0]] + [swap(cs[j], "tensor", j) for j in range(1, peers)]
    u_next, d_next = swap(u_part, "dp", 1), swap(d_part, "dp", 2)
    *ctx, u_next, d_next = after(*ctx, u_next, d_next)
    u2a = jnp.concatenate([u_part, u_next])
    d2a = jnp.concatenate([d_part, d_next])
    pack2, u2a, d2a = after(pack2, u2a, d2a)
    pack3 = swap(pack2, "tensor", 1)
    packs = [pack, pack1, pack2, pack3]
    u2b = swap(u2a, "dp", 2)
    d2b = swap(d2a, "dp", 1)
    far_ctx = [whole(ctx[0])] + [loose(x) for x in ctx[1:]]
    far_packs = [whole(pack)] + [loose(p) for p in packs[1:]]
    share = (inputs, ((batch, rows, d), lambda ref, info: ref.at[:, pl.ds(pl.multiple_of(info[2] * rows, rows), rows), :]))
    nv1, r1, *low = call(
        "first_norm",
        first_norm_kernel,
        info,
        [share, par, *far_ctx, *far_packs],
        [SDS((n, d), f32), SDS((n, 1), f32), SDS((rows, d), bf16), SDS((rows, d), bf16)],
        [pltpu.VMEM((batch, rows, d), bf16)],
        vmem=NEAR,
    )
    low2 = [swap(x, "tensor", 1) for x in low]
    pair = SDS((2, n, units), bf16)
    part = SDS((n, d), f32)
    sides = pltpu.VMEM((2, n, d), bf16)
    act0, slope0, own, sib = call(
        "feed",
        feed_kernel,
        info,
        [*low, *low2, far_packs[0], whole(up_weight), whole(down_weight)],
        [pair, pair, part, part],
        [sides],
        vmem=NEAR,
        width=width,
        far=False,
    )
    halves = [Raw(x, False) for x in (u2a, u2b, d2a, d2b)]
    both = [pltpu.VMEM((d, units), bf16), pltpu.VMEM((units, d), bf16), pltpu.SemaphoreType.DMA((2, 4))]
    act1, slope1, own, sib = call(
        "feed",
        feed_kernel,
        info,
        [*low, *low2, far_packs[2], *halves, own, sib],
        [pair, pair, part, SDS((n, d), bf16)],
        [sides, *both],
        vmem=NEAR,
        width=width,
        far=True,
    )
    got = swap(sib, "tensor", 1)
    outputs, gsec, gs_low, small2 = call(
        "second_norm",
        second_norm_kernel,
        info,
        [whole(cotangent), par, nv1, own, got],
        [[SDS((batch, rows, d), bf16)], part, SDS((n, d), bf16), SDS((8, d), f32)],
        vmem=NEAR,
    )
    gs_low2 = swap(gs_low, "tensor", 1)
    gh, own, sib, ub = call(
        "feed_back",
        feed_back_kernel,
        info,
        [gs_low, gs_low2, slope0, slope1, whole(up_weight), whole(down_weight), *halves],
        [SDS((2, 2, n, units), bf16), part, SDS((n, d), bf16), SDS((8, d), f32)],
        [sides, *both],
        vmem=NEAR,
    )
    got = swap(sib, "tensor", 1)
    block = units // parts
    half_shape = (parts // 2, block, d)
    down_far_keep, down_keep, down_send = call(
        "down_grads",
        down_grads_kernel,
        info,
        [act0, act1, gs_low, gs_low2],
        [[SDS(half_shape, bf16)], [SDS(half_shape, bf16)], [SDS((2, *half_shape), bf16)]],
        [pltpu.VMEM((2, *half_shape), bf16)],
        vmem=NEAR,
        parts=parts,
    )
    down_got = swap(down_send, "dp", 1)
    gfi, g0, g1, g2, g3, okeep, osend, small1 = call(
        "first_back",
        first_back_kernel,
        info,
        [par, nv1, r1, own, got, gsec, small2, *far_ctx, *far_packs],
        [
            [part],
            *[[SDS((batch, width, rows), bf16)]] * 4,
            *[[SDS((2, width + 8, d), bf16)]] * 2,
            SDS((8, d), f32),
        ],
        [pltpu.VMEM((n, d), bf16)],
        vmem=NEAR,
    )
    gctx = [g0] + [swap(g, "tensor", j) for j, g in ((1, g1), (2, g2), (3, g3))]
    got_o = swap(osend, "tensor", 1)
    joint = block + width // parts
    cut = parts // 2 * joint
    up_far_keep, up_far_send, up_keep, up_send, small = call(
        "up_grads",
        up_grads_kernel,
        info,
        [*low, *low2, gh, whole(okeep), loose(got_o), small1, ub],
        [
            [SDS((cut, d), bf16)],
            [SDS((cut + 16, d), bf16)],
            [SDS((cut, d), bf16)],
            [SDS((cut, d), bf16)],
            SDS((8, d), f32),
        ],
        [pltpu.VMEM((2, parts // 2, joint, d), bf16), sides],
        vmem=NEAR,
        parts=parts,
        width=width,
    )
    *gctx, up_far_send = after(*gctx, up_far_send)
    up_far_got = swap(up_far_send, "dp", 2)
    *gctx, up_far_keep = after(*gctx, up_far_keep)
    lows, biases, terms_of = [], [], []
    for s in range(batch):
        keep, send, low_grads, db = attend_bwd(s, info, w_t, *saved, gctx, d)
        biases.append(db)
        if s == 0:
            send, up_far_got, down_got = after(send, up_far_got, down_got)
        else:
            send, low_grads, down_y, up_got, up_more, far = after(send, low_grads, down_y, up_got, up_more, far)
            terms_of[0].append(far)
        near = swap(send, "tensor", 1)
        in_sum = summed([keep[1], near[1]]).astype(bf16)
        terms_of.append([keep[0], near[0]])
        if s == 0:
            lows.append(low_grads)
            down_sum = summed([down_far_keep, down_got[0]]).astype(bf16)
            shape = ([2] * (bits - 1)) + [joint, d]
            small = small + pair_sum(up_far_got, cut, 8)
            terms = [x.reshape(shape) for x in (up_far_keep, up_far_got[:cut])]
            up_far_kept, up_far_next = halve_sum(terms, bits - 2, bit_of[0])
            up_far_rows = with_rows(up_far_next, small)
            tied = after(down_sum, up_far_rows, in_sum, up_send, *gctx)
            (down_sum, up_far_rows, in_sum, up_send), gctx = tied[:4], tied[4:]
            down_y = swap(down_sum, "tensor", 2)
            up_got = swap(up_send, "dp", 2)
            up_more = swap(up_far_rows, "dp", 1)
            far = swap(in_sum, "tensor", 2)
    shape = ([2] * (bits - 1)) + [block, d]
    down_terms = [x.reshape(shape) for x in (down_keep, down_got[1], down_y)]
    down_kept, down_next = halve_sum(down_terms, bits - 2, bit_of[1])
    at = up_far_next.size // d
    small = small + pair_sum(up_more, at, 8)
    small = jnp.concatenate([small[0:6], small[7:8], small[6:7]])
    up_y_next = summed(up_far_kept + [up_more[:at].reshape(up_far_next.shape)]).astype(bf16)
    up_y_rows = with_rows(up_y_next, small)
    shape = ([2] * (bits - 1)) + [joint, d]
    up_kept, up_next = halve_sum([x.reshape(shape) for x in (up_keep, up_got)], bits - 2, bit_of[0])
    low_grads, down_next, up_y_rows, up_next = after(low_grads, down_next, up_y_rows, up_next)
    lows.append(low_grads)
    down_more = swap(down_next, "dp", 2)
    up_y = swap(up_y_rows, "tensor", 2)
    up_more = swap(up_next, "dp", 1)
    m = 3 * d // 4
    operands = []
    for s in range(batch):
        operands += [(inputs, (inputs.shape[1:], functools.partial(nth, s))), whole(lows[s])]
    w_keep, w_send, db = call(
        "project_grads",
        project_grads_kernel,
        info,
        [*operands, *biases],
        [[SDS((m, 2 * width), bf16)], [SDS((m + 8, 2 * width), bf16)], SDS((1, 2 * width), f32)],
        [pltpu.VMEM((3, d, width), f32), pltpu.VMEM((3, width, d), f32), pltpu.VMEM((2, m, 2 * width), bf16)],
        parts=parts,
    )
    w_send, down_more, up_y, up_more = after(w_send, down_more, up_y, up_more)
    down_more, up_y, up_more, in_sum = after(down_more, up_y, up_more, in_sum)
    got = swap(w_send, "dp", 1)
    got, in_sum = after(got, in_sum)
    terms_of[1].append(swap(in_sum, "tensor", 2))
    down_terms = down_kept + [down_more]
    at = up_y_next.size // d
    small = jnp.concatenate([small[0:6], small[7:8], small[7:8]]) + pair_sum(up_y, at, 8)
    up_terms = up_kept + [up_more, up_y[:at].reshape(up_y_next.shape)]
    for i in range(2, bits):
        down_terms, sent = halve_sum(down_terms, bits - 1 - i, bit_of[i])
        down_got = swap(sent, "dp", 1 << i)
        up_terms, sent = halve_sum(up_terms, bits - 1 - i, bit_of[i])
        up_got = swap(with_rows(sent, small), "dp", 1 << i)
        if i == bits - 1:
            break
        down_terms, up_terms, small = with_received(down_terms, down_got, up_terms, up_got, sent, small)
    row = 3 * (d // parts) // 2
    at = parts // 2 * row
    shape = ([2] * (bits - 1)) + [row, 2 * width]
    terms = [x.reshape(shape) for x in (w_keep, got[:at])]
    db = db + got[at : at + 1].astype(f32) + got[at + 1 : at + 2].astype(f32)
    input_grad = jnp.stack([
        (summed(x) + gfi[s * rows : (s + 1) * rows]).astype(bf16)
        for s, x in enumerate(terms_of)
    ])
    for i in range(1, bits):
        kept, rows_sent, more = halve_with(terms, terms[0].ndim - 3, db, "dp", 1 << i, bit_of[i])
        if i == bits - 1:
            _, down_got, up_got = after(rows_sent, down_got, up_got)
        terms, db = kept, db + more
    down_terms, up_terms, small = with_received(down_terms, down_got, up_terms, up_got, sent, small)
    down_sum = summed(down_terms)
    up_sum = summed(up_terms)
    mine = small
    qkv_sum = summed(terms)
    qkv_sum = jnp.concatenate([qkv_sum[:, :width], qkv_sum[:, width:]], axis=0).reshape(3, -1, width)
    qkv_sum = jnp.transpose(qkv_sum, (1, 0, 2))
    db = db.reshape(2, width)
    return (
        outputs,
        input_grad,
        qkv_sum,
        db,
        up_sum[block:],
        mine[0],
        mine[1],
        mine[2],
        up_sum[:block],
        mine[6],
        down_sum,
        mine[3],
        mine[4],
        mine[5],
    )


def pair_sum(array, at, n):
    return array[at : at + n].astype(f32) + array[at + n : at + 2 * n].astype(f32)


def with_rows(array, rows):
    flat = array.reshape(-1, array.shape[-1])
    high = rows.astype(bf16)
    low = (rows - high.astype(f32)).astype(bf16)
    return jnp.concatenate([flat, high, low], axis=0)


def halve_with(terms, axis, rows, name, bit, mine):
    other = [lax.dynamic_index_in_dim(t, 1 - mine, axis, keepdims=False) for t in terms]
    kept = [lax.dynamic_index_in_dim(t, mine, axis, keepdims=False) for t in terms]
    other = summed(other).astype(bf16)
    sent = with_rows(other, rows)
    got = swap(sent, name, bit)
    cut = other.size // other.shape[-1]
    return kept + [got[:cut].reshape(other.shape)], sent, pair_sum(got, cut, rows.shape[0])


def with_received(down_terms, down_got, up_terms, up_got, sent, small):
    at = sent.size // sent.shape[-1]
    small = small + pair_sum(up_got, at, small.shape[0])
    return down_terms + [down_got], up_terms + [up_got[:at].reshape(sent.shape)], small


def after(*values):
    return lax.optimization_barrier(values)


def solution(mesh):
    in_specs = (
        P("dp", None, None),
        P("dp", "tensor", None),
        P("dp"),
        P(None, None, "tensor"),
        P(None, "tensor"),
        P("tensor", None),
        P(),
        P(),
        P(),
        P(None, "tensor"),
        P("tensor"),
        P("tensor", None),
        P(),
        P(),
        P(),
    )
    out_specs = (
        P("dp", "tensor", None),
        P("dp", "tensor", None),
        P("dp", None, "tensor"),
        P(None, "tensor"),
        P(("tensor", "dp"), None),
        P(),
        P(),
        P(),
        P("dp", "tensor"),
        P("tensor"),
        P(("tensor", "dp"), None),
        P(),
        P(),
        P(),
    )
    return jax.shard_map(body, mesh=mesh, in_specs=in_specs, out_specs=out_specs, check_vma=False)
```

```python
import functools

import jax
import jax.numpy as jnp
from jax import lax
from jax.experimental import pallas as pl
from jax.experimental.pallas import tpu as pltpu
from jax.sharding import PartitionSpec as P

HEAD = 64
WIDE, LANES = 192, 256
NEAR = 30
NT = (((1,), (1,)), ((), ()))
NN = (((1,), (0,)), ((), ()))
TN = (((0,), (0,)), ((), ()))
bf16 = jnp.bfloat16
f32 = jnp.float32
VM = pl.BlockSpec(memory_space=pltpu.VMEM)
SDS = jax.ShapeDtypeStruct


def mm(a, b, dims=NN):
    return lax.dot_general(a, b, dims, preferred_element_type=f32)


class Fetch:
    def __init__(self, src, dst, sem):
        self.dst, self.copy = dst, pltpu.make_async_copy(src, dst, sem)
        self.copy.start()
        self.waiting = True

    def __call__(self):
        if self.waiting:
            self.copy.wait()
            self.waiting = False
        return self.dst


class Pieces:
    def __init__(self, copies, dst):
        self.copies, self.dst = copies, dst
        for c in copies:
            c.start()

    def __call__(self):
        for c in self.copies:
            c.wait()
        self.copies = []
        return self.dst


def pieces(info, a, b, dst, sem, z_first):
    part = a.shape[0] // 2
    copies = []
    for src, other in ((a, 0), (b, 1)):
        for i in range(2):
            flips = (other, i) if z_first else (i, other)
            at = 2 * (info[3] ^ flips[0]) + (info[4] ^ flips[1])
            rows = pl.ds(pl.multiple_of(at * part, part), part)
            copies.append(pltpu.make_async_copy(src.at[pl.ds(i * part, part)], dst.at[rows], sem.at[len(copies)]))
    return Pieces(copies, dst)


class Flush:
    def __init__(self, src, dst, sem):
        self.src, self.copy = src, pltpu.make_async_copy(src, dst, sem)
        self.started = False

    def start(self):
        if not self.started:
            self.copy.start()
        self.started = True


def call(name, body, info, ins, outs, scratch=(), vmem=58, which=0, cost=1000, **static):
    far_in = [i for i, a in enumerate(ins) if isinstance(a, tuple)]
    pinned = [i for i in far_in if len(ins[i]) == 2]
    far_out = [i for i, o in enumerate(outs) if isinstance(o, list)]
    raw_in = [i for i, a in enumerate(ins) if isinstance(a, Raw)]
    raw_out = [i for i, o in enumerate(outs) if isinstance(o, Raw)]
    pinned += [i for i in raw_in if ins[i].pinned]
    any_in = far_in + raw_in
    arrays = [a[0] if isinstance(a, tuple) else a.value if isinstance(a, Raw) else a for a in ins]
    shapes = [o[0] if isinstance(o, list) else o.value if isinstance(o, Raw) else o for o in outs]
    picked = [a[1] if isinstance(a, tuple) else None for a in ins]
    n_in, n_out = len(ins), len(outs)

    def kernel(lengths_ref, which_ref, *refs):
        dp = lax.axis_index("dp")
        at = which_ref[0]
        info_ref = (lengths_ref[0], lengths_ref[1], lax.axis_index("tensor"), dp & 1, (dp >> 1) & 1, at, lengths_ref[at], lengths_ref)
        in_refs, refs = refs[:n_in], refs[n_in:]
        out_refs, refs = refs[:n_out], refs[n_out:]
        sem, refs = refs[-1], refs[:-1]
        buffers, rest = refs[: len(far_in) + len(far_out)], refs[len(far_in) + len(far_out) :]
        args = list(in_refs)
        for j, i in enumerate(far_in):
            view = picked[i][1]
            args[i] = Fetch(view(in_refs[i], info_ref), buffers[j], sem.at[j])
        results = list(out_refs)
        flushes = []
        for j, i in enumerate(far_out):
            at = len(far_in) + j
            results[i] = Flush(buffers[at], out_refs[i], sem.at[at])
            flushes.append(results[i])
        body(info_ref, *args, *results, *rest, **static)
        for i in far_in:
            args[i]()
        for f in flushes:
            f.start()
        for f in flushes:
            f.copy.wait()

    hbm = pl.BlockSpec(memory_space=pltpu.HBM)
    buffers = [pltpu.VMEM(picked[i][0], arrays[i].dtype) for i in far_in]
    buffers += [pltpu.VMEM(shapes[i].shape, shapes[i].dtype) for i in far_out]
    return pl.pallas_call(
        kernel,
        out_shape=[pltpu.HBM(o.shape, o.dtype) if i in far_out + raw_out else o for i, o in enumerate(shapes)],
        grid_spec=pltpu.PrefetchScalarGridSpec(
            num_scalar_prefetch=2,
            grid=(1,),
            in_specs=[hbm if i in pinned else pl.BlockSpec(memory_space=pl.ANY) if i in any_in else VM for i in range(n_in)],
            out_specs=[hbm if i in far_out + raw_out else VM for i in range(n_out)],
            scratch_shapes=[*buffers, *scratch, pltpu.SemaphoreType.DMA((max(1, len(far_in) + len(far_out)),))],
        ),
        compiler_params=pltpu.CompilerParams(vmem_limit_bytes=vmem << 20),
        cost_estimate=pl.CostEstimate(flops=cost, bytes_accessed=1000, transcendentals=0),
        name=name,
    )(info, jnp.full((1,), which, jnp.int32), *[pltpu.with_memory_space_constraint(a, pltpu.HBM) if i in pinned else a for i, a in enumerate(arrays)])


class Raw:
    def __init__(self, value, pinned=True):
        self.value, self.pinned = value, pinned


def ref(x):
    return x() if isinstance(x, Fetch) else x.src if isinstance(x, Flush) else x


def whole(a):
    return (a, (a.shape, lambda ref, info: ref))


def loose(a):
    return (*whole(a), None)


def prepare_kernel(info, out_in, bias, up_in, dn_in, pack, up_half, dn_half):
    for src, dst in ((up_in, up_half), (dn_in, dn_half)):
        dst.src[...] = src()[...]
        dst.start()
    out_w = out_in()
    width, d = out_w.shape
    pack.src[0:width, :] = out_w[...]
    pack.src[width : width + 8, :] = jnp.broadcast_to(bias[...].reshape(1, d), (8, d))


def prepare(info, out_w, bias, up, dn):
    width, d = out_w.shape
    part = up.shape[0] // 4
    view = lambda ref, info: ref.at[pl.ds(pl.multiple_of((2 * info[3] + info[4]) * part, part), part)]
    ins = [whole(out_w), bias, (up, ((part, d), view)), (dn, ((part, d), view))]
    return call("prepare", prepare_kernel, info, ins, [[SDS((width + 8, d), bf16)]] + [[SDS((part, d), bf16)]] * 2)


def head_cols(a, h, extra=()):
    lane = lax.broadcasted_iota(jnp.int32, a.shape, 1)
    out = jnp.where((lane >= HEAD * h) & (lane < HEAD * (h + 1)), a, jnp.zeros_like(a))
    for i, e in enumerate(extra):
        out = jnp.where(lane == WIDE + i, e, out)
    return out


def tail_cols(rows, values):
    lane = lax.broadcasted_iota(jnp.int32, (rows, LANES - WIDE), 1)
    out = jnp.zeros((rows, LANES - WIDE), f32)
    for i, v in enumerate(values):
        out = jnp.where(lane == i, v, out)
    return out.astype(bf16)


def attend_fwd_kernel(info, x_hbm, w_ref, b_ref, *rest):
    far, outs = rest[:5], rest[5:9]
    x_all, *near, v_t, s_all, sem_in, sem_out = rest[9:]
    q_all, k_all, v_all, lse_all, c_all = near
    me = info[2]
    batch, peers, width, block = c_all.shape
    seq = peers * block
    heads = width // HEAD

    def fetch(s):
        return pltpu.make_async_copy(x_hbm.at[s], x_all.at[s], sem_in.at[s])

    def flush(s, i):
        return pltpu.make_async_copy(near[i].at[s], far[i].at[s], sem_out.at[s, i])

    for s in range(batch):
        fetch(s).start()
    w = w_ref()

    def one_sequence(s, carry):
        length = info[7][s]
        fetch(s).wait()
        x = x_all[s]
        k_all[s, :, 0:WIDE] = mm(x, w[1], NT).astype(bf16)
        row = lax.broadcasted_iota(jnp.int32, (seq, 1), 0)
        k_all[s, :, WIDE:LANES] = tail_cols(seq, (jnp.where(row < length, 0.0, -1e30),))
        q = mm(x, w[0], NT) + b_ref[0:1, :].astype(f32)
        q_all[s, :, 0:WIDE] = q.astype(bf16) * jnp.asarray(0.125, bf16)
        q_all[s, :, WIDE:LANES] = tail_cols(seq, (1.0,))
        v = (mm(x, w[2], NT) + b_ref[1:2, :].astype(f32)).astype(bf16)
        v_all[s] = v
        v_t[...] = v.T
        for i in range(3):
            flush(s, i).start()

        def two_blocks(n, carry):
            qb = q_all[s, pl.ds(pl.multiple_of(n * 2 * block, 2 * block), 2 * block), :]
            one = jnp.ones_like(qb[:, 0:1])
            for h in range(heads):
                s_all[h] = mm(k_all[s], head_cols(qb, h, (one,)), NT)
            for h in range(heads):
                top = jnp.max(s_all[h], axis=0, keepdims=True)
                p = jnp.exp(s_all[h] - top)
                total = jnp.sum(p, axis=0, keepdims=True)
                rows = slice(HEAD * h, HEAD * (h + 1))
                out = (mm(v_t[rows, :], p.astype(bf16)) * (1.0 / total)).astype(bf16)
                lse = top + jnp.log(total)
                for j in range(2):
                    cols = slice(block * j, block * (j + 1))
                    c_all[s, 2 * n + j, rows, :] = out[:, cols]
                    lse_all[s, 2 * n + j, h : h + 1, :] = lse[:, cols]
            return carry

        lax.fori_loop(0, peers // 2, two_blocks, 0)
        for i in range(3, 5):
            flush(s, i).start()
        for k, out in enumerate(outs):
            out.src[s] = c_all[s, me ^ k]
        return carry

    lax.fori_loop(0, batch, one_sequence, 0)
    for out in outs:
        out.start()
    for s in range(batch):
        for i in range(5):
            flush(s, i).wait()


def attend_fwd(info, inputs, w_t, bias, peers):
    batch, seq, d = inputs.shape
    width = w_t.shape[1]
    block = seq // peers
    far = [SDS((batch, seq, LANES), bf16)] * 2 + [SDS((batch, seq, width), bf16)]
    far += [SDS((batch, peers, 8, block), f32), SDS((batch, peers, width, block), bf16)]
    scratch = [pltpu.VMEM(inputs.shape, bf16), *[pltpu.VMEM(o.shape, o.dtype) for o in far]]
    scratch += [pltpu.VMEM((width, seq), bf16), pltpu.VMEM((width // HEAD, seq, 2 * block), f32)]
    scratch += [pltpu.SemaphoreType.DMA((batch,)), pltpu.SemaphoreType.DMA((batch, 5))]
    return call(
        "attend_fwd",
        attend_fwd_kernel,
        info,
        [Raw(inputs), whole(w_t), bias],
        [Raw(o) for o in far] + [[SDS((batch, width, block), bf16)]] * peers,
        scratch,
    )


def nth(at, ref, info):
    return ref.at[at]


def of_sequence(a):
    return (a, (a.shape[1:], lambda ref, info: ref.at[info[5]]))


def attend_bwd_kernel(info, x_ref, q_in, k_in, v_in, lse_in, c_in, *rest):
    w_ref = x_ref
    peers = 4
    gs, rest = rest[:peers], rest[peers:]
    keep, send, low_out, db_ref, dq_t, dk, dv, k_t, g_ref = rest
    low = low_out.src
    length = info[6]
    me = info[2]
    k_ref, q_ref, v_ref = k_in(), q_in(), v_in()
    lse_ref, c_ref = lse_in(), c_in()
    _, width, block = c_ref.shape
    heads = width // HEAD
    k_t[...] = k_ref[:, 0:WIDE].T
    dk[...] = jnp.zeros_like(dk)
    dv[...] = jnp.zeros_like(dv)
    for k in range(peers):
        g_ref[me ^ k] = gs[k]()[...]

    def one_block(s, carry):
        at = pl.multiple_of(s * block, block)

        @pl.when(at >= length)
        def _():
            dq_t[:, pl.ds(at, block)] = jnp.zeros((width, block), f32)

        @pl.when(at < length)
        def _():
            qb = q_ref[pl.ds(at, block), :]
            g_t = g_ref[s]
            g = g_t.T
            prod_t = g_t.astype(f32) * c_ref[s].astype(f32)
            for h in range(heads):
                rows = slice(HEAD * h, HEAD * (h + 1))
                qh = head_cols(qb, h)
                gh = head_cols(g, h)
                scores = mm(k_ref[...], qh, NT)
                row = lax.broadcasted_iota(jnp.int32, scores.shape, 0)
                p = jnp.where(row < length, jnp.exp(scores - lse_ref[s, h : h + 1, :]), 0.0)
                dp = mm(v_ref[...], gh, NT)
                inner = jnp.sum(prod_t[rows], axis=0, keepdims=True)
                ds = (p * (dp - inner)).astype(bf16)
                dv[...] += mm(p.astype(bf16), gh)
                dk[...] += mm(ds, qh)
                dq_t[rows, pl.ds(at, block)] = mm(k_t[rows, :], ds) * 0.125

        return carry

    lax.fori_loop(0, peers, one_block, 0)
    low[0] = dq_t[...].T.astype(bf16)
    low[1] = dk[:, 0:WIDE].astype(bf16)
    low[2] = dv[...].astype(bf16)
    w = w_ref()
    for s in range(peers):
        at = pl.multiple_of((me ^ s) * block, block)
        total = sum(mm(low[i, pl.ds(at, block), :], w[i]) for i in range(3))
        (send if s % 2 else keep).src[s // 2] = total.astype(bf16)
    send.start()
    keep.start()
    db_ref[...] = jnp.concatenate([rowsum(low[i].astype(f32)) for i in (0, 2)], axis=1)


def attend_bwd(which, info, w_t, q, k, v, lse, c, gs, d):
    _, peers, width, block = c.shape
    seq = peers * block
    outs = [[SDS((2, block, d), bf16)]] * 2 + [[SDS((3, seq, width), bf16)], SDS((1, 2 * width), f32)]
    scratch = [
        pltpu.VMEM((width, seq), f32),
        pltpu.VMEM((seq, LANES), f32),
        pltpu.VMEM((seq, width), f32),
        pltpu.VMEM((width, seq), bf16),
        pltpu.VMEM((peers, width, block), bf16),
    ]
    ins = [whole(w_t)] + [of_sequence(a) for a in (q, k, v, lse, c)]
    ins += [(g, ((width, block), lambda ref, info: ref.at[info[5]]), None) for g in gs]
    return call("attend_bwd", attend_bwd_kernel, info, ins, outs, scratch, which=which, cost=2 * 10**10)


def project_grads_kernel(info, x0, low0, x1, low1, db0, db1, keep, send, db_ref, dw, acc, pair, *, parts):
    _, d, width = dw.shape
    x, low = x0(), low0()
    for i in range(3):
        acc[i] = mm(low[i].T, x[...])
    x, low = x1(), low1()
    for i in range(3):
        dw[i] = (acc[i] + mm(low[i].T, x[...])).T
    rows = d // parts
    half = 3 * rows // 2
    for b in range(parts):
        flat = dw[:, b * rows : (b + 1) * rows, :].reshape(3 * rows, width)
        flat = jnp.concatenate([flat[0:half], flat[half : 2 * half]], axis=1).astype(bf16)
        pair[(b & 1) ^ info[3], (b >> 1) * half : (b // 2 + 1) * half, :] = flat
    n = keep.src.shape[0]
    send.src[0:n, :] = pair[1]
    keep.src[...] = pair[0]
    db = db0[...] + db1[...]
    db_ref[...] = db
    high = db.astype(bf16)
    send.src[n : n + 8, :] = jnp.concatenate(
        [high, (db - high.astype(f32)).astype(bf16), jnp.zeros((6, 2 * width), bf16)], axis=0
    )
    send.start()


def gelu_parts(h):
    t = 1.0 / (1.0 + (0.3275911 * 0.7071067811865476) * jnp.abs(h))
    poly = t * (0.127414796 + t * (-0.142248368 + t * (0.7107068705 + t * (-0.7265760135 + t * 0.5307027145))))
    bell = jnp.exp2((-0.5 * 1.4426950408889634) * (h * h))
    tail = poly * bell
    cum = jnp.where(h < 0, tail, 1.0 - tail)
    return h * cum, cum + h * (bell * 0.3989422804014327)


def norm_parts(v):
    center = v - jnp.mean(v, axis=1, keepdims=True)
    r = lax.rsqrt(jnp.mean(center * center, axis=1, keepdims=True) + 1e-12)
    return center * r, r


def norm_back(u, gain, nv, r):
    gu = u * gain
    return r * (gu - jnp.mean(gu, axis=1, keepdims=True) - nv * jnp.mean(gu * nv, axis=1, keepdims=True))


def rows_of(vectors):
    return jnp.concatenate([v[...].reshape(1, -1).astype(f32) for v in vectors], axis=0)


def rowsum(v):
    return jnp.sum(v, axis=0, keepdims=True)


def first_norm_kernel(info, x_in, *rest):
    par, rest = rows_of(rest[:6]), rest[6:]
    nv_ref, r_ref, low0, low1, low = rest[8:]
    cs, packs = [c() for c in rest[:4]], [p() for p in rest[4:8]]
    x_ref = x_in()
    batch, rows = x_ref.shape[:2]
    width = cs[0].shape[1]

    def one_sequence(s, carry):
        here = pl.ds(pl.multiple_of(s * rows, rows), rows)
        total = par[0:1, :] + x_ref[s].astype(f32)
        for k in range(4):
            total = total + mm(cs[k][s], packs[k][0:width, :], TN)
        nv, r = norm_parts(total)
        nv_ref[here, :] = nv
        r_ref[here, :] = r
        low[s] = (nv * par[1:2, :] + par[2:3, :]).astype(bf16)
        return carry

    lax.fori_loop(0, batch, one_sequence, 0)
    low0[...] = low[0]
    low1[...] = low[1]


def feed_kernel(info, *rest, width, far):
    low, (pack, *rest) = rest[:4], rest[4:]
    if far:
        u_a, u_b, d_a, d_b, p_own, p_sib, act_out, slope_out, own, sib, both, up, dn, sem = rest
        up = pieces(info, u_a, u_b, up, sem.at[0], False)
        dn = pieces(info, d_a, d_b, dn, sem.at[1], True)
        up = up()
    else:
        u_in, d_in, act_out, slope_out, own, sib, both = rest
        up = u_in()
    act, slope = ref(act_out), ref(slope_out)
    units = up.shape[1]
    bias = pack()
    step = 256
    n = low[0].shape[0]
    for i, x in enumerate(low):
        both[i // 2, (i % 2) * n : (i % 2 + 1) * n, :] = x[...]

    def side(j, carry):
        def chunk(n, carry):
            cols = pl.ds(pl.multiple_of(n * step, step), step)
            hidden = mm(both[j], up[:, cols]) + bias[width : width + 1, cols].astype(f32)
            a, g = gelu_parts(hidden)
            act[j, :, cols] = a.astype(bf16)
            slope[j, :, cols] = g.astype(bf16)
            return carry

        return lax.fori_loop(0, units // step, chunk, carry)

    lax.fori_loop(0, 2, side, 0)
    if far:
        dn = dn()
        sib[...] = (p_sib[...] + mm(act[1], dn[...])).astype(bf16)
        own[...] = p_own[...] + mm(act[0], dn[...])
    else:
        dn = d_in()
        own[...] = mm(act[0], dn[...])
        sib[...] = mm(act[1], dn[...])


def second_norm_kernel(info, cot_in, *rest):
    par, (nv_in, own, got, outs, gsec_out, gs_low, small) = rows_of(rest[:6]), rest[6:]
    cot, nv_ref, gsec = cot_in(), ref(nv_in), ref(gsec_out)
    batch, rows, d = cot.shape

    def one_sequence(s, sums):
        here = pl.ds(pl.multiple_of(s * rows, rows), rows)
        total = own[here, :] + got[here, :].astype(f32) + par[3:4, :] + (nv_ref[here, :] * par[1:2, :] + par[2:3, :])
        nv, r = norm_parts(total)
        outs.src[s] = (nv * par[4:5, :] + par[5:6, :]).astype(bf16)
        at = info[2] * rows + lax.broadcasted_iota(jnp.int32, (rows, 1), 0)
        seed = jnp.where(at < info[7][s], cot[s].astype(f32), 0.0)
        g = norm_back(seed, par[4:5, :], nv, r)
        gsec[here, :] = g
        gs_low[here, :] = g.astype(bf16)
        return tuple(a + rowsum(b) for a, b in zip(sums, (g, seed * nv, seed)))

    sums = lax.fori_loop(0, batch, one_sequence, (jnp.zeros((1, d), f32),) * 3)
    small[...] = jnp.concatenate([*sums, jnp.zeros((5, d), f32)], axis=0)


def feed_back_kernel(info, gs, gs2, slope0, slope1, up0, dn0, u_a, u_b, d_a, d_b, gh_out, own, sib, ub, sides, up2, dn2, sem):
    gh = ref(gh_out)
    units = up0.dst.shape[1]
    dn2 = pieces(info, d_a, d_b, dn2, sem.at[1], True)
    up2 = pieces(info, u_a, u_b, up2, sem.at[0], False)
    ub[...] = jnp.zeros_like(ub)
    sides[0] = gs[...]
    sides[1] = gs2[...]
    step = 256
    for k, slope in enumerate((ref(slope0), ref(slope1))):
        if k:
            dn = dn2()
        else:
            dn = dn0()

        def side(j, carry):
            def chunk(n, carry):
                cols = pl.ds(pl.multiple_of(n * step, step), step)
                ga = mm(sides[j], dn[cols, :], NT)
                h = (ga * slope[j, :, cols].astype(f32)).astype(bf16)
                gh[k, j, :, cols] = h
                ub[k : k + 1, cols] += rowsum(h.astype(f32))
                return carry

            return lax.fori_loop(0, units // step, chunk, carry)

        lax.fori_loop(0, 2, side, 0)
    up2 = up2()
    up = up0()
    sib[...] = (mm(gh[0, 1], up[...], NT) + mm(gh[1, 1], up2[...], NT)).astype(bf16)
    own[...] = mm(gh[0, 0], up[...], NT) + mm(gh[1, 0], up2[...], NT)


def first_back_kernel(info, *rest):
    par, (nv_in, r_ref, own, got, gsec_in, small2, *rest) = rows_of(rest[:6]), rest[6:]
    cs, packs = [c() for c in rest[:4]], rest[4:8]
    gfi, g0, g1, g2, g3, okeep, osend, small, ga_low = rest[8:]
    nv_ref, gsec = ref(nv_in), ref(gsec_in)
    packs = [p() for p in packs]
    n, d = own.shape
    rows = n // 2
    width = cs[0].shape[1]

    def one_sequence(s, sums):
        here = pl.ds(pl.multiple_of(s * rows, rows), rows)
        u = own[here, :] + got[here, :].astype(f32) + gsec[here, :]
        nv = nv_ref[here, :]
        g = norm_back(u, par[1:2, :], nv, r_ref[here, :])
        gfi.src[here, :] = g
        low = g.astype(bf16)
        ga_low[here, :] = low
        for k, out in enumerate((g0, g1, g2, g3)):
            out.src[s] = mm(packs[k][0:width, :], low, NT).astype(bf16)
        return tuple(a + rowsum(b) for a, b in zip(sums, (g, u * nv, u)))

    sums = lax.fori_loop(0, 2, one_sequence, (jnp.zeros((1, d), f32),) * 3)
    for out in (g3, g2, g1, g0, gfi):
        out.start()
    for k in range(4):
        total = mm(cs[k][0], ga_low[0:rows, :]) + mm(cs[k][1], ga_low[rows:n, :])
        (osend if k % 2 else okeep).src[k // 2, 0:width, :] = total.astype(bf16)
    both = jnp.concatenate([*sums, small2[0:3, :], jnp.zeros((2, d), f32)], axis=0)
    small[...] = both
    high = both.astype(bf16)
    osend.src[0, width : width + 8, :] = high
    osend.src[1, width : width + 8, :] = (both - high.astype(f32)).astype(bf16)


def down_grads_kernel(info, act0, act1, gs, gs2, far_keep, keep, send, scr, *, parts):
    units = act0.shape[2]
    block = units // parts
    step = 384
    for k, (act, mine) in enumerate(((act1, far_keep), (act0, keep))):

        def chunk(m, carry):
            cols = pl.ds(pl.multiple_of(m * step, step), step)
            total = mm(act[0, :, cols], gs[...], TN) + mm(act[1, :, cols], gs2[...], TN)
            total = total.astype(bf16)
            for i in range(step // block):
                scr[(i & 1) ^ info[3], m * (step // block // 2) + (i >> 1)] = total[i * block : (i + 1) * block]
            return carry

        lax.fori_loop(0, units // step, chunk, 0)
        send.src[k] = scr[1]
        mine.src[...] = scr[0]
    send.start()


def up_grads_kernel(info, *rest, parts, width):
    lows, (gh_in, okeep, ogot, small, ub, far_keep, far_send, keep, send, sums, scr, both_low) = rest[:4], rest[4:]
    n = lows[0].shape[0]
    for i, x in enumerate(lows):
        both_low[i // 2, (i % 2) * n : (i % 2 + 1) * n, :] = x[...]
    low, low2 = both_low.at[0], both_low.at[1]
    gh = ref(gh_in)
    units = low.shape[1]
    block = units // parts
    extra = width // parts
    joint = block + extra
    n = parts // 2 * joint
    step = 384
    got = ogot()
    both = small[...] + got[0, width : width + 8, :].astype(f32) + got[1, width : width + 8, :].astype(f32)
    both = jnp.concatenate([both[0:6], ub[0:2, :]], axis=0)
    sums[...] = both
    high = both.astype(bf16)
    far_send.src[n : n + 8, :] = high
    far_send.src[n + 8 : n + 16, :] = (both - high.astype(f32)).astype(bf16)
    for k, mine, theirs in ((1, far_keep, far_send), (0, keep, send)):

        def chunk(m, carry):
            cols = pl.ds(pl.multiple_of(m * step, step), step)
            total = mm(low[:, cols], gh[k, 0], TN) + mm(low2[:, cols], gh[k, 1], TN)
            total = total.astype(bf16)
            for i in range(step // block):
                at = (m * (step // block // 4) + (i >> 2)) * 2 + (i & 1)
                scr[((i >> 1) & 1) ^ info[4], at, 0:block, :] = total[i * block : (i + 1) * block]
            return carry

        lax.fori_loop(0, units // step, chunk, 0)
        o = (okeep()[k, 0:width, :].astype(f32) + got[k, 0:width, :].astype(f32)).astype(bf16)
        for b in range(parts):
            at = (b >> 2) * 2 + (b & 1)
            scr[((b >> 1) & 1) ^ info[4], at, block:joint, :] = o[b * extra : (b + 1) * extra]
        for b in range(parts // 2):
            theirs.src[b * joint : (b + 1) * joint, :] = scr[1, b]
            mine.src[b * joint : (b + 1) * joint, :] = scr[0, b]
        theirs.start()
        mine.start()


def swap(x, axis, bit):
    size = lax.axis_size(axis)
    return lax.ppermute(x, axis, [(i, i ^ bit) for i in range(size)])


def summed(parts):
    return sum(p.astype(f32) for p in parts)


def spread(array, axis, parts):
    bits = parts.bit_length() - 1
    return array.reshape(*array.shape[:axis], *([2] * bits), array.shape[axis] // parts, *array.shape[axis + 1 :])


def halve_sum(terms, axis, mine):
    other = [lax.dynamic_index_in_dim(t, 1 - mine, axis, keepdims=False) for t in terms]
    kept = [lax.dynamic_index_in_dim(t, mine, axis, keepdims=False) for t in terms]
    return kept, summed(other).astype(bf16)


def halve(terms, axis, bit, mine):
    other = [lax.dynamic_index_in_dim(t, 1 - mine, axis, keepdims=False) for t in terms]
    kept = [lax.dynamic_index_in_dim(t, mine, axis, keepdims=False) for t in terms]
    other = summed(other).astype(bf16)
    return kept + [swap(other, "dp", bit)], other


def body(
    inputs,
    cotangent,
    lengths,
    qkv_weight,
    qkv_bias,
    out_weight,
    out_bias,
    first_gain,
    first_shift,
    up_weight,
    up_bias,
    down_weight,
    down_bias,
    second_gain,
    second_shift,
):
    batch, seq, d = inputs.shape
    rows = cotangent.shape[1]
    n = batch * rows
    width = out_weight.shape[0]
    units = up_weight.shape[1]
    peers = lax.axis_size("tensor")
    parts = lax.axis_size("dp")
    bits = parts.bit_length() - 1
    t = lax.axis_index("tensor")
    dp = lax.axis_index("dp")
    bit_of = [(dp >> i) & 1 for i in range(bits)]
    info = lengths
    par = [out_bias, first_gain, first_shift, down_bias, second_gain, second_shift]
    w_t = jnp.transpose(qkv_weight, (1, 2, 0))
    pack, u_part, d_part = prepare(info, out_weight, up_bias, up_weight, down_weight)
    pack2 = swap(pack, "tensor", 2)
    pack1 = swap(pack, "tensor", 1)
    u_part = swap(u_part, "tensor", 2)
    d_part = swap(d_part, "tensor", 2)
    q, k, v, lse, c, *cs = attend_fwd(info, inputs, w_t, qkv_bias, peers)
    saved = (q, k, v, lse, c)
    *cs, pack1, pack2, u_part, d_part = after(*cs, pack1, pack2, u_part, d_part)
    ctx = [cs[0]] + [swap(cs[j], "tensor", j) for j in range(1, peers)]
    u_next, d_next = swap(u_part, "dp", 1), swap(d_part, "dp", 2)
    *ctx, u_next, d_next = after(*ctx, u_next, d_next)
    u2a = jnp.concatenate([u_part, u_next])
    d2a = jnp.concatenate([d_part, d_next])
    pack2, u2a, d2a = after(pack2, u2a, d2a)
    pack3 = swap(pack2, "tensor", 1)
    packs = [pack, pack1, pack2, pack3]
    u2b = swap(u2a, "dp", 2)
    d2b = swap(d2a, "dp", 1)
    far_ctx = [whole(ctx[0])] + [loose(x) for x in ctx[1:]]
    far_packs = [whole(pack)] + [loose(p) for p in packs[1:]]
    share = (inputs, ((batch, rows, d), lambda ref, info: ref.at[:, pl.ds(pl.multiple_of(info[2] * rows, rows), rows), :]))
    nv1, r1, *low = call(
        "first_norm",
        first_norm_kernel,
        info,
        [share, *par, *far_ctx, *far_packs],
        [SDS((n, d), f32), SDS((n, 1), f32), SDS((rows, d), bf16), SDS((rows, d), bf16)],
        [pltpu.VMEM((batch, rows, d), bf16)],
        vmem=NEAR,
    )
    low2 = [swap(x, "tensor", 1) for x in low]
    pair = SDS((2, n, units), bf16)
    part = SDS((n, d), f32)
    sides = pltpu.VMEM((2, n, d), bf16)
    act0, slope0, own, sib = call(
        "feed",
        feed_kernel,
        info,
        [*low, *low2, far_packs[0], whole(up_weight), whole(down_weight)],
        [pair, pair, part, part],
        [sides],
        vmem=NEAR,
        width=width,
        far=False,
    )
    halves = [Raw(x, False) for x in (u2a, u2b, d2a, d2b)]
    both = [pltpu.VMEM((d, units), bf16), pltpu.VMEM((units, d), bf16), pltpu.SemaphoreType.DMA((2, 4))]
    act1, slope1, own, sib = call(
        "feed",
        feed_kernel,
        info,
        [*low, *low2, far_packs[2], *halves, own, sib],
        [pair, pair, part, SDS((n, d), bf16)],
        [sides, *both],
        vmem=NEAR,
        width=width,
        far=True,
    )
    got = swap(sib, "tensor", 1)
    outputs, gsec, gs_low, small2 = call(
        "second_norm",
        second_norm_kernel,
        info,
        [whole(cotangent), *par, nv1, own, got],
        [[SDS((batch, rows, d), bf16)], part, SDS((n, d), bf16), SDS((8, d), f32)],
        vmem=NEAR,
    )
    gs_low2 = swap(gs_low, "tensor", 1)
    gh, own, sib, ub = call(
        "feed_back",
        feed_back_kernel,
        info,
        [gs_low, gs_low2, slope0, slope1, whole(up_weight), whole(down_weight), *halves],
        [SDS((2, 2, n, units), bf16), part, SDS((n, d), bf16), SDS((8, d), f32)],
        [sides, *both],
        vmem=NEAR,
    )
    got = swap(sib, "tensor", 1)
    block = units // parts
    half_shape = (parts // 2, block, d)
    down_far_keep, down_keep, down_send = call(
        "down_grads",
        down_grads_kernel,
        info,
        [act0, act1, gs_low, gs_low2],
        [[SDS(half_shape, bf16)], [SDS(half_shape, bf16)], [SDS((2, *half_shape), bf16)]],
        [pltpu.VMEM((2, *half_shape), bf16)],
        vmem=NEAR,
        parts=parts,
    )
    down_got = swap(down_send, "dp", 1)
    gfi, g0, g1, g2, g3, okeep, osend, small1 = call(
        "first_back",
        first_back_kernel,
        info,
        [*par, nv1, r1, own, got, gsec, small2, *far_ctx, *far_packs],
        [
            [part],
            *[[SDS((batch, width, rows), bf16)]] * 4,
            *[[SDS((2, width + 8, d), bf16)]] * 2,
            SDS((8, d), f32),
        ],
        [pltpu.VMEM((n, d), bf16)],
        vmem=NEAR,
    )
    gctx = [g0] + [swap(g, "tensor", j) for j, g in ((1, g1), (2, g2), (3, g3))]
    got_o = swap(osend, "tensor", 1)
    joint = block + width // parts
    cut = parts // 2 * joint
    up_far_keep, up_far_send, up_keep, up_send, small = call(
        "up_grads",
        up_grads_kernel,
        info,
        [*low, *low2, gh, whole(okeep), loose(got_o), small1, ub],
        [
            [SDS((cut, d), bf16)],
            [SDS((cut + 16, d), bf16)],
            [SDS((cut, d), bf16)],
            [SDS((cut, d), bf16)],
            SDS((8, d), f32),
        ],
        [pltpu.VMEM((2, parts // 2, joint, d), bf16), sides],
        vmem=NEAR,
        parts=parts,
        width=width,
    )
    *gctx, up_far_send = after(*gctx, up_far_send)
    up_far_got = swap(up_far_send, "dp", 2)
    *gctx, up_far_keep = after(*gctx, up_far_keep)
    lows, biases, keeps = [], [], []
    for s in range(batch):
        keep, send, low_grads, db = attend_bwd(s, info, w_t, *saved, gctx, d)
        biases.append(db)
        if s == 0:
            send, up_far_got, down_got = after(send, up_far_got, down_got)
        else:
            send, low_grads, down_y, up_got, up_more, near = after(send, low_grads, down_y, up_got, up_more, near)
            keeps.append(near)
        keeps.append(keep)
        near = swap(send, "tensor", 1)
        if s == 0:
            lows.append(low_grads)
            down_sum = summed([down_far_keep, down_got[0]]).astype(bf16)
            shape = ([2] * (bits - 1)) + [joint, d]
            small = small + pair_sum(up_far_got, cut, 8)
            terms = [x.reshape(shape) for x in (up_far_keep, up_far_got[:cut])]
            up_far_kept, up_far_next = halve_sum(terms, bits - 2, bit_of[0])
            up_far_rows = with_rows(up_far_next, small)
            tied = after(down_sum, up_far_rows, up_send, *gctx)
            (down_sum, up_far_rows, up_send), gctx = tied[:3], tied[3:]
            down_y = swap(down_sum, "tensor", 2)
            up_got = swap(up_send, "dp", 2)
            up_more = swap(up_far_rows, "dp", 1)
    keeps.append(near)
    shape = ([2] * (bits - 1)) + [block, d]
    down_terms = [x.reshape(shape) for x in (down_keep, down_got[1], down_y)]
    down_kept, down_next = halve_sum(down_terms, bits - 2, bit_of[1])
    at = up_far_next.size // d
    small = small + pair_sum(up_more, at, 8)
    small = jnp.concatenate([small[0:6], small[7:8], small[6:7]])
    up_y_next = summed(up_far_kept + [up_more[:at].reshape(up_far_next.shape)]).astype(bf16)
    up_y_rows = with_rows(up_y_next, small)
    shape = ([2] * (bits - 1)) + [joint, d]
    up_kept, up_next = halve_sum([x.reshape(shape) for x in (up_keep, up_got)], bits - 2, bit_of[0])
    low_grads, down_next, up_y_rows, up_next = after(low_grads, down_next, up_y_rows, up_next)
    lows.append(low_grads)
    down_more = swap(down_next, "dp", 2)
    up_y = swap(up_y_rows, "tensor", 2)
    up_more = swap(up_next, "dp", 1)
    m = 3 * d // 4
    operands = []
    for s in range(batch):
        operands += [(inputs, (inputs.shape[1:], functools.partial(nth, s))), whole(lows[s])]
    w_keep, w_send, db = call(
        "project_grads",
        project_grads_kernel,
        info,
        [*operands, *biases],
        [[SDS((m, 2 * width), bf16)], [SDS((m + 8, 2 * width), bf16)], SDS((1, 2 * width), f32)],
        [pltpu.VMEM((3, d, width), f32), pltpu.VMEM((3, width, d), f32), pltpu.VMEM((2, m, 2 * width), bf16)],
        parts=parts,
    )
    w_send, down_more, up_y, up_more = after(w_send, down_more, up_y, up_more)
    keep0, near0, keep1, near1 = keeps
    in_sums = [summed([k[1], x[1]]).astype(bf16) for k, x in ((keep0, near0), (keep1, near1))]
    down_more, up_y, up_more, *in_sums = after(down_more, up_y, up_more, *in_sums)
    got = swap(w_send, "dp", 1)
    got, *in_sums = after(got, *in_sums)
    far = [swap(x, "tensor", 2) for x in in_sums]
    down_terms = down_kept + [down_more]
    at = up_y_next.size // d
    small = jnp.concatenate([small[0:6], small[7:8], small[7:8]]) + pair_sum(up_y, at, 8)
    up_terms = up_kept + [up_more, up_y[:at].reshape(up_y_next.shape)]
    for i in range(2, bits):
        down_terms, sent = halve_sum(down_terms, bits - 1 - i, bit_of[i])
        down_got = swap(sent, "dp", 1 << i)
        up_terms, sent = halve_sum(up_terms, bits - 1 - i, bit_of[i])
        up_got = swap(with_rows(sent, small), "dp", 1 << i)
        if i == bits - 1:
            break
        down_terms, up_terms, small = with_received(down_terms, down_got, up_terms, up_got, sent, small)
    row = 3 * (d // parts) // 2
    at = parts // 2 * row
    shape = ([2] * (bits - 1)) + [row, 2 * width]
    terms = [x.reshape(shape) for x in (w_keep, got[:at])]
    db = db + got[at : at + 1].astype(f32) + got[at + 1 : at + 2].astype(f32)
    for i in range(1, bits):
        kept, rows_sent, more = halve_with(terms, terms[0].ndim - 3, db, "dp", 1 << i, bit_of[i])
        if i == bits - 1:
            _, down_got, up_got = after(rows_sent, down_got, up_got)
        terms, db = kept, db + more
    down_terms, up_terms, small = with_received(down_terms, down_got, up_terms, up_got, sent, small)
    down_sum = summed(down_terms)
    up_sum = summed(up_terms)
    mine = small
    input_grad = jnp.stack([
        (summed([k[0], x[0], y]) + gfi[s * rows : (s + 1) * rows]).astype(bf16)
        for s, (k, x, y) in enumerate(((keep0, near0, far[0]), (keep1, near1, far[1])))
    ])
    qkv_sum = summed(terms)
    qkv_sum = jnp.concatenate([qkv_sum[:, :width], qkv_sum[:, width:]], axis=0).reshape(3, -1, width)
    qkv_sum = jnp.transpose(qkv_sum, (1, 0, 2))
    db = db.reshape(2, width)
    return (
        outputs,
        input_grad,
        qkv_sum,
        db,
        up_sum[block:],
        mine[0],
        mine[1],
        mine[2],
        up_sum[:block],
        mine[6],
        down_sum,
        mine[3],
        mine[4],
        mine[5],
    )


def pair_sum(array, at, n):
    return array[at : at + n].astype(f32) + array[at + n : at + 2 * n].astype(f32)


def with_rows(array, rows):
    flat = array.reshape(-1, array.shape[-1])
    high = rows.astype(bf16)
    low = (rows - high.astype(f32)).astype(bf16)
    return jnp.concatenate([flat, high, low], axis=0)


def halve_with(terms, axis, rows, name, bit, mine):
    other = [lax.dynamic_index_in_dim(t, 1 - mine, axis, keepdims=False) for t in terms]
    kept = [lax.dynamic_index_in_dim(t, mine, axis, keepdims=False) for t in terms]
    other = summed(other).astype(bf16)
    sent = with_rows(other, rows)
    got = swap(sent, name, bit)
    cut = other.size // other.shape[-1]
    return kept + [got[:cut].reshape(other.shape)], sent, pair_sum(got, cut, rows.shape[0])


def with_received(down_terms, down_got, up_terms, up_got, sent, small):
    at = sent.size // sent.shape[-1]
    small = small + pair_sum(up_got, at, small.shape[0])
    return down_terms + [down_got], up_terms + [up_got[:at].reshape(sent.shape)], small


def after(*values):
    return lax.optimization_barrier(values)


def solution(mesh):
    in_specs = (
        P("dp", None, None),
        P("dp", "tensor", None),
        P("dp"),
        P(None, None, "tensor"),
        P(None, "tensor"),
        P("tensor", None),
        P(),
        P(),
        P(),
        P(None, "tensor"),
        P("tensor"),
        P("tensor", None),
        P(),
        P(),
        P(),
    )
    out_specs = (
        P("dp", "tensor", None),
        P("dp", "tensor", None),
        P("dp", None, "tensor"),
        P(None, "tensor"),
        P(("tensor", "dp"), None),
        P(),
        P(),
        P(),
        P("dp", "tensor"),
        P("tensor"),
        P(("tensor", "dp"), None),
        P(),
        P(),
        P(),
    )
    return jax.shard_map(body, mesh=mesh, in_specs=in_specs, out_specs=out_specs, check_vma=False)
```

```python
import functools

import jax
import jax.numpy as jnp
from jax import lax
from jax.experimental import pallas as pl
from jax.experimental.pallas import tpu as pltpu
from jax.sharding import PartitionSpec as P

HEAD = 64
WIDE, LANES = 192, 256
NEAR = 30
NT = (((1,), (1,)), ((), ()))
NN = (((1,), (0,)), ((), ()))
TN = (((0,), (0,)), ((), ()))
bf16 = jnp.bfloat16
f32 = jnp.float32
VM = pl.BlockSpec(memory_space=pltpu.VMEM)
SDS = jax.ShapeDtypeStruct


def mm(a, b, dims=NN):
    return lax.dot_general(a, b, dims, preferred_element_type=f32)


class Fetch:
    def __init__(self, src, dst, sem):
        self.dst, self.copy = dst, pltpu.make_async_copy(src, dst, sem)
        self.copy.start()
        self.waiting = True

    def __call__(self):
        if self.waiting:
            self.copy.wait()
            self.waiting = False
        return self.dst


class Pieces:
    def __init__(self, copies, dst):
        self.copies, self.dst = copies, dst
        for c in copies:
            c.start()

    def __call__(self):
        for c in self.copies:
            c.wait()
        self.copies = []
        return self.dst


def pieces(info, a, b, dst, sem, z_first):
    part = a.shape[0] // 2
    copies = []
    for src, other in ((a, 0), (b, 1)):
        for i in range(2):
            flips = (other, i) if z_first else (i, other)
            at = 2 * (info[3] ^ flips[0]) + (info[4] ^ flips[1])
            rows = pl.ds(pl.multiple_of(at * part, part), part)
            copies.append(pltpu.make_async_copy(src.at[pl.ds(i * part, part)], dst.at[rows], sem.at[len(copies)]))
    return Pieces(copies, dst)


class Flush:
    def __init__(self, src, dst, sem):
        self.src, self.copy = src, pltpu.make_async_copy(src, dst, sem)
        self.started = False

    def start(self):
        if not self.started:
            self.copy.start()
        self.started = True


def call(name, body, info, ins, outs, scratch=(), vmem=58, which=0, cost=1000, **static):
    far_in = [i for i, a in enumerate(ins) if isinstance(a, tuple)]
    pinned = [i for i in far_in if len(ins[i]) == 2]
    far_out = [i for i, o in enumerate(outs) if isinstance(o, list)]
    raw_in = [i for i, a in enumerate(ins) if isinstance(a, Raw)]
    raw_out = [i for i, o in enumerate(outs) if isinstance(o, Raw)]
    pinned += [i for i in raw_in if ins[i].pinned]
    any_in = far_in + raw_in
    arrays = [a[0] if isinstance(a, tuple) else a.value if isinstance(a, Raw) else a for a in ins]
    shapes = [o[0] if isinstance(o, list) else o.value if isinstance(o, Raw) else o for o in outs]
    picked = [a[1] if isinstance(a, tuple) else None for a in ins]
    n_in, n_out = len(ins), len(outs)

    def kernel(lengths_ref, which_ref, *refs):
        dp = lax.axis_index("dp")
        at = which_ref[0]
        info_ref = (lengths_ref[0], lengths_ref[1], lax.axis_index("tensor"), dp & 1, (dp >> 1) & 1, at, lengths_ref[at], lengths_ref)
        in_refs, refs = refs[:n_in], refs[n_in:]
        out_refs, refs = refs[:n_out], refs[n_out:]
        sem, refs = refs[-1], refs[:-1]
        buffers, rest = refs[: len(far_in) + len(far_out)], refs[len(far_in) + len(far_out) :]
        args = list(in_refs)
        for j, i in enumerate(far_in):
            view = picked[i][1]
            args[i] = Fetch(view(in_refs[i], info_ref), buffers[j], sem.at[j])
        results = list(out_refs)
        flushes = []
        for j, i in enumerate(far_out):
            at = len(far_in) + j
            results[i] = Flush(buffers[at], out_refs[i], sem.at[at])
            flushes.append(results[i])
        body(info_ref, *args, *results, *rest, **static)
        for i in far_in:
            args[i]()
        for f in flushes:
            f.start()
        for f in flushes:
            f.copy.wait()

    hbm = pl.BlockSpec(memory_space=pltpu.HBM)
    buffers = [pltpu.VMEM(picked[i][0], arrays[i].dtype) for i in far_in]
    buffers += [pltpu.VMEM(shapes[i].shape, shapes[i].dtype) for i in far_out]
    return pl.pallas_call(
        kernel,
        out_shape=[pltpu.HBM(o.shape, o.dtype) if i in far_out + raw_out else o for i, o in enumerate(shapes)],
        grid_spec=pltpu.PrefetchScalarGridSpec(
            num_scalar_prefetch=2,
            grid=(1,),
            in_specs=[hbm if i in pinned else pl.BlockSpec(memory_space=pl.ANY) if i in any_in else VM for i in range(n_in)],
            out_specs=[hbm if i in far_out + raw_out else VM for i in range(n_out)],
            scratch_shapes=[*buffers, *scratch, pltpu.SemaphoreType.DMA((max(1, len(far_in) + len(far_out)),))],
        ),
        compiler_params=pltpu.CompilerParams(vmem_limit_bytes=vmem << 20),
        cost_estimate=pl.CostEstimate(flops=cost, bytes_accessed=1000, transcendentals=0),
        name=name,
    )(info, jnp.full((1,), which, jnp.int32), *[pltpu.with_memory_space_constraint(a, pltpu.HBM) if i in pinned else a for i, a in enumerate(arrays)])


class Raw:
    def __init__(self, value, pinned=True):
        self.value, self.pinned = value, pinned


def ref(x):
    return x() if isinstance(x, Fetch) else x.src if isinstance(x, Flush) else x


def whole(a):
    return (a, (a.shape, lambda ref, info: ref))


def loose(a):
    return (*whole(a), None)


def prepare_kernel(info, out_in, bias, up_in, dn_in, pack, up_half, dn_half):
    for src, dst in ((up_in, up_half), (dn_in, dn_half)):
        dst.src[...] = src()[...]
        dst.start()
    out_w = out_in()
    width, d = out_w.shape
    pack.src[0:width, :] = out_w[...]
    pack.src[width : width + 8, :] = jnp.broadcast_to(bias[...].reshape(1, d), (8, d))


def prepare(info, out_w, bias, up, dn):
    width, d = out_w.shape
    part = up.shape[0] // 4
    view = lambda ref, info: ref.at[pl.ds(pl.multiple_of((2 * info[3] + info[4]) * part, part), part)]
    ins = [whole(out_w), bias, (up, ((part, d), view)), (dn, ((part, d), view))]
    return call("prepare", prepare_kernel, info, ins, [[SDS((width + 8, d), bf16)]] + [[SDS((part, d), bf16)]] * 2)


def head_cols(a, h, extra=()):
    lane = lax.broadcasted_iota(jnp.int32, a.shape, 1)
    out = jnp.where((lane >= HEAD * h) & (lane < HEAD * (h + 1)), a, jnp.zeros_like(a))
    for i, e in enumerate(extra):
        out = jnp.where(lane == WIDE + i, e, out)
    return out


def tail_cols(rows, values):
    lane = lax.broadcasted_iota(jnp.int32, (rows, LANES - WIDE), 1)
    out = jnp.zeros((rows, LANES - WIDE), f32)
    for i, v in enumerate(values):
        out = jnp.where(lane == i, v, out)
    return out.astype(bf16)


def attend_fwd_kernel(info, x_hbm, w_ref, b_ref, *rest):
    far, outs = rest[:5], rest[5:9]
    x_all, *near, v_t, s_all, sem_in, sem_out = rest[9:]
    q_all, k_all, v_all, lse_all, c_all = near
    me = info[2]
    batch, peers, width, block = c_all.shape
    seq = peers * block
    heads = width // HEAD

    def fetch(s):
        return pltpu.make_async_copy(x_hbm.at[s], x_all.at[s], sem_in.at[s])

    def flush(s, i):
        return pltpu.make_async_copy(near[i].at[s], far[i].at[s], sem_out.at[s, i])

    for s in range(batch):
        fetch(s).start()
    w = w_ref()

    def one_sequence(s, carry):
        length = info[7][s]
        fetch(s).wait()
        x = x_all[s]
        k_all[s, :, 0:WIDE] = mm(x, w[1], NT).astype(bf16)
        row = lax.broadcasted_iota(jnp.int32, (seq, 1), 0)
        k_all[s, :, WIDE:LANES] = tail_cols(seq, (jnp.where(row < length, 0.0, -1e30),))
        q = mm(x, w[0], NT) + b_ref[0:1, :].astype(f32)
        q_all[s, :, 0:WIDE] = q.astype(bf16) * jnp.asarray(0.125, bf16)
        q_all[s, :, WIDE:LANES] = tail_cols(seq, (1.0,))
        v = (mm(x, w[2], NT) + b_ref[1:2, :].astype(f32)).astype(bf16)
        v_all[s] = v
        v_t[...] = v.T
        for i in range(3):
            flush(s, i).start()

        def two_blocks(n, carry):
            qb = q_all[s, pl.ds(pl.multiple_of(n * 2 * block, 2 * block), 2 * block), :]
            one = jnp.ones_like(qb[:, 0:1])
            for h in range(heads):
                s_all[h] = mm(k_all[s], head_cols(qb, h, (one,)), NT)
            for h in range(heads):
                top = jnp.max(s_all[h], axis=0, keepdims=True)
                p = jnp.exp(s_all[h] - top)
                total = jnp.sum(p, axis=0, keepdims=True)
                rows = slice(HEAD * h, HEAD * (h + 1))
                out = (mm(v_t[rows, :], p.astype(bf16)) * (1.0 / total)).astype(bf16)
                lse = top + jnp.log(total)
                for j in range(2):
                    cols = slice(block * j, block * (j + 1))
                    c_all[s, 2 * n + j, rows, :] = out[:, cols]
                    lse_all[s, 2 * n + j, h : h + 1, :] = lse[:, cols]
            return carry

        lax.fori_loop(0, peers // 2, two_blocks, 0)
        for i in range(3, 5):
            flush(s, i).start()
        for k, out in enumerate(outs):
            out.src[s] = c_all[s, me ^ k]
        return carry

    lax.fori_loop(0, batch, one_sequence, 0)
    for out in outs:
        out.start()
    for s in range(batch):
        for i in range(5):
            flush(s, i).wait()


def attend_fwd(info, inputs, w_t, bias, peers):
    batch, seq, d = inputs.shape
    width = w_t.shape[1]
    block = seq // peers
    far = [SDS((batch, seq, LANES), bf16)] * 2 + [SDS((batch, seq, width), bf16)]
    far += [SDS((batch, peers, 8, block), f32), SDS((batch, peers, width, block), bf16)]
    scratch = [pltpu.VMEM(inputs.shape, bf16), *[pltpu.VMEM(o.shape, o.dtype) for o in far]]
    scratch += [pltpu.VMEM((width, seq), bf16), pltpu.VMEM((width // HEAD, seq, 2 * block), f32)]
    scratch += [pltpu.SemaphoreType.DMA((batch,)), pltpu.SemaphoreType.DMA((batch, 5))]
    return call(
        "attend_fwd",
        attend_fwd_kernel,
        info,
        [Raw(inputs), whole(w_t), bias],
        [Raw(o) for o in far] + [[SDS((batch, width, block), bf16)]] * peers,
        scratch,
    )


def nth(at, ref, info):
    return ref.at[at]


def of_sequence(a):
    return (a, (a.shape[1:], lambda ref, info: ref.at[info[5]]))


def attend_bwd_kernel(info, x_ref, q_in, k_in, v_in, lse_in, c_in, *rest):
    w_ref = x_ref
    peers = 4
    gs, rest = rest[:peers], rest[peers:]
    keep, send, low_out, db_ref, dq_t, dk, dv, k_t, g_ref = rest
    low = low_out.src
    length = info[6]
    me = info[2]
    k_ref, q_ref, v_ref = k_in(), q_in(), v_in()
    lse_ref, c_ref = lse_in(), c_in()
    _, width, block = c_ref.shape
    heads = width // HEAD
    k_t[...] = k_ref[:, 0:WIDE].T
    dk[...] = jnp.zeros_like(dk)
    dv[...] = jnp.zeros_like(dv)
    for k in range(peers):
        g_ref[me ^ k] = gs[k]()[...]

    def one_block(s, carry):
        at = pl.multiple_of(s * block, block)

        @pl.when(at >= length)
        def _():
            dq_t[:, pl.ds(at, block)] = jnp.zeros((width, block), f32)

        @pl.when(at < length)
        def _():
            qb = q_ref[pl.ds(at, block), :]
            g_t = g_ref[s]
            g = g_t.T
            prod_t = g_t.astype(f32) * c_ref[s].astype(f32)
            for h in range(heads):
                rows = slice(HEAD * h, HEAD * (h + 1))
                qh = head_cols(qb, h)
                gh = head_cols(g, h)
                scores = mm(k_ref[...], qh, NT)
                row = lax.broadcasted_iota(jnp.int32, scores.shape, 0)
                p = jnp.where(row < length, jnp.exp(scores - lse_ref[s, h : h + 1, :]), 0.0)
                dp = mm(v_ref[...], gh, NT)
                inner = jnp.sum(prod_t[rows], axis=0, keepdims=True)
                ds = (p * (dp - inner)).astype(bf16)
                dv[...] += mm(p.astype(bf16), gh)
                dk[...] += mm(ds, qh)
                dq_t[rows, pl.ds(at, block)] = mm(k_t[rows, :], ds) * 0.125

        return carry

    lax.fori_loop(0, peers, one_block, 0)
    low[0] = dq_t[...].T.astype(bf16)
    low[1] = dk[:, 0:WIDE].astype(bf16)
    low[2] = dv[...].astype(bf16)
    w = w_ref()
    for s in range(peers):
        at = pl.multiple_of((me ^ s) * block, block)
        total = sum(mm(low[i, pl.ds(at, block), :], w[i]) for i in range(3))
        (send if s % 2 else keep).src[s // 2] = total.astype(bf16)
    send.start()
    keep.start()
    db_ref[...] = jnp.concatenate([rowsum(low[i].astype(f32)) for i in (0, 2)], axis=1)


def attend_bwd(which, info, w_t, q, k, v, lse, c, gs, d):
    _, peers, width, block = c.shape
    seq = peers * block
    outs = [[SDS((2, block, d), bf16)]] * 2 + [[SDS((3, seq, width), bf16)], SDS((1, 2 * width), f32)]
    scratch = [
        pltpu.VMEM((width, seq), f32),
        pltpu.VMEM((seq, LANES), f32),
        pltpu.VMEM((seq, width), f32),
        pltpu.VMEM((width, seq), bf16),
        pltpu.VMEM((peers, width, block), bf16),
    ]
    ins = [whole(w_t)] + [of_sequence(a) for a in (q, k, v, lse, c)]
    ins += [(g, ((width, block), lambda ref, info: ref.at[info[5]]), None) for g in gs]
    return call("attend_bwd", attend_bwd_kernel, info, ins, outs, scratch, which=which, cost=2 * 10**10)


def project_grads_kernel(info, x0, low0, x1, low1, db0, db1, keep, send, db_ref, dw, acc, pair, *, parts):
    _, d, width = dw.shape
    x, low = x0(), low0()
    for i in range(3):
        acc[i] = mm(low[i].T, x[...])
    x, low = x1(), low1()
    for i in range(3):
        dw[i] = (acc[i] + mm(low[i].T, x[...])).T
    rows = d // parts
    half = 3 * rows // 2
    for b in range(parts):
        flat = dw[:, b * rows : (b + 1) * rows, :].reshape(3 * rows, width)
        flat = jnp.concatenate([flat[0:half], flat[half : 2 * half]], axis=1).astype(bf16)
        pair[(b & 1) ^ info[3], (b >> 1) * half : (b // 2 + 1) * half, :] = flat
    n = keep.src.shape[0]
    send.src[0:n, :] = pair[1]
    keep.src[...] = pair[0]
    db = db0[...] + db1[...]
    db_ref[...] = db
    high = db.astype(bf16)
    send.src[n : n + 8, :] = jnp.concatenate(
        [high, (db - high.astype(f32)).astype(bf16), jnp.zeros((6, 2 * width), bf16)], axis=0
    )
    send.start()


def gelu_parts(h):
    t = 1.0 / (1.0 + (0.3275911 * 0.7071067811865476) * jnp.abs(h))
    poly = t * (0.127414796 + t * (-0.142248368 + t * (0.7107068705 + t * (-0.7265760135 + t * 0.5307027145))))
    bell = jnp.exp2((-0.5 * 1.4426950408889634) * (h * h))
    tail = poly * bell
    cum = jnp.where(h < 0, tail, 1.0 - tail)
    return h * cum, cum + h * (bell * 0.3989422804014327)


def norm_parts(v):
    center = v - jnp.mean(v, axis=1, keepdims=True)
    r = lax.rsqrt(jnp.mean(center * center, axis=1, keepdims=True) + 1e-12)
    return center * r, r


def norm_back(u, gain, nv, r):
    gu = u * gain
    return r * (gu - jnp.mean(gu, axis=1, keepdims=True) - nv * jnp.mean(gu * nv, axis=1, keepdims=True))


def rows_of(vectors):
    return jnp.concatenate([v[...].reshape(1, -1).astype(f32) for v in vectors], axis=0)


def rowsum(v):
    return jnp.sum(v, axis=0, keepdims=True)


def first_norm_kernel(info, x_in, *rest):
    par, rest = rows_of(rest[:6]), rest[6:]
    nv_ref, r_ref, low0, low1, low = rest[8:]
    cs, packs = [c() for c in rest[:4]], [p() for p in rest[4:8]]
    x_ref = x_in()
    batch, rows = x_ref.shape[:2]
    width = cs[0].shape[1]

    def one_sequence(s, carry):
        here = pl.ds(pl.multiple_of(s * rows, rows), rows)
        total = par[0:1, :] + x_ref[s].astype(f32)
        for k in range(4):
            total = total + mm(cs[k][s], packs[k][0:width, :], TN)
        nv, r = norm_parts(total)
        nv_ref[here, :] = nv
        r_ref[here, :] = r
        low[s] = (nv * par[1:2, :] + par[2:3, :]).astype(bf16)
        return carry

    lax.fori_loop(0, batch, one_sequence, 0)
    low0[...] = low[0]
    low1[...] = low[1]


def feed_kernel(info, *rest, width, far):
    low, (pack, *rest) = rest[:4], rest[4:]
    if far:
        u_a, u_b, d_a, d_b, p_own, p_sib, act_out, slope_out, own, sib, both, up, dn, sem = rest
        up = pieces(info, u_a, u_b, up, sem.at[0], False)
        dn = pieces(info, d_a, d_b, dn, sem.at[1], True)
        up = up()
    else:
        u_in, d_in, act_out, slope_out, own, sib, both = rest
        up = u_in()
    act, slope = ref(act_out), ref(slope_out)
    units = up.shape[1]
    bias = pack()
    step = 256
    n = low[0].shape[0]
    for i, x in enumerate(low):
        both[i // 2, (i % 2) * n : (i % 2 + 1) * n, :] = x[...]

    def side(j, carry):
        def chunk(n, carry):
            cols = pl.ds(pl.multiple_of(n * step, step), step)
            hidden = mm(both[j], up[:, cols]) + bias[width : width + 1, cols].astype(f32)
            a, g = gelu_parts(hidden)
            act[j, :, cols] = a.astype(bf16)
            slope[j, :, cols] = g.astype(bf16)
            return carry

        return lax.fori_loop(0, units // step, chunk, carry)

    lax.fori_loop(0, 2, side, 0)
    if far:
        dn = dn()
        sib[...] = (p_sib[...] + mm(act[1], dn[...])).astype(bf16)
        own[...] = p_own[...] + mm(act[0], dn[...])
    else:
        dn = d_in()
        own[...] = mm(act[0], dn[...])
        sib[...] = mm(act[1], dn[...])


def second_norm_kernel(info, cot_in, *rest):
    par, (nv_in, own, got, outs, gsec_out, gs_low, small) = rows_of(rest[:6]), rest[6:]
    cot, nv_ref, gsec = cot_in(), ref(nv_in), ref(gsec_out)
    batch, rows, d = cot.shape

    def one_sequence(s, sums):
        here = pl.ds(pl.multiple_of(s * rows, rows), rows)
        total = own[here, :] + got[here, :].astype(f32) + par[3:4, :] + (nv_ref[here, :] * par[1:2, :] + par[2:3, :])
        nv, r = norm_parts(total)
        outs.src[s] = (nv * par[4:5, :] + par[5:6, :]).astype(bf16)
        at = info[2] * rows + lax.broadcasted_iota(jnp.int32, (rows, 1), 0)
        seed = jnp.where(at < info[7][s], cot[s].astype(f32), 0.0)
        g = norm_back(seed, par[4:5, :], nv, r)
        gsec[here, :] = g
        gs_low[here, :] = g.astype(bf16)
        return tuple(a + rowsum(b) for a, b in zip(sums, (g, seed * nv, seed)))

    sums = lax.fori_loop(0, batch, one_sequence, (jnp.zeros((1, d), f32),) * 3)
    small[...] = jnp.concatenate([*sums, jnp.zeros((5, d), f32)], axis=0)


def feed_back_kernel(info, gs, gs2, slope0, slope1, up0, dn0, u_a, u_b, d_a, d_b, gh_out, own, sib, ub, sides, up2, dn2, sem):
    gh = ref(gh_out)
    units = up0.dst.shape[1]
    dn2 = pieces(info, d_a, d_b, dn2, sem.at[1], True)
    up2 = pieces(info, u_a, u_b, up2, sem.at[0], False)
    ub[...] = jnp.zeros_like(ub)
    sides[0] = gs[...]
    sides[1] = gs2[...]
    step = 256
    for k, slope in enumerate((ref(slope0), ref(slope1))):
        if k:
            dn = dn2()
        else:
            dn = dn0()

        def side(j, carry):
            def chunk(n, carry):
                cols = pl.ds(pl.multiple_of(n * step, step), step)
                ga = mm(sides[j], dn[cols, :], NT)
                h = (ga * slope[j, :, cols].astype(f32)).astype(bf16)
                gh[k, j, :, cols] = h
                ub[k : k + 1, cols] += rowsum(h.astype(f32))
                return carry

            return lax.fori_loop(0, units // step, chunk, carry)

        lax.fori_loop(0, 2, side, 0)
    up2 = up2()
    up = up0()
    sib[...] = (mm(gh[0, 1], up[...], NT) + mm(gh[1, 1], up2[...], NT)).astype(bf16)
    own[...] = mm(gh[0, 0], up[...], NT) + mm(gh[1, 0], up2[...], NT)


def first_back_kernel(info, *rest):
    par, (nv_in, r_ref, own, got, gsec_in, small2, *rest) = rows_of(rest[:6]), rest[6:]
    cs, packs = [c() for c in rest[:4]], rest[4:8]
    gfi, g0, g1, g2, g3, okeep, osend, small, ga_low = rest[8:]
    nv_ref, gsec = ref(nv_in), ref(gsec_in)
    packs = [p() for p in packs]
    n, d = own.shape
    rows = n // 2
    width = cs[0].shape[1]

    def one_sequence(s, sums):
        here = pl.ds(pl.multiple_of(s * rows, rows), rows)
        u = own[here, :] + got[here, :].astype(f32) + gsec[here, :]
        nv = nv_ref[here, :]
        g = norm_back(u, par[1:2, :], nv, r_ref[here, :])
        gfi.src[here, :] = g
        low = g.astype(bf16)
        ga_low[here, :] = low
        for k, out in enumerate((g0, g1, g2, g3)):
            out.src[s] = mm(packs[k][0:width, :], low, NT).astype(bf16)
        return tuple(a + rowsum(b) for a, b in zip(sums, (g, u * nv, u)))

    sums = lax.fori_loop(0, 2, one_sequence, (jnp.zeros((1, d), f32),) * 3)
    for out in (g3, g2, g1, g0, gfi):
        out.start()
    for k in range(4):
        total = mm(cs[k][0], ga_low[0:rows, :]) + mm(cs[k][1], ga_low[rows:n, :])
        (osend if k % 2 else okeep).src[k // 2, 0:width, :] = total.astype(bf16)
    both = jnp.concatenate([*sums, small2[0:3, :], jnp.zeros((2, d), f32)], axis=0)
    small[...] = both
    high = both.astype(bf16)
    osend.src[0, width : width + 8, :] = high
    osend.src[1, width : width + 8, :] = (both - high.astype(f32)).astype(bf16)


def down_grads_kernel(info, act0, act1, gs, gs2, far_keep, keep, send, scr, *, parts):
    units = act0.shape[2]
    block = units // parts
    step = 384
    for k, (act, mine) in enumerate(((act1, far_keep), (act0, keep))):

        def chunk(m, carry):
            cols = pl.ds(pl.multiple_of(m * step, step), step)
            total = mm(act[0, :, cols], gs[...], TN) + mm(act[1, :, cols], gs2[...], TN)
            total = total.astype(bf16)
            for i in range(step // block):
                scr[(i & 1) ^ info[3], m * (step // block // 2) + (i >> 1)] = total[i * block : (i + 1) * block]
            return carry

        lax.fori_loop(0, units // step, chunk, 0)
        send.src[k] = scr[1]
        mine.src[...] = scr[0]
    send.start()


def up_grads_kernel(info, *rest, parts, width):
    lows, (gh_in, okeep, ogot, small, ub, far_keep, far_send, keep, send, sums, scr, both_low) = rest[:4], rest[4:]
    n = lows[0].shape[0]
    for i, x in enumerate(lows):
        both_low[i // 2, (i % 2) * n : (i % 2 + 1) * n, :] = x[...]
    low, low2 = both_low.at[0], both_low.at[1]
    gh = ref(gh_in)
    units = low.shape[1]
    block = units // parts
    extra = width // parts
    joint = block + extra
    n = parts // 2 * joint
    step = 384
    got = ogot()
    both = small[...] + got[0, width : width + 8, :].astype(f32) + got[1, width : width + 8, :].astype(f32)
    both = jnp.concatenate([both[0:6], ub[0:2, :]], axis=0)
    sums[...] = both
    high = both.astype(bf16)
    far_send.src[n : n + 8, :] = high
    far_send.src[n + 8 : n + 16, :] = (both - high.astype(f32)).astype(bf16)
    for k, mine, theirs in ((1, far_keep, far_send), (0, keep, send)):

        def chunk(m, carry):
            cols = pl.ds(pl.multiple_of(m * step, step), step)
            total = mm(low[:, cols], gh[k, 0], TN) + mm(low2[:, cols], gh[k, 1], TN)
            total = total.astype(bf16)
            for i in range(step // block):
                at = (m * (step // block // 4) + (i >> 2)) * 2 + (i & 1)
                scr[((i >> 1) & 1) ^ info[4], at, 0:block, :] = total[i * block : (i + 1) * block]
            return carry

        lax.fori_loop(0, units // step, chunk, 0)
        o = (okeep()[k, 0:width, :].astype(f32) + got[k, 0:width, :].astype(f32)).astype(bf16)
        for b in range(parts):
            at = (b >> 2) * 2 + (b & 1)
            scr[((b >> 1) & 1) ^ info[4], at, block:joint, :] = o[b * extra : (b + 1) * extra]
        for b in range(parts // 2):
            theirs.src[b * joint : (b + 1) * joint, :] = scr[1, b]
            mine.src[b * joint : (b + 1) * joint, :] = scr[0, b]
        theirs.start()
        mine.start()


def swap(x, axis, bit):
    size = lax.axis_size(axis)
    return lax.ppermute(x, axis, [(i, i ^ bit) for i in range(size)])


def summed(parts):
    return sum(p.astype(f32) for p in parts)


def spread(array, axis, parts):
    bits = parts.bit_length() - 1
    return array.reshape(*array.shape[:axis], *([2] * bits), array.shape[axis] // parts, *array.shape[axis + 1 :])


def halve_sum(terms, axis, mine):
    other = [lax.dynamic_index_in_dim(t, 1 - mine, axis, keepdims=False) for t in terms]
    kept = [lax.dynamic_index_in_dim(t, mine, axis, keepdims=False) for t in terms]
    return kept, summed(other).astype(bf16)


def halve(terms, axis, bit, mine):
    other = [lax.dynamic_index_in_dim(t, 1 - mine, axis, keepdims=False) for t in terms]
    kept = [lax.dynamic_index_in_dim(t, mine, axis, keepdims=False) for t in terms]
    other = summed(other).astype(bf16)
    return kept + [swap(other, "dp", bit)], other


def body(
    inputs,
    cotangent,
    lengths,
    qkv_weight,
    qkv_bias,
    out_weight,
    out_bias,
    first_gain,
    first_shift,
    up_weight,
    up_bias,
    down_weight,
    down_bias,
    second_gain,
    second_shift,
):
    batch, seq, d = inputs.shape
    rows = cotangent.shape[1]
    n = batch * rows
    width = out_weight.shape[0]
    units = up_weight.shape[1]
    peers = lax.axis_size("tensor")
    parts = lax.axis_size("dp")
    bits = parts.bit_length() - 1
    t = lax.axis_index("tensor")
    dp = lax.axis_index("dp")
    bit_of = [(dp >> i) & 1 for i in range(bits)]
    info = lengths
    par = [out_bias, first_gain, first_shift, down_bias, second_gain, second_shift]
    w_t = jnp.transpose(qkv_weight, (1, 2, 0))
    pack, u_part, d_part = prepare(info, out_weight, up_bias, up_weight, down_weight)
    pack2 = swap(pack, "tensor", 2)
    pack1 = swap(pack, "tensor", 1)
    u_part = swap(u_part, "tensor", 2)
    d_part = swap(d_part, "tensor", 2)
    q, k, v, lse, c, *cs = attend_fwd(info, inputs, w_t, qkv_bias, peers)
    saved = (q, k, v, lse, c)
    *cs, pack1, pack2, u_part, d_part = after(*cs, pack1, pack2, u_part, d_part)
    ctx = [cs[0]] + [swap(cs[j], "tensor", j) for j in range(1, peers)]
    u_next, d_next = swap(u_part, "dp", 1), swap(d_part, "dp", 2)
    *ctx, u_next, d_next = after(*ctx, u_next, d_next)
    u2a = jnp.concatenate([u_part, u_next])
    d2a = jnp.concatenate([d_part, d_next])
    pack2, u2a, d2a = after(pack2, u2a, d2a)
    pack3 = swap(pack2, "tensor", 1)
    packs = [pack, pack1, pack2, pack3]
    u2b = swap(u2a, "dp", 2)
    d2b = swap(d2a, "dp", 1)
    far_ctx = [whole(ctx[0])] + [loose(x) for x in ctx[1:]]
    far_packs = [whole(pack)] + [loose(p) for p in packs[1:]]
    share = (inputs, ((batch, rows, d), lambda ref, info: ref.at[:, pl.ds(pl.multiple_of(info[2] * rows, rows), rows), :]))
    nv1, r1, *low = call(
        "first_norm",
        first_norm_kernel,
        info,
        [share, *par, *far_ctx, *far_packs],
        [SDS((n, d), f32), SDS((n, 1), f32), SDS((rows, d), bf16), SDS((rows, d), bf16)],
        [pltpu.VMEM((batch, rows, d), bf16)],
        vmem=NEAR,
    )
    low2 = [swap(x, "tensor", 1) for x in low]
    pair = SDS((2, n, units), bf16)
    part = SDS((n, d), f32)
    sides = pltpu.VMEM((2, n, d), bf16)
    act0, slope0, own, sib = call(
        "feed",
        feed_kernel,
        info,
        [*low, *low2, far_packs[0], whole(up_weight), whole(down_weight)],
        [pair, pair, part, part],
        [sides],
        vmem=NEAR,
        width=width,
        far=False,
    )
    halves = [Raw(x, False) for x in (u2a, u2b, d2a, d2b)]
    both = [pltpu.VMEM((d, units), bf16), pltpu.VMEM((units, d), bf16), pltpu.SemaphoreType.DMA((2, 4))]
    act1, slope1, own, sib = call(
        "feed",
        feed_kernel,
        info,
        [*low, *low2, far_packs[2], *halves, own, sib],
        [pair, pair, part, SDS((n, d), bf16)],
        [sides, *both],
        vmem=NEAR,
        width=width,
        far=True,
    )
    got = swap(sib, "tensor", 1)
    outputs, gsec, gs_low, small2 = call(
        "second_norm",
        second_norm_kernel,
        info,
        [whole(cotangent), *par, nv1, own, got],
        [[SDS((batch, rows, d), bf16)], part, SDS((n, d), bf16), SDS((8, d), f32)],
        vmem=NEAR,
    )
    gs_low2 = swap(gs_low, "tensor", 1)
    gh, own, sib, ub = call(
        "feed_back",
        feed_back_kernel,
        info,
        [gs_low, gs_low2, slope0, slope1, whole(up_weight), whole(down_weight), *halves],
        [SDS((2, 2, n, units), bf16), part, SDS((n, d), bf16), SDS((8, d), f32)],
        [sides, *both],
        vmem=NEAR,
    )
    got = swap(sib, "tensor", 1)
    block = units // parts
    half_shape = (parts // 2, block, d)
    down_far_keep, down_keep, down_send = call(
        "down_grads",
        down_grads_kernel,
        info,
        [act0, act1, gs_low, gs_low2],
        [[SDS(half_shape, bf16)], [SDS(half_shape, bf16)], [SDS((2, *half_shape), bf16)]],
        [pltpu.VMEM((2, *half_shape), bf16)],
        vmem=NEAR,
        parts=parts,
    )
    down_got = swap(down_send, "dp", 1)
    gfi, g0, g1, g2, g3, okeep, osend, small1 = call(
        "first_back",
        first_back_kernel,
        info,
        [*par, nv1, r1, own, got, gsec, small2, *far_ctx, *far_packs],
        [
            [part],
            *[[SDS((batch, width, rows), bf16)]] * 4,
            *[[SDS((2, width + 8, d), bf16)]] * 2,
            SDS((8, d), f32),
        ],
        [pltpu.VMEM((n, d), bf16)],
        vmem=NEAR,
    )
    gctx = [g0] + [swap(g, "tensor", j) for j, g in ((1, g1), (2, g2), (3, g3))]
    got_o = swap(osend, "tensor", 1)
    joint = block + width // parts
    cut = parts // 2 * joint
    up_far_keep, up_far_send, up_keep, up_send, small = call(
        "up_grads",
        up_grads_kernel,
        info,
        [*low, *low2, gh, whole(okeep), loose(got_o), small1, ub],
        [
            [SDS((cut, d), bf16)],
            [SDS((cut + 16, d), bf16)],
            [SDS((cut, d), bf16)],
            [SDS((cut, d), bf16)],
            SDS((8, d), f32),
        ],
        [pltpu.VMEM((2, parts // 2, joint, d), bf16), sides],
        vmem=NEAR,
        parts=parts,
        width=width,
    )
    *gctx, up_far_send = after(*gctx, up_far_send)
    up_far_got = swap(up_far_send, "dp", 2)
    *gctx, up_far_keep = after(*gctx, up_far_keep)
    lows, biases, keeps = [], [], []
    for s in range(batch):
        keep, send, low_grads, db = attend_bwd(s, info, w_t, *saved, gctx, d)
        biases.append(db)
        if s == 0:
            send, up_far_got, down_got = after(send, up_far_got, down_got)
        else:
            send, low_grads, down_y, up_got, up_more, near = after(send, low_grads, down_y, up_got, up_more, near)
            keeps.append(near)
        keeps.append(keep)
        near = swap(send, "tensor", 1)
        if s == 0:
            lows.append(low_grads)
            down_sum = summed([down_far_keep, down_got[0]]).astype(bf16)
            shape = ([2] * (bits - 1)) + [joint, d]
            small = small + pair_sum(up_far_got, cut, 8)
            terms = [x.reshape(shape) for x in (up_far_keep, up_far_got[:cut])]
            up_far_kept, up_far_next = halve_sum(terms, bits - 2, bit_of[0])
            up_far_rows = with_rows(up_far_next, small)
            tied = after(down_sum, up_far_rows, up_send, *gctx)
            (down_sum, up_far_rows, up_send), gctx = tied[:3], tied[3:]
            down_y = swap(down_sum, "tensor", 2)
            up_got = swap(up_send, "dp", 2)
            up_more = swap(up_far_rows, "dp", 1)
    keeps.append(near)
    shape = ([2] * (bits - 1)) + [block, d]
    down_terms = [x.reshape(shape) for x in (down_keep, down_got[1], down_y)]
    down_kept, down_next = halve_sum(down_terms, bits - 2, bit_of[1])
    at = up_far_next.size // d
    small = small + pair_sum(up_more, at, 8)
    small = jnp.concatenate([small[0:6], small[7:8], small[6:7]])
    up_y_next = summed(up_far_kept + [up_more[:at].reshape(up_far_next.shape)]).astype(bf16)
    up_y_rows = with_rows(up_y_next, small)
    shape = ([2] * (bits - 1)) + [joint, d]
    up_kept, up_next = halve_sum([x.reshape(shape) for x in (up_keep, up_got)], bits - 2, bit_of[0])
    low_grads, down_next, up_y_rows, up_next = after(low_grads, down_next, up_y_rows, up_next)
    lows.append(low_grads)
    down_more = swap(down_next, "dp", 2)
    up_y = swap(up_y_rows, "tensor", 2)
    up_more = swap(up_next, "dp", 1)
    m = 3 * d // 4
    operands = []
    for s in range(batch):
        operands += [(inputs, (inputs.shape[1:], functools.partial(nth, s))), whole(lows[s])]
    w_keep, w_send, db = call(
        "project_grads",
        project_grads_kernel,
        info,
        [*operands, *biases],
        [[SDS((m, 2 * width), bf16)], [SDS((m + 8, 2 * width), bf16)], SDS((1, 2 * width), f32)],
        [pltpu.VMEM((3, d, width), f32), pltpu.VMEM((3, width, d), f32), pltpu.VMEM((2, m, 2 * width), bf16)],
        parts=parts,
    )
    w_send, down_more, up_y, up_more = after(w_send, down_more, up_y, up_more)
    keep0, near0, keep1, near1 = keeps
    in_sums = [summed([k[1], x[1]]).astype(bf16) for k, x in ((keep0, near0), (keep1, near1))]
    down_more, up_y, up_more, in_sums[1] = after(down_more, up_y, up_more, in_sums[1])
    got = swap(w_send, "dp", 1)
    in_sums[0], _ = after(in_sums[0], w_send)
    far = [swap(x, "tensor", 2) for x in in_sums]
    got, far[0] = after(got, far[0])
    down_terms = down_kept + [down_more]
    at = up_y_next.size // d
    small = jnp.concatenate([small[0:6], small[7:8], small[7:8]]) + pair_sum(up_y, at, 8)
    up_terms = up_kept + [up_more, up_y[:at].reshape(up_y_next.shape)]
    for i in range(2, bits):
        down_terms, sent = halve_sum(down_terms, bits - 1 - i, bit_of[i])
        down_got = swap(sent, "dp", 1 << i)
        up_terms, sent = halve_sum(up_terms, bits - 1 - i, bit_of[i])
        up_rows = with_rows(sent, small)
        if i == 2:
            got, down_got, up_rows = after(got, down_got, up_rows)
        up_got = swap(up_rows, "dp", 1 << i)
        if i == bits - 1:
            break
        down_terms, up_terms, small = with_received(down_terms, down_got, up_terms, up_got, sent, small)
    row = 3 * (d // parts) // 2
    at = parts // 2 * row
    shape = ([2] * (bits - 1)) + [row, 2 * width]
    terms = [x.reshape(shape) for x in (w_keep, got[:at])]
    db = db + got[at : at + 1].astype(f32) + got[at + 1 : at + 2].astype(f32)
    for i in range(1, bits):
        kept, rows_sent, more = halve_with(terms, terms[0].ndim - 3, db, "dp", 1 << i, bit_of[i])
        if i == bits - 1:
            _, down_got, up_got = after(rows_sent, down_got, up_got)
        terms, db = kept, db + more
    down_terms, up_terms, small = with_received(down_terms, down_got, up_terms, up_got, sent, small)
    down_sum = summed(down_terms)
    up_sum = summed(up_terms)
    mine = small
    input_grad = jnp.stack([
        (summed([k[0], x[0], y]) + gfi[s * rows : (s + 1) * rows]).astype(bf16)
        for s, (k, x, y) in enumerate(((keep0, near0, far[0]), (keep1, near1, far[1])))
    ])
    qkv_sum = summed(terms)
    qkv_sum = jnp.concatenate([qkv_sum[:, :width], qkv_sum[:, width:]], axis=0).reshape(3, -1, width)
    qkv_sum = jnp.transpose(qkv_sum, (1, 0, 2))
    db = db.reshape(2, width)
    return (
        outputs,
        input_grad,
        qkv_sum,
        db,
        up_sum[block:],
        mine[0],
        mine[1],
        mine[2],
        up_sum[:block],
        mine[6],
        down_sum,
        mine[3],
        mine[4],
        mine[5],
    )


def pair_sum(array, at, n):
    return array[at : at + n].astype(f32) + array[at + n : at + 2 * n].astype(f32)


def with_rows(array, rows):
    flat = array.reshape(-1, array.shape[-1])
    high = rows.astype(bf16)
    low = (rows - high.astype(f32)).astype(bf16)
    return jnp.concatenate([flat, high, low], axis=0)


def halve_with(terms, axis, rows, name, bit, mine):
    other = [lax.dynamic_index_in_dim(t, 1 - mine, axis, keepdims=False) for t in terms]
    kept = [lax.dynamic_index_in_dim(t, mine, axis, keepdims=False) for t in terms]
    other = summed(other).astype(bf16)
    sent = with_rows(other, rows)
    got = swap(sent, name, bit)
    cut = other.size // other.shape[-1]
    return kept + [got[:cut].reshape(other.shape)], sent, pair_sum(got, cut, rows.shape[0])


def with_received(down_terms, down_got, up_terms, up_got, sent, small):
    at = sent.size // sent.shape[-1]
    small = small + pair_sum(up_got, at, small.shape[0])
    return down_terms + [down_got], up_terms + [up_got[:at].reshape(sent.shape)], small


def after(*values):
    return lax.optimization_barrier(values)


def solution(mesh):
    in_specs = (
        P("dp", None, None),
        P("dp", "tensor", None),
        P("dp"),
        P(None, None, "tensor"),
        P(None, "tensor"),
        P("tensor", None),
        P(),
        P(),
        P(),
        P(None, "tensor"),
        P("tensor"),
        P("tensor", None),
        P(),
        P(),
        P(),
    )
    out_specs = (
        P("dp", "tensor", None),
        P("dp", "tensor", None),
        P("dp", None, "tensor"),
        P(None, "tensor"),
        P(("tensor", "dp"), None),
        P(),
        P(),
        P(),
        P("dp", "tensor"),
        P("tensor"),
        P(("tensor", "dp"), None),
        P(),
        P(),
        P(),
    )
    return jax.shard_map(body, mesh=mesh, in_specs=in_specs, out_specs=out_specs, check_vma=False)
```

```python
import functools

import jax
import jax.numpy as jnp
from jax import lax
from jax.experimental import pallas as pl
from jax.experimental.pallas import tpu as pltpu
from jax.sharding import PartitionSpec as P

HEAD = 64
WIDE, LANES = 192, 256
NEAR = 30
NT = (((1,), (1,)), ((), ()))
NN = (((1,), (0,)), ((), ()))
TN = (((0,), (0,)), ((), ()))
bf16 = jnp.bfloat16
f32 = jnp.float32
VM = pl.BlockSpec(memory_space=pltpu.VMEM)
SDS = jax.ShapeDtypeStruct


def mm(a, b, dims=NN):
    return lax.dot_general(a, b, dims, preferred_element_type=f32)


class Fetch:
    def __init__(self, src, dst, sem):
        self.dst, self.copy = dst, pltpu.make_async_copy(src, dst, sem)
        self.copy.start()
        self.waiting = True

    def __call__(self):
        if self.waiting:
            self.copy.wait()
            self.waiting = False
        return self.dst


class Pieces:
    def __init__(self, copies, dst):
        self.copies, self.dst = copies, dst
        for c in copies:
            c.start()

    def __call__(self):
        for c in self.copies:
            c.wait()
        self.copies = []
        return self.dst


def pieces(info, a, b, dst, sem, z_first):
    part = a.shape[0] // 2
    copies = []
    for src, other in ((a, 0), (b, 1)):
        for i in range(2):
            flips = (other, i) if z_first else (i, other)
            at = 2 * (info[3] ^ flips[0]) + (info[4] ^ flips[1])
            rows = pl.ds(pl.multiple_of(at * part, part), part)
            copies.append(pltpu.make_async_copy(src.at[pl.ds(i * part, part)], dst.at[rows], sem.at[len(copies)]))
    return Pieces(copies, dst)


class Flush:
    def __init__(self, src, dst, sem):
        self.src, self.copy = src, pltpu.make_async_copy(src, dst, sem)
        self.started = False

    def start(self):
        if not self.started:
            self.copy.start()
        self.started = True


def call(name, body, info, ins, outs, scratch=(), vmem=58, which=0, cost=1000, **static):
    far_in = [i for i, a in enumerate(ins) if isinstance(a, tuple)]
    pinned = [i for i in far_in if len(ins[i]) == 2]
    far_out = [i for i, o in enumerate(outs) if isinstance(o, list)]
    raw_in = [i for i, a in enumerate(ins) if isinstance(a, Raw)]
    raw_out = [i for i, o in enumerate(outs) if isinstance(o, Raw)]
    pinned += [i for i in raw_in if ins[i].pinned]
    any_in = far_in + raw_in
    arrays = [a[0] if isinstance(a, tuple) else a.value if isinstance(a, Raw) else a for a in ins]
    shapes = [o[0] if isinstance(o, list) else o.value if isinstance(o, Raw) else o for o in outs]
    picked = [a[1] if isinstance(a, tuple) else None for a in ins]
    n_in, n_out = len(ins), len(outs)

    def kernel(lengths_ref, which_ref, *refs):
        dp = lax.axis_index("dp")
        at = which_ref[0]
        info_ref = (lengths_ref[0], lengths_ref[1], lax.axis_index("tensor"), dp & 1, (dp >> 1) & 1, at, lengths_ref[at], lengths_ref)
        in_refs, refs = refs[:n_in], refs[n_in:]
        out_refs, refs = refs[:n_out], refs[n_out:]
        sem, refs = refs[-1], refs[:-1]
        buffers, rest = refs[: len(far_in) + len(far_out)], refs[len(far_in) + len(far_out) :]
        args = list(in_refs)
        for j, i in enumerate(far_in):
            view = picked[i][1]
            args[i] = Fetch(view(in_refs[i], info_ref), buffers[j], sem.at[j])
        results = list(out_refs)
        flushes = []
        for j, i in enumerate(far_out):
            at = len(far_in) + j
            results[i] = Flush(buffers[at], out_refs[i], sem.at[at])
            flushes.append(results[i])
        body(info_ref, *args, *results, *rest, **static)
        for i in far_in:
            args[i]()
        for f in flushes:
            f.start()
        for f in flushes:
            f.copy.wait()

    hbm = pl.BlockSpec(memory_space=pltpu.HBM)
    buffers = [pltpu.VMEM(picked[i][0], arrays[i].dtype) for i in far_in]
    buffers += [pltpu.VMEM(shapes[i].shape, shapes[i].dtype) for i in far_out]
    return pl.pallas_call(
        kernel,
        out_shape=[pltpu.HBM(o.shape, o.dtype) if i in far_out + raw_out else o for i, o in enumerate(shapes)],
        grid_spec=pltpu.PrefetchScalarGridSpec(
            num_scalar_prefetch=2,
            grid=(1,),
            in_specs=[hbm if i in pinned else pl.BlockSpec(memory_space=pl.ANY) if i in any_in else VM for i in range(n_in)],
            out_specs=[hbm if i in far_out + raw_out else VM for i in range(n_out)],
            scratch_shapes=[*buffers, *scratch, pltpu.SemaphoreType.DMA((max(1, len(far_in) + len(far_out)),))],
        ),
        compiler_params=pltpu.CompilerParams(vmem_limit_bytes=vmem << 20),
        cost_estimate=pl.CostEstimate(flops=cost, bytes_accessed=1000, transcendentals=0),
        name=name,
    )(info, jnp.full((1,), which, jnp.int32), *[pltpu.with_memory_space_constraint(a, pltpu.HBM) if i in pinned else a for i, a in enumerate(arrays)])


class Raw:
    def __init__(self, value, pinned=True):
        self.value, self.pinned = value, pinned


def ref(x):
    return x() if isinstance(x, Fetch) else x.src if isinstance(x, Flush) else x


def whole(a):
    return (a, (a.shape, lambda ref, info: ref))


def loose(a):
    return (*whole(a), None)


def prepare_kernel(info, out_in, bias, up_in, dn_in, pack, up_half, dn_half):
    for src, dst in ((up_in, up_half), (dn_in, dn_half)):
        dst.src[...] = src()[...]
        dst.start()
    out_w = out_in()
    width, d = out_w.shape
    pack.src[0:width, :] = out_w[...]
    pack.src[width : width + 8, :] = jnp.broadcast_to(bias[...].reshape(1, d), (8, d))


def prepare(info, out_w, bias, up, dn):
    width, d = out_w.shape
    part = up.shape[0] // 4
    view = lambda ref, info: ref.at[pl.ds(pl.multiple_of((2 * info[3] + info[4]) * part, part), part)]
    ins = [whole(out_w), bias, (up, ((part, d), view)), (dn, ((part, d), view))]
    return call("prepare", prepare_kernel, info, ins, [[SDS((width + 8, d), bf16)]] + [[SDS((part, d), bf16)]] * 2)


def head_cols(a, h, extra=()):
    lane = lax.broadcasted_iota(jnp.int32, a.shape, 1)
    out = jnp.where((lane >= HEAD * h) & (lane < HEAD * (h + 1)), a, jnp.zeros_like(a))
    for i, e in enumerate(extra):
        out = jnp.where(lane == WIDE + i, e, out)
    return out


def tail_cols(rows, values):
    lane = lax.broadcasted_iota(jnp.int32, (rows, LANES - WIDE), 1)
    out = jnp.zeros((rows, LANES - WIDE), f32)
    for i, v in enumerate(values):
        out = jnp.where(lane == i, v, out)
    return out.astype(bf16)


def attend_fwd_kernel(info, x_hbm, w_ref, b_ref, *rest):
    far, outs = rest[:5], rest[5:9]
    x_all, *near, v_t, s_all, sem_in, sem_out = rest[9:]
    q_all, k_all, v_all, lse_all, c_all = near
    me = info[2]
    batch, peers, width, block = c_all.shape
    seq = peers * block
    heads = width // HEAD

    def fetch(s):
        return pltpu.make_async_copy(x_hbm.at[s], x_all.at[s], sem_in.at[s])

    def flush(s, i):
        return pltpu.make_async_copy(near[i].at[s], far[i].at[s], sem_out.at[s, i])

    for s in range(batch):
        fetch(s).start()
    w = w_ref()

    def one_sequence(s, carry):
        length = info[7][s]
        fetch(s).wait()
        x = x_all[s]
        k_all[s, :, 0:WIDE] = mm(x, w[1], NT).astype(bf16)
        row = lax.broadcasted_iota(jnp.int32, (seq, 1), 0)
        k_all[s, :, WIDE:LANES] = tail_cols(seq, (jnp.where(row < length, 0.0, -1e30),))
        q = mm(x, w[0], NT) + b_ref[0:1, :].astype(f32)
        q_all[s, :, 0:WIDE] = q.astype(bf16) * jnp.asarray(0.125, bf16)
        q_all[s, :, WIDE:LANES] = tail_cols(seq, (1.0,))
        v = (mm(x, w[2], NT) + b_ref[1:2, :].astype(f32)).astype(bf16)
        v_all[s] = v
        v_t[...] = v.T
        for i in range(3):
            flush(s, i).start()

        def two_blocks(n, carry):
            qb = q_all[s, pl.ds(pl.multiple_of(n * 2 * block, 2 * block), 2 * block), :]
            one = jnp.ones_like(qb[:, 0:1])
            for h in range(heads):
                s_all[h] = mm(k_all[s], head_cols(qb, h, (one,)), NT)
            for h in range(heads):
                top = jnp.max(s_all[h], axis=0, keepdims=True)
                p = jnp.exp(s_all[h] - top)
                total = jnp.sum(p, axis=0, keepdims=True)
                rows = slice(HEAD * h, HEAD * (h + 1))
                out = (mm(v_t[rows, :], p.astype(bf16)) * (1.0 / total)).astype(bf16)
                lse = top + jnp.log(total)
                for j in range(2):
                    cols = slice(block * j, block * (j + 1))
                    c_all[s, 2 * n + j, rows, :] = out[:, cols]
                    lse_all[s, 2 * n + j, h : h + 1, :] = lse[:, cols]
            return carry

        lax.fori_loop(0, peers // 2, two_blocks, 0)
        for i in range(3, 5):
            flush(s, i).start()
        for k, out in enumerate(outs):
            out.src[s] = c_all[s, me ^ k]
        return carry

    lax.fori_loop(0, batch, one_sequence, 0)
    for out in outs:
        out.start()
    for s in range(batch):
        for i in range(5):
            flush(s, i).wait()


def attend_fwd(info, inputs, w_t, bias, peers):
    batch, seq, d = inputs.shape
    width = w_t.shape[1]
    block = seq // peers
    far = [SDS((batch, seq, LANES), bf16)] * 2 + [SDS((batch, seq, width), bf16)]
    far += [SDS((batch, peers, 8, block), f32), SDS((batch, peers, width, block), bf16)]
    scratch = [pltpu.VMEM(inputs.shape, bf16), *[pltpu.VMEM(o.shape, o.dtype) for o in far]]
    scratch += [pltpu.VMEM((width, seq), bf16), pltpu.VMEM((width // HEAD, seq, 2 * block), f32)]
    scratch += [pltpu.SemaphoreType.DMA((batch,)), pltpu.SemaphoreType.DMA((batch, 5))]
    return call(
        "attend_fwd",
        attend_fwd_kernel,
        info,
        [Raw(inputs), whole(w_t), bias],
        [Raw(o) for o in far] + [[SDS((batch, width, block), bf16)]] * peers,
        scratch,
    )


def nth(at, ref, info):
    return ref.at[at]


def of_sequence(a):
    return (a, (a.shape[1:], lambda ref, info: ref.at[info[5]]))


def attend_bwd_kernel(info, x_ref, q_in, k_in, v_in, lse_in, c_in, *rest):
    w_ref = x_ref
    peers = 4
    gs, rest = rest[:peers], rest[peers:]
    keep, send, low_out, db_ref, dq_t, dk, dv, k_t, g_ref = rest
    low = low_out.src
    length = info[6]
    me = info[2]
    k_ref, q_ref, v_ref = k_in(), q_in(), v_in()
    lse_ref, c_ref = lse_in(), c_in()
    _, width, block = c_ref.shape
    heads = width // HEAD
    k_t[...] = k_ref[:, 0:WIDE].T
    dk[...] = jnp.zeros_like(dk)
    dv[...] = jnp.zeros_like(dv)
    for k in range(peers):
        g_ref[me ^ k] = gs[k]()[...]

    def one_block(s, carry):
        at = pl.multiple_of(s * block, block)

        @pl.when(at >= length)
        def _():
            dq_t[:, pl.ds(at, block)] = jnp.zeros((width, block), f32)

        @pl.when(at < length)
        def _():
            qb = q_ref[pl.ds(at, block), :]
            g_t = g_ref[s]
            g = g_t.T
            prod_t = g_t.astype(f32) * c_ref[s].astype(f32)
            for h in range(heads):
                rows = slice(HEAD * h, HEAD * (h + 1))
                qh = head_cols(qb, h)
                gh = head_cols(g, h)
                scores = mm(k_ref[...], qh, NT)
                row = lax.broadcasted_iota(jnp.int32, scores.shape, 0)
                p = jnp.where(row < length, jnp.exp(scores - lse_ref[s, h : h + 1, :]), 0.0)
                dp = mm(v_ref[...], gh, NT)
                inner = jnp.sum(prod_t[rows], axis=0, keepdims=True)
                ds = (p * (dp - inner)).astype(bf16)
                dv[...] += mm(p.astype(bf16), gh)
                dk[...] += mm(ds, qh)
                dq_t[rows, pl.ds(at, block)] = mm(k_t[rows, :], ds) * 0.125

        return carry

    lax.fori_loop(0, peers, one_block, 0)
    low[0] = dq_t[...].T.astype(bf16)
    low[1] = dk[:, 0:WIDE].astype(bf16)
    low[2] = dv[...].astype(bf16)
    w = w_ref()
    for s in range(peers):
        at = pl.multiple_of((me ^ s) * block, block)
        total = sum(mm(low[i, pl.ds(at, block), :], w[i]) for i in range(3))
        (send if s % 2 else keep).src[s // 2] = total.astype(bf16)
    send.start()
    keep.start()
    db_ref[...] = jnp.concatenate([rowsum(low[i].astype(f32)) for i in (0, 2)], axis=1)


def attend_bwd(which, info, w_t, q, k, v, lse, c, gs, d):
    _, peers, width, block = c.shape
    seq = peers * block
    outs = [[SDS((2, block, d), bf16)]] * 2 + [[SDS((3, seq, width), bf16)], SDS((1, 2 * width), f32)]
    scratch = [
        pltpu.VMEM((width, seq), f32),
        pltpu.VMEM((seq, LANES), f32),
        pltpu.VMEM((seq, width), f32),
        pltpu.VMEM((width, seq), bf16),
        pltpu.VMEM((peers, width, block), bf16),
    ]
    ins = [whole(w_t)] + [of_sequence(a) for a in (q, k, v, lse, c)]
    ins += [(g, ((width, block), lambda ref, info: ref.at[info[5]]), None) for g in gs]
    return call("attend_bwd", attend_bwd_kernel, info, ins, outs, scratch, which=which, cost=2 * 10**10)


def project_grads_kernel(info, x0, low0, x1, low1, db0, db1, keep, send, db_ref, dw, acc, pair, *, parts):
    _, d, width = dw.shape
    x, low = x0(), low0()
    for i in range(3):
        acc[i] = mm(low[i].T, x[...])
    x, low = x1(), low1()
    for i in range(3):
        dw[i] = (acc[i] + mm(low[i].T, x[...])).T
    rows = d // parts
    half = 3 * rows // 2
    for b in range(parts):
        flat = dw[:, b * rows : (b + 1) * rows, :].reshape(3 * rows, width)
        flat = jnp.concatenate([flat[0:half], flat[half : 2 * half]], axis=1).astype(bf16)
        pair[(b & 1) ^ info[3], (b >> 1) * half : (b // 2 + 1) * half, :] = flat
    n = keep.src.shape[0]
    send.src[0:n, :] = pair[1]
    keep.src[...] = pair[0]
    db = db0[...] + db1[...]
    db_ref[...] = db
    high = db.astype(bf16)
    send.src[n : n + 8, :] = jnp.concatenate(
        [high, (db - high.astype(f32)).astype(bf16), jnp.zeros((6, 2 * width), bf16)], axis=0
    )
    send.start()


def gelu_parts(h):
    t = 1.0 / (1.0 + (0.3275911 * 0.7071067811865476) * jnp.abs(h))
    poly = t * (0.127414796 + t * (-0.142248368 + t * (0.7107068705 + t * (-0.7265760135 + t * 0.5307027145))))
    bell = jnp.exp2((-0.5 * 1.4426950408889634) * (h * h))
    tail = poly * bell
    cum = jnp.where(h < 0, tail, 1.0 - tail)
    return h * cum, cum + h * (bell * 0.3989422804014327)


def norm_parts(v):
    center = v - jnp.mean(v, axis=1, keepdims=True)
    r = lax.rsqrt(jnp.mean(center * center, axis=1, keepdims=True) + 1e-12)
    return center * r, r


def norm_back(u, gain, nv, r):
    gu = u * gain
    return r * (gu - jnp.mean(gu, axis=1, keepdims=True) - nv * jnp.mean(gu * nv, axis=1, keepdims=True))


def rows_of(vectors):
    return jnp.concatenate([v[...].reshape(1, -1).astype(f32) for v in vectors], axis=0)


def rowsum(v):
    return jnp.sum(v, axis=0, keepdims=True)


def first_norm_kernel(info, x_in, *rest):
    par, rest = rows_of(rest[:6]), rest[6:]
    nv_ref, r_ref, low0, low1, low = rest[8:]
    cs, packs = [c() for c in rest[:4]], [p() for p in rest[4:8]]
    x_ref = x_in()
    batch, rows = x_ref.shape[:2]
    width = cs[0].shape[1]

    def one_sequence(s, carry):
        here = pl.ds(pl.multiple_of(s * rows, rows), rows)
        total = par[0:1, :] + x_ref[s].astype(f32)
        for k in range(4):
            total = total + mm(cs[k][s], packs[k][0:width, :], TN)
        nv, r = norm_parts(total)
        nv_ref[here, :] = nv
        r_ref[here, :] = r
        low[s] = (nv * par[1:2, :] + par[2:3, :]).astype(bf16)
        return carry

    lax.fori_loop(0, batch, one_sequence, 0)
    low0[...] = low[0]
    low1[...] = low[1]


def feed_kernel(info, *rest, width, far):
    low, (pack, *rest) = rest[:4], rest[4:]
    if far:
        u_a, u_b, d_a, d_b, p_own, p_sib, act_out, slope_out, own, sib, both, up, dn, sem = rest
        up = pieces(info, u_a, u_b, up, sem.at[0], False)
        dn = pieces(info, d_a, d_b, dn, sem.at[1], True)
        up = up()
    else:
        u_in, d_in, act_out, slope_out, own, sib, both = rest
        up = u_in()
    act, slope = ref(act_out), ref(slope_out)
    units = up.shape[1]
    bias = pack()
    step = 256
    n = low[0].shape[0]
    for i, x in enumerate(low):
        both[i * n : (i + 1) * n, :] = x[...]
    n = 2 * n

    def chunk(m, carry):
        cols = pl.ds(pl.multiple_of(m * step, step), step)
        hidden = mm(both[...], up[:, cols]) + bias[width : width + 1, cols].astype(f32)
        a, g = gelu_parts(hidden)
        act[:, cols] = a.astype(bf16)
        slope[:, cols] = g.astype(bf16)
        return carry

    lax.fori_loop(0, units // step, chunk, 0)
    if far:
        dn = dn()
        total = mm(act[...], dn[...])
        sib[...] = (p_sib[...] + total[n:]).astype(bf16)
        own[...] = p_own[...] + total[:n]
    else:
        dn = d_in()
        total = mm(act[...], dn[...])
        own[...] = total[:n]
        sib[...] = total[n:]


def second_norm_kernel(info, cot_in, *rest):
    par, (nv_in, own, got, outs, gsec_out, gs_low, small) = rows_of(rest[:6]), rest[6:]
    cot, nv_ref, gsec = cot_in(), ref(nv_in), ref(gsec_out)
    batch, rows, d = cot.shape

    def one_sequence(s, sums):
        here = pl.ds(pl.multiple_of(s * rows, rows), rows)
        total = own[here, :] + got[here, :].astype(f32) + par[3:4, :] + (nv_ref[here, :] * par[1:2, :] + par[2:3, :])
        nv, r = norm_parts(total)
        outs.src[s] = (nv * par[4:5, :] + par[5:6, :]).astype(bf16)
        at = info[2] * rows + lax.broadcasted_iota(jnp.int32, (rows, 1), 0)
        seed = jnp.where(at < info[7][s], cot[s].astype(f32), 0.0)
        g = norm_back(seed, par[4:5, :], nv, r)
        gsec[here, :] = g
        gs_low[here, :] = g.astype(bf16)
        return tuple(a + rowsum(b) for a, b in zip(sums, (g, seed * nv, seed)))

    sums = lax.fori_loop(0, batch, one_sequence, (jnp.zeros((1, d), f32),) * 3)
    small[...] = jnp.concatenate([*sums, jnp.zeros((5, d), f32)], axis=0)


def feed_back_kernel(info, gs, gs2, slope0, slope1, up0, dn0, u_a, u_b, d_a, d_b, gh_out, own, sib, ub, sides, up2, dn2, sem):
    gh = ref(gh_out)
    units = up0.dst.shape[1]
    dn2 = pieces(info, d_a, d_b, dn2, sem.at[1], True)
    up2 = pieces(info, u_a, u_b, up2, sem.at[0], False)
    ub[...] = jnp.zeros_like(ub)
    n = gs.shape[0]
    sides[0:n, :] = gs[...]
    sides[n : 2 * n, :] = gs2[...]
    step = 256
    for k, slope in enumerate((ref(slope0), ref(slope1))):
        if k:
            dn = dn2()
        else:
            dn = dn0()

        def chunk(m, carry):
            cols = pl.ds(pl.multiple_of(m * step, step), step)
            ga = mm(sides[...], dn[cols, :], NT)
            h = (ga * slope[:, cols].astype(f32)).astype(bf16)
            gh[k, :, cols] = h
            ub[k : k + 1, cols] += rowsum(h.astype(f32))
            return carry

        lax.fori_loop(0, units // step, chunk, 0)
    up2 = up2()
    up = up0()
    total = mm(gh[0], up[...], NT) + mm(gh[1], up2[...], NT)
    sib[...] = total[n:].astype(bf16)
    own[...] = total[:n]


def first_back_kernel(info, *rest):
    par, (nv_in, r_ref, own, got, gsec_in, small2, *rest) = rows_of(rest[:6]), rest[6:]
    cs, packs = [c() for c in rest[:4]], rest[4:8]
    gfi, g0, g1, g2, g3, okeep, osend, small, ga_low = rest[8:]
    nv_ref, gsec = ref(nv_in), ref(gsec_in)
    packs = [p() for p in packs]
    n, d = own.shape
    rows = n // 2
    width = cs[0].shape[1]

    def one_sequence(s, sums):
        here = pl.ds(pl.multiple_of(s * rows, rows), rows)
        u = own[here, :] + got[here, :].astype(f32) + gsec[here, :]
        nv = nv_ref[here, :]
        g = norm_back(u, par[1:2, :], nv, r_ref[here, :])
        gfi.src[here, :] = g
        low = g.astype(bf16)
        ga_low[here, :] = low
        for k, out in enumerate((g0, g1, g2, g3)):
            out.src[s] = mm(packs[k][0:width, :], low, NT).astype(bf16)
        return tuple(a + rowsum(b) for a, b in zip(sums, (g, u * nv, u)))

    sums = lax.fori_loop(0, 2, one_sequence, (jnp.zeros((1, d), f32),) * 3)
    for out in (g3, g2, g1, g0, gfi):
        out.start()
    for k in range(4):
        total = mm(cs[k][0], ga_low[0:rows, :]) + mm(cs[k][1], ga_low[rows:n, :])
        (osend if k % 2 else okeep).src[k // 2, 0:width, :] = total.astype(bf16)
    both = jnp.concatenate([*sums, small2[0:3, :], jnp.zeros((2, d), f32)], axis=0)
    small[...] = both
    high = both.astype(bf16)
    osend.src[0, width : width + 8, :] = high
    osend.src[1, width : width + 8, :] = (both - high.astype(f32)).astype(bf16)


def down_grads_kernel(info, act0, act1, gs, gs2, far_keep, keep, send, scr, sides, *, parts):
    units = act0.shape[1]
    n = gs.shape[0]
    sides[0:n, :] = gs[...]
    sides[n : 2 * n, :] = gs2[...]
    block = units // parts
    step = 384
    for k, (act, mine) in enumerate(((act1, far_keep), (act0, keep))):

        def chunk(m, carry):
            cols = pl.ds(pl.multiple_of(m * step, step), step)
            total = mm(act[:, cols], sides[...], TN).astype(bf16)
            for i in range(step // block):
                scr[(i & 1) ^ info[3], m * (step // block // 2) + (i >> 1)] = total[i * block : (i + 1) * block]
            return carry

        lax.fori_loop(0, units // step, chunk, 0)
        send.src[k] = scr[1]
        mine.src[...] = scr[0]
    send.start()


def up_grads_kernel(info, *rest, parts, width):
    lows, (gh_in, okeep, ogot, small, ub, far_keep, far_send, keep, send, sums, scr, both_low) = rest[:4], rest[4:]
    n = lows[0].shape[0]
    for i, x in enumerate(lows):
        both_low[i * n : (i + 1) * n, :] = x[...]
    gh = ref(gh_in)
    units = both_low.shape[1]
    block = units // parts
    extra = width // parts
    joint = block + extra
    n = parts // 2 * joint
    step = 384
    got = ogot()
    both = small[...] + got[0, width : width + 8, :].astype(f32) + got[1, width : width + 8, :].astype(f32)
    both = jnp.concatenate([both[0:6], ub[0:2, :]], axis=0)
    sums[...] = both
    high = both.astype(bf16)
    far_send.src[n : n + 8, :] = high
    far_send.src[n + 8 : n + 16, :] = (both - high.astype(f32)).astype(bf16)
    for k, mine, theirs in ((1, far_keep, far_send), (0, keep, send)):

        def chunk(m, carry):
            cols = pl.ds(pl.multiple_of(m * step, step), step)
            total = mm(both_low[:, cols], gh[k], TN).astype(bf16)
            for i in range(step // block):
                at = (m * (step // block // 4) + (i >> 2)) * 2 + (i & 1)
                scr[((i >> 1) & 1) ^ info[4], at, 0:block, :] = total[i * block : (i + 1) * block]
            return carry

        lax.fori_loop(0, units // step, chunk, 0)
        o = (okeep()[k, 0:width, :].astype(f32) + got[k, 0:width, :].astype(f32)).astype(bf16)
        for b in range(parts):
            at = (b >> 2) * 2 + (b & 1)
            scr[((b >> 1) & 1) ^ info[4], at, block:joint, :] = o[b * extra : (b + 1) * extra]
        for b in range(parts // 2):
            theirs.src[b * joint : (b + 1) * joint, :] = scr[1, b]
            mine.src[b * joint : (b + 1) * joint, :] = scr[0, b]
        theirs.start()
        mine.start()


def swap(x, axis, bit):
    size = lax.axis_size(axis)
    return lax.ppermute(x, axis, [(i, i ^ bit) for i in range(size)])


def summed(parts):
    return sum(p.astype(f32) for p in parts)


def spread(array, axis, parts):
    bits = parts.bit_length() - 1
    return array.reshape(*array.shape[:axis], *([2] * bits), array.shape[axis] // parts, *array.shape[axis + 1 :])


def halve_sum(terms, axis, mine):
    other = [lax.dynamic_index_in_dim(t, 1 - mine, axis, keepdims=False) for t in terms]
    kept = [lax.dynamic_index_in_dim(t, mine, axis, keepdims=False) for t in terms]
    return kept, summed(other).astype(bf16)


def halve(terms, axis, bit, mine):
    other = [lax.dynamic_index_in_dim(t, 1 - mine, axis, keepdims=False) for t in terms]
    kept = [lax.dynamic_index_in_dim(t, mine, axis, keepdims=False) for t in terms]
    other = summed(other).astype(bf16)
    return kept + [swap(other, "dp", bit)], other


def body(
    inputs,
    cotangent,
    lengths,
    qkv_weight,
    qkv_bias,
    out_weight,
    out_bias,
    first_gain,
    first_shift,
    up_weight,
    up_bias,
    down_weight,
    down_bias,
    second_gain,
    second_shift,
):
    batch, seq, d = inputs.shape
    rows = cotangent.shape[1]
    n = batch * rows
    width = out_weight.shape[0]
    units = up_weight.shape[1]
    peers = lax.axis_size("tensor")
    parts = lax.axis_size("dp")
    bits = parts.bit_length() - 1
    t = lax.axis_index("tensor")
    dp = lax.axis_index("dp")
    bit_of = [(dp >> i) & 1 for i in range(bits)]
    info = lengths
    par = [out_bias, first_gain, first_shift, down_bias, second_gain, second_shift]
    w_t = jnp.transpose(qkv_weight, (1, 2, 0))
    pack, u_part, d_part = prepare(info, out_weight, up_bias, up_weight, down_weight)
    pack2 = swap(pack, "tensor", 2)
    pack1 = swap(pack, "tensor", 1)
    u_part = swap(u_part, "tensor", 2)
    d_part = swap(d_part, "tensor", 2)
    q, k, v, lse, c, *cs = attend_fwd(info, inputs, w_t, qkv_bias, peers)
    saved = (q, k, v, lse, c)
    *cs, pack1, pack2, u_part, d_part = after(*cs, pack1, pack2, u_part, d_part)
    ctx = [cs[0]] + [swap(cs[j], "tensor", j) for j in range(1, peers)]
    u_next, d_next = swap(u_part, "dp", 1), swap(d_part, "dp", 2)
    *ctx, u_next, d_next = after(*ctx, u_next, d_next)
    u2a = jnp.concatenate([u_part, u_next])
    d2a = jnp.concatenate([d_part, d_next])
    pack2, u2a, d2a = after(pack2, u2a, d2a)
    pack3 = swap(pack2, "tensor", 1)
    packs = [pack, pack1, pack2, pack3]
    u2b = swap(u2a, "dp", 2)
    d2b = swap(d2a, "dp", 1)
    far_ctx = [whole(ctx[0])] + [loose(x) for x in ctx[1:]]
    far_packs = [whole(pack)] + [loose(p) for p in packs[1:]]
    share = (inputs, ((batch, rows, d), lambda ref, info: ref.at[:, pl.ds(pl.multiple_of(info[2] * rows, rows), rows), :]))
    nv1, r1, *low = call(
        "first_norm",
        first_norm_kernel,
        info,
        [share, *par, *far_ctx, *far_packs],
        [SDS((n, d), f32), SDS((n, 1), f32), SDS((rows, d), bf16), SDS((rows, d), bf16)],
        [pltpu.VMEM((batch, rows, d), bf16)],
        vmem=NEAR,
    )
    low2 = [swap(x, "tensor", 1) for x in low]
    pair = SDS((2 * n, units), bf16)
    part = SDS((n, d), f32)
    sides = pltpu.VMEM((2 * n, d), bf16)
    act0, slope0, own, sib = call(
        "feed",
        feed_kernel,
        info,
        [*low, *low2, far_packs[0], whole(up_weight), whole(down_weight)],
        [pair, pair, part, part],
        [sides],
        vmem=NEAR,
        width=width,
        far=False,
    )
    halves = [Raw(x, False) for x in (u2a, u2b, d2a, d2b)]
    both = [pltpu.VMEM((d, units), bf16), pltpu.VMEM((units, d), bf16), pltpu.SemaphoreType.DMA((2, 4))]
    act1, slope1, own, sib = call(
        "feed",
        feed_kernel,
        info,
        [*low, *low2, far_packs[2], *halves, own, sib],
        [pair, pair, part, SDS((n, d), bf16)],
        [sides, *both],
        vmem=NEAR,
        width=width,
        far=True,
    )
    got = swap(sib, "tensor", 1)
    outputs, gsec, gs_low, small2 = call(
        "second_norm",
        second_norm_kernel,
        info,
        [whole(cotangent), *par, nv1, own, got],
        [[SDS((batch, rows, d), bf16)], part, SDS((n, d), bf16), SDS((8, d), f32)],
        vmem=NEAR,
    )
    gs_low2 = swap(gs_low, "tensor", 1)
    gh, own, sib, ub = call(
        "feed_back",
        feed_back_kernel,
        info,
        [gs_low, gs_low2, slope0, slope1, whole(up_weight), whole(down_weight), *halves],
        [SDS((2, 2 * n, units), bf16), part, SDS((n, d), bf16), SDS((8, d), f32)],
        [sides, *both],
        vmem=NEAR,
    )
    got = swap(sib, "tensor", 1)
    block = units // parts
    half_shape = (parts // 2, block, d)
    down_far_keep, down_keep, down_send = call(
        "down_grads",
        down_grads_kernel,
        info,
        [act0, act1, gs_low, gs_low2],
        [[SDS(half_shape, bf16)], [SDS(half_shape, bf16)], [SDS((2, *half_shape), bf16)]],
        [pltpu.VMEM((2, *half_shape), bf16), sides],
        vmem=NEAR,
        parts=parts,
    )
    down_got = swap(down_send, "dp", 1)
    gfi, g0, g1, g2, g3, okeep, osend, small1 = call(
        "first_back",
        first_back_kernel,
        info,
        [*par, nv1, r1, own, got, gsec, small2, *far_ctx, *far_packs],
        [
            [part],
            *[[SDS((batch, width, rows), bf16)]] * 4,
            *[[SDS((2, width + 8, d), bf16)]] * 2,
            SDS((8, d), f32),
        ],
        [pltpu.VMEM((n, d), bf16)],
        vmem=NEAR,
    )
    gctx = [g0] + [swap(g, "tensor", j) for j, g in ((1, g1), (2, g2), (3, g3))]
    got_o = swap(osend, "tensor", 1)
    joint = block + width // parts
    cut = parts // 2 * joint
    up_far_keep, up_far_send, up_keep, up_send, small = call(
        "up_grads",
        up_grads_kernel,
        info,
        [*low, *low2, gh, whole(okeep), loose(got_o), small1, ub],
        [
            [SDS((cut, d), bf16)],
            [SDS((cut + 16, d), bf16)],
            [SDS((cut, d), bf16)],
            [SDS((cut, d), bf16)],
            SDS((8, d), f32),
        ],
        [pltpu.VMEM((2, parts // 2, joint, d), bf16), sides],
        vmem=NEAR,
        parts=parts,
        width=width,
    )
    *gctx, up_far_send = after(*gctx, up_far_send)
    up_far_got = swap(up_far_send, "dp", 2)
    *gctx, up_far_keep = after(*gctx, up_far_keep)
    lows, biases, keeps = [], [], []
    for s in range(batch):
        keep, send, low_grads, db = attend_bwd(s, info, w_t, *saved, gctx, d)
        biases.append(db)
        if s == 0:
            send, up_far_got, down_got = after(send, up_far_got, down_got)
        else:
            send, low_grads, down_y, up_got, up_more, near = after(send, low_grads, down_y, up_got, up_more, near)
            keeps.append(near)
        keeps.append(keep)
        near = swap(send, "tensor", 1)
        if s == 0:
            lows.append(low_grads)
            down_sum = summed([down_far_keep, down_got[0]]).astype(bf16)
            shape = ([2] * (bits - 1)) + [joint, d]
            small = small + pair_sum(up_far_got, cut, 8)
            terms = [x.reshape(shape) for x in (up_far_keep, up_far_got[:cut])]
            up_far_kept, up_far_next = halve_sum(terms, bits - 2, bit_of[0])
            up_far_rows = with_rows(up_far_next, small)
            tied = after(down_sum, up_far_rows, up_send, *gctx)
            (down_sum, up_far_rows, up_send), gctx = tied[:3], tied[3:]
            down_y = swap(down_sum, "tensor", 2)
            up_got = swap(up_send, "dp", 2)
            up_more = swap(up_far_rows, "dp", 1)
    keeps.append(near)
    shape = ([2] * (bits - 1)) + [block, d]
    down_terms = [x.reshape(shape) for x in (down_keep, down_got[1], down_y)]
    down_kept, down_next = halve_sum(down_terms, bits - 2, bit_of[1])
    at = up_far_next.size // d
    small = small + pair_sum(up_more, at, 8)
    small = jnp.concatenate([small[0:6], small[7:8], small[6:7]])
    up_y_next = summed(up_far_kept + [up_more[:at].reshape(up_far_next.shape)]).astype(bf16)
    up_y_rows = with_rows(up_y_next, small)
    shape = ([2] * (bits - 1)) + [joint, d]
    up_kept, up_next = halve_sum([x.reshape(shape) for x in (up_keep, up_got)], bits - 2, bit_of[0])
    low_grads, down_next, up_y_rows, up_next = after(low_grads, down_next, up_y_rows, up_next)
    lows.append(low_grads)
    down_more = swap(down_next, "dp", 2)
    up_y = swap(up_y_rows, "tensor", 2)
    up_more = swap(up_next, "dp", 1)
    m = 3 * d // 4
    operands = []
    for s in range(batch):
        operands += [(inputs, (inputs.shape[1:], functools.partial(nth, s))), whole(lows[s])]
    w_keep, w_send, db = call(
        "project_grads",
        project_grads_kernel,
        info,
        [*operands, *biases],
        [[SDS((m, 2 * width), bf16)], [SDS((m + 8, 2 * width), bf16)], SDS((1, 2 * width), f32)],
        [pltpu.VMEM((3, d, width), f32), pltpu.VMEM((3, width, d), f32), pltpu.VMEM((2, m, 2 * width), bf16)],
        parts=parts,
    )
    w_send, down_more, up_y, up_more = after(w_send, down_more, up_y, up_more)
    keep0, near0, keep1, near1 = keeps
    in_sums = [summed([k[1], x[1]]).astype(bf16) for k, x in ((keep0, near0), (keep1, near1))]
    down_more, up_y, up_more, in_sums[1] = after(down_more, up_y, up_more, in_sums[1])
    got = swap(w_send, "dp", 1)
    in_sums[0], _ = after(in_sums[0], w_send)
    far = [swap(x, "tensor", 2) for x in in_sums]
    got, far[0] = after(got, far[0])
    down_terms = down_kept + [down_more]
    at = up_y_next.size // d
    small = jnp.concatenate([small[0:6], small[7:8], small[7:8]]) + pair_sum(up_y, at, 8)
    up_terms = up_kept + [up_more, up_y[:at].reshape(up_y_next.shape)]
    for i in range(2, bits):
        down_terms, sent = halve_sum(down_terms, bits - 1 - i, bit_of[i])
        down_got = swap(sent, "dp", 1 << i)
        up_terms, sent = halve_sum(up_terms, bits - 1 - i, bit_of[i])
        up_rows = with_rows(sent, small)
        if i == 2:
            got, down_got, up_rows = after(got, down_got, up_rows)
        up_got = swap(up_rows, "dp", 1 << i)
        if i == bits - 1:
            break
        down_terms, up_terms, small = with_received(down_terms, down_got, up_terms, up_got, sent, small)
    row = 3 * (d // parts) // 2
    at = parts // 2 * row
    shape = ([2] * (bits - 1)) + [row, 2 * width]
    terms = [x.reshape(shape) for x in (w_keep, got[:at])]
    db = db + got[at : at + 1].astype(f32) + got[at + 1 : at + 2].astype(f32)
    for i in range(1, bits):
        kept, rows_sent, more = halve_with(terms, terms[0].ndim - 3, db, "dp", 1 << i, bit_of[i])
        if i == bits - 1:
            _, down_got, up_got = after(rows_sent, down_got, up_got)
        terms, db = kept, db + more
    down_terms, up_terms, small = with_received(down_terms, down_got, up_terms, up_got, sent, small)
    down_sum = summed(down_terms)
    up_sum = summed(up_terms)
    mine = small
    input_grad = jnp.stack([
        (summed([k[0], x[0], y]) + gfi[s * rows : (s + 1) * rows]).astype(bf16)
        for s, (k, x, y) in enumerate(((keep0, near0, far[0]), (keep1, near1, far[1])))
    ])
    qkv_sum = summed(terms)
    qkv_sum = jnp.concatenate([qkv_sum[:, :width], qkv_sum[:, width:]], axis=0).reshape(3, -1, width)
    qkv_sum = jnp.transpose(qkv_sum, (1, 0, 2))
    db = db.reshape(2, width)
    return (
        outputs,
        input_grad,
        qkv_sum,
        db,
        up_sum[block:],
        mine[0],
        mine[1],
        mine[2],
        up_sum[:block],
        mine[6],
        down_sum,
        mine[3],
        mine[4],
        mine[5],
    )


def pair_sum(array, at, n):
    return array[at : at + n].astype(f32) + array[at + n : at + 2 * n].astype(f32)


def with_rows(array, rows):
    flat = array.reshape(-1, array.shape[-1])
    high = rows.astype(bf16)
    low = (rows - high.astype(f32)).astype(bf16)
    return jnp.concatenate([flat, high, low], axis=0)


def halve_with(terms, axis, rows, name, bit, mine):
    other = [lax.dynamic_index_in_dim(t, 1 - mine, axis, keepdims=False) for t in terms]
    kept = [lax.dynamic_index_in_dim(t, mine, axis, keepdims=False) for t in terms]
    other = summed(other).astype(bf16)
    sent = with_rows(other, rows)
    got = swap(sent, name, bit)
    cut = other.size // other.shape[-1]
    return kept + [got[:cut].reshape(other.shape)], sent, pair_sum(got, cut, rows.shape[0])


def with_received(down_terms, down_got, up_terms, up_got, sent, small):
    at = sent.size // sent.shape[-1]
    small = small + pair_sum(up_got, at, small.shape[0])
    return down_terms + [down_got], up_terms + [up_got[:at].reshape(sent.shape)], small


def after(*values):
    return lax.optimization_barrier(values)


def solution(mesh):
    in_specs = (
        P("dp", None, None),
        P("dp", "tensor", None),
        P("dp"),
        P(None, None, "tensor"),
        P(None, "tensor"),
        P("tensor", None),
        P(),
        P(),
        P(),
        P(None, "tensor"),
        P("tensor"),
        P("tensor", None),
        P(),
        P(),
        P(),
    )
    out_specs = (
        P("dp", "tensor", None),
        P("dp", "tensor", None),
        P("dp", None, "tensor"),
        P(None, "tensor"),
        P(("tensor", "dp"), None),
        P(),
        P(),
        P(),
        P("dp", "tensor"),
        P("tensor"),
        P(("tensor", "dp"), None),
        P(),
        P(),
        P(),
    )
    return jax.shard_map(body, mesh=mesh, in_specs=in_specs, out_specs=out_specs, check_vma=False)
```

```python
import functools

import jax
import jax.numpy as jnp
from jax import lax
from jax.experimental import pallas as pl
from jax.experimental.pallas import tpu as pltpu
from jax.sharding import PartitionSpec as P

HEAD = 64
WIDE, LANES = 192, 256
NEAR = 30
NT = (((1,), (1,)), ((), ()))
NN = (((1,), (0,)), ((), ()))
TN = (((0,), (0,)), ((), ()))
bf16 = jnp.bfloat16
f32 = jnp.float32
VM = pl.BlockSpec(memory_space=pltpu.VMEM)
SDS = jax.ShapeDtypeStruct


def mm(a, b, dims=NN):
    return lax.dot_general(a, b, dims, preferred_element_type=f32)


class Fetch:
    def __init__(self, src, dst, sem):
        self.dst, self.copy = dst, pltpu.make_async_copy(src, dst, sem)
        self.copy.start()
        self.waiting = True

    def __call__(self):
        if self.waiting:
            self.copy.wait()
            self.waiting = False
        return self.dst


class Pieces:
    def __init__(self, copies, dst):
        self.copies, self.dst = copies, dst
        for c in copies:
            c.start()

    def __call__(self):
        for c in self.copies:
            c.wait()
        self.copies = []
        return self.dst


def pieces(info, a, b, dst, sem, z_first):
    part = a.shape[0] // 2
    copies = []
    for src, other in ((a, 0), (b, 1)):
        for i in range(2):
            flips = (other, i) if z_first else (i, other)
            at = 2 * (info[3] ^ flips[0]) + (info[4] ^ flips[1])
            rows = pl.ds(pl.multiple_of(at * part, part), part)
            copies.append(pltpu.make_async_copy(src.at[pl.ds(i * part, part)], dst.at[rows], sem.at[len(copies)]))
    return Pieces(copies, dst)


class Flush:
    def __init__(self, src, dst, sem):
        self.src, self.copy = src, pltpu.make_async_copy(src, dst, sem)
        self.started = False

    def start(self):
        if not self.started:
            self.copy.start()
        self.started = True


def call(name, body, info, ins, outs, scratch=(), vmem=58, which=0, cost=1000, **static):
    far_in = [i for i, a in enumerate(ins) if isinstance(a, tuple)]
    pinned = [i for i in far_in if len(ins[i]) == 2]
    far_out = [i for i, o in enumerate(outs) if isinstance(o, list)]
    raw_in = [i for i, a in enumerate(ins) if isinstance(a, Raw)]
    raw_out = [i for i, o in enumerate(outs) if isinstance(o, Raw)]
    pinned += [i for i in raw_in if ins[i].pinned]
    any_in = far_in + raw_in
    arrays = [a[0] if isinstance(a, tuple) else a.value if isinstance(a, Raw) else a for a in ins]
    shapes = [o[0] if isinstance(o, list) else o.value if isinstance(o, Raw) else o for o in outs]
    picked = [a[1] if isinstance(a, tuple) else None for a in ins]
    n_in, n_out = len(ins), len(outs)

    def kernel(lengths_ref, which_ref, *refs):
        dp = lax.axis_index("dp")
        at = which_ref[0]
        info_ref = (lengths_ref[0], lengths_ref[1], lax.axis_index("tensor"), dp & 1, (dp >> 1) & 1, at, lengths_ref[at], lengths_ref)
        in_refs, refs = refs[:n_in], refs[n_in:]
        out_refs, refs = refs[:n_out], refs[n_out:]
        sem, refs = refs[-1], refs[:-1]
        buffers, rest = refs[: len(far_in) + len(far_out)], refs[len(far_in) + len(far_out) :]
        args = list(in_refs)
        for j, i in enumerate(far_in):
            view = picked[i][1]
            args[i] = Fetch(view(in_refs[i], info_ref), buffers[j], sem.at[j])
        results = list(out_refs)
        flushes = []
        for j, i in enumerate(far_out):
            at = len(far_in) + j
            results[i] = Flush(buffers[at], out_refs[i], sem.at[at])
            flushes.append(results[i])
        body(info_ref, *args, *results, *rest, **static)
        for i in far_in:
            args[i]()
        for f in flushes:
            f.start()
        for f in flushes:
            f.copy.wait()

    hbm = pl.BlockSpec(memory_space=pltpu.HBM)
    buffers = [pltpu.VMEM(picked[i][0], arrays[i].dtype) for i in far_in]
    buffers += [pltpu.VMEM(shapes[i].shape, shapes[i].dtype) for i in far_out]
    return pl.pallas_call(
        kernel,
        out_shape=[pltpu.HBM(o.shape, o.dtype) if i in far_out + raw_out else o for i, o in enumerate(shapes)],
        grid_spec=pltpu.PrefetchScalarGridSpec(
            num_scalar_prefetch=2,
            grid=(1,),
            in_specs=[hbm if i in pinned else pl.BlockSpec(memory_space=pl.ANY) if i in any_in else VM for i in range(n_in)],
            out_specs=[hbm if i in far_out + raw_out else VM for i in range(n_out)],
            scratch_shapes=[*buffers, *scratch, pltpu.SemaphoreType.DMA((max(1, len(far_in) + len(far_out)),))],
        ),
        compiler_params=pltpu.CompilerParams(vmem_limit_bytes=vmem << 20),
        cost_estimate=pl.CostEstimate(flops=cost, bytes_accessed=1000, transcendentals=0),
        name=name,
    )(info, jnp.full((1,), which, jnp.int32), *[pltpu.with_memory_space_constraint(a, pltpu.HBM) if i in pinned else a for i, a in enumerate(arrays)])


class Raw:
    def __init__(self, value, pinned=True):
        self.value, self.pinned = value, pinned


def ref(x):
    return x() if isinstance(x, Fetch) else x.src if isinstance(x, Flush) else x


def whole(a):
    return (a, (a.shape, lambda ref, info: ref))


def loose(a):
    return (*whole(a), None)


def prepare_kernel(info, out_in, bias, up_in, dn_in, pack, up_half, dn_half):
    for src, dst in ((up_in, up_half), (dn_in, dn_half)):
        dst.src[...] = src()[...]
        dst.start()
    out_w = out_in()
    width, d = out_w.shape
    pack.src[0:width, :] = out_w[...]
    pack.src[width : width + 8, :] = jnp.broadcast_to(bias[...].reshape(1, d), (8, d))


def prepare(info, out_w, bias, up, dn):
    width, d = out_w.shape
    part = up.shape[0] // 4
    view = lambda ref, info: ref.at[pl.ds(pl.multiple_of((2 * info[3] + info[4]) * part, part), part)]
    ins = [whole(out_w), bias, (up, ((part, d), view)), (dn, ((part, d), view))]
    return call("prepare", prepare_kernel, info, ins, [[SDS((width + 8, d), bf16)]] + [[SDS((part, d), bf16)]] * 2)


def head_cols(a, h, extra=()):
    lane = lax.broadcasted_iota(jnp.int32, a.shape, 1)
    out = jnp.where((lane >= HEAD * h) & (lane < HEAD * (h + 1)), a, jnp.zeros_like(a))
    for i, e in enumerate(extra):
        out = jnp.where(lane == WIDE + i, e, out)
    return out


def tail_cols(rows, values):
    lane = lax.broadcasted_iota(jnp.int32, (rows, LANES - WIDE), 1)
    out = jnp.zeros((rows, LANES - WIDE), f32)
    for i, v in enumerate(values):
        out = jnp.where(lane == i, v, out)
    return out.astype(bf16)


def attend_fwd_kernel(info, x_hbm, w_ref, b_ref, *rest):
    far, outs = rest[:5], rest[5:9]
    x_all, *near, v_t, s_all, sem_in, sem_out = rest[9:]
    q_all, k_all, v_all, lse_all, c_all = near
    me = info[2]
    batch, peers, width, block = c_all.shape
    seq = peers * block
    heads = width // HEAD

    def fetch(s):
        return pltpu.make_async_copy(x_hbm.at[s], x_all.at[s], sem_in.at[s])

    def flush(s, i):
        return pltpu.make_async_copy(near[i].at[s], far[i].at[s], sem_out.at[s, i])

    for s in range(batch):
        fetch(s).start()
    w = w_ref()

    def one_sequence(s, carry):
        length = info[7][s]
        fetch(s).wait()
        x = x_all[s]
        k_all[s, :, 0:WIDE] = mm(x, w[1], NT).astype(bf16)
        row = lax.broadcasted_iota(jnp.int32, (seq, 1), 0)
        k_all[s, :, WIDE:LANES] = tail_cols(seq, (jnp.where(row < length, 0.0, -1e30),))
        q = mm(x, w[0], NT) + b_ref[0:1, :].astype(f32)
        q_all[s, :, 0:WIDE] = q.astype(bf16) * jnp.asarray(0.125, bf16)
        q_all[s, :, WIDE:LANES] = tail_cols(seq, (1.0,))
        v = (mm(x, w[2], NT) + b_ref[1:2, :].astype(f32)).astype(bf16)
        v_all[s] = v
        v_t[...] = v.T
        for i in range(3):
            flush(s, i).start()

        def two_blocks(n, carry):
            qb = q_all[s, pl.ds(pl.multiple_of(n * 2 * block, 2 * block), 2 * block), :]
            one = jnp.ones_like(qb[:, 0:1])
            for h in range(heads):
                s_all[h] = mm(k_all[s], head_cols(qb, h, (one,)), NT)
            for h in range(heads):
                top = jnp.max(s_all[h], axis=0, keepdims=True)
                p = jnp.exp(s_all[h] - top)
                total = jnp.sum(p, axis=0, keepdims=True)
                rows = slice(HEAD * h, HEAD * (h + 1))
                out = (mm(v_t[rows, :], p.astype(bf16)) * (1.0 / total)).astype(bf16)
                lse = top + jnp.log(total)
                for j in range(2):
                    cols = slice(block * j, block * (j + 1))
                    c_all[s, 2 * n + j, rows, :] = out[:, cols]
                    lse_all[s, 2 * n + j, h : h + 1, :] = lse[:, cols]
            return carry

        lax.fori_loop(0, peers // 2, two_blocks, 0)
        for i in range(3, 5):
            flush(s, i).start()
        for k, out in enumerate(outs):
            out.src[s] = c_all[s, me ^ k]
        return carry

    lax.fori_loop(0, batch, one_sequence, 0)
    for out in outs:
        out.start()
    for s in range(batch):
        for i in range(5):
            flush(s, i).wait()


def attend_fwd(info, inputs, w_t, bias, peers):
    batch, seq, d = inputs.shape
    width = w_t.shape[1]
    block = seq // peers
    far = [SDS((batch, seq, LANES), bf16)] * 2 + [SDS((batch, seq, width), bf16)]
    far += [SDS((batch, peers, 8, block), f32), SDS((batch, peers, width, block), bf16)]
    scratch = [pltpu.VMEM(inputs.shape, bf16), *[pltpu.VMEM(o.shape, o.dtype) for o in far]]
    scratch += [pltpu.VMEM((width, seq), bf16), pltpu.VMEM((width // HEAD, seq, 2 * block), f32)]
    scratch += [pltpu.SemaphoreType.DMA((batch,)), pltpu.SemaphoreType.DMA((batch, 5))]
    return call(
        "attend_fwd",
        attend_fwd_kernel,
        info,
        [Raw(inputs), whole(w_t), bias],
        [Raw(o) for o in far] + [[SDS((batch, width, block), bf16)]] * peers,
        scratch,
    )


def nth(at, ref, info):
    return ref.at[at]


def of_sequence(a):
    return (a, (a.shape[1:], lambda ref, info: ref.at[info[5]]))


def attend_bwd_kernel(info, x_ref, q_in, k_in, v_in, lse_in, c_in, *rest):
    w_ref = x_ref
    peers = 4
    gs, rest = rest[:peers], rest[peers:]
    keep, send, low_out, db_ref, dq_t, dk, dv, k_t, g_ref = rest
    low = low_out.src
    length = info[6]
    me = info[2]
    k_ref, q_ref, v_ref = k_in(), q_in(), v_in()
    lse_ref, c_ref = lse_in(), c_in()
    _, width, block = c_ref.shape
    heads = width // HEAD
    k_t[...] = k_ref[:, 0:WIDE].T
    dk[...] = jnp.zeros_like(dk)
    dv[...] = jnp.zeros_like(dv)
    for k in range(peers):
        g_ref[me ^ k] = gs[k]()[...]

    def one_block(s, carry):
        at = pl.multiple_of(s * block, block)

        @pl.when(at >= length)
        def _():
            dq_t[:, pl.ds(at, block)] = jnp.zeros((width, block), f32)

        @pl.when(at < length)
        def _():
            qb = q_ref[pl.ds(at, block), :]
            g_t = g_ref[s]
            g = g_t.T
            prod_t = g_t.astype(f32) * c_ref[s].astype(f32)
            for h in range(heads):
                rows = slice(HEAD * h, HEAD * (h + 1))
                qh = head_cols(qb, h)
                gh = head_cols(g, h)
                scores = mm(k_ref[...], qh, NT)
                row = lax.broadcasted_iota(jnp.int32, scores.shape, 0)
                p = jnp.where(row < length, jnp.exp(scores - lse_ref[s, h : h + 1, :]), 0.0)
                dp = mm(v_ref[...], gh, NT)
                inner = jnp.sum(prod_t[rows], axis=0, keepdims=True)
                ds = (p * (dp - inner)).astype(bf16)
                dv[...] += mm(p.astype(bf16), gh)
                dk[...] += mm(ds, qh)
                dq_t[rows, pl.ds(at, block)] = mm(k_t[rows, :], ds) * 0.125

        return carry

    lax.fori_loop(0, peers, one_block, 0)
    low[0] = dq_t[...].T.astype(bf16)
    low[1] = dk[:, 0:WIDE].astype(bf16)
    low[2] = dv[...].astype(bf16)
    w = w_ref()
    for s in range(peers):
        at = pl.multiple_of((me ^ s) * block, block)
        total = sum(mm(low[i, pl.ds(at, block), :], w[i]) for i in range(3))
        (send if s % 2 else keep).src[s // 2] = total.astype(bf16)
    send.start()
    keep.start()
    db_ref[...] = jnp.concatenate([rowsum(low[i].astype(f32)) for i in (0, 2)], axis=1)


def attend_bwd(which, info, w_t, q, k, v, lse, c, gs, d):
    _, peers, width, block = c.shape
    seq = peers * block
    outs = [[SDS((2, block, d), bf16)]] * 2 + [[SDS((3, seq, width), bf16)], SDS((1, 2 * width), f32)]
    scratch = [
        pltpu.VMEM((width, seq), f32),
        pltpu.VMEM((seq, LANES), f32),
        pltpu.VMEM((seq, width), f32),
        pltpu.VMEM((width, seq), bf16),
        pltpu.VMEM((peers, width, block), bf16),
    ]
    ins = [whole(w_t)] + [of_sequence(a) for a in (q, k, v, lse, c)]
    ins += [(g, ((width, block), lambda ref, info: ref.at[info[5]]), None) for g in gs]
    return call("attend_bwd", attend_bwd_kernel, info, ins, outs, scratch, which=which, cost=2 * 10**10)


def project_grads_kernel(info, x0, low0, x1, low1, db0, db1, keep, send, db_ref, dw, acc, pair, *, parts):
    _, d, width = dw.shape
    x, low = x0(), low0()
    for i in range(3):
        acc[i] = mm(low[i].T, x[...])
    x, low = x1(), low1()
    for i in range(3):
        dw[i] = (acc[i] + mm(low[i].T, x[...])).T
    rows = d // parts
    half = 3 * rows // 2
    for b in range(parts):
        flat = dw[:, b * rows : (b + 1) * rows, :].reshape(3 * rows, width)
        flat = jnp.concatenate([flat[0:half], flat[half : 2 * half]], axis=1).astype(bf16)
        pair[(b & 1) ^ info[3], (b >> 1) * half : (b // 2 + 1) * half, :] = flat
    n = keep.src.shape[0]
    send.src[0:n, :] = pair[1]
    keep.src[...] = pair[0]
    db = db0[...] + db1[...]
    db_ref[...] = db
    high = db.astype(bf16)
    send.src[n : n + 8, :] = jnp.concatenate(
        [high, (db - high.astype(f32)).astype(bf16), jnp.zeros((6, 2 * width), bf16)], axis=0
    )
    send.start()


def gelu_parts(h):
    t = 1.0 / (1.0 + (0.3275911 * 0.7071067811865476) * jnp.abs(h))
    poly = t * (0.127414796 + t * (-0.142248368 + t * (0.7107068705 + t * (-0.7265760135 + t * 0.5307027145))))
    bell = jnp.exp2((-0.5 * 1.4426950408889634) * (h * h))
    tail = poly * bell
    cum = jnp.where(h < 0, tail, 1.0 - tail)
    return h * cum, cum + h * (bell * 0.3989422804014327)


def norm_parts(v):
    center = v - jnp.mean(v, axis=1, keepdims=True)
    r = lax.rsqrt(jnp.mean(center * center, axis=1, keepdims=True) + 1e-12)
    return center * r, r


def norm_back(u, gain, nv, r):
    gu = u * gain
    return r * (gu - jnp.mean(gu, axis=1, keepdims=True) - nv * jnp.mean(gu * nv, axis=1, keepdims=True))


def rows_of(vectors):
    return jnp.concatenate([v[...].reshape(1, -1).astype(f32) for v in vectors], axis=0)


def rowsum(v):
    return jnp.sum(v, axis=0, keepdims=True)


def first_norm_kernel(info, x_in, *rest):
    par, rest = rows_of(rest[:6]), rest[6:]
    nv_ref, r_ref, low0, low1, low = rest[8:]
    cs, packs = [c() for c in rest[:4]], [p() for p in rest[4:8]]
    x_ref = x_in()
    batch, rows = x_ref.shape[:2]
    width = cs[0].shape[1]

    def one_sequence(s, carry):
        here = pl.ds(pl.multiple_of(s * rows, rows), rows)
        total = par[0:1, :] + x_ref[s].astype(f32)
        for k in range(4):
            total = total + mm(cs[k][s], packs[k][0:width, :], TN)
        nv, r = norm_parts(total)
        nv_ref[here, :] = nv
        r_ref[here, :] = r
        low[s] = (nv * par[1:2, :] + par[2:3, :]).astype(bf16)
        return carry

    lax.fori_loop(0, batch, one_sequence, 0)
    low0[...] = low[0]
    low1[...] = low[1]


def feed_kernel(info, *rest, width, far):
    low, (pack, *rest) = rest[:4], rest[4:]
    if far:
        u_a, u_b, d_a, d_b, p_own, p_sib, act_out, slope_out, own, sib, both, up, dn, sem = rest
        up = pieces(info, u_a, u_b, up, sem.at[0], False)
        dn = pieces(info, d_a, d_b, dn, sem.at[1], True)
        up = up()
    else:
        u_in, d_in, act_out, slope_out, own, sib, both = rest
        up = u_in()
    act, slope = ref(act_out), ref(slope_out)
    units = up.shape[1]
    bias = pack()
    step = 256
    n = low[0].shape[0]
    for i, x in enumerate(low):
        both[i * n : (i + 1) * n, :] = x[...]
    n = 2 * n

    def chunk(m, carry):
        cols = pl.ds(pl.multiple_of(m * step, step), step)
        hidden = mm(both[...], up[:, cols]) + bias[width : width + 1, cols].astype(f32)
        a, g = gelu_parts(hidden)
        act[:, cols] = a.astype(bf16)
        slope[:, cols] = g.astype(bf16)
        return carry

    lax.fori_loop(0, units // step, chunk, 0)
    if far:
        dn = dn()
        total = mm(act[...], dn[...])
        sib[...] = (p_sib[...] + total[n:]).astype(bf16)
        own[...] = p_own[...] + total[:n]
    else:
        dn = d_in()
        total = mm(act[...], dn[...])
        own[...] = total[:n]
        sib[...] = total[n:]


def second_norm_kernel(info, cot_in, *rest):
    par, (nv_in, own, got, outs, gsec_out, gs_low, small) = rows_of(rest[:6]), rest[6:]
    cot, nv_ref, gsec = cot_in(), ref(nv_in), ref(gsec_out)
    batch, rows, d = cot.shape

    def one_sequence(s, sums):
        here = pl.ds(pl.multiple_of(s * rows, rows), rows)
        total = own[here, :] + got[here, :].astype(f32) + par[3:4, :] + (nv_ref[here, :] * par[1:2, :] + par[2:3, :])
        nv, r = norm_parts(total)
        outs.src[s] = (nv * par[4:5, :] + par[5:6, :]).astype(bf16)
        at = info[2] * rows + lax.broadcasted_iota(jnp.int32, (rows, 1), 0)
        seed = jnp.where(at < info[7][s], cot[s].astype(f32), 0.0)
        g = norm_back(seed, par[4:5, :], nv, r)
        gsec[here, :] = g
        gs_low[here, :] = g.astype(bf16)
        return tuple(a + rowsum(b) for a, b in zip(sums, (g, seed * nv, seed)))

    sums = lax.fori_loop(0, batch, one_sequence, (jnp.zeros((1, d), f32),) * 3)
    small[...] = jnp.concatenate([*sums, jnp.zeros((5, d), f32)], axis=0)


def feed_back_kernel(info, gs, gs2, slope0, slope1, up0, dn0, u_a, u_b, d_a, d_b, gh_out, own, sib, ub, sides, up2, dn2, sem):
    gh = ref(gh_out)
    units = up0.dst.shape[1]
    dn2 = pieces(info, d_a, d_b, dn2, sem.at[1], True)
    up2 = pieces(info, u_a, u_b, up2, sem.at[0], False)
    ub[...] = jnp.zeros_like(ub)
    n = gs.shape[0]
    sides[0:n, :] = gs[...]
    sides[n : 2 * n, :] = gs2[...]
    step = 256
    for k, slope in enumerate((ref(slope0), ref(slope1))):
        if k:
            dn = dn2()
        else:
            dn = dn0()

        def chunk(m, carry):
            cols = pl.ds(pl.multiple_of(m * step, step), step)
            ga = mm(sides[...], dn[cols, :], NT)
            h = (ga * slope[:, cols].astype(f32)).astype(bf16)
            gh[k, :, cols] = h
            ub[k : k + 1, cols] += rowsum(h.astype(f32))
            return carry

        lax.fori_loop(0, units // step, chunk, 0)
    up2 = up2()
    up = up0()
    total = mm(gh[0], up[...], NT) + mm(gh[1], up2[...], NT)
    sib[...] = total[n:].astype(bf16)
    own[...] = total[:n]


def first_back_kernel(info, *rest):
    par, (nv_in, r_ref, own, got, gsec_in, small2, *rest) = rows_of(rest[:6]), rest[6:]
    cs, packs = [c() for c in rest[:4]], rest[4:8]
    gfi, g0, g1, g2, g3, okeep, osend, small, ga_low = rest[8:]
    nv_ref, gsec = ref(nv_in), ref(gsec_in)
    packs = [p() for p in packs]
    n, d = own.shape
    rows = n // 2
    width = cs[0].shape[1]

    def one_sequence(s, sums):
        here = pl.ds(pl.multiple_of(s * rows, rows), rows)
        u = own[here, :] + got[here, :].astype(f32) + gsec[here, :]
        nv = nv_ref[here, :]
        g = norm_back(u, par[1:2, :], nv, r_ref[here, :])
        gfi.src[here, :] = g
        low = g.astype(bf16)
        ga_low[here, :] = low
        for k, out in enumerate((g0, g1, g2, g3)):
            out.src[s] = mm(packs[k][0:width, :], low, NT).astype(bf16)
        return tuple(a + rowsum(b) for a, b in zip(sums, (g, u * nv, u)))

    sums = lax.fori_loop(0, 2, one_sequence, (jnp.zeros((1, d), f32),) * 3)
    for out in (g3, g2, g1, g0, gfi):
        out.start()
    for k in range(4):
        total = mm(cs[k][0], ga_low[0:rows, :]) + mm(cs[k][1], ga_low[rows:n, :])
        (osend if k % 2 else okeep).src[k // 2, 0:width, :] = total.astype(bf16)
    both = jnp.concatenate([*sums, small2[0:3, :], jnp.zeros((2, d), f32)], axis=0)
    small[...] = both
    high = both.astype(bf16)
    osend.src[0, width : width + 8, :] = high
    osend.src[1, width : width + 8, :] = (both - high.astype(f32)).astype(bf16)


def down_grads_kernel(info, act0, act1, gs, gs2, far_keep, keep, send, scr, sides, *, parts):
    units = act0.shape[1]
    n = gs.shape[0]
    sides[0:n, :] = gs[...]
    sides[n : 2 * n, :] = gs2[...]
    block = units // parts
    step = 384
    for k, (act, mine) in enumerate(((act1, far_keep), (act0, keep))):

        def chunk(m, carry):
            cols = pl.ds(pl.multiple_of(m * step, step), step)
            total = mm(act[:, cols], sides[...], TN).astype(bf16)
            for i in range(step // block):
                scr[(i & 1) ^ info[3], m * (step // block // 2) + (i >> 1)] = total[i * block : (i + 1) * block]
            return carry

        lax.fori_loop(0, units // step, chunk, 0)
        send.src[k] = scr[1]
        mine.src[...] = scr[0]
    send.start()


def up_grads_kernel(info, *rest, parts, width):
    lows, (gh_in, okeep, ogot, small, ub, far_keep, far_send, keep, send, sums, scr, both_low) = rest[:4], rest[4:]
    n = lows[0].shape[0]
    for i, x in enumerate(lows):
        both_low[i * n : (i + 1) * n, :] = x[...]
    gh = ref(gh_in)
    units = both_low.shape[1]
    block = units // parts
    extra = width // parts
    joint = block + extra
    n = parts // 2 * joint
    step = 384
    got = ogot()
    both = small[...] + got[0, width : width + 8, :].astype(f32) + got[1, width : width + 8, :].astype(f32)
    both = jnp.concatenate([both[0:6], ub[0:2, :]], axis=0)
    sums[...] = both
    high = both.astype(bf16)
    far_send.src[n : n + 8, :] = high
    far_send.src[n + 8 : n + 16, :] = (both - high.astype(f32)).astype(bf16)
    for k, mine, theirs in ((1, far_keep, far_send), (0, keep, send)):

        def chunk(m, carry):
            cols = pl.ds(pl.multiple_of(m * step, step), step)
            total = mm(both_low[:, cols], gh[k], TN).astype(bf16)
            for i in range(step // block):
                at = (m * (step // block // 4) + (i >> 2)) * 2 + (i & 1)
                scr[((i >> 1) & 1) ^ info[4], at, 0:block, :] = total[i * block : (i + 1) * block]
            return carry

        lax.fori_loop(0, units // step, chunk, 0)
        o = (okeep()[k, 0:width, :].astype(f32) + got[k, 0:width, :].astype(f32)).astype(bf16)
        for b in range(parts):
            at = (b >> 2) * 2 + (b & 1)
            scr[((b >> 1) & 1) ^ info[4], at, block:joint, :] = o[b * extra : (b + 1) * extra]
        for b in range(parts // 2):
            theirs.src[b * joint : (b + 1) * joint, :] = scr[1, b]
            mine.src[b * joint : (b + 1) * joint, :] = scr[0, b]
        theirs.start()
        mine.start()


def swap(x, axis, bit):
    size = lax.axis_size(axis)
    return lax.ppermute(x, axis, [(i, i ^ bit) for i in range(size)])


def summed(parts):
    return sum(p.astype(f32) for p in parts)


def spread(array, axis, parts):
    bits = parts.bit_length() - 1
    return array.reshape(*array.shape[:axis], *([2] * bits), array.shape[axis] // parts, *array.shape[axis + 1 :])


def halve_sum(terms, axis, mine):
    other = [lax.dynamic_index_in_dim(t, 1 - mine, axis, keepdims=False) for t in terms]
    kept = [lax.dynamic_index_in_dim(t, mine, axis, keepdims=False) for t in terms]
    return kept, summed(other).astype(bf16)


def halve(terms, axis, bit, mine):
    other = [lax.dynamic_index_in_dim(t, 1 - mine, axis, keepdims=False) for t in terms]
    kept = [lax.dynamic_index_in_dim(t, mine, axis, keepdims=False) for t in terms]
    other = summed(other).astype(bf16)
    return kept + [swap(other, "dp", bit)], other


def body(
    inputs,
    cotangent,
    lengths,
    qkv_weight,
    qkv_bias,
    out_weight,
    out_bias,
    first_gain,
    first_shift,
    up_weight,
    up_bias,
    down_weight,
    down_bias,
    second_gain,
    second_shift,
):
    batch, seq, d = inputs.shape
    rows = cotangent.shape[1]
    n = batch * rows
    width = out_weight.shape[0]
    units = up_weight.shape[1]
    peers = lax.axis_size("tensor")
    parts = lax.axis_size("dp")
    bits = parts.bit_length() - 1
    t = lax.axis_index("tensor")
    dp = lax.axis_index("dp")
    bit_of = [(dp >> i) & 1 for i in range(bits)]
    info = lengths
    par = [out_bias, first_gain, first_shift, down_bias, second_gain, second_shift]
    w_t = jnp.transpose(qkv_weight, (1, 2, 0))
    pack, u_part, d_part = prepare(info, out_weight, up_bias, up_weight, down_weight)
    pack2 = swap(pack, "tensor", 2)
    pack1 = swap(pack, "tensor", 1)
    u_part = swap(u_part, "tensor", 2)
    d_part = swap(d_part, "tensor", 2)
    q, k, v, lse, c, *cs = attend_fwd(info, inputs, w_t, qkv_bias, peers)
    saved = (q, k, v, lse, c)
    *cs, pack1, pack2, u_part, d_part = after(*cs, pack1, pack2, u_part, d_part)
    ctx = [cs[0]] + [swap(cs[j], "tensor", j) for j in range(1, peers)]
    u_next, d_next = swap(u_part, "dp", 1), swap(d_part, "dp", 2)
    *ctx, u_next, d_next = after(*ctx, u_next, d_next)
    u2a = jnp.concatenate([u_part, u_next])
    d2a = jnp.concatenate([d_part, d_next])
    pack2, u2a, d2a = after(pack2, u2a, d2a)
    pack3 = swap(pack2, "tensor", 1)
    packs = [pack, pack1, pack2, pack3]
    u2b = swap(u2a, "dp", 2)
    d2b = swap(d2a, "dp", 1)
    far_ctx = [whole(ctx[0])] + [loose(x) for x in ctx[1:]]
    far_packs = [whole(pack)] + [loose(p) for p in packs[1:]]
    share = (inputs, ((batch, rows, d), lambda ref, info: ref.at[:, pl.ds(pl.multiple_of(info[2] * rows, rows), rows), :]))
    nv1, r1, *low = call(
        "first_norm",
        first_norm_kernel,
        info,
        [share, *par, *far_ctx, *far_packs],
        [SDS((n, d), f32), SDS((n, 1), f32), SDS((rows, d), bf16), SDS((rows, d), bf16)],
        [pltpu.VMEM((batch, rows, d), bf16)],
        vmem=NEAR,
    )
    low2 = [swap(x, "tensor", 1) for x in low]
    pair = SDS((2 * n, units), bf16)
    part = SDS((n, d), f32)
    sides = pltpu.VMEM((2 * n, d), bf16)
    act0, slope0, own, sib = call(
        "feed",
        feed_kernel,
        info,
        [*low, *low2, far_packs[0], whole(up_weight), whole(down_weight)],
        [pair, pair, part, part],
        [sides],
        vmem=NEAR,
        width=width,
        far=False,
    )
    halves = [Raw(x, False) for x in (u2a, u2b, d2a, d2b)]
    both = [pltpu.VMEM((d, units), bf16), pltpu.VMEM((units, d), bf16), pltpu.SemaphoreType.DMA((2, 4))]
    act1, slope1, own, sib = call(
        "feed",
        feed_kernel,
        info,
        [*low, *low2, far_packs[2], *halves, own, sib],
        [pair, pair, part, SDS((n, d), bf16)],
        [sides, *both],
        vmem=NEAR,
        width=width,
        far=True,
    )
    got = swap(sib, "tensor", 1)
    outputs, gsec, gs_low, small2 = call(
        "second_norm",
        second_norm_kernel,
        info,
        [whole(cotangent), *par, nv1, own, got],
        [[SDS((batch, rows, d), bf16)], part, SDS((n, d), bf16), SDS((8, d), f32)],
        vmem=NEAR,
    )
    gs_low2 = swap(gs_low, "tensor", 1)
    gh, own, sib, ub = call(
        "feed_back",
        feed_back_kernel,
        info,
        [gs_low, gs_low2, slope0, slope1, whole(up_weight), whole(down_weight), *halves],
        [SDS((2, 2 * n, units), bf16), part, SDS((n, d), bf16), SDS((8, d), f32)],
        [sides, *both],
        vmem=NEAR,
    )
    got = swap(sib, "tensor", 1)
    block = units // parts
    half_shape = (parts // 2, block, d)
    down_far_keep, down_keep, down_send = call(
        "down_grads",
        down_grads_kernel,
        info,
        [act0, act1, gs_low, gs_low2],
        [[SDS(half_shape, bf16)], [SDS(half_shape, bf16)], [SDS((2, *half_shape), bf16)]],
        [pltpu.VMEM((2, *half_shape), bf16), sides],
        vmem=NEAR,
        parts=parts,
    )
    down_got = swap(down_send, "dp", 1)
    got, down_far_keep = after(got, down_far_keep)
    gfi, g0, g1, g2, g3, okeep, osend, small1 = call(
        "first_back",
        first_back_kernel,
        info,
        [*par, nv1, r1, own, got, gsec, small2, *far_ctx, *far_packs],
        [
            [part],
            *[[SDS((batch, width, rows), bf16)]] * 4,
            *[[SDS((2, width + 8, d), bf16)]] * 2,
            SDS((8, d), f32),
        ],
        [pltpu.VMEM((n, d), bf16)],
        vmem=NEAR,
    )
    gctx = [g0] + [swap(g, "tensor", j) for j, g in ((1, g1), (2, g2), (3, g3))]
    got_o = swap(osend, "tensor", 1)
    joint = block + width // parts
    cut = parts // 2 * joint
    up_far_keep, up_far_send, up_keep, up_send, small = call(
        "up_grads",
        up_grads_kernel,
        info,
        [*low, *low2, gh, whole(okeep), loose(got_o), small1, ub],
        [
            [SDS((cut, d), bf16)],
            [SDS((cut + 16, d), bf16)],
            [SDS((cut, d), bf16)],
            [SDS((cut, d), bf16)],
            SDS((8, d), f32),
        ],
        [pltpu.VMEM((2, parts // 2, joint, d), bf16), sides],
        vmem=NEAR,
        parts=parts,
        width=width,
    )
    *gctx, up_far_send = after(*gctx, up_far_send)
    up_far_got = swap(up_far_send, "dp", 2)
    *gctx, up_far_keep = after(*gctx, up_far_keep)
    lows, biases, keeps = [], [], []
    for s in range(batch):
        keep, send, low_grads, db = attend_bwd(s, info, w_t, *saved, gctx, d)
        biases.append(db)
        if s == 0:
            send, up_far_got, down_got = after(send, up_far_got, down_got)
        else:
            send, low_grads, down_y, up_got, up_more, near = after(send, low_grads, down_y, up_got, up_more, near)
            keeps.append(near)
        keeps.append(keep)
        near = swap(send, "tensor", 1)
        if s == 0:
            lows.append(low_grads)
            down_sum = summed([down_far_keep, down_got[0]]).astype(bf16)
            shape = ([2] * (bits - 1)) + [joint, d]
            small = small + pair_sum(up_far_got, cut, 8)
            terms = [x.reshape(shape) for x in (up_far_keep, up_far_got[:cut])]
            up_far_kept, up_far_next = halve_sum(terms, bits - 2, bit_of[0])
            up_far_rows = with_rows(up_far_next, small)
            tied = after(down_sum, up_far_rows, up_send, *gctx)
            (down_sum, up_far_rows, up_send), gctx = tied[:3], tied[3:]
            down_y = swap(down_sum, "tensor", 2)
            up_got = swap(up_send, "dp", 2)
            up_more = swap(up_far_rows, "dp", 1)
    keeps.append(near)
    shape = ([2] * (bits - 1)) + [block, d]
    down_terms = [x.reshape(shape) for x in (down_keep, down_got[1], down_y)]
    down_kept, down_next = halve_sum(down_terms, bits - 2, bit_of[1])
    at = up_far_next.size // d
    small = small + pair_sum(up_more, at, 8)
    small = jnp.concatenate([small[0:6], small[7:8], small[6:7]])
    up_y_next = summed(up_far_kept + [up_more[:at].reshape(up_far_next.shape)]).astype(bf16)
    up_y_rows = with_rows(up_y_next, small)
    shape = ([2] * (bits - 1)) + [joint, d]
    up_kept, up_next = halve_sum([x.reshape(shape) for x in (up_keep, up_got)], bits - 2, bit_of[0])
    low_grads, down_next, up_y_rows, up_next = after(low_grads, down_next, up_y_rows, up_next)
    lows.append(low_grads)
    down_more = swap(down_next, "dp", 2)
    up_y = swap(up_y_rows, "tensor", 2)
    up_more = swap(up_next, "dp", 1)
    m = 3 * d // 4
    operands = []
    for s in range(batch):
        operands += [(inputs, (inputs.shape[1:], functools.partial(nth, s))), whole(lows[s])]
    w_keep, w_send, db = call(
        "project_grads",
        project_grads_kernel,
        info,
        [*operands, *biases],
        [[SDS((m, 2 * width), bf16)], [SDS((m + 8, 2 * width), bf16)], SDS((1, 2 * width), f32)],
        [pltpu.VMEM((3, d, width), f32), pltpu.VMEM((3, width, d), f32), pltpu.VMEM((2, m, 2 * width), bf16)],
        parts=parts,
    )
    w_send, down_more, up_y, up_more = after(w_send, down_more, up_y, up_more)
    keep0, near0, keep1, near1 = keeps
    in_sums = [summed([k[1], x[1]]).astype(bf16) for k, x in ((keep0, near0), (keep1, near1))]
    down_more, up_y, up_more, in_sums[1] = after(down_more, up_y, up_more, in_sums[1])
    got = swap(w_send, "dp", 1)
    in_sums[0], _ = after(in_sums[0], w_send)
    far = [swap(x, "tensor", 2) for x in in_sums]
    got, far[0] = after(got, far[0])
    down_terms = down_kept + [down_more]
    at = up_y_next.size // d
    small = jnp.concatenate([small[0:6], small[7:8], small[7:8]]) + pair_sum(up_y, at, 8)
    up_terms = up_kept + [up_more, up_y[:at].reshape(up_y_next.shape)]
    for i in range(2, bits):
        down_terms, sent = halve_sum(down_terms, bits - 1 - i, bit_of[i])
        down_got = swap(sent, "dp", 1 << i)
        up_terms, sent = halve_sum(up_terms, bits - 1 - i, bit_of[i])
        up_rows = with_rows(sent, small)
        if i == 2:
            got, down_got, up_rows = after(got, down_got, up_rows)
        up_got = swap(up_rows, "dp", 1 << i)
        if i == bits - 1:
            break
        down_terms, up_terms, small = with_received(down_terms, down_got, up_terms, up_got, sent, small)
    row = 3 * (d // parts) // 2
    at = parts // 2 * row
    shape = ([2] * (bits - 1)) + [row, 2 * width]
    terms = [x.reshape(shape) for x in (w_keep, got[:at])]
    db = db + got[at : at + 1].astype(f32) + got[at + 1 : at + 2].astype(f32)
    for i in range(1, bits):
        kept, rows_sent, more = halve_with(terms, terms[0].ndim - 3, db, "dp", 1 << i, bit_of[i])
        if i == bits - 1:
            _, down_got, up_got = after(rows_sent, down_got, up_got)
        terms, db = kept, db + more
    down_terms, up_terms, small = with_received(down_terms, down_got, up_terms, up_got, sent, small)
    down_sum = summed(down_terms)
    up_sum = summed(up_terms)
    mine = small
    input_grad = jnp.stack([
        (summed([k[0], x[0], y]) + gfi[s * rows : (s + 1) * rows]).astype(bf16)
        for s, (k, x, y) in enumerate(((keep0, near0, far[0]), (keep1, near1, far[1])))
    ])
    qkv_sum = summed(terms)
    qkv_sum = jnp.concatenate([qkv_sum[:, :width], qkv_sum[:, width:]], axis=0).reshape(3, -1, width)
    qkv_sum = jnp.transpose(qkv_sum, (1, 0, 2))
    db = db.reshape(2, width)
    return (
        outputs,
        input_grad,
        qkv_sum,
        db,
        up_sum[block:],
        mine[0],
        mine[1],
        mine[2],
        up_sum[:block],
        mine[6],
        down_sum,
        mine[3],
        mine[4],
        mine[5],
    )


def pair_sum(array, at, n):
    return array[at : at + n].astype(f32) + array[at + n : at + 2 * n].astype(f32)


def with_rows(array, rows):
    flat = array.reshape(-1, array.shape[-1])
    high = rows.astype(bf16)
    low = (rows - high.astype(f32)).astype(bf16)
    return jnp.concatenate([flat, high, low], axis=0)


def halve_with(terms, axis, rows, name, bit, mine):
    other = [lax.dynamic_index_in_dim(t, 1 - mine, axis, keepdims=False) for t in terms]
    kept = [lax.dynamic_index_in_dim(t, mine, axis, keepdims=False) for t in terms]
    other = summed(other).astype(bf16)
    sent = with_rows(other, rows)
    got = swap(sent, name, bit)
    cut = other.size // other.shape[-1]
    return kept + [got[:cut].reshape(other.shape)], sent, pair_sum(got, cut, rows.shape[0])


def with_received(down_terms, down_got, up_terms, up_got, sent, small):
    at = sent.size // sent.shape[-1]
    small = small + pair_sum(up_got, at, small.shape[0])
    return down_terms + [down_got], up_terms + [up_got[:at].reshape(sent.shape)], small


def after(*values):
    return lax.optimization_barrier(values)


def solution(mesh):
    in_specs = (
        P("dp", None, None),
        P("dp", "tensor", None),
        P("dp"),
        P(None, None, "tensor"),
        P(None, "tensor"),
        P("tensor", None),
        P(),
        P(),
        P(),
        P(None, "tensor"),
        P("tensor"),
        P("tensor", None),
        P(),
        P(),
        P(),
    )
    out_specs = (
        P("dp", "tensor", None),
        P("dp", "tensor", None),
        P("dp", None, "tensor"),
        P(None, "tensor"),
        P(("tensor", "dp"), None),
        P(),
        P(),
        P(),
        P("dp", "tensor"),
        P("tensor"),
        P(("tensor", "dp"), None),
        P(),
        P(),
        P(),
    )
    return jax.shard_map(body, mesh=mesh, in_specs=in_specs, out_specs=out_specs, check_vma=False)
```

```python
import functools

import jax
import jax.numpy as jnp
from jax import lax
from jax.experimental import pallas as pl
from jax.experimental.pallas import tpu as pltpu
from jax.sharding import PartitionSpec as P

HEAD = 64
WIDE, LANES = 192, 256
NEAR = 30
NT = (((1,), (1,)), ((), ()))
NN = (((1,), (0,)), ((), ()))
TN = (((0,), (0,)), ((), ()))
bf16 = jnp.bfloat16
f32 = jnp.float32
VM = pl.BlockSpec(memory_space=pltpu.VMEM)
SDS = jax.ShapeDtypeStruct


def mm(a, b, dims=NN):
    return lax.dot_general(a, b, dims, preferred_element_type=f32)


class Fetch:
    def __init__(self, src, dst, sem):
        self.dst, self.copy = dst, pltpu.make_async_copy(src, dst, sem)
        self.copy.start()
        self.waiting = True

    def __call__(self):
        if self.waiting:
            self.copy.wait()
            self.waiting = False
        return self.dst


class Pieces:
    def __init__(self, copies, dst):
        self.copies, self.dst = copies, dst
        for c in copies:
            c.start()

    def __call__(self):
        for c in self.copies:
            c.wait()
        self.copies = []
        return self.dst


def pieces(info, a, b, dst, sem, z_first):
    part = a.shape[0] // 2
    copies = []
    for src, other in ((a, 0), (b, 1)):
        for i in range(2):
            flips = (other, i) if z_first else (i, other)
            at = 2 * (info[3] ^ flips[0]) + (info[4] ^ flips[1])
            rows = pl.ds(pl.multiple_of(at * part, part), part)
            copies.append(pltpu.make_async_copy(src.at[pl.ds(i * part, part)], dst.at[rows], sem.at[len(copies)]))
    return Pieces(copies, dst)


class Flush:
    def __init__(self, src, dst, sem):
        self.src, self.copy = src, pltpu.make_async_copy(src, dst, sem)
        self.started = False

    def start(self):
        if not self.started:
            self.copy.start()
        self.started = True


def call(name, body, info, ins, outs, scratch=(), vmem=58, which=0, cost=1000, **static):
    far_in = [i for i, a in enumerate(ins) if isinstance(a, tuple)]
    pinned = [i for i in far_in if len(ins[i]) == 2]
    far_out = [i for i, o in enumerate(outs) if isinstance(o, list)]
    raw_in = [i for i, a in enumerate(ins) if isinstance(a, Raw)]
    raw_out = [i for i, o in enumerate(outs) if isinstance(o, Raw)]
    pinned += [i for i in raw_in if ins[i].pinned]
    any_in = far_in + raw_in
    arrays = [a[0] if isinstance(a, tuple) else a.value if isinstance(a, Raw) else a for a in ins]
    shapes = [o[0] if isinstance(o, list) else o.value if isinstance(o, Raw) else o for o in outs]
    picked = [a[1] if isinstance(a, tuple) else None for a in ins]
    n_in, n_out = len(ins), len(outs)

    def kernel(lengths_ref, which_ref, *refs):
        dp = lax.axis_index("dp")
        at = which_ref[0]
        info_ref = (lengths_ref[0], lengths_ref[1], lax.axis_index("tensor"), dp & 1, (dp >> 1) & 1, at, lengths_ref[at], lengths_ref)
        in_refs, refs = refs[:n_in], refs[n_in:]
        out_refs, refs = refs[:n_out], refs[n_out:]
        sem, refs = refs[-1], refs[:-1]
        buffers, rest = refs[: len(far_in) + len(far_out)], refs[len(far_in) + len(far_out) :]
        args = list(in_refs)
        for j, i in enumerate(far_in):
            view = picked[i][1]
            args[i] = Fetch(view(in_refs[i], info_ref), buffers[j], sem.at[j])
        results = list(out_refs)
        flushes = []
        for j, i in enumerate(far_out):
            at = len(far_in) + j
            results[i] = Flush(buffers[at], out_refs[i], sem.at[at])
            flushes.append(results[i])
        body(info_ref, *args, *results, *rest, **static)
        for i in far_in:
            args[i]()
        for f in flushes:
            f.start()
        for f in flushes:
            f.copy.wait()

    hbm = pl.BlockSpec(memory_space=pltpu.HBM)
    buffers = [pltpu.VMEM(picked[i][0], arrays[i].dtype) for i in far_in]
    buffers += [pltpu.VMEM(shapes[i].shape, shapes[i].dtype) for i in far_out]
    return pl.pallas_call(
        kernel,
        out_shape=[pltpu.HBM(o.shape, o.dtype) if i in far_out + raw_out else o for i, o in enumerate(shapes)],
        grid_spec=pltpu.PrefetchScalarGridSpec(
            num_scalar_prefetch=2,
            grid=(1,),
            in_specs=[hbm if i in pinned else pl.BlockSpec(memory_space=pl.ANY) if i in any_in else VM for i in range(n_in)],
            out_specs=[hbm if i in far_out + raw_out else VM for i in range(n_out)],
            scratch_shapes=[*buffers, *scratch, pltpu.SemaphoreType.DMA((max(1, len(far_in) + len(far_out)),))],
        ),
        compiler_params=pltpu.CompilerParams(vmem_limit_bytes=vmem << 20),
        cost_estimate=pl.CostEstimate(flops=cost, bytes_accessed=1000, transcendentals=0),
        name=name,
    )(info, jnp.full((1,), which, jnp.int32), *[pltpu.with_memory_space_constraint(a, pltpu.HBM) if i in pinned else a for i, a in enumerate(arrays)])


class Raw:
    def __init__(self, value, pinned=True):
        self.value, self.pinned = value, pinned


def ref(x):
    return x() if isinstance(x, Fetch) else x.src if isinstance(x, Flush) else x


def whole(a):
    return (a, (a.shape, lambda ref, info: ref))


def loose(a):
    return (*whole(a), None)


def prepare_kernel(info, out_in, bias, up_in, dn_in, pack, up_half, dn_half):
    for src, dst in ((up_in, up_half), (dn_in, dn_half)):
        dst.src[...] = src()[...]
        dst.start()
    out_w = out_in()
    width, d = out_w.shape
    pack.src[0:width, :] = out_w[...]
    pack.src[width : width + 8, :] = jnp.broadcast_to(bias[...].reshape(1, d), (8, d))


def prepare(info, out_w, bias, up, dn):
    width, d = out_w.shape
    part = up.shape[0] // 4
    view = lambda ref, info: ref.at[pl.ds(pl.multiple_of((2 * info[3] + info[4]) * part, part), part)]
    ins = [whole(out_w), bias, (up, ((part, d), view)), (dn, ((part, d), view))]
    return call("prepare", prepare_kernel, info, ins, [[SDS((width + 8, d), bf16)]] + [[SDS((part, d), bf16)]] * 2)


def head_cols(a, h, extra=()):
    lane = lax.broadcasted_iota(jnp.int32, a.shape, 1)
    out = jnp.where((lane >= HEAD * h) & (lane < HEAD * (h + 1)), a, jnp.zeros_like(a))
    for i, e in enumerate(extra):
        out = jnp.where(lane == WIDE + i, e, out)
    return out


def tail_cols(rows, values):
    lane = lax.broadcasted_iota(jnp.int32, (rows, LANES - WIDE), 1)
    out = jnp.zeros((rows, LANES - WIDE), f32)
    for i, v in enumerate(values):
        out = jnp.where(lane == i, v, out)
    return out.astype(bf16)


def attend_fwd_kernel(info, x_hbm, w_ref, b_ref, *rest):
    far, outs = rest[:5], rest[5:9]
    x_all, *near, v_t, s_all, sem_in, sem_out = rest[9:]
    q_all, k_all, v_all, lse_all, c_all = near
    me = info[2]
    batch, peers, width, block = c_all.shape
    seq = peers * block
    heads = width // HEAD

    def fetch(s):
        return pltpu.make_async_copy(x_hbm.at[s], x_all.at[s], sem_in.at[s])

    def flush(s, i):
        return pltpu.make_async_copy(near[i].at[s], far[i].at[s], sem_out.at[s, i])

    for s in range(batch):
        fetch(s).start()
    w = w_ref()

    def one_sequence(s, carry):
        length = info[7][s]
        fetch(s).wait()
        x = x_all[s]
        k_all[s, :, 0:WIDE] = mm(x, w[1], NT).astype(bf16)
        row = lax.broadcasted_iota(jnp.int32, (seq, 1), 0)
        k_all[s, :, WIDE:LANES] = tail_cols(seq, (jnp.where(row < length, 0.0, -1e30),))
        q = mm(x, w[0], NT) + b_ref[0:1, :].astype(f32)
        q_all[s, :, 0:WIDE] = q.astype(bf16) * jnp.asarray(0.125, bf16)
        q_all[s, :, WIDE:LANES] = tail_cols(seq, (1.0,))
        v = (mm(x, w[2], NT) + b_ref[1:2, :].astype(f32)).astype(bf16)
        v_all[s] = v
        v_t[...] = v.T
        for i in range(3):
            flush(s, i).start()

        def two_blocks(n, carry):
            qb = q_all[s, pl.ds(pl.multiple_of(n * 2 * block, 2 * block), 2 * block), :]
            one = jnp.ones_like(qb[:, 0:1])
            for h in range(heads):
                s_all[h] = mm(k_all[s], head_cols(qb, h, (one,)), NT)
            for h in range(heads):
                top = jnp.max(s_all[h], axis=0, keepdims=True)
                p = jnp.exp(s_all[h] - top)
                total = jnp.sum(p, axis=0, keepdims=True)
                rows = slice(HEAD * h, HEAD * (h + 1))
                out = (mm(v_t[rows, :], p.astype(bf16)) * (1.0 / total)).astype(bf16)
                lse = top + jnp.log(total)
                for j in range(2):
                    cols = slice(block * j, block * (j + 1))
                    c_all[s, 2 * n + j, rows, :] = out[:, cols]
                    lse_all[s, 2 * n + j, h : h + 1, :] = lse[:, cols]
            return carry

        lax.fori_loop(0, peers // 2, two_blocks, 0)
        for i in range(3, 5):
            flush(s, i).start()
        for k, out in enumerate(outs):
            out.src[s] = c_all[s, me ^ k]
        return carry

    lax.fori_loop(0, batch, one_sequence, 0)
    for out in outs:
        out.start()
    for s in range(batch):
        for i in range(5):
            flush(s, i).wait()


def attend_fwd(info, inputs, w_t, bias, peers):
    batch, seq, d = inputs.shape
    width = w_t.shape[1]
    block = seq // peers
    far = [SDS((batch, seq, LANES), bf16)] * 2 + [SDS((batch, seq, width), bf16)]
    far += [SDS((batch, peers, 8, block), f32), SDS((batch, peers, width, block), bf16)]
    scratch = [pltpu.VMEM(inputs.shape, bf16), *[pltpu.VMEM(o.shape, o.dtype) for o in far]]
    scratch += [pltpu.VMEM((width, seq), bf16), pltpu.VMEM((width // HEAD, seq, 2 * block), f32)]
    scratch += [pltpu.SemaphoreType.DMA((batch,)), pltpu.SemaphoreType.DMA((batch, 5))]
    return call(
        "attend_fwd",
        attend_fwd_kernel,
        info,
        [Raw(inputs), whole(w_t), bias],
        [Raw(o) for o in far] + [[SDS((batch, width, block), bf16)]] * peers,
        scratch,
    )


def nth(at, ref, info):
    return ref.at[at]


def of_sequence(a):
    return (a, (a.shape[1:], lambda ref, info: ref.at[info[5]]))


def attend_bwd_kernel(info, x_ref, q_in, k_in, v_in, lse_in, c_in, *rest):
    w_ref = x_ref
    peers = 4
    gs, rest = rest[:peers], rest[peers:]
    keep, send, low_out, db_ref, dq_t, dk, dv, k_t, g_ref = rest
    low = low_out.src
    length = info[6]
    me = info[2]
    k_ref, q_ref, v_ref = k_in(), q_in(), v_in()
    lse_ref, c_ref = lse_in(), c_in()
    _, width, block = c_ref.shape
    heads = width // HEAD
    k_t[...] = k_ref[:, 0:WIDE].T
    dk[...] = jnp.zeros_like(dk)
    dv[...] = jnp.zeros_like(dv)
    for k in range(peers):
        g_ref[me ^ k] = gs[k]()[...]

    def one_block(s, carry):
        at = pl.multiple_of(s * block, block)

        @pl.when(at >= length)
        def _():
            dq_t[:, pl.ds(at, block)] = jnp.zeros((width, block), f32)

        @pl.when(at < length)
        def _():
            qb = q_ref[pl.ds(at, block), :]
            g_t = g_ref[s]
            g = g_t.T
            prod_t = g_t.astype(f32) * c_ref[s].astype(f32)
            for h in range(heads):
                rows = slice(HEAD * h, HEAD * (h + 1))
                qh = head_cols(qb, h)
                gh = head_cols(g, h)
                scores = mm(k_ref[...], qh, NT)
                row = lax.broadcasted_iota(jnp.int32, scores.shape, 0)
                p = jnp.where(row < length, jnp.exp(scores - lse_ref[s, h : h + 1, :]), 0.0)
                dp = mm(v_ref[...], gh, NT)
                inner = jnp.sum(prod_t[rows], axis=0, keepdims=True)
                ds = (p * (dp - inner)).astype(bf16)
                dv[...] += mm(p.astype(bf16), gh)
                dk[...] += mm(ds, qh)
                dq_t[rows, pl.ds(at, block)] = mm(k_t[rows, :], ds) * 0.125

        return carry

    lax.fori_loop(0, peers, one_block, 0)
    low[0] = dq_t[...].T.astype(bf16)
    low[1] = dk[:, 0:WIDE].astype(bf16)
    low[2] = dv[...].astype(bf16)
    w = w_ref()
    for s in range(peers):
        at = pl.multiple_of((me ^ s) * block, block)
        total = sum(mm(low[i, pl.ds(at, block), :], w[i]) for i in range(3))
        (send if s % 2 else keep).src[s // 2] = total.astype(bf16)
    send.start()
    keep.start()
    db_ref[...] = jnp.concatenate([rowsum(low[i].astype(f32)) for i in (0, 2)], axis=1)


def attend_bwd(which, info, w_t, q, k, v, lse, c, gs, d):
    _, peers, width, block = c.shape
    seq = peers * block
    outs = [[SDS((2, block, d), bf16)]] * 2 + [[SDS((3, seq, width), bf16)], SDS((1, 2 * width), f32)]
    scratch = [
        pltpu.VMEM((width, seq), f32),
        pltpu.VMEM((seq, LANES), f32),
        pltpu.VMEM((seq, width), f32),
        pltpu.VMEM((width, seq), bf16),
        pltpu.VMEM((peers, width, block), bf16),
    ]
    ins = [whole(w_t)] + [of_sequence(a) for a in (q, k, v, lse, c)]
    ins += [(g, ((width, block), lambda ref, info: ref.at[info[5]]), None) for g in gs]
    return call("attend_bwd", attend_bwd_kernel, info, ins, outs, scratch, which=which, cost=2 * 10**10)


def project_grads_kernel(info, x0, low0, x1, low1, db0, db1, keep, send, db_ref, dw, acc, pair, *, parts):
    _, d, width = dw.shape
    x, low = x0(), low0()
    for i in range(3):
        acc[i] = mm(low[i].T, x[...])
    x, low = x1(), low1()
    for i in range(3):
        dw[i] = (acc[i] + mm(low[i].T, x[...])).T
    rows = d // parts
    half = 3 * rows // 2
    for b in range(parts):
        flat = dw[:, b * rows : (b + 1) * rows, :].reshape(3 * rows, width)
        flat = jnp.concatenate([flat[0:half], flat[half : 2 * half]], axis=1).astype(bf16)
        pair[(b & 1) ^ info[3], (b >> 1) * half : (b // 2 + 1) * half, :] = flat
    n = keep.src.shape[0]
    send.src[0:n, :] = pair[1]
    keep.src[...] = pair[0]
    db = db0[...] + db1[...]
    db_ref[...] = db
    high = db.astype(bf16)
    send.src[n : n + 8, :] = jnp.concatenate(
        [high, (db - high.astype(f32)).astype(bf16), jnp.zeros((6, 2 * width), bf16)], axis=0
    )
    send.start()


def gelu_parts(h):
    t = 1.0 / (1.0 + (0.3275911 * 0.7071067811865476) * jnp.abs(h))
    poly = t * (0.127414796 + t * (-0.142248368 + t * (0.7107068705 + t * (-0.7265760135 + t * 0.5307027145))))
    bell = jnp.exp2((-0.5 * 1.4426950408889634) * (h * h))
    tail = poly * bell
    cum = jnp.where(h < 0, tail, 1.0 - tail)
    return h * cum, cum + h * (bell * 0.3989422804014327)


def norm_parts(v):
    center = v - jnp.mean(v, axis=1, keepdims=True)
    r = lax.rsqrt(jnp.mean(center * center, axis=1, keepdims=True) + 1e-12)
    return center * r, r


def norm_back(u, gain, nv, r):
    gu = u * gain
    return r * (gu - jnp.mean(gu, axis=1, keepdims=True) - nv * jnp.mean(gu * nv, axis=1, keepdims=True))


def rows_of(vectors):
    return jnp.concatenate([v[...].reshape(1, -1).astype(f32) for v in vectors], axis=0)


def rowsum(v):
    return jnp.sum(v, axis=0, keepdims=True)


def first_norm_kernel(info, x_in, *rest):
    par, rest = rows_of(rest[:6]), rest[6:]
    nv_ref, r_ref, low0, low1, low = rest[8:]
    cs, packs = [c() for c in rest[:4]], [p() for p in rest[4:8]]
    x_ref = x_in()
    batch, rows = x_ref.shape[:2]
    width = cs[0].shape[1]

    def one_sequence(s, carry):
        here = pl.ds(pl.multiple_of(s * rows, rows), rows)
        total = par[0:1, :] + x_ref[s].astype(f32)
        for k in range(4):
            total = total + mm(cs[k][s], packs[k][0:width, :], TN)
        nv, r = norm_parts(total)
        nv_ref[here, :] = nv
        r_ref[here, :] = r
        low[s] = (nv * par[1:2, :] + par[2:3, :]).astype(bf16)
        return carry

    lax.fori_loop(0, batch, one_sequence, 0)
    low0[...] = low[0]
    low1[...] = low[1]


def feed_kernel(info, *rest, width, far):
    low, (pack, *rest) = rest[:4], rest[4:]
    if far:
        u_a, u_b, d_a, d_b, p_own, p_sib, act_out, slope_out, own, sib, both, up, dn, sem = rest
        up = pieces(info, u_a, u_b, up, sem.at[0], False)
        dn = pieces(info, d_a, d_b, dn, sem.at[1], True)
        up = up()
    else:
        u_in, d_in, act_out, slope_out, own, sib, both = rest
        up = u_in()
    act, slope = ref(act_out), ref(slope_out)
    units = up.shape[1]
    bias = pack()
    step = 256
    n = low[0].shape[0]
    for i, x in enumerate(low):
        both[i * n : (i + 1) * n, :] = x[...]
    n = 2 * n

    def chunk(m, carry):
        cols = pl.ds(pl.multiple_of(m * step, step), step)
        hidden = mm(both[...], up[:, cols]) + bias[width : width + 1, cols].astype(f32)
        a, g = gelu_parts(hidden)
        act[:, cols] = a.astype(bf16)
        slope[:, cols] = g.astype(bf16)
        return carry

    lax.fori_loop(0, units // step, chunk, 0)
    if far:
        dn = dn()
        total = mm(act[...], dn[...])
        sib[...] = (p_sib[...] + total[n:]).astype(bf16)
        own[...] = p_own[...] + total[:n]
    else:
        dn = d_in()
        total = mm(act[...], dn[...])
        own[...] = total[:n]
        sib[...] = total[n:]


def second_norm_kernel(info, cot_in, *rest):
    par, (nv_in, own, got, outs, gsec_out, gs_low, small) = rows_of(rest[:6]), rest[6:]
    cot, nv_ref, gsec = cot_in(), ref(nv_in), ref(gsec_out)
    batch, rows, d = cot.shape

    def one_sequence(s, sums):
        here = pl.ds(pl.multiple_of(s * rows, rows), rows)
        total = own[here, :] + got[here, :].astype(f32) + par[3:4, :] + (nv_ref[here, :] * par[1:2, :] + par[2:3, :])
        nv, r = norm_parts(total)
        outs.src[s] = (nv * par[4:5, :] + par[5:6, :]).astype(bf16)
        at = info[2] * rows + lax.broadcasted_iota(jnp.int32, (rows, 1), 0)
        seed = jnp.where(at < info[7][s], cot[s].astype(f32), 0.0)
        g = norm_back(seed, par[4:5, :], nv, r)
        gsec[here, :] = g
        gs_low[here, :] = g.astype(bf16)
        return tuple(a + rowsum(b) for a, b in zip(sums, (g, seed * nv, seed)))

    sums = lax.fori_loop(0, batch, one_sequence, (jnp.zeros((1, d), f32),) * 3)
    small[...] = jnp.concatenate([*sums, jnp.zeros((5, d), f32)], axis=0)


def feed_back_kernel(info, gs, gs2, slope0, slope1, up0, dn0, u_a, u_b, d_a, d_b, gh_out, own, sib, ub, sides, up2, dn2, sem):
    gh = ref(gh_out)
    units = up0.dst.shape[1]
    dn2 = pieces(info, d_a, d_b, dn2, sem.at[1], True)
    up2 = pieces(info, u_a, u_b, up2, sem.at[0], False)
    ub[...] = jnp.zeros_like(ub)
    n = gs.shape[0]
    sides[0:n, :] = gs[...]
    sides[n : 2 * n, :] = gs2[...]
    step = 256
    for k, slope in enumerate((ref(slope0), ref(slope1))):
        if k:
            dn = dn2()
        else:
            dn = dn0()

        def chunk(m, carry):
            cols = pl.ds(pl.multiple_of(m * step, step), step)
            ga = mm(sides[...], dn[cols, :], NT)
            h = (ga * slope[:, cols].astype(f32)).astype(bf16)
            gh[k, :, cols] = h
            ub[k : k + 1, cols] += rowsum(h.astype(f32))
            return carry

        lax.fori_loop(0, units // step, chunk, 0)
    up2 = up2()
    up = up0()
    total = mm(gh[0], up[...], NT) + mm(gh[1], up2[...], NT)
    sib[...] = total[n:].astype(bf16)
    own[...] = total[:n]


def first_back_kernel(info, *rest):
    par, (nv_in, r_ref, own, got, gsec_in, small2, *rest) = rows_of(rest[:6]), rest[6:]
    cs, packs = [c() for c in rest[:4]], rest[4:8]
    gfi, g0, g1, g2, g3, okeep, osend, small, ga_low = rest[8:]
    nv_ref, gsec = ref(nv_in), ref(gsec_in)
    packs = [p() for p in packs]
    n, d = own.shape
    rows = n // 2
    width = cs[0].shape[1]

    def one_sequence(s, sums):
        here = pl.ds(pl.multiple_of(s * rows, rows), rows)
        u = own[here, :] + got[here, :].astype(f32) + gsec[here, :]
        nv = nv_ref[here, :]
        g = norm_back(u, par[1:2, :], nv, r_ref[here, :])
        gfi.src[here, :] = g
        low = g.astype(bf16)
        ga_low[here, :] = low
        for k, out in enumerate((g0, g1, g2, g3)):
            out.src[s] = mm(packs[k][0:width, :], low, NT).astype(bf16)
        return tuple(a + rowsum(b) for a, b in zip(sums, (g, u * nv, u)))

    sums = lax.fori_loop(0, 2, one_sequence, (jnp.zeros((1, d), f32),) * 3)
    for out in (g3, g2, g1, g0, gfi):
        out.start()
    for k in range(4):
        total = mm(cs[k][0], ga_low[0:rows, :]) + mm(cs[k][1], ga_low[rows:n, :])
        (osend if k % 2 else okeep).src[k // 2, 0:width, :] = total.astype(bf16)
    both = jnp.concatenate([*sums, small2[0:3, :], jnp.zeros((2, d), f32)], axis=0)
    small[...] = both
    high = both.astype(bf16)
    osend.src[0, width : width + 8, :] = high
    osend.src[1, width : width + 8, :] = (both - high.astype(f32)).astype(bf16)


def down_grads_kernel(info, act0, act1, gs, gs2, far_keep, keep, send, scr, sides, *, parts):
    units = act0.shape[1]
    n = gs.shape[0]
    sides[0:n, :] = gs[...]
    sides[n : 2 * n, :] = gs2[...]
    block = units // parts
    step = 384
    for k, (act, mine) in enumerate(((act1, far_keep), (act0, keep))):

        def chunk(m, carry):
            cols = pl.ds(pl.multiple_of(m * step, step), step)
            total = mm(act[:, cols], sides[...], TN).astype(bf16)
            for i in range(step // block):
                scr[(i & 1) ^ info[3], m * (step // block // 2) + (i >> 1)] = total[i * block : (i + 1) * block]
            return carry

        lax.fori_loop(0, units // step, chunk, 0)
        send.src[k] = scr[1]
        mine.src[...] = scr[0]
    send.start()


def up_grads_kernel(info, *rest, parts, width):
    lows, (gh_in, okeep, ogot, small, ub, far_keep, far_send, keep, send, sums, scr, both_low) = rest[:4], rest[4:]
    n = lows[0].shape[0]
    for i, x in enumerate(lows):
        both_low[i * n : (i + 1) * n, :] = x[...]
    gh = ref(gh_in)
    units = both_low.shape[1]
    block = units // parts
    extra = width // parts
    joint = block + extra
    n = parts // 2 * joint
    step = 384
    got = ogot()
    both = small[...] + got[0, width : width + 8, :].astype(f32) + got[1, width : width + 8, :].astype(f32)
    both = jnp.concatenate([both[0:6], ub[0:2, :]], axis=0)
    sums[...] = both
    high = both.astype(bf16)
    far_send.src[n : n + 8, :] = high
    far_send.src[n + 8 : n + 16, :] = (both - high.astype(f32)).astype(bf16)
    for k, mine, theirs in ((1, far_keep, far_send), (0, keep, send)):

        def chunk(m, carry):
            cols = pl.ds(pl.multiple_of(m * step, step), step)
            total = mm(both_low[:, cols], gh[k], TN).astype(bf16)
            for i in range(step // block):
                at = (m * (step // block // 4) + (i >> 2)) * 2 + (i & 1)
                scr[((i >> 1) & 1) ^ info[4], at, 0:block, :] = total[i * block : (i + 1) * block]
            return carry

        lax.fori_loop(0, units // step, chunk, 0)
        o = (okeep()[k, 0:width, :].astype(f32) + got[k, 0:width, :].astype(f32)).astype(bf16)
        for b in range(parts):
            at = (b >> 2) * 2 + (b & 1)
            scr[((b >> 1) & 1) ^ info[4], at, block:joint, :] = o[b * extra : (b + 1) * extra]
        for b in range(parts // 2):
            theirs.src[b * joint : (b + 1) * joint, :] = scr[1, b]
            mine.src[b * joint : (b + 1) * joint, :] = scr[0, b]
        theirs.start()
        mine.start()


def swap(x, axis, bit):
    size = lax.axis_size(axis)
    return lax.ppermute(x, axis, [(i, i ^ bit) for i in range(size)])


def summed(parts):
    return sum(p.astype(f32) for p in parts)


def spread(array, axis, parts):
    bits = parts.bit_length() - 1
    return array.reshape(*array.shape[:axis], *([2] * bits), array.shape[axis] // parts, *array.shape[axis + 1 :])


def halve_sum(terms, axis, mine):
    other = [lax.dynamic_index_in_dim(t, 1 - mine, axis, keepdims=False) for t in terms]
    kept = [lax.dynamic_index_in_dim(t, mine, axis, keepdims=False) for t in terms]
    return kept, summed(other).astype(bf16)


def halve(terms, axis, bit, mine):
    other = [lax.dynamic_index_in_dim(t, 1 - mine, axis, keepdims=False) for t in terms]
    kept = [lax.dynamic_index_in_dim(t, mine, axis, keepdims=False) for t in terms]
    other = summed(other).astype(bf16)
    return kept + [swap(other, "dp", bit)], other


def body(
    inputs,
    cotangent,
    lengths,
    qkv_weight,
    qkv_bias,
    out_weight,
    out_bias,
    first_gain,
    first_shift,
    up_weight,
    up_bias,
    down_weight,
    down_bias,
    second_gain,
    second_shift,
):
    batch, seq, d = inputs.shape
    rows = cotangent.shape[1]
    n = batch * rows
    width = out_weight.shape[0]
    units = up_weight.shape[1]
    peers = lax.axis_size("tensor")
    parts = lax.axis_size("dp")
    bits = parts.bit_length() - 1
    t = lax.axis_index("tensor")
    dp = lax.axis_index("dp")
    bit_of = [(dp >> i) & 1 for i in range(bits)]
    info = lengths
    par = [out_bias, first_gain, first_shift, down_bias, second_gain, second_shift]
    w_t = jnp.transpose(qkv_weight, (1, 2, 0))
    pack, u_part, d_part = prepare(info, out_weight, up_bias, up_weight, down_weight)
    pack2 = swap(pack, "tensor", 2)
    pack1 = swap(pack, "tensor", 1)
    u_part = swap(u_part, "tensor", 2)
    d_part = swap(d_part, "tensor", 2)
    q, k, v, lse, c, *cs = attend_fwd(info, inputs, w_t, qkv_bias, peers)
    saved = (q, k, v, lse, c)
    *cs, pack1, pack2, u_part, d_part = after(*cs, pack1, pack2, u_part, d_part)
    ctx = [cs[0]] + [swap(cs[j], "tensor", j) for j in range(1, peers)]
    u_next, d_next = swap(u_part, "dp", 1), swap(d_part, "dp", 2)
    *ctx, u_next, d_next = after(*ctx, u_next, d_next)
    u2a = jnp.concatenate([u_part, u_next])
    d2a = jnp.concatenate([d_part, d_next])
    pack2, u2a, d2a = after(pack2, u2a, d2a)
    pack3 = swap(pack2, "tensor", 1)
    packs = [pack, pack1, pack2, pack3]
    u2b = swap(u2a, "dp", 2)
    d2b = swap(d2a, "dp", 1)
    far_ctx = [whole(ctx[0])] + [loose(x) for x in ctx[1:]]
    far_packs = [whole(pack)] + [loose(p) for p in packs[1:]]
    share = (inputs, ((batch, rows, d), lambda ref, info: ref.at[:, pl.ds(pl.multiple_of(info[2] * rows, rows), rows), :]))
    nv1, r1, *low = call(
        "first_norm",
        first_norm_kernel,
        info,
        [share, *par, *far_ctx, *far_packs],
        [SDS((n, d), f32), SDS((n, 1), f32), SDS((rows, d), bf16), SDS((rows, d), bf16)],
        [pltpu.VMEM((batch, rows, d), bf16)],
        vmem=NEAR,
    )
    low2 = [swap(x, "tensor", 1) for x in low]
    pair = SDS((2 * n, units), bf16)
    part = SDS((n, d), f32)
    sides = pltpu.VMEM((2 * n, d), bf16)
    act0, slope0, own, sib = call(
        "feed",
        feed_kernel,
        info,
        [*low, *low2, far_packs[0], whole(up_weight), whole(down_weight)],
        [pair, pair, part, part],
        [sides],
        vmem=NEAR,
        width=width,
        far=False,
    )
    halves = [Raw(x, False) for x in (u2a, u2b, d2a, d2b)]
    both = [pltpu.VMEM((d, units), bf16), pltpu.VMEM((units, d), bf16), pltpu.SemaphoreType.DMA((2, 4))]
    act1, slope1, own, sib = call(
        "feed",
        feed_kernel,
        info,
        [*low, *low2, far_packs[2], *halves, own, sib],
        [pair, pair, part, SDS((n, d), bf16)],
        [sides, *both],
        vmem=NEAR,
        width=width,
        far=True,
    )
    got = swap(sib, "tensor", 1)
    outputs, gsec, gs_low, small2 = call(
        "second_norm",
        second_norm_kernel,
        info,
        [whole(cotangent), *par, nv1, own, got],
        [[SDS((batch, rows, d), bf16)], part, SDS((n, d), bf16), SDS((8, d), f32)],
        vmem=NEAR,
    )
    gs_low2 = swap(gs_low, "tensor", 1)
    gh, own, sib, ub = call(
        "feed_back",
        feed_back_kernel,
        info,
        [gs_low, gs_low2, slope0, slope1, whole(up_weight), whole(down_weight), *halves],
        [SDS((2, 2 * n, units), bf16), part, SDS((n, d), bf16), SDS((8, d), f32)],
        [sides, *both],
        vmem=NEAR,
    )
    got = swap(sib, "tensor", 1)
    block = units // parts
    half_shape = (parts // 2, block, d)
    down_far_keep, down_keep, down_send = call(
        "down_grads",
        down_grads_kernel,
        info,
        [act0, act1, gs_low, gs_low2],
        [[SDS(half_shape, bf16)], [SDS(half_shape, bf16)], [SDS((2, *half_shape), bf16)]],
        [pltpu.VMEM((2, *half_shape), bf16), sides],
        vmem=NEAR,
        parts=parts,
    )
    down_got = swap(down_send, "dp", 1)
    got, down_far_keep = after(got, down_far_keep)
    gfi, g0, g1, g2, g3, okeep, osend, small1 = call(
        "first_back",
        first_back_kernel,
        info,
        [*par, nv1, r1, own, got, gsec, small2, *far_ctx, *far_packs],
        [
            [part],
            *[[SDS((batch, width, rows), bf16)]] * 4,
            *[[SDS((2, width + 8, d), bf16)]] * 2,
            SDS((8, d), f32),
        ],
        [pltpu.VMEM((n, d), bf16)],
        vmem=NEAR,
    )
    gctx = [g0] + [swap(g, "tensor", j) for j, g in ((1, g1), (2, g2), (3, g3))]
    got_o = swap(osend, "tensor", 1)
    joint = block + width // parts
    cut = parts // 2 * joint
    up_far_keep, up_far_send, up_keep, up_send, small = call(
        "up_grads",
        up_grads_kernel,
        info,
        [*low, *low2, gh, whole(okeep), loose(got_o), small1, ub],
        [
            [SDS((cut, d), bf16)],
            [SDS((cut + 16, d), bf16)],
            [SDS((cut, d), bf16)],
            [SDS((cut, d), bf16)],
            SDS((8, d), f32),
        ],
        [pltpu.VMEM((2, parts // 2, joint, d), bf16), sides],
        vmem=NEAR,
        parts=parts,
        width=width,
    )
    *gctx, up_far_send = after(*gctx, up_far_send)
    up_far_got = swap(up_far_send, "dp", 2)
    *gctx, up_far_keep = after(*gctx, up_far_keep)
    lows, biases, keeps = [], [], []
    for s in range(batch):
        keep, send, low_grads, db = attend_bwd(s, info, w_t, *saved, gctx, d)
        biases.append(db)
        if s == 0:
            send, up_far_got, down_got = after(send, up_far_got, down_got)
        else:
            send, low_grads, down_y, up_got, up_more, near = after(send, low_grads, down_y, up_got, up_more, near)
            keeps.append(near)
        keeps.append(keep)
        near = swap(send, "tensor", 1)
        if s == 0:
            lows.append(low_grads)
            down_sum = summed([down_far_keep, down_got[0]]).astype(bf16)
            shape = ([2] * (bits - 1)) + [joint, d]
            small = small + pair_sum(up_far_got, cut, 8)
            terms = [x.reshape(shape) for x in (up_far_keep, up_far_got[:cut])]
            up_far_kept, up_far_next = halve_sum(terms, bits - 2, bit_of[0])
            up_far_rows = with_rows(up_far_next, small)
            tied = after(down_sum, up_far_rows, up_send, *gctx)
            (down_sum, up_far_rows, up_send), gctx = tied[:3], tied[3:]
            down_y = swap(down_sum, "tensor", 2)
            up_got = swap(up_send, "dp", 2)
            up_more = swap(up_far_rows, "dp", 1)
    keeps.append(near)
    shape = ([2] * (bits - 1)) + [block, d]
    down_terms = [x.reshape(shape) for x in (down_keep, down_got[1], down_y)]
    down_kept, down_next = halve_sum(down_terms, bits - 2, bit_of[1])
    at = up_far_next.size // d
    small = small + pair_sum(up_more, at, 8)
    small = jnp.concatenate([small[0:6], small[7:8], small[6:7]])
    up_y_next = summed(up_far_kept + [up_more[:at].reshape(up_far_next.shape)]).astype(bf16)
    up_y_rows = with_rows(up_y_next, small)
    shape = ([2] * (bits - 1)) + [joint, d]
    up_kept, up_next = halve_sum([x.reshape(shape) for x in (up_keep, up_got)], bits - 2, bit_of[0])
    low_grads, down_next, up_y_rows, up_next = after(low_grads, down_next, up_y_rows, up_next)
    lows.append(low_grads)
    down_more = swap(down_next, "dp", 2)
    up_y = swap(up_y_rows, "tensor", 2)
    up_more = swap(up_next, "dp", 1)
    m = 3 * d // 4
    operands = []
    for s in range(batch):
        operands += [(inputs, (inputs.shape[1:], functools.partial(nth, s))), whole(lows[s])]
    w_keep, w_send, db = call(
        "project_grads",
        project_grads_kernel,
        info,
        [*operands, *biases],
        [[SDS((m, 2 * width), bf16)], [SDS((m + 8, 2 * width), bf16)], SDS((1, 2 * width), f32)],
        [pltpu.VMEM((3, d, width), f32), pltpu.VMEM((3, width, d), f32), pltpu.VMEM((2, m, 2 * width), bf16)],
        parts=parts,
    )
    w_send, down_more, up_y, up_more = after(w_send, down_more, up_y, up_more)
    keep0, near0, keep1, near1 = keeps
    in_sums = [summed([k[1], x[1]]).astype(bf16) for k, x in ((keep0, near0), (keep1, near1))]
    down_more, up_y, up_more, in_sums[1] = after(down_more, up_y, up_more, in_sums[1])
    got = swap(w_send, "dp", 1)
    in_sums[0], _ = after(in_sums[0], w_send)
    far = [swap(x, "tensor", 2) for x in in_sums]
    got, far[0] = after(got, far[0])
    down_terms = down_kept + [down_more]
    at = up_y_next.size // d
    small = jnp.concatenate([small[0:6], small[7:8], small[7:8]]) + pair_sum(up_y, at, 8)
    up_terms = up_kept + [up_more, up_y[:at].reshape(up_y_next.shape)]
    for i in range(2, bits):
        down_terms, sent = halve_sum(down_terms, bits - 1 - i, bit_of[i])
        down_got = swap(sent, "dp", 1 << i)
        up_terms, sent = halve_sum(up_terms, bits - 1 - i, bit_of[i])
        up_rows = with_rows(sent, small)
        if i == 2:
            got, down_got, up_rows = after(got, down_got, up_rows)
        up_got = swap(up_rows, "dp", 1 << i)
        if i == bits - 1:
            break
        down_terms, up_terms, small = with_received(down_terms, down_got, up_terms, up_got, sent, small)
    row = 3 * (d // parts) // 2
    at = parts // 2 * row
    shape = ([2] * (bits - 1)) + [row, 2 * width]
    terms = [x.reshape(shape) for x in (w_keep, got[:at])]
    db = db + got[at : at + 1].astype(f32) + got[at + 1 : at + 2].astype(f32)
    for i in range(1, bits):
        kept, rows_sent, more = halve_with(terms, terms[0].ndim - 3, db, "dp", 1 << i, bit_of[i])
        if i == bits - 1:
            _, down_got, up_got = after(rows_sent, down_got, up_got)
        terms, db = kept, db + more
    down_terms, up_terms, small = with_received(down_terms, down_got, up_terms, up_got, sent, small)
    down_sum = summed(down_terms)
    up_sum = summed(up_terms)
    mine = small
    input_grad = jnp.stack([
        (summed([k[0], x[0], y]) + gfi[s * rows : (s + 1) * rows]).astype(bf16)
        for s, (k, x, y) in enumerate(((keep0, near0, far[0]), (keep1, near1, far[1])))
    ])
    sides = [jnp.concatenate([x[:, :width], x[:, width:]], axis=0) for x in terms[:-1]]
    last = jnp.concatenate([terms[-1][:, :width], terms[-1][:, width:]], axis=0)
    qkv_sum = (summed(sides) + last.astype(f32)).reshape(3, -1, width)
    qkv_sum = jnp.transpose(qkv_sum, (1, 0, 2))
    db = db.reshape(2, width)
    return (
        outputs,
        input_grad,
        qkv_sum,
        db,
        up_sum[block:],
        mine[0],
        mine[1],
        mine[2],
        up_sum[:block],
        mine[6],
        down_sum,
        mine[3],
        mine[4],
        mine[5],
    )


def pair_sum(array, at, n):
    return array[at : at + n].astype(f32) + array[at + n : at + 2 * n].astype(f32)


def with_rows(array, rows):
    flat = array.reshape(-1, array.shape[-1])
    high = rows.astype(bf16)
    low = (rows - high.astype(f32)).astype(bf16)
    return jnp.concatenate([flat, high, low], axis=0)


def halve_with(terms, axis, rows, name, bit, mine):
    other = [lax.dynamic_index_in_dim(t, 1 - mine, axis, keepdims=False) for t in terms]
    kept = [lax.dynamic_index_in_dim(t, mine, axis, keepdims=False) for t in terms]
    other = summed(other).astype(bf16)
    sent = with_rows(other, rows)
    got = swap(sent, name, bit)
    cut = other.size // other.shape[-1]
    return kept + [got[:cut].reshape(other.shape)], sent, pair_sum(got, cut, rows.shape[0])


def with_received(down_terms, down_got, up_terms, up_got, sent, small):
    at = sent.size // sent.shape[-1]
    small = small + pair_sum(up_got, at, small.shape[0])
    return down_terms + [down_got], up_terms + [up_got[:at].reshape(sent.shape)], small


def after(*values):
    return lax.optimization_barrier(values)


def solution(mesh):
    in_specs = (
        P("dp", None, None),
        P("dp", "tensor", None),
        P("dp"),
        P(None, None, "tensor"),
        P(None, "tensor"),
        P("tensor", None),
        P(),
        P(),
        P(),
        P(None, "tensor"),
        P("tensor"),
        P("tensor", None),
        P(),
        P(),
        P(),
    )
    out_specs = (
        P("dp", "tensor", None),
        P("dp", "tensor", None),
        P("dp", None, "tensor"),
        P(None, "tensor"),
        P(("tensor", "dp"), None),
        P(),
        P(),
        P(),
        P("dp", "tensor"),
        P("tensor"),
        P(("tensor", "dp"), None),
        P(),
        P(),
        P(),
    )
    return jax.shard_map(body, mesh=mesh, in_specs=in_specs, out_specs=out_specs, check_vma=False)
```

```python
import functools

import jax
import jax.numpy as jnp
from jax import lax
from jax.experimental import pallas as pl
from jax.experimental.pallas import tpu as pltpu
from jax.sharding import PartitionSpec as P

HEAD = 64
WIDE, LANES = 192, 256
NEAR = 30
NT = (((1,), (1,)), ((), ()))
NN = (((1,), (0,)), ((), ()))
TN = (((0,), (0,)), ((), ()))
bf16 = jnp.bfloat16
f32 = jnp.float32
VM = pl.BlockSpec(memory_space=pltpu.VMEM)
SDS = jax.ShapeDtypeStruct


def mm(a, b, dims=NN):
    return lax.dot_general(a, b, dims, preferred_element_type=f32)


class Fetch:
    def __init__(self, src, dst, sem):
        self.dst, self.copy = dst, pltpu.make_async_copy(src, dst, sem)
        self.copy.start()
        self.waiting = True

    def __call__(self):
        if self.waiting:
            self.copy.wait()
            self.waiting = False
        return self.dst


class Pieces:
    def __init__(self, copies, dst):
        self.copies, self.dst = copies, dst
        for c in copies:
            c.start()

    def __call__(self):
        for c in self.copies:
            c.wait()
        self.copies = []
        return self.dst


def pieces(info, a, b, dst, sem, z_first):
    part = a.shape[0] // 2
    copies = []
    for src, other in ((a, 0), (b, 1)):
        for i in range(2):
            flips = (other, i) if z_first else (i, other)
            at = 2 * (info[3] ^ flips[0]) + (info[4] ^ flips[1])
            rows = pl.ds(pl.multiple_of(at * part, part), part)
            copies.append(pltpu.make_async_copy(src.at[pl.ds(i * part, part)], dst.at[rows], sem.at[len(copies)]))
    return Pieces(copies, dst)


class Flush:
    def __init__(self, src, dst, sem):
        self.src, self.copy = src, pltpu.make_async_copy(src, dst, sem)
        self.started = False

    def start(self):
        if not self.started:
            self.copy.start()
        self.started = True


def call(name, body, info, ins, outs, scratch=(), vmem=58, which=0, cost=1000, **static):
    far_in = [i for i, a in enumerate(ins) if isinstance(a, tuple)]
    pinned = [i for i in far_in if len(ins[i]) == 2]
    far_out = [i for i, o in enumerate(outs) if isinstance(o, list)]
    raw_in = [i for i, a in enumerate(ins) if isinstance(a, Raw)]
    raw_out = [i for i, o in enumerate(outs) if isinstance(o, Raw)]
    pinned += [i for i in raw_in if ins[i].pinned]
    any_in = far_in + raw_in
    arrays = [a[0] if isinstance(a, tuple) else a.value if isinstance(a, Raw) else a for a in ins]
    shapes = [o[0] if isinstance(o, list) else o.value if isinstance(o, Raw) else o for o in outs]
    picked = [a[1] if isinstance(a, tuple) else None for a in ins]
    n_in, n_out = len(ins), len(outs)

    def kernel(lengths_ref, which_ref, *refs):
        dp = lax.axis_index("dp")
        at = which_ref[0]
        info_ref = (lengths_ref[0], lengths_ref[1], lax.axis_index("tensor"), dp & 1, (dp >> 1) & 1, at, lengths_ref[at], lengths_ref)
        in_refs, refs = refs[:n_in], refs[n_in:]
        out_refs, refs = refs[:n_out], refs[n_out:]
        sem, refs = refs[-1], refs[:-1]
        buffers, rest = refs[: len(far_in) + len(far_out)], refs[len(far_in) + len(far_out) :]
        args = list(in_refs)
        for j, i in enumerate(far_in):
            view = picked[i][1]
            args[i] = Fetch(view(in_refs[i], info_ref), buffers[j], sem.at[j])
        results = list(out_refs)
        flushes = []
        for j, i in enumerate(far_out):
            at = len(far_in) + j
            results[i] = Flush(buffers[at], out_refs[i], sem.at[at])
            flushes.append(results[i])
        body(info_ref, *args, *results, *rest, **static)
        for i in far_in:
            args[i]()
        for f in flushes:
            f.start()
        for f in flushes:
            f.copy.wait()

    hbm = pl.BlockSpec(memory_space=pltpu.HBM)
    buffers = [pltpu.VMEM(picked[i][0], arrays[i].dtype) for i in far_in]
    buffers += [pltpu.VMEM(shapes[i].shape, shapes[i].dtype) for i in far_out]
    return pl.pallas_call(
        kernel,
        out_shape=[pltpu.HBM(o.shape, o.dtype) if i in far_out + raw_out else o for i, o in enumerate(shapes)],
        grid_spec=pltpu.PrefetchScalarGridSpec(
            num_scalar_prefetch=2,
            grid=(1,),
            in_specs=[hbm if i in pinned else pl.BlockSpec(memory_space=pl.ANY) if i in any_in else VM for i in range(n_in)],
            out_specs=[hbm if i in far_out + raw_out else VM for i in range(n_out)],
            scratch_shapes=[*buffers, *scratch, pltpu.SemaphoreType.DMA((max(1, len(far_in) + len(far_out)),))],
        ),
        compiler_params=pltpu.CompilerParams(vmem_limit_bytes=vmem << 20),
        cost_estimate=pl.CostEstimate(flops=cost, bytes_accessed=1000, transcendentals=0),
        name=name,
    )(info, jnp.full((1,), which, jnp.int32), *[pltpu.with_memory_space_constraint(a, pltpu.HBM) if i in pinned else a for i, a in enumerate(arrays)])


class Raw:
    def __init__(self, value, pinned=True):
        self.value, self.pinned = value, pinned


def ref(x):
    return x() if isinstance(x, Fetch) else x.src if isinstance(x, Flush) else x


def whole(a):
    return (a, (a.shape, lambda ref, info: ref))


def loose(a):
    return (*whole(a), None)


def prepare_kernel(info, out_in, bias, up_in, dn_in, pack, up_half, dn_half):
    for src, dst in ((up_in, up_half), (dn_in, dn_half)):
        dst.src[...] = src()[...]
        dst.start()
    out_w = out_in()
    width, d = out_w.shape
    pack.src[0:width, :] = out_w[...]
    pack.src[width : width + 8, :] = jnp.broadcast_to(bias[...].reshape(1, d), (8, d))


def prepare(info, out_w, bias, up, dn):
    width, d = out_w.shape
    part = up.shape[0] // 4
    view = lambda ref, info: ref.at[pl.ds(pl.multiple_of((2 * info[3] + info[4]) * part, part), part)]
    ins = [whole(out_w), bias, (up, ((part, d), view)), (dn, ((part, d), view))]
    return call("prepare", prepare_kernel, info, ins, [[SDS((width + 8, d), bf16)]] + [[SDS((part, d), bf16)]] * 2)


def head_cols(a, h, extra=()):
    lane = lax.broadcasted_iota(jnp.int32, a.shape, 1)
    out = jnp.where((lane >= HEAD * h) & (lane < HEAD * (h + 1)), a, jnp.zeros_like(a))
    for i, e in enumerate(extra):
        out = jnp.where(lane == WIDE + i, e, out)
    return out


def tail_cols(rows, values):
    lane = lax.broadcasted_iota(jnp.int32, (rows, LANES - WIDE), 1)
    out = jnp.zeros((rows, LANES - WIDE), f32)
    for i, v in enumerate(values):
        out = jnp.where(lane == i, v, out)
    return out.astype(bf16)


def attend_fwd_kernel(info, x_hbm, w_ref, b_ref, *rest):
    far, outs = rest[:5], rest[5:9]
    x_all, *near, v_t, s_all, sem_in, sem_out = rest[9:]
    q_all, k_all, v_all, lse_all, c_all = near
    me = info[2]
    batch, peers, width, block = c_all.shape
    seq = peers * block
    heads = width // HEAD

    def fetch(s):
        return pltpu.make_async_copy(x_hbm.at[s], x_all.at[s], sem_in.at[s])

    def flush(s, i):
        return pltpu.make_async_copy(near[i].at[s], far[i].at[s], sem_out.at[s, i])

    for s in range(batch):
        fetch(s).start()
    w = w_ref()

    def one_sequence(s, carry):
        length = info[7][s]
        fetch(s).wait()
        x = x_all[s]
        k_all[s, :, 0:WIDE] = mm(x, w[1], NT).astype(bf16)
        row = lax.broadcasted_iota(jnp.int32, (seq, 1), 0)
        k_all[s, :, WIDE:LANES] = tail_cols(seq, (jnp.where(row < length, 0.0, -1e30),))
        q = mm(x, w[0], NT) + b_ref[0:1, :].astype(f32)
        q_all[s, :, 0:WIDE] = q.astype(bf16) * jnp.asarray(0.125, bf16)
        q_all[s, :, WIDE:LANES] = tail_cols(seq, (1.0,))
        v = (mm(x, w[2], NT) + b_ref[1:2, :].astype(f32)).astype(bf16)
        v_all[s] = v
        v_t[...] = v.T
        for i in range(3):
            flush(s, i).start()

        def two_blocks(n, carry):
            qb = q_all[s, pl.ds(pl.multiple_of(n * 2 * block, 2 * block), 2 * block), :]
            one = jnp.ones_like(qb[:, 0:1])
            for h in range(heads):
                s_all[h] = mm(k_all[s], head_cols(qb, h, (one,)), NT)
            for h in range(heads):
                top = jnp.max(s_all[h], axis=0, keepdims=True)
                p = jnp.exp(s_all[h] - top)
                total = jnp.sum(p, axis=0, keepdims=True)
                rows = slice(HEAD * h, HEAD * (h + 1))
                out = (mm(v_t[rows, :], p.astype(bf16)) * (1.0 / total)).astype(bf16)
                lse = top + jnp.log(total)
                for j in range(2):
                    cols = slice(block * j, block * (j + 1))
                    c_all[s, 2 * n + j, rows, :] = out[:, cols]
                    lse_all[s, 2 * n + j, h : h + 1, :] = lse[:, cols]
            return carry

        lax.fori_loop(0, peers // 2, two_blocks, 0)
        for i in range(3, 5):
            flush(s, i).start()
        for k, out in enumerate(outs):
            out.src[s] = c_all[s, me ^ k]
        return carry

    lax.fori_loop(0, batch, one_sequence, 0)
    for out in outs:
        out.start()
    for s in range(batch):
        for i in range(5):
            flush(s, i).wait()


def attend_fwd(info, inputs, w_t, bias, peers):
    batch, seq, d = inputs.shape
    width = w_t.shape[1]
    block = seq // peers
    far = [SDS((batch, seq, LANES), bf16)] * 2 + [SDS((batch, seq, width), bf16)]
    far += [SDS((batch, peers, 8, block), f32), SDS((batch, peers, width, block), bf16)]
    scratch = [pltpu.VMEM(inputs.shape, bf16), *[pltpu.VMEM(o.shape, o.dtype) for o in far]]
    scratch += [pltpu.VMEM((width, seq), bf16), pltpu.VMEM((width // HEAD, seq, 2 * block), f32)]
    scratch += [pltpu.SemaphoreType.DMA((batch,)), pltpu.SemaphoreType.DMA((batch, 5))]
    return call(
        "attend_fwd",
        attend_fwd_kernel,
        info,
        [Raw(inputs), whole(w_t), bias],
        [Raw(o) for o in far] + [[SDS((batch, width, block), bf16)]] * peers,
        scratch,
    )


def nth(at, ref, info):
    return ref.at[at]


def of_sequence(a):
    return (a, (a.shape[1:], lambda ref, info: ref.at[info[5]]))


def attend_bwd_kernel(info, x_ref, q_in, k_in, v_in, lse_in, c_in, *rest):
    w_ref = x_ref
    peers = 4
    gs, rest = rest[:peers], rest[peers:]
    keep, send, low_out, db_ref, dq_t, dk, dv, k_t, g_ref = rest
    low = low_out.src
    length = info[6]
    me = info[2]
    k_ref, q_ref, v_ref = k_in(), q_in(), v_in()
    lse_ref, c_ref = lse_in(), c_in()
    _, width, block = c_ref.shape
    heads = width // HEAD
    k_t[...] = k_ref[:, 0:WIDE].T
    dk[...] = jnp.zeros_like(dk)
    dv[...] = jnp.zeros_like(dv)
    for k in range(peers):
        g_ref[me ^ k] = gs[k]()[...]

    def one_block(s, carry):
        at = pl.multiple_of(s * block, block)

        @pl.when(at >= length)
        def _():
            dq_t[:, pl.ds(at, block)] = jnp.zeros((width, block), f32)

        @pl.when(at < length)
        def _():
            qb = q_ref[pl.ds(at, block), :]
            g_t = g_ref[s]
            g = g_t.T
            prod_t = g_t.astype(f32) * c_ref[s].astype(f32)
            for h in range(heads):
                rows = slice(HEAD * h, HEAD * (h + 1))
                qh = head_cols(qb, h)
                gh = head_cols(g, h)
                scores = mm(k_ref[...], qh, NT)
                row = lax.broadcasted_iota(jnp.int32, scores.shape, 0)
                p = jnp.where(row < length, jnp.exp(scores - lse_ref[s, h : h + 1, :]), 0.0)
                dp = mm(v_ref[...], gh, NT)
                inner = jnp.sum(prod_t[rows], axis=0, keepdims=True)
                ds = (p * (dp - inner)).astype(bf16)
                dv[...] += mm(p.astype(bf16), gh)
                dk[...] += mm(ds, qh)
                dq_t[rows, pl.ds(at, block)] = mm(k_t[rows, :], ds) * 0.125

        return carry

    lax.fori_loop(0, peers, one_block, 0)
    low[0] = dq_t[...].T.astype(bf16)
    low[1] = dk[:, 0:WIDE].astype(bf16)
    low[2] = dv[...].astype(bf16)
    w = w_ref()
    for s in range(peers):
        at = pl.multiple_of((me ^ s) * block, block)
        total = sum(mm(low[i, pl.ds(at, block), :], w[i]) for i in range(3))
        (send if s % 2 else keep).src[s // 2] = total.astype(bf16)
    send.start()
    keep.start()
    db_ref[...] = jnp.concatenate([rowsum(low[i].astype(f32)) for i in (0, 2)], axis=1)


def attend_bwd(which, info, w_t, q, k, v, lse, c, gs, d):
    _, peers, width, block = c.shape
    seq = peers * block
    outs = [[SDS((2, block, d), bf16)]] * 2 + [[SDS((3, seq, width), bf16)], SDS((1, 2 * width), f32)]
    scratch = [
        pltpu.VMEM((width, seq), f32),
        pltpu.VMEM((seq, LANES), f32),
        pltpu.VMEM((seq, width), f32),
        pltpu.VMEM((width, seq), bf16),
        pltpu.VMEM((peers, width, block), bf16),
    ]
    ins = [whole(w_t)] + [of_sequence(a) for a in (q, k, v, lse, c)]
    ins += [(g, ((width, block), lambda ref, info: ref.at[info[5]]), None) for g in gs]
    return call("attend_bwd", attend_bwd_kernel, info, ins, outs, scratch, which=which, cost=2 * 10**10)


def project_grads_kernel(info, x0, low0, x1, low1, db0, db1, keep, send, db_ref, dw, acc, pair, *, parts):
    _, d, width = dw.shape
    x, low = x0(), low0()
    for i in range(3):
        acc[i] = mm(low[i].T, x[...])
    x, low = x1(), low1()
    for i in range(3):
        dw[i] = (acc[i] + mm(low[i].T, x[...])).T
    rows = d // parts
    half = 3 * rows // 2
    for b in range(parts):
        flat = dw[:, b * rows : (b + 1) * rows, :].reshape(3 * rows, width)
        flat = jnp.concatenate([flat[0:half], flat[half : 2 * half]], axis=1).astype(bf16)
        pair[(b & 1) ^ info[3], (b >> 1) * half : (b // 2 + 1) * half, :] = flat
    n = keep.src.shape[0]
    send.src[0:n, :] = pair[1]
    keep.src[...] = pair[0]
    db = db0[...] + db1[...]
    db_ref[...] = db
    high = db.astype(bf16)
    send.src[n : n + 8, :] = jnp.concatenate(
        [high, (db - high.astype(f32)).astype(bf16), jnp.zeros((6, 2 * width), bf16)], axis=0
    )
    send.start()


def gelu_parts(h):
    t = 1.0 / (1.0 + (0.3275911 * 0.7071067811865476) * jnp.abs(h))
    poly = t * (0.127414796 + t * (-0.142248368 + t * (0.7107068705 + t * (-0.7265760135 + t * 0.5307027145))))
    bell = jnp.exp2((-0.5 * 1.4426950408889634) * (h * h))
    tail = poly * bell
    cum = jnp.where(h < 0, tail, 1.0 - tail)
    return h * cum, cum + h * (bell * 0.3989422804014327)


def norm_parts(v):
    center = v - jnp.mean(v, axis=1, keepdims=True)
    r = lax.rsqrt(jnp.mean(center * center, axis=1, keepdims=True) + 1e-12)
    return center * r, r


def norm_back(u, gain, nv, r):
    gu = u * gain
    return r * (gu - jnp.mean(gu, axis=1, keepdims=True) - nv * jnp.mean(gu * nv, axis=1, keepdims=True))


def rows_of(vectors):
    return jnp.concatenate([v[...].reshape(1, -1).astype(f32) for v in vectors], axis=0)


def rowsum(v):
    return jnp.sum(v, axis=0, keepdims=True)


def first_norm_kernel(info, x_in, *rest):
    par, rest = rows_of(rest[:6]), rest[6:]
    nv_ref, r_ref, low0, low1, low = rest[8:]
    cs, packs = [c() for c in rest[:4]], [p() for p in rest[4:8]]
    x_ref = x_in()
    batch, rows = x_ref.shape[:2]
    width = cs[0].shape[1]

    def one_sequence(s, carry):
        here = pl.ds(pl.multiple_of(s * rows, rows), rows)
        total = par[0:1, :] + x_ref[s].astype(f32)
        for k in range(4):
            total = total + mm(cs[k][s], packs[k][0:width, :], TN)
        nv, r = norm_parts(total)
        nv_ref[here, :] = nv
        r_ref[here, :] = r
        low[s] = (nv * par[1:2, :] + par[2:3, :]).astype(bf16)
        return carry

    lax.fori_loop(0, batch, one_sequence, 0)
    low0[...] = low[0]
    low1[...] = low[1]


def feed_kernel(info, *rest, width, far):
    low, (pack, *rest) = rest[:4], rest[4:]
    if far:
        u_a, u_b, d_a, d_b, p_own, p_sib, act_out, slope_out, own, sib, both, up, dn, sem = rest
        up = pieces(info, u_a, u_b, up, sem.at[0], False)
        dn = pieces(info, d_a, d_b, dn, sem.at[1], True)
        up = up()
    else:
        u_in, d_in, act_out, slope_out, own, sib, both = rest
        up = u_in()
    act, slope = ref(act_out), ref(slope_out)
    units = up.shape[1]
    bias = pack()
    step = 256
    n = low[0].shape[0]
    for i, x in enumerate(low):
        both[i * n : (i + 1) * n, :] = x[...]
    n = 2 * n

    def chunk(m, carry):
        cols = pl.ds(pl.multiple_of(m * step, step), step)
        hidden = mm(both[...], up[:, cols]) + bias[width : width + 1, cols].astype(f32)
        a, g = gelu_parts(hidden)
        act[:, cols] = a.astype(bf16)
        slope[:, cols] = g.astype(bf16)
        return carry

    lax.fori_loop(0, units // step, chunk, 0)
    if far:
        dn = dn()
        total = mm(act[...], dn[...])
        sib[...] = (p_sib[...] + total[n:]).astype(bf16)
        own[...] = p_own[...] + total[:n]
    else:
        dn = d_in()
        total = mm(act[...], dn[...])
        own[...] = total[:n]
        sib[...] = total[n:]


def second_norm_kernel(info, cot_in, *rest):
    par, (nv_in, own, got, outs, gsec_out, gs_low, small) = rows_of(rest[:6]), rest[6:]
    cot, nv_ref, gsec = cot_in(), ref(nv_in), ref(gsec_out)
    batch, rows, d = cot.shape

    def one_sequence(s, sums):
        here = pl.ds(pl.multiple_of(s * rows, rows), rows)
        total = own[here, :] + got[here, :].astype(f32) + par[3:4, :] + (nv_ref[here, :] * par[1:2, :] + par[2:3, :])
        nv, r = norm_parts(total)
        outs.src[s] = (nv * par[4:5, :] + par[5:6, :]).astype(bf16)
        at = info[2] * rows + lax.broadcasted_iota(jnp.int32, (rows, 1), 0)
        seed = jnp.where(at < info[7][s], cot[s].astype(f32), 0.0)
        g = norm_back(seed, par[4:5, :], nv, r)
        gsec[here, :] = g
        gs_low[here, :] = g.astype(bf16)
        return tuple(a + rowsum(b) for a, b in zip(sums, (g, seed * nv, seed)))

    sums = lax.fori_loop(0, batch, one_sequence, (jnp.zeros((1, d), f32),) * 3)
    small[...] = jnp.concatenate([*sums, jnp.zeros((5, d), f32)], axis=0)


def feed_back_kernel(info, gs, gs2, slope0, slope1, up0, dn0, u_a, u_b, d_a, d_b, gh_out, own, sib, ub, sides, up2, dn2, sem):
    gh = ref(gh_out)
    units = up0.dst.shape[1]
    dn2 = pieces(info, d_a, d_b, dn2, sem.at[1], True)
    up2 = pieces(info, u_a, u_b, up2, sem.at[0], False)
    ub[...] = jnp.zeros_like(ub)
    n = gs.shape[0]
    sides[0:n, :] = gs[...]
    sides[n : 2 * n, :] = gs2[...]
    step = 256
    for k, slope in enumerate((ref(slope0), ref(slope1))):
        if k:
            dn = dn2()
        else:
            dn = dn0()

        def chunk(m, carry):
            cols = pl.ds(pl.multiple_of(m * step, step), step)
            ga = mm(sides[...], dn[cols, :], NT)
            h = (ga * slope[:, cols].astype(f32)).astype(bf16)
            gh[k, :, cols] = h
            ub[k : k + 1, cols] += rowsum(h.astype(f32))
            return carry

        lax.fori_loop(0, units // step, chunk, 0)
    up2 = up2()
    up = up0()
    total = mm(gh[0], up[...], NT) + mm(gh[1], up2[...], NT)
    sib[...] = total[n:].astype(bf16)
    own[...] = total[:n]


def first_back_kernel(info, *rest):
    par, (nv_in, r_ref, own, got, gsec_in, small2, *rest) = rows_of(rest[:6]), rest[6:]
    cs, packs = [c() for c in rest[:4]], rest[4:8]
    gfi, g0, g1, g2, g3, okeep, osend, small, ga_low = rest[8:]
    nv_ref, gsec = ref(nv_in), ref(gsec_in)
    packs = [p() for p in packs]
    n, d = own.shape
    rows = n // 2
    width = cs[0].shape[1]

    def one_sequence(s, sums):
        here = pl.ds(pl.multiple_of(s * rows, rows), rows)
        u = own[here, :] + got[here, :].astype(f32) + gsec[here, :]
        nv = nv_ref[here, :]
        g = norm_back(u, par[1:2, :], nv, r_ref[here, :])
        gfi.src[here, :] = g
        low = g.astype(bf16)
        ga_low[here, :] = low
        for k, out in enumerate((g0, g1, g2, g3)):
            out.src[s] = mm(packs[k][0:width, :], low, NT).astype(bf16)
        return tuple(a + rowsum(b) for a, b in zip(sums, (g, u * nv, u)))

    sums = lax.fori_loop(0, 2, one_sequence, (jnp.zeros((1, d), f32),) * 3)
    for out in (g3, g2, g1, g0, gfi):
        out.start()
    for k in range(4):
        total = mm(cs[k][0], ga_low[0:rows, :]) + mm(cs[k][1], ga_low[rows:n, :])
        (osend if k % 2 else okeep).src[k // 2, 0:width, :] = total.astype(bf16)
    both = jnp.concatenate([*sums, small2[0:3, :], jnp.zeros((2, d), f32)], axis=0)
    small[...] = both
    high = both.astype(bf16)
    osend.src[0, width : width + 8, :] = high
    osend.src[1, width : width + 8, :] = (both - high.astype(f32)).astype(bf16)


def down_grads_kernel(info, act0, act1, gs, gs2, far_keep, keep, send, scr, sides, *, parts):
    units = act0.shape[1]
    n = gs.shape[0]
    sides[0:n, :] = gs[...]
    sides[n : 2 * n, :] = gs2[...]
    block = units // parts
    step = 384
    for k, (act, mine) in enumerate(((act1, far_keep), (act0, keep))):

        def chunk(m, carry):
            cols = pl.ds(pl.multiple_of(m * step, step), step)
            total = mm(act[:, cols], sides[...], TN).astype(bf16)
            for i in range(step // block):
                scr[(i & 1) ^ info[3], m * (step // block // 2) + (i >> 1)] = total[i * block : (i + 1) * block]
            return carry

        lax.fori_loop(0, units // step, chunk, 0)
        send.src[k] = scr[1]
        mine.src[...] = scr[0]
    send.start()


def up_grads_kernel(info, *rest, parts, width):
    lows, (gh_in, okeep, ogot, small, ub, far_keep, far_send, keep, send, sums, scr, both_low) = rest[:4], rest[4:]
    n = lows[0].shape[0]
    for i, x in enumerate(lows):
        both_low[i * n : (i + 1) * n, :] = x[...]
    gh = ref(gh_in)
    units = both_low.shape[1]
    block = units // parts
    extra = width // parts
    joint = block + extra
    n = parts // 2 * joint
    step = 384
    got = ogot()
    both = small[...] + got[0, width : width + 8, :].astype(f32) + got[1, width : width + 8, :].astype(f32)
    both = jnp.concatenate([both[0:6], ub[0:2, :]], axis=0)
    sums[...] = both
    high = both.astype(bf16)
    far_send.src[n : n + 8, :] = high
    far_send.src[n + 8 : n + 16, :] = (both - high.astype(f32)).astype(bf16)
    for k, mine, theirs in ((1, far_keep, far_send), (0, keep, send)):

        def chunk(m, carry):
            cols = pl.ds(pl.multiple_of(m * step, step), step)
            total = mm(both_low[:, cols], gh[k], TN).astype(bf16)
            for i in range(step // block):
                at = (m * (step // block // 4) + (i >> 2)) * 2 + (i & 1)
                scr[((i >> 1) & 1) ^ info[4], at, 0:block, :] = total[i * block : (i + 1) * block]
            return carry

        lax.fori_loop(0, units // step, chunk, 0)
        o = (okeep()[k, 0:width, :].astype(f32) + got[k, 0:width, :].astype(f32)).astype(bf16)
        for b in range(parts):
            at = (b >> 2) * 2 + (b & 1)
            scr[((b >> 1) & 1) ^ info[4], at, block:joint, :] = o[b * extra : (b + 1) * extra]
        for b in range(parts // 2):
            theirs.src[b * joint : (b + 1) * joint, :] = scr[1, b]
            mine.src[b * joint : (b + 1) * joint, :] = scr[0, b]
        theirs.start()
        mine.start()


def swap(x, axis, bit):
    size = lax.axis_size(axis)
    return lax.ppermute(x, axis, [(i, i ^ bit) for i in range(size)])


def summed(parts):
    return sum(p.astype(f32) for p in parts)


def spread(array, axis, parts):
    bits = parts.bit_length() - 1
    return array.reshape(*array.shape[:axis], *([2] * bits), array.shape[axis] // parts, *array.shape[axis + 1 :])


def halve_sum(terms, axis, mine):
    other = [lax.dynamic_index_in_dim(t, 1 - mine, axis, keepdims=False) for t in terms]
    kept = [lax.dynamic_index_in_dim(t, mine, axis, keepdims=False) for t in terms]
    return kept, summed(other).astype(bf16)


def halve(terms, axis, bit, mine):
    other = [lax.dynamic_index_in_dim(t, 1 - mine, axis, keepdims=False) for t in terms]
    kept = [lax.dynamic_index_in_dim(t, mine, axis, keepdims=False) for t in terms]
    other = summed(other).astype(bf16)
    return kept + [swap(other, "dp", bit)], other


def body(
    inputs,
    cotangent,
    lengths,
    qkv_weight,
    qkv_bias,
    out_weight,
    out_bias,
    first_gain,
    first_shift,
    up_weight,
    up_bias,
    down_weight,
    down_bias,
    second_gain,
    second_shift,
):
    batch, seq, d = inputs.shape
    rows = cotangent.shape[1]
    n = batch * rows
    width = out_weight.shape[0]
    units = up_weight.shape[1]
    peers = lax.axis_size("tensor")
    parts = lax.axis_size("dp")
    bits = parts.bit_length() - 1
    t = lax.axis_index("tensor")
    dp = lax.axis_index("dp")
    bit_of = [(dp >> i) & 1 for i in range(bits)]
    info = lengths
    par = [out_bias, first_gain, first_shift, down_bias, second_gain, second_shift]
    w_t = jnp.transpose(qkv_weight, (1, 2, 0))
    pack, u_part, d_part = prepare(info, out_weight, up_bias, up_weight, down_weight)
    pack2 = swap(pack, "tensor", 2)
    pack1 = swap(pack, "tensor", 1)
    u_part = swap(u_part, "tensor", 2)
    d_part = swap(d_part, "tensor", 2)
    q, k, v, lse, c, *cs = attend_fwd(info, inputs, w_t, qkv_bias, peers)
    saved = (q, k, v, lse, c)
    *cs, pack1, pack2, u_part, d_part = after(*cs, pack1, pack2, u_part, d_part)
    ctx = [cs[0]] + [swap(cs[j], "tensor", j) for j in range(1, peers)]
    u_next, d_next = swap(u_part, "dp", 1), swap(d_part, "dp", 2)
    *ctx, u_next, d_next = after(*ctx, u_next, d_next)
    u2a = jnp.concatenate([u_part, u_next])
    d2a = jnp.concatenate([d_part, d_next])
    pack2, u2a, d2a = after(pack2, u2a, d2a)
    pack3 = swap(pack2, "tensor", 1)
    packs = [pack, pack1, pack2, pack3]
    u2b = swap(u2a, "dp", 2)
    d2b = swap(d2a, "dp", 1)
    far_ctx = [whole(ctx[0])] + [loose(x) for x in ctx[1:]]
    far_packs = [whole(pack)] + [loose(p) for p in packs[1:]]
    share = (inputs, ((batch, rows, d), lambda ref, info: ref.at[:, pl.ds(pl.multiple_of(info[2] * rows, rows), rows), :]))
    nv1, r1, *low = call(
        "first_norm",
        first_norm_kernel,
        info,
        [share, *par, *far_ctx, *far_packs],
        [SDS((n, d), f32), SDS((n, 1), f32), SDS((rows, d), bf16), SDS((rows, d), bf16)],
        [pltpu.VMEM((batch, rows, d), bf16)],
        vmem=NEAR,
    )
    low2 = [swap(x, "tensor", 1) for x in low]
    pair = SDS((2 * n, units), bf16)
    part = SDS((n, d), f32)
    sides = pltpu.VMEM((2 * n, d), bf16)
    act0, slope0, own, sib = call(
        "feed",
        feed_kernel,
        info,
        [*low, *low2, far_packs[0], whole(up_weight), whole(down_weight)],
        [pair, pair, part, part],
        [sides],
        vmem=NEAR,
        width=width,
        far=False,
    )
    halves = [Raw(x, False) for x in (u2a, u2b, d2a, d2b)]
    both = [pltpu.VMEM((d, units), bf16), pltpu.VMEM((units, d), bf16), pltpu.SemaphoreType.DMA((2, 4))]
    act1, slope1, own, sib = call(
        "feed",
        feed_kernel,
        info,
        [*low, *low2, far_packs[2], *halves, own, sib],
        [pair, pair, part, SDS((n, d), bf16)],
        [sides, *both],
        vmem=NEAR,
        width=width,
        far=True,
    )
    got = swap(sib, "tensor", 1)
    outputs, gsec, gs_low, small2 = call(
        "second_norm",
        second_norm_kernel,
        info,
        [whole(cotangent), *par, nv1, own, got],
        [[SDS((batch, rows, d), bf16)], part, SDS((n, d), bf16), SDS((8, d), f32)],
        vmem=NEAR,
    )
    gs_low2 = swap(gs_low, "tensor", 1)
    gh, own, sib, ub = call(
        "feed_back",
        feed_back_kernel,
        info,
        [gs_low, gs_low2, slope0, slope1, whole(up_weight), whole(down_weight), *halves],
        [SDS((2, 2 * n, units), bf16), part, SDS((n, d), bf16), SDS((8, d), f32)],
        [sides, *both],
        vmem=NEAR,
    )
    got = swap(sib, "tensor", 1)
    block = units // parts
    half_shape = (parts // 2, block, d)
    down_far_keep, down_keep, down_send = call(
        "down_grads",
        down_grads_kernel,
        info,
        [act0, act1, gs_low, gs_low2],
        [[SDS(half_shape, bf16)], [SDS(half_shape, bf16)], [SDS((2, *half_shape), bf16)]],
        [pltpu.VMEM((2, *half_shape), bf16), sides],
        vmem=NEAR,
        parts=parts,
    )
    down_got = swap(down_send, "dp", 1)
    got, down_far_keep = after(got, down_far_keep)
    gfi, g0, g1, g2, g3, okeep, osend, small1 = call(
        "first_back",
        first_back_kernel,
        info,
        [*par, nv1, r1, own, got, gsec, small2, *far_ctx, *far_packs],
        [
            [part],
            *[[SDS((batch, width, rows), bf16)]] * 4,
            *[[SDS((2, width + 8, d), bf16)]] * 2,
            SDS((8, d), f32),
        ],
        [pltpu.VMEM((n, d), bf16)],
        vmem=NEAR,
    )
    gctx = [g0] + [swap(g, "tensor", j) for j, g in ((1, g1), (2, g2), (3, g3))]
    got_o = swap(osend, "tensor", 1)
    joint = block + width // parts
    cut = parts // 2 * joint
    up_far_keep, up_far_send, up_keep, up_send, small = call(
        "up_grads",
        up_grads_kernel,
        info,
        [*low, *low2, gh, whole(okeep), loose(got_o), small1, ub],
        [
            [SDS((cut, d), bf16)],
            [SDS((cut + 16, d), bf16)],
            [SDS((cut, d), bf16)],
            [SDS((cut, d), bf16)],
            SDS((8, d), f32),
        ],
        [pltpu.VMEM((2, parts // 2, joint, d), bf16), sides],
        vmem=NEAR,
        parts=parts,
        width=width,
    )
    *gctx, up_far_send = after(*gctx, up_far_send)
    up_far_got = swap(up_far_send, "dp", 2)
    *gctx, up_far_keep = after(*gctx, up_far_keep)
    lows, biases, keeps = [], [], []
    for s in range(batch):
        keep, send, low_grads, db = attend_bwd(s, info, w_t, *saved, gctx, d)
        biases.append(db)
        if s == 0:
            send, up_far_got, down_got = after(send, up_far_got, down_got)
        else:
            send, low_grads, down_y, up_got, up_more, near = after(send, low_grads, down_y, up_got, up_more, near)
            keeps.append(near)
        keeps.append(keep)
        near = swap(send, "tensor", 1)
        if s == 0:
            lows.append(low_grads)
            down_sum = summed([down_far_keep, down_got[0]]).astype(bf16)
            shape = ([2] * (bits - 1)) + [joint, d]
            small = small + pair_sum(up_far_got, cut, 8)
            terms = [x.reshape(shape) for x in (up_far_keep, up_far_got[:cut])]
            up_far_kept, up_far_next = halve_sum(terms, bits - 2, bit_of[0])
            up_far_rows = with_rows(up_far_next, small)
            tied = after(down_sum, up_far_rows, up_send, *gctx)
            (down_sum, up_far_rows, up_send), gctx = tied[:3], tied[3:]
            down_y = swap(down_sum, "tensor", 2)
            up_got = swap(up_send, "dp", 2)
            up_more = swap(up_far_rows, "dp", 1)
    keeps.append(near)
    shape = ([2] * (bits - 1)) + [block, d]
    down_terms = [x.reshape(shape) for x in (down_keep, down_got[1], down_y)]
    down_kept, down_next = halve_sum(down_terms, bits - 2, bit_of[1])
    at = up_far_next.size // d
    small = small + pair_sum(up_more, at, 8)
    small = jnp.concatenate([small[0:6], small[7:8], small[6:7]])
    up_y_next = summed(up_far_kept + [up_more[:at].reshape(up_far_next.shape)]).astype(bf16)
    up_y_rows = with_rows(up_y_next, small)
    shape = ([2] * (bits - 1)) + [joint, d]
    up_kept, up_next = halve_sum([x.reshape(shape) for x in (up_keep, up_got)], bits - 2, bit_of[0])
    low_grads, down_next, up_y_rows, up_next = after(low_grads, down_next, up_y_rows, up_next)
    lows.append(low_grads)
    down_more = swap(down_next, "dp", 2)
    up_y = swap(up_y_rows, "tensor", 2)
    up_more = swap(up_next, "dp", 1)
    m = 3 * d // 4
    operands = []
    for s in range(batch):
        operands += [(inputs, (inputs.shape[1:], functools.partial(nth, s))), whole(lows[s])]
    w_keep, w_send, db = call(
        "project_grads",
        project_grads_kernel,
        info,
        [*operands, *biases],
        [[SDS((m, 2 * width), bf16)], [SDS((m + 8, 2 * width), bf16)], SDS((1, 2 * width), f32)],
        [pltpu.VMEM((3, d, width), f32), pltpu.VMEM((3, width, d), f32), pltpu.VMEM((2, m, 2 * width), bf16)],
        parts=parts,
    )
    w_send, down_more, up_y, up_more = after(w_send, down_more, up_y, up_more)
    keep0, near0, keep1, near1 = keeps
    in_sums = [summed([k[1], x[1]]).astype(bf16) for k, x in ((keep0, near0), (keep1, near1))]
    down_more, up_y, up_more, in_sums[1] = after(down_more, up_y, up_more, in_sums[1])
    got = swap(w_send, "dp", 1)
    in_sums[0], _ = after(in_sums[0], w_send)
    far = [swap(x, "tensor", 2) for x in in_sums]
    got, far[0] = after(got, far[0])
    down_terms = down_kept + [down_more]
    at = up_y_next.size // d
    small = jnp.concatenate([small[0:6], small[7:8], small[7:8]]) + pair_sum(up_y, at, 8)
    up_terms = up_kept + [up_more, up_y[:at].reshape(up_y_next.shape)]
    for i in range(2, bits):
        down_terms, sent = halve_sum(down_terms, bits - 1 - i, bit_of[i])
        down_got = swap(sent, "dp", 1 << i)
        up_terms, sent = halve_sum(up_terms, bits - 1 - i, bit_of[i])
        up_rows = with_rows(sent, small)
        if i == 2:
            got, down_got, up_rows = after(got, down_got, up_rows)
        up_got = swap(up_rows, "dp", 1 << i)
        if i == bits - 1:
            break
        down_terms, up_terms, small = with_received(down_terms, down_got, up_terms, up_got, sent, small)
    row = 3 * (d // parts) // 2
    at = parts // 2 * row
    shape = ([2] * (bits - 1)) + [row, 2 * width]
    terms = [x.reshape(shape) for x in (w_keep, got[:at])]
    db = db + got[at : at + 1].astype(f32) + got[at + 1 : at + 2].astype(f32)
    for i in range(1, bits):
        kept, rows_sent, more = halve_with(terms, terms[0].ndim - 3, db, "dp", 1 << i, bit_of[i])
        if i == bits - 1:
            _, down_got, up_got = after(rows_sent, down_got, up_got)
        terms, db = kept, db + more
    down_terms, up_terms, small = with_received(down_terms, down_got, up_terms, up_got, sent, small)
    down_sum = summed(down_terms)
    up_sum, out_sum = summed([x[:block] for x in up_terms]), summed([x[block:] for x in up_terms])
    mine = small
    input_grad = jnp.stack([
        (summed([k[0], x[0], y]) + gfi[s * rows : (s + 1) * rows]).astype(bf16)
        for s, (k, x, y) in enumerate(((keep0, near0, far[0]), (keep1, near1, far[1])))
    ])
    sides = [jnp.concatenate([x[:, :width], x[:, width:]], axis=0) for x in terms[:-1]]
    last = jnp.concatenate([terms[-1][:, :width], terms[-1][:, width:]], axis=0)
    qkv_sum = (summed(sides) + last.astype(f32)).reshape(3, -1, width)
    qkv_sum = jnp.transpose(qkv_sum, (1, 0, 2))
    db = db.reshape(2, width)
    return (
        outputs,
        input_grad,
        qkv_sum,
        db,
        out_sum,
        mine[0],
        mine[1],
        mine[2],
        up_sum,
        mine[6],
        down_sum,
        mine[3],
        mine[4],
        mine[5],
    )


def pair_sum(array, at, n):
    return array[at : at + n].astype(f32) + array[at + n : at + 2 * n].astype(f32)


def with_rows(array, rows):
    flat = array.reshape(-1, array.shape[-1])
    high = rows.astype(bf16)
    low = (rows - high.astype(f32)).astype(bf16)
    return jnp.concatenate([flat, high, low], axis=0)


def halve_with(terms, axis, rows, name, bit, mine):
    other = [lax.dynamic_index_in_dim(t, 1 - mine, axis, keepdims=False) for t in terms]
    kept = [lax.dynamic_index_in_dim(t, mine, axis, keepdims=False) for t in terms]
    other = summed(other).astype(bf16)
    sent = with_rows(other, rows)
    got = swap(sent, name, bit)
    cut = other.size // other.shape[-1]
    return kept + [got[:cut].reshape(other.shape)], sent, pair_sum(got, cut, rows.shape[0])


def with_received(down_terms, down_got, up_terms, up_got, sent, small):
    at = sent.size // sent.shape[-1]
    small = small + pair_sum(up_got, at, small.shape[0])
    return down_terms + [down_got], up_terms + [up_got[:at].reshape(sent.shape)], small


def after(*values):
    return lax.optimization_barrier(values)


def solution(mesh):
    in_specs = (
        P("dp", None, None),
        P("dp", "tensor", None),
        P("dp"),
        P(None, None, "tensor"),
        P(None, "tensor"),
        P("tensor", None),
        P(),
        P(),
        P(),
        P(None, "tensor"),
        P("tensor"),
        P("tensor", None),
        P(),
        P(),
        P(),
    )
    out_specs = (
        P("dp", "tensor", None),
        P("dp", "tensor", None),
        P("dp", None, "tensor"),
        P(None, "tensor"),
        P(("tensor", "dp"), None),
        P(),
        P(),
        P(),
        P("dp", "tensor"),
        P("tensor"),
        P(("tensor", "dp"), None),
        P(),
        P(),
        P(),
    )
    return jax.shard_map(body, mesh=mesh, in_specs=in_specs, out_specs=out_specs, check_vma=False)
```
